32 devices in a mesh: fsdp: 8 (over z, y), replica: 4 (over x, core).
Axes of the slice: x: 2, y: 2, z: 4, core: 2. Of those that a mesh axis runs over, the one named last changes fastest.
Arguments:
- layer_stack: bfloat16 [2, 32, 64, 9, 1024], P(None, ('fsdp', 'replica')), may hold values from -6 to 6
- out_cotangent: bfloat16 [2, 32, 64, 1024], P(None, ('fsdp', 'replica')), may hold values from -6 to 6
- pic_start: int32 [2, 32], P(None, ('fsdp', 'replica')), may hold values from 0 to 32, as said below
- doc_split: int32 [2, 32], P(None, ('fsdp', 'replica')), may hold values from 16 to 64, as said below
- mix_gain: float32 [1024], replicated, may hold values from 0.25 to 1.75
- mix_up: bfloat16 [1024, 36], P('fsdp'), may hold values from -0.1875 to 0.1875
- mix_down: float32 [36, 36], replicated, may hold values from -1 to 1
- mix_static: float32 [4, 9], replicated, may hold values from -1 to 1
- norm_gain: float32 [4, 1024], replicated, may hold values from 0.25 to 1.75
- norm_bias: float32 [4, 1024], replicated, may hold values from -2 to 2
- query_key_value: bfloat16 [3, 1024, 1024], P(None, 'fsdp'), may hold values from -0.1875 to 0.1875
- out_weight: bfloat16 [1024, 1024], P('fsdp'), may hold values from -0.75 to 0.75
- up_weight: bfloat16 [1024, 4096], P('fsdp'), may hold values from -0.1875 to 0.1875
- down_weight: bfloat16 [4096, 1024], P('fsdp'), may hold values from -0.125 to 0.125
Outputs:
- layer_output: bfloat16 [2, 32, 64, 1024], P(None, ('fsdp', 'replica'))
- coefficients: float32 [2, 32, 64, 4, 9], P(None, ('fsdp', 'replica'))
- stack_grad: bfloat16 [2, 32, 64, 9, 1024], P(None, ('fsdp', 'replica'))
- mix_gain_grad: float32 [1024], replicated
- mix_up_grad: float32 [1024, 36], P('fsdp')
- mix_down_grad: float32 [36, 36], replicated
- mix_static_grad: float32 [4, 9], replicated
- norm_gain_grad: float32 [4, 1024], replicated
- norm_bias_grad: float32 [4, 1024], replicated
- projection_grad: float32 [3, 1024, 1024], P(None, 'fsdp')
- out_weight_grad: float32 [1024, 1024], P('fsdp')
- up_weight_grad: float32 [1024, 4096], P('fsdp')
- down_weight_grad: float32 [4096, 1024], P('fsdp')
The draws below stay inside these ranges and needn't reach their ends.
Inputs may be any that keep to these rules, and one draw needn't show every extreme that they name: `pic_start`: a multiple of 16; the picture span lies inside its sequence. `doc_split`: a multiple of 16; 64 means a single document.
All inputs are finite; a program needn't handle non-finite values.
Results may differ from the reference program's by a relative error of at most 0.015.
Values may be sent and summed in bfloat16 or wider, within the bound.
No kernel may reach another device: no remote copies, remote signals or barrier semaphores. Data moves between devices by JAX's collectives and lax.ppermute only.
A program may use at most 256 MiB of HBM per device.

```python
import math
import jax
import jax.numpy as jnp
from jax import lax

D = 1024
FF = 4096
HEADS = 16
HEAD_DIM = 64
ROTARY = 16
STREAMS_IN = 9
MIX_HIDDEN = 36
SEQ = 64
PIC = 32
ALIGN = 16
MICRO = 2
BATCH = 32


def draw_pic_start(key, part):
    slots = (SEQ - PIC) // ALIGN + 1
    return (jax.random.randint(jax.random.fold_in(key, 11), (MICRO, BATCH), 0, slots) * ALIGN).astype(jnp.int32)


def draw_doc_split(key, part):
    slots = SEQ // ALIGN
    return (jax.random.randint(jax.random.fold_in(key, 23), (MICRO, BATCH), 1, slots + 1) * ALIGN).astype(jnp.int32)


def levels(key, dims, split, low, high):
    def one(dim, shards_of):
        draws = jax.random.uniform(jax.random.fold_in(jax.random.fold_in(key, 6), dim), (shards_of,), jnp.float32, low / len(split), high / len(split))
        return jnp.repeat(jnp.exp(draws), dims[dim] // shards_of).reshape((-1,) + (1,) * (len(dims) - dim - 1))

    loudness = one(*split[0])
    for cut in split[1:]:
        loudness = loudness * one(*cut)
    return loudness


def gaussian(stream_key, shape, width, limit, cuts=(), kind=jnp.bfloat16):
    factor_of = levels(stream_key, shape, cuts, -0.22, 0.18) if cuts else 1.0
    entries = jax.random.normal(stream_key, shape, jnp.float32) * width * factor_of
    return jnp.minimum(jnp.maximum(entries, -limit), limit).astype(kind)


def setup_inputs(seed: int = 0) -> dict:
    seeds = jax.random.split(jax.random.key(seed), 15)
    return {
        "layer_stack": gaussian(seeds[0], (MICRO, BATCH, SEQ, STREAMS_IN, D), 1.0, 6.0, ((1, 32),)),
        "out_cotangent": gaussian(seeds[1], (MICRO, BATCH, SEQ, D), 1.0, 6.0, ((1, 32),)),
        "pic_start": draw_pic_start(jax.random.fold_in(seeds[14], 71), 0),
        "doc_split": draw_doc_split(jax.random.fold_in(seeds[14], 71), 0),
        "mix_gain": jnp.clip(1.0 + 0.15 * jax.random.normal(seeds[4], (D,), jnp.float32), 0.25, 1.75),
        "mix_up": gaussian(seeds[5], (D, MIX_HIDDEN), D ** -0.5, 0.1875, ((0, 8),)),
        "mix_down": gaussian(seeds[6], (MIX_HIDDEN, 4 * STREAMS_IN), MIX_HIDDEN ** -0.5, 1.0, (), jnp.float32),
        "mix_static": jnp.clip(jax.random.uniform(seeds[7], (4, STREAMS_IN), jnp.float32, -1.0, 1.0), -1.0, 1.0),
        "norm_gain": jnp.clip(1.0 + 0.15 * jax.random.normal(seeds[8], (4, D), jnp.float32), 0.25, 1.75),
        "norm_bias": gaussian(seeds[9], (4, D), 0.3, 2.0, (), jnp.float32),
        "query_key_value": gaussian(seeds[10], (3, D, D), D ** -0.5, 0.1875, ((1, 8),)),
        "out_weight": gaussian(seeds[11], (D, D), (D // 16) ** -0.5, 0.75, ((0, 8),)),
        "up_weight": gaussian(seeds[12], (D, FF), D ** -0.5, 0.1875, ((0, 8),)),
        "down_weight": gaussian(seeds[13], (FF, D), (FF // 2) ** -0.5, 0.125, ((0, 8),)),
    }


@jax.custom_vjp
def low(v):
    return lax.optimization_barrier(v.astype(jnp.bfloat16)).astype(jnp.float32)

@jax.custom_vjp
def low_back(v):
    return v

def low_keep(v):
    return (low(v), None)

def low_pass(kept, grad):
    return (grad,)

def back_keep(v):
    return (v, None)

def back_low(kept, grad):
    return (low(grad),)
low.defvjp(low_keep, low_pass)
low_back.defvjp(back_keep, back_low)
EPSILON = 1e-05
HIGHEST = lax.Precision.HIGHEST

def layer_norm(values, gain_row, bias_row):
    center = values - lax.optimization_barrier(jnp.mean(values, axis=-1, keepdims=True))
    spread = lax.optimization_barrier(jnp.mean(center * center, axis=-1, keepdims=True))
    return center * lax.rsqrt(spread + EPSILON) * gain_row + bias_row

def rotary_tables():
    half_rot = ROTARY // 2
    inverse = jnp.exp(-math.log(10000.0) * (2.0 * jnp.arange(half_rot, dtype=jnp.float32) / ROTARY))
    angles = jnp.arange(SEQ, dtype=jnp.float32)[:, None] * inverse[None, :]
    return (jnp.cos(angles)[:, None, :], jnp.sin(angles)[:, None, :])

def rotate(values, cos_table, sin_table):
    half_rot = ROTARY // 2
    first_half = values[..., :half_rot]
    second = values[..., half_rot:ROTARY]
    return jnp.concatenate([first_half * cos_table - second * sin_table, second * cos_table + first_half * sin_table, values[..., ROTARY:]], axis=-1)

def allowed_mask(starts, splits):
    positions = jnp.arange(SEQ, dtype=jnp.int32)
    second_doc = positions[None, :] >= splits[:, None]
    picture = (positions[None, :] >= starts[:, None]) & (positions[None, :] < starts[:, None] + PIC)
    same_doc = second_doc[:, :, None] == second_doc[:, None, :]
    causal = positions[:, None] >= positions[None, :]
    both_pic = picture[:, :, None] & picture[:, None, :]
    return same_doc & (causal[None] | both_pic)

def forward(layer_stack, mix_gain, mix_up, mix_down, mix_static, norm_gain, norm_bias, query_key_value, out_weight, up_weight, down_weight, starts, splits):
    seq_count = layer_stack.shape[0]
    model_width = layer_stack.shape[-1]
    last_layer = layer_stack[:, :, STREAMS_IN - 1, :]
    rms_scale = lax.rsqrt(lax.optimization_barrier(jnp.mean(last_layer * last_layer, axis=-1, keepdims=True)) + EPSILON)
    mixed_in = low(last_layer * rms_scale * mix_gain)
    hidden_pre = low_back(jnp.einsum('nsd,dk->nsk', mixed_in, mix_up, precision=HIGHEST))
    hidden_mix = low(jax.nn.gelu(hidden_pre, approximate=False))
    coef_rows = jnp.einsum('nsk,kc->nsc', hidden_mix, mix_down, precision=HIGHEST) + mix_static.reshape(-1)
    coef_rows = coef_rows.reshape(seq_count, SEQ, 4, STREAMS_IN)
    streams = jnp.einsum('nsrl,nsld->nsrd', coef_rows, layer_stack, precision=HIGHEST)
    normed = [low(layer_norm(streams[:, :, stream], norm_gain[stream], norm_bias[stream])) for stream in range(4)]
    linear = [low_back(jnp.einsum('nsd,de->nse', normed[stream], query_key_value[stream], precision=HIGHEST)) for stream in range(3)]
    head_shape = (seq_count, SEQ, HEADS, HEAD_DIM)
    cos_table, sin_table = rotary_tables()
    queries = low(rotate(linear[0].reshape(head_shape), cos_table, sin_table))
    key_rot = low(rotate(linear[1].reshape(head_shape), cos_table, sin_table))
    values = low(linear[2].reshape(head_shape))
    allowed = allowed_mask(starts, splits)
    scores = low_back(jnp.einsum('nqhe,nkhe->nhqk', queries, key_rot, precision=HIGHEST) * HEAD_DIM ** (-0.5))
    scores = jnp.where(allowed[:, None], scores, -1e+30)
    soft_probs = low(jax.nn.softmax(scores, axis=-1))
    attended = low(low_back(jnp.einsum('nhqk,nkhe->nqhe', soft_probs, values, precision=HIGHEST))).reshape(seq_count, SEQ, model_width)
    attn_out = low_back(jnp.einsum('nsd,de->nse', attended, out_weight, precision=HIGHEST))
    up_pre = low_back(jnp.einsum('nsd,df->nsf', normed[3], up_weight, precision=HIGHEST))
    gated_act = low(jax.nn.gelu(up_pre, approximate=False))
    feed_out = low_back(jnp.einsum('nsf,fd->nsd', gated_act, down_weight, precision=HIGHEST))
    return (streams[:, :, 3] + attn_out + feed_out, coef_rows)

def reference(layer_stack, out_cotangent, pic_start, doc_split, mix_gain, mix_up, mix_down, mix_static, norm_gain, norm_bias, query_key_value, out_weight, up_weight, down_weight):
    seq_total = MICRO * BATCH
    group_size = math.gcd(seq_total, max(1, 4096 // SEQ))
    step_count = seq_total // group_size
    model_width = layer_stack.shape[-1]
    stacks = layer_stack.reshape(step_count, group_size, SEQ, STREAMS_IN, model_width)
    cotangents = out_cotangent.reshape(step_count, group_size, SEQ, model_width)
    start_rows = pic_start.reshape(step_count, group_size).astype(jnp.int32)
    split_rows = doc_split.reshape(step_count, group_size).astype(jnp.int32)
    params = (mix_gain.astype(jnp.float32), mix_up.astype(jnp.float32), mix_down.astype(jnp.float32), mix_static.astype(jnp.float32), norm_gain.astype(jnp.float32), norm_bias.astype(jnp.float32), query_key_value.astype(jnp.float32), out_weight.astype(jnp.float32), up_weight.astype(jnp.float32), down_weight.astype(jnp.float32))

    def one_step(totals, pieces):
        stack_part, grad_part, start_part, split_part = pieces

        def wrapped(stack_float, *weights):
            return forward(stack_float, *weights, start_part, split_part)
        (result, coef_rows), pull = jax.vjp(wrapped, stack_part.astype(jnp.float32), *params)
        grads = pull((grad_part.astype(jnp.float32), jnp.zeros_like(coef_rows)))
        new_totals = tuple((total_item + grad_item for total_item, grad_item in zip(totals, grads[1:])))
        return (new_totals, (result.astype(jnp.bfloat16), coef_rows, grads[0].astype(jnp.bfloat16)))
    initial = tuple((jnp.zeros_like(item) for item in params))
    totals, (results, coef_all, stack_grads) = lax.scan(one_step, initial, (stacks, cotangents, start_rows, split_rows))
    layer_output = results.reshape(MICRO, BATCH, SEQ, model_width)
    coefficients = coef_all.reshape(MICRO, BATCH, SEQ, 4, STREAMS_IN)
    stack_grad = stack_grads.reshape(MICRO, BATCH, SEQ, STREAMS_IN, model_width)
    return (layer_output, coefficients, stack_grad, totals[0], totals[1], totals[2], totals[3], totals[4], totals[5], totals[6], totals[7], totals[8], totals[9])
```

```python
import math

import jax
import jax.numpy as jnp
from jax import lax
from jax.sharding import PartitionSpec as P

HEADS = 16
HEAD_DIM = 64
ROTARY = 16
STREAMS_IN = 9
SEQ = 64
PIC = 32


EPSILON = 1e-05
ROOT_HALF = 0.7071067811865476
NORMAL_PEAK = 0.3989422804014327
HIGHEST = lax.Precision.HIGHEST


def as_sent(value):

    def short(part):
        return part.astype(jnp.bfloat16) if part.dtype == jnp.float32 else part

    return jax.tree.map(short, value)


def gelu_value(values):
    return 0.5 * values * (1.0 + lax.erf(values * ROOT_HALF))


def gelu_slope(values):
    return 0.5 * (1.0 + lax.erf(values * ROOT_HALF)) + values * NORMAL_PEAK * jnp.exp(
        -0.5 * values * values
    )


def matmul(left_side, right_side):
    return jnp.dot(left_side, right_side, preferred_element_type=jnp.float32)


def outer_sum(left_side, right_side):
    return lax.dot_general(
        left_side, right_side, (((0,), (0,)), ((), ())), preferred_element_type=jnp.float32
    )


def back_product(left_side, right_side):
    return lax.dot_general(
        left_side, right_side, (((1,), (1,)), ((), ())), preferred_element_type=jnp.float32
    )


def rotary_tables():
    half_rot = ROTARY // 2
    inverse = jnp.exp(-math.log(10000.0) * (2.0 * jnp.arange(half_rot, dtype=jnp.float32) / ROTARY))
    angles = jnp.arange(SEQ, dtype=jnp.float32)[:, None] * inverse[None, :]
    return (jnp.cos(angles)[:, None, :], jnp.sin(angles)[:, None, :])


def rotate(values, cos_table, sin_table):
    half_rot = ROTARY // 2
    first_half = values[..., :half_rot]
    second = values[..., half_rot:ROTARY]
    return jnp.concatenate(
        [
            first_half * cos_table - second * sin_table,
            second * cos_table + first_half * sin_table,
            values[..., ROTARY:],
        ],
        axis=-1,
    )


def allowed_mask(starts, splits):
    positions = jnp.arange(SEQ, dtype=jnp.int32)
    second_doc = positions[None, :] >= splits[:, None]
    picture = (positions[None, :] >= starts[:, None]) & (positions[None, :] < starts[:, None] + PIC)
    same_doc = second_doc[:, :, None] == second_doc[:, None, :]
    causal = positions[:, None] >= positions[None, :]
    both_pic = picture[:, :, None] & picture[:, None, :]
    return same_doc & (causal[None] | both_pic)


def masked_scores(queries, key_rot, allowed):
    scores = jnp.einsum(
        "nqhe,nkhe->nhqk", queries, key_rot, preferred_element_type=jnp.float32
    ) * HEAD_DIM ** (-0.5)
    return jnp.where(allowed[:, None], scores, -1e30)


def on_device(
    layer_stack,
    out_cotangent,
    pic_start,
    doc_split,
    mix_gain,
    mix_up,
    mix_down,
    mix_static,
    norm_gain,
    norm_bias,
    query_key_value,
    out_weight,
    up_weight,
    down_weight,
):
    micro_total = layer_stack.shape[0]
    local_seqs = layer_stack.shape[1]
    model_width = layer_stack.shape[-1]
    groups = [(0, micro_total)]
    cos_table, sin_table = rotary_tables()
    output_list = []
    coef_list = []
    grad_list = []
    shard_total = None
    small_total = None
    for first_micro, micro_count in groups:
        seq_count = micro_count * local_seqs
        row_count = seq_count * SEQ
        head_shape = (seq_count, SEQ, HEADS, HEAD_DIM)
        flat_stack = layer_stack[first_micro : first_micro + micro_count].reshape(
            row_count, STREAMS_IN, model_width
        )
        grad_rows = out_cotangent[first_micro : first_micro + micro_count].reshape(
            row_count, model_width
        )
        starts = pic_start[first_micro : first_micro + micro_count].reshape(seq_count)
        splits = doc_split[first_micro : first_micro + micro_count].reshape(seq_count)
        allowed = allowed_mask(starts, splits)
        mix_up_full, projection_full, out_full = (
            lax.all_gather(mix_up, "fsdp", axis=0, tiled=True),
            lax.all_gather(query_key_value, "fsdp", axis=1, tiled=True),
            lax.all_gather(out_weight, "fsdp", axis=0, tiled=True),
        )
        up_full, down_full = (
            lax.all_gather(up_weight, "fsdp", axis=0, tiled=True),
            lax.all_gather(down_weight, "fsdp", axis=0, tiled=True),
        )
        last_layer = flat_stack[:, STREAMS_IN - 1, :].astype(jnp.float32)
        rms_scale = lax.rsqrt(jnp.mean(last_layer * last_layer, axis=-1, keepdims=True) + EPSILON)
        mixed_in = (last_layer * rms_scale * mix_gain).astype(jnp.bfloat16)
        hidden_pre = matmul(mixed_in, mix_up_full)
        hidden_mix = gelu_value(hidden_pre).astype(jnp.bfloat16)
        hidden_wide = hidden_mix.astype(jnp.float32)
        coef_flat = jnp.dot(hidden_wide, mix_down, precision=HIGHEST) + mix_static.reshape(-1)
        coef_rows = coef_flat.reshape(row_count, 4, STREAMS_IN)
        streams = coef_rows[:, :, 0, None] * flat_stack[:, None, 0, :].astype(jnp.float32)
        for layer_index in range(1, STREAMS_IN):
            streams = streams + coef_rows[:, :, layer_index, None] * flat_stack[
                :, None, layer_index, :
            ].astype(jnp.float32)
        center = streams - jnp.mean(streams, axis=-1, keepdims=True)
        inv_std = lax.rsqrt(jnp.mean(center * center, axis=-1, keepdims=True) + EPSILON)
        scaled = center * inv_std
        normed = (scaled * norm_gain + norm_bias).astype(jnp.bfloat16)
        query_lin = matmul(normed[:, 0], projection_full[0])
        key_lin = matmul(normed[:, 1], projection_full[1])
        value_lin = matmul(normed[:, 2], projection_full[2])
        queries = rotate(query_lin.reshape(head_shape), cos_table, sin_table).astype(jnp.bfloat16)
        key_rot = rotate(key_lin.reshape(head_shape), cos_table, sin_table).astype(jnp.bfloat16)
        values = value_lin.astype(jnp.bfloat16).reshape(head_shape)
        scores = masked_scores(queries, key_rot, allowed)
        row_top = jnp.max(scores, axis=-1, keepdims=True)
        exponent = jnp.exp(scores - row_top)
        row_total = jnp.sum(exponent, axis=-1, keepdims=True)
        soft_probs = exponent / row_total
        log_total = row_top + jnp.log(row_total)
        attended = (
            jnp.einsum(
                "nhqk,nkhe->nqhe",
                soft_probs.astype(jnp.bfloat16),
                values,
                preferred_element_type=jnp.float32,
            )
            .astype(jnp.bfloat16)
            .reshape(row_count, model_width)
        )
        attn_out = matmul(attended, out_full)
        up_pre = matmul(normed[:, 3], up_full)
        gated_act = gelu_value(up_pre).astype(jnp.bfloat16)
        feed_out = matmul(gated_act, down_full)
        output_list.append((streams[:, 3] + attn_out + feed_out).astype(jnp.bfloat16))
        coef_list.append(coef_rows)
        mix_up_back, projection_back, out_back = (
            lax.all_gather(mix_up, "fsdp", axis=0, tiled=True),
            lax.all_gather(query_key_value, "fsdp", axis=1, tiled=True),
            lax.all_gather(out_weight, "fsdp", axis=0, tiled=True),
        )
        up_back, down_back = (
            lax.all_gather(up_weight, "fsdp", axis=0, tiled=True),
            lax.all_gather(down_weight, "fsdp", axis=0, tiled=True),
        )
        grad_down = outer_sum(gated_act, grad_rows)
        grad_gated = back_product(grad_rows, down_back)
        grad_up_pre = (grad_gated * gelu_slope(up_pre)).astype(jnp.bfloat16)
        grad_up = outer_sum(normed[:, 3], grad_up_pre)
        grad_norm_feed = back_product(grad_up_pre, up_back)
        feed_shards = (
            lax.psum_scatter(
                grad_up.astype(jnp.bfloat16), "fsdp", scatter_dimension=0, tiled=True
            ).astype(jnp.float32),
            lax.psum_scatter(
                grad_down.astype(jnp.bfloat16), "fsdp", scatter_dimension=0, tiled=True
            ).astype(jnp.float32),
        )
        grad_out_weight = outer_sum(attended, grad_rows)
        grad_attended = back_product(grad_rows, out_back).astype(jnp.bfloat16).reshape(head_shape)
        scores_again = masked_scores(queries, key_rot, allowed)
        probs_again = jnp.exp(scores_again - log_total)
        grad_probs = jnp.einsum(
            "nqhe,nkhe->nhqk", grad_attended, values, preferred_element_type=jnp.float32
        )
        grad_value = (
            jnp.einsum(
                "nhqk,nqhe->nkhe",
                probs_again.astype(jnp.bfloat16),
                grad_attended,
                preferred_element_type=jnp.float32,
            )
            .astype(jnp.bfloat16)
            .reshape(row_count, model_width)
        )
        delta_rows = jnp.sum(probs_again * grad_probs, axis=-1, keepdims=True)
        grad_scores = (probs_again * (grad_probs - delta_rows)).astype(jnp.bfloat16)
        score_scale = HEAD_DIM ** (-0.5)
        grad_query_rot = (
            jnp.einsum("nhqk,nkhe->nqhe", grad_scores, key_rot, preferred_element_type=jnp.float32)
            * score_scale
        )
        grad_key_rot = (
            jnp.einsum("nhqk,nqhe->nkhe", grad_scores, queries, preferred_element_type=jnp.float32)
            * score_scale
        )
        grad_query = (
            rotate(grad_query_rot, cos_table, -sin_table)
            .astype(jnp.bfloat16)
            .reshape(row_count, model_width)
        )
        grad_key = (
            rotate(grad_key_rot, cos_table, -sin_table)
            .astype(jnp.bfloat16)
            .reshape(row_count, model_width)
        )
        grad_linear = (grad_query, grad_key, grad_value)
        grad_projection = jnp.stack(
            [outer_sum(normed[:, stream], grad_linear[stream]) for stream in range(3)]
        )
        grad_normed = jnp.stack(
            [back_product(grad_linear[stream], projection_back[stream]) for stream in range(3)]
            + [grad_norm_feed],
            axis=1,
        )
        gain_grad = jnp.sum(grad_normed * scaled, axis=0)
        bias_grad = jnp.sum(grad_normed, axis=0)
        grad_scaled = grad_normed * norm_gain
        grad_streams = inv_std * (
            grad_scaled
            - jnp.mean(grad_scaled, axis=-1, keepdims=True)
            - scaled * jnp.mean(grad_scaled * scaled, axis=-1, keepdims=True)
        )
        grad_streams = grad_streams + jnp.concatenate(
            [
                jnp.zeros((row_count, 3, model_width), jnp.float32),
                grad_rows[:, None, :].astype(jnp.float32),
            ],
            axis=1,
        )
        grad_coef = jnp.stack(
            [
                jnp.sum(
                    grad_streams * flat_stack[:, None, layer_index, :].astype(jnp.float32), axis=-1
                )
                for layer_index in range(STREAMS_IN)
            ],
            axis=-1,
        )
        grad_coef_flat = grad_coef.reshape(row_count, 4 * STREAMS_IN)
        static_grad = jnp.sum(grad_coef_flat, axis=0).reshape(4, STREAMS_IN)
        down_mix_grad = jnp.dot(hidden_wide.T, grad_coef_flat, precision=HIGHEST)
        grad_hidden = (
            jnp.dot(grad_coef_flat, mix_down.T, precision=HIGHEST) * gelu_slope(hidden_pre)
        ).astype(jnp.bfloat16)
        grad_mix_up = outer_sum(mixed_in, grad_hidden)
        grad_mixed = back_product(grad_hidden, mix_up_back)
        gain_mix_grad = jnp.sum(grad_mixed * last_layer * rms_scale, axis=0)
        weighted = grad_mixed * mix_gain
        grad_last = rms_scale * (
            weighted
            - last_layer
            * rms_scale
            * rms_scale
            * jnp.mean(weighted * last_layer, axis=-1, keepdims=True)
        )
        per_layer = [
            jnp.sum(coef_rows[:, :, layer_index, None] * grad_streams, axis=1)
            for layer_index in range(STREAMS_IN)
        ]
        per_layer[STREAMS_IN - 1] = per_layer[STREAMS_IN - 1] + grad_last
        grad_list.append(jnp.stack(per_layer, axis=1).astype(jnp.bfloat16))
        attention_shards = (
            lax.psum_scatter(
                grad_mix_up.astype(jnp.bfloat16), "fsdp", scatter_dimension=0, tiled=True
            ).astype(jnp.float32),
            lax.psum_scatter(
                grad_projection.astype(jnp.bfloat16), "fsdp", scatter_dimension=1, tiled=True
            ).astype(jnp.float32),
            lax.psum_scatter(
                grad_out_weight.astype(jnp.bfloat16), "fsdp", scatter_dimension=0, tiled=True
            ).astype(jnp.float32),
        )
        shards = attention_shards + feed_shards
        shards = jax.tree.map(
            lambda part: part.astype(jnp.float32), lax.psum(as_sent(shards), "replica")
        )
        smalls = (gain_mix_grad, down_mix_grad, static_grad, gain_grad, bias_grad)
        if shard_total is None:
            shard_total = shards
            small_total = smalls
        else:
            shard_total = tuple(
                (total_item + new_item for total_item, new_item in zip(shard_total, shards))
            )
            small_total = tuple(
                (total_item + new_item for total_item, new_item in zip(small_total, smalls))
            )
    small_total = lax.psum(small_total, ("fsdp", "replica"))
    layer_output = jnp.concatenate(output_list, axis=0).reshape(
        micro_total, local_seqs, SEQ, model_width
    )
    coefficients = jnp.concatenate(coef_list, axis=0).reshape(
        micro_total, local_seqs, SEQ, 4, STREAMS_IN
    )
    stack_grad = jnp.concatenate(grad_list, axis=0).reshape(
        micro_total, local_seqs, SEQ, STREAMS_IN, model_width
    )
    return (
        layer_output,
        coefficients,
        stack_grad,
        small_total[0],
        shard_total[0],
        small_total[1],
        small_total[2],
        small_total[3],
        small_total[4],
        shard_total[1],
        shard_total[2],
        shard_total[3],
        shard_total[4],
    )


def bits_swap(size, bit):
    return [(index, index ^ bit) for index in range(size)]


CORE_SWAP = bits_swap(4, 1)
X_SWAP = bits_swap(4, 2)
Y_SWAP = bits_swap(8, 1)
Z_SWAP_NEAR = bits_swap(8, 2)
Z_SWAP_FAR = bits_swap(8, 4)


def z_pairs(moves):
    return [(2 * src + col, 2 * dst + col) for src, dst in moves for col in range(2)]


def pick(cond, first, second):
    return jnp.where(cond, first, second)


def order_two(flag, own, other, axis):
    first = pick(flag == 0, own, other)
    second = pick(flag == 0, other, own)
    return jnp.concatenate([first, second], axis=axis)


def gather_fsdp(piece, z, y):
    up_first = lax.ppermute(piece, "fsdp", z_pairs([(0, 1), (1, 2), (2, 3)]))
    down_first = lax.ppermute(piece, "fsdp", z_pairs([(1, 0), (2, 1), (3, 2)]))
    side_own = lax.ppermute(piece, "fsdp", Y_SWAP)
    up_second = lax.ppermute(up_first, "fsdp", z_pairs([(1, 2), (2, 3)]))
    down_second = lax.ppermute(down_first, "fsdp", z_pairs([(1, 0), (2, 1)]))
    side_a = lax.ppermute(pick(z == 0, down_first, up_first), "fsdp", Y_SWAP)
    last = lax.ppermute(
        pick(z == 2, up_second, down_second), "fsdp", z_pairs([(2, 3), (1, 0)])
    )
    second_any = pick(z < 2, down_second, up_second)
    inner = (z == 1) | (z == 2)
    side_b = lax.ppermute(pick(inner, down_first, second_any), "fsdp", Y_SWAP)
    side_c = lax.ppermute(pick(inner, second_any, last), "fsdp", Y_SWAP)
    table = lambda values: jnp.asarray(values, jnp.int32)[z]
    out = jnp.zeros((8,) + piece.shape, piece.dtype)

    def put(out, value, z_from, col):
        return lax.dynamic_update_index_in_dim(out, value, 2 * z_from + col, 0)

    out = put(out, piece, z, y)
    out = put(out, side_own, z, 1 - y)
    near = pick(z == 0, down_first, up_first)
    out = put(out, near, table([1, 0, 1, 2]), y)
    out = put(out, side_a, table([1, 0, 1, 2]), 1 - y)
    middle = pick(inner, down_first, second_any)
    out = put(out, middle, table([2, 2, 3, 1]), y)
    out = put(out, side_b, table([2, 2, 3, 1]), 1 - y)
    far = pick(inner, second_any, last)
    out = put(out, far, table([3, 3, 0, 0]), y)
    out = put(out, side_c, table([3, 3, 0, 0]), 1 - y)
    return out


def scatter_fsdp(parts, z, y):
    def chunk(z_to, col):
        return lax.dynamic_index_in_dim(parts, 2 * z_to + col, 0, keepdims=False)

    def add(first, second):
        return (first.astype(jnp.float32) + second.astype(jnp.float32)).astype(jnp.bfloat16)

    table = lambda values: jnp.asarray(values, jnp.int32)[z]
    rounds = (table([3, 3, 0, 0]), table([2, 2, 1, 1]), table([1, 0, 3, 2]), z)
    sums = []
    for z_to in rounds:
        came = lax.ppermute(chunk(z_to, 1 - y), "fsdp", Y_SWAP)
        sums.append(add(chunk(z_to, y), came))
    first = lax.ppermute(sums[0], "fsdp", z_pairs([(0, 1), (3, 2)]))
    up_send = add(pick(z == 0, sums[1], sums[0]), first)
    down_send = add(pick(z == 3, sums[1], sums[0]), first)
    up_one = lax.ppermute(up_send, "fsdp", z_pairs([(0, 1), (1, 2)]))
    down_one = lax.ppermute(down_send, "fsdp", z_pairs([(3, 2), (2, 1)]))
    up_two = lax.ppermute(
        add(pick(z == 1, sums[1], sums[2]), up_one), "fsdp", z_pairs([(0, 1), (1, 2), (2, 3)])
    )
    down_two = lax.ppermute(
        add(pick(z == 2, sums[1], sums[2]), down_one), "fsdp", z_pairs([(3, 2), (2, 1), (1, 0)])
    )
    return (
        sums[3].astype(jnp.float32) + up_two.astype(jnp.float32) + down_two.astype(jnp.float32)
    )


def gather_group(block):
    across = lax.ppermute(block, "replica", X_SWAP)
    pair = jnp.stack([block, across])
    return jnp.concatenate([pair, lax.ppermute(pair, "replica", CORE_SWAP)])


def scatter_group(blocks):
    low = blocks.astype(jnp.bfloat16)
    half = blocks[:2] + lax.ppermute(low[2:], "replica", CORE_SWAP).astype(jnp.float32)
    came = lax.ppermute(half[1].astype(jnp.bfloat16), "replica", X_SWAP)
    return half[0] + came.astype(jnp.float32)


def on_device_tensor(
    layer_stack,
    out_cotangent,
    pic_start,
    doc_split,
    mix_gain,
    mix_up,
    mix_down,
    mix_static,
    norm_gain,
    norm_bias,
    query_key_value,
    out_weight,
    up_weight,
    down_weight,
):
    fsdp_index = lax.axis_index("fsdp")
    z, y = fsdp_index // 2, fsdp_index % 2
    member = lax.axis_index("replica")
    x, core = member // 2, member % 2
    micro_total, local_seqs, _, _, width = layer_stack.shape
    seqs = micro_total * local_seqs
    rows = seqs * SEQ
    flat_stack = layer_stack.reshape(rows, STREAMS_IN, width)
    grad_rows = out_cotangent.reshape(rows, width)

    def index(array, place, axis):
        return lax.dynamic_index_in_dim(array, place, axis, keepdims=False)

    head_place = 2 * core + x
    projection_piece = index(query_key_value.reshape(3, 128, 4, 4, 64), head_place, 3).reshape(
        384, 256
    )
    out_piece = lax.dynamic_slice(out_weight, (64 * x, 512 * core), (64, 512))
    out_piece = jnp.concatenate([out_piece[:, :256], out_piece[:, 256:]])
    attention_piece = jnp.concatenate([projection_piece, out_piece])
    up_piece = index(up_weight.reshape(128, 8, 4, 128), member, 2).reshape(128, width)
    down_piece = index(down_weight.reshape(4, 128, width), member, 0)
    feed_piece = jnp.concatenate([up_piece, down_piece])

    up_two = order_two(y, mix_up, lax.ppermute(mix_up, "fsdp", Y_SWAP), 0)
    up_four = order_two(z % 2, up_two, lax.ppermute(up_two, "fsdp", Z_SWAP_NEAR), 0)
    mix_up_full = order_two(z // 2, up_four, lax.ppermute(up_four, "fsdp", Z_SWAP_FAR), 0)

    attention_all = gather_fsdp(attention_piece, z, y)
    feed_all = gather_fsdp(feed_piece, z, y)

    bounds = jnp.concatenate([pic_start.reshape(seqs), doc_split.reshape(seqs)])
    bound_rows = jnp.zeros((16, width), jnp.bfloat16)
    bound_rows = bound_rows.at[: 2 * seqs, :].set(
        jnp.broadcast_to(bounds.astype(jnp.bfloat16)[:, None], (2 * seqs, width))
    )
    packet = gather_group(jnp.concatenate([grad_rows, bound_rows]))
    grad_group = packet[:, :rows].reshape(4 * rows, width)
    bound_group = packet[:, rows : rows + 2 * seqs, 0].astype(jnp.int32)
    starts = bound_group[:, :seqs].reshape(4 * seqs)
    splits = bound_group[:, seqs:].reshape(4 * seqs)

    last_layer = flat_stack[:, STREAMS_IN - 1, :].astype(jnp.float32)
    rms_scale = lax.rsqrt(jnp.mean(last_layer * last_layer, axis=-1, keepdims=True) + EPSILON)
    mixed_in = (last_layer * rms_scale * mix_gain).astype(jnp.bfloat16)
    hidden_pre = matmul(mixed_in, mix_up_full)
    hidden_mix = gelu_value(hidden_pre).astype(jnp.bfloat16)
    hidden_wide = hidden_mix.astype(jnp.float32)
    coef_flat = jnp.dot(hidden_wide, mix_down, precision=HIGHEST) + mix_static.reshape(-1)
    layers = [flat_stack[:, index_l, :].astype(jnp.float32) for index_l in range(STREAMS_IN)]

    def coef(stream, index_l):
        place = stream * STREAMS_IN + index_l
        return coef_flat[:, place : place + 1]

    streams = []
    for stream in range(4):
        total = coef(stream, 0) * layers[0]
        for index_l in range(1, STREAMS_IN):
            total = total + coef(stream, index_l) * layers[index_l]
        streams.append(total)
    scaled = []
    inv_std = []
    normed = []
    for stream in range(4):
        center = streams[stream] - jnp.mean(streams[stream], axis=-1, keepdims=True)
        inverse = lax.rsqrt(jnp.mean(center * center, axis=-1, keepdims=True) + EPSILON)
        inv_std.append(inverse)
        scaled.append(center * inverse)
        normed.append(
            (scaled[stream] * norm_gain[stream] + norm_bias[stream]).astype(jnp.bfloat16)
        )
    normed_group = gather_group(jnp.stack(normed))
    normed_group = jnp.swapaxes(normed_group, 0, 1).reshape(4, 4 * rows, width)

    group_seqs = 4 * seqs
    group_rows = 4 * rows
    projection = attention_all[:, :384].reshape(8, 3, 128, 256)
    projection = jnp.swapaxes(projection, 0, 1).reshape(3, width, 256)
    out_half = attention_all[:, 384:].reshape(4, 2, 2, 64, 256)
    out_half = jnp.swapaxes(out_half, 2, 3).reshape(4, 2, 64, 512)
    out_keep = index(out_half, core, 1)
    out_came = lax.ppermute(index(out_half, 1 - core, 1), "replica", CORE_SWAP)
    out_rows = order_two(core, out_keep, out_came, 2).reshape(256, width)
    head_shape = (group_seqs, SEQ, 4, HEAD_DIM)
    cos_table, sin_table = rotary_tables()
    linear = [matmul(normed_group[stream], projection[stream]) for stream in range(3)]
    queries = rotate(linear[0].reshape(head_shape), cos_table, sin_table).astype(jnp.bfloat16)
    key_rot = rotate(linear[1].reshape(head_shape), cos_table, sin_table).astype(jnp.bfloat16)
    values = linear[2].astype(jnp.bfloat16).reshape(head_shape)
    allowed = allowed_mask(starts, splits)
    scores = masked_scores(queries, key_rot, allowed)
    exponent = jnp.exp(scores - jnp.max(scores, axis=-1, keepdims=True))
    soft_probs = exponent / jnp.sum(exponent, axis=-1, keepdims=True)
    probs_low = soft_probs.astype(jnp.bfloat16)

    def pair(equation, first, second):
        return jnp.einsum(equation, first, second, preferred_element_type=jnp.float32)

    attended = pair("nhqk,nkhe->nqhe", probs_low, values).astype(jnp.bfloat16)
    attended = attended.reshape(group_rows, 256)
    grad_attended = back_product(grad_group, out_rows).astype(jnp.bfloat16).reshape(head_shape)
    grad_probs = pair("nqhe,nkhe->nhqk", grad_attended, values)
    grad_value = pair("nhqk,nqhe->nkhe", probs_low, grad_attended).astype(jnp.bfloat16)
    delta_rows = jnp.sum(soft_probs * grad_probs, axis=-1, keepdims=True)
    grad_scores = (soft_probs * (grad_probs - delta_rows)).astype(jnp.bfloat16)
    score_scale = HEAD_DIM ** (-0.5)
    grad_query = pair("nhqk,nkhe->nqhe", grad_scores, key_rot) * score_scale
    grad_key = pair("nhqk,nqhe->nkhe", grad_scores, queries) * score_scale
    grad_linear = [
        rotate(grad_query, cos_table, -sin_table).astype(jnp.bfloat16),
        rotate(grad_key, cos_table, -sin_table).astype(jnp.bfloat16),
        grad_value,
    ]
    grad_linear = [item.reshape(group_rows, 256) for item in grad_linear]
    attn_part = matmul(attended, out_rows)
    out_grad = outer_sum(attended, grad_group).astype(jnp.bfloat16).reshape(4, 64, 2, 512)
    projection_grad = jnp.stack(
        [outer_sum(normed_group[stream], grad_linear[stream]) for stream in range(3)]
    ).astype(jnp.bfloat16)
    norm_parts = [back_product(grad_linear[stream], projection[stream]) for stream in range(3)]

    up_all = feed_all[:, :128].reshape(width, width)
    down_all = feed_all[:, 128:].reshape(width, width)
    up_pre = matmul(normed_group[3], up_all)
    gated_act = gelu_value(up_pre).astype(jnp.bfloat16)
    feed_part = matmul(gated_act, down_all)
    grad_gated = back_product(grad_group, down_all)
    grad_up_pre = (grad_gated * gelu_slope(up_pre)).astype(jnp.bfloat16)
    down_grad = outer_sum(gated_act, grad_group).astype(jnp.bfloat16)
    up_grad = outer_sum(normed_group[3], grad_up_pre).astype(jnp.bfloat16)
    norm_parts.append(back_product(grad_up_pre, up_all))

    feed_parts = jnp.concatenate(
        [up_grad.reshape(8, 128, width), down_grad.reshape(8, 128, width)], axis=1
    )
    feed_shard = scatter_fsdp(feed_parts, z, y)
    out_keep = index(out_grad, core, 2)
    out_came = lax.ppermute(index(out_grad, 1 - core, 2), "replica", CORE_SWAP)
    out_even = pick(core == 0, out_keep, out_came)
    out_odd = pick(core == 0, out_came, out_keep)
    out_parts = jnp.stack([out_even, out_odd], axis=1).reshape(8, 64, 512)
    out_parts = jnp.concatenate([out_parts[..., :256], out_parts[..., 256:]], axis=1)
    projection_parts = jnp.swapaxes(projection_grad.reshape(3, 8, 128, 256), 0, 1)
    attention_parts = jnp.concatenate(
        [projection_parts.reshape(8, 384, 256), out_parts], axis=1
    )
    attention_shard = scatter_fsdp(attention_parts, z, y)

    def spread(shard):
        low = shard.astype(jnp.bfloat16)
        by_x = order_two(x, low[None], lax.ppermute(low, "replica", X_SWAP)[None], 0)
        came = lax.ppermute(by_x, "replica", CORE_SWAP)
        return order_two(core, by_x[:, None], came[:, None], 1).astype(jnp.float32)

    feed_full = spread(feed_shard)
    up_full_grad = feed_full[:, :, :128].reshape(4, 128, 8, 128)
    up_full_grad = jnp.transpose(up_full_grad, (1, 2, 0, 3)).reshape(128, 4 * width)
    down_full_grad = feed_full[:, :, 128:].reshape(512, width)
    attention_full = spread(attention_shard)
    projection_full_grad = attention_full[:, :, :384].reshape(2, 2, 3, 128, 4, 64)
    projection_full_grad = jnp.transpose(projection_full_grad, (2, 3, 4, 1, 0, 5)).reshape(
        3, 128, width
    )
    out_full_grad = attention_full[:, :, 384:].reshape(2, 2, 2, 64, 256)
    out_full_grad = jnp.transpose(out_full_grad, (0, 3, 1, 2, 4)).reshape(128, width)

    mixed_out = scatter_group((attn_part + feed_part).reshape(4, rows, width))
    layer_output = (streams[3] + mixed_out).astype(jnp.bfloat16)
    norm_blocks = jnp.stack([part.reshape(4, rows, width) for part in norm_parts], axis=1)
    grad_normed = scatter_group(norm_blocks)

    gain_rows = []
    bias_rows = []
    grad_streams = []
    for stream in range(4):
        grad_item = grad_normed[stream]
        gain_rows.append(jnp.sum(grad_item * scaled[stream], axis=0))
        bias_rows.append(jnp.sum(grad_item, axis=0))
        weighted = grad_item * norm_gain[stream]
        moved = inv_std[stream] * (
            weighted
            - jnp.mean(weighted, axis=-1, keepdims=True)
            - scaled[stream] * jnp.mean(weighted * scaled[stream], axis=-1, keepdims=True)
        )
        if stream == 3:
            moved = moved + grad_rows.astype(jnp.float32)
        grad_streams.append(moved)
    grad_coef = jnp.stack(
        [
            jnp.sum(grad_streams[stream] * layers[index_l], axis=-1)
            for stream in range(4)
            for index_l in range(STREAMS_IN)
        ],
        axis=-1,
    )
    static_row = jnp.sum(grad_coef, axis=0)
    down_mix_part = jnp.dot(hidden_wide.T, grad_coef, precision=HIGHEST)
    grad_hidden = (
        jnp.dot(grad_coef, mix_down.T, precision=HIGHEST) * gelu_slope(hidden_pre)
    ).astype(jnp.bfloat16)
    mix_up_part = outer_sum(grad_hidden, mixed_in)
    grad_mixed = back_product(grad_hidden, mix_up_full)
    gain_mix_row = jnp.sum(grad_mixed * last_layer * rms_scale, axis=0)
    weighted = grad_mixed * mix_gain
    grad_last = rms_scale * (
        weighted
        - last_layer
        * rms_scale
        * rms_scale
        * jnp.mean(weighted * last_layer, axis=-1, keepdims=True)
    )
    per_layer = []
    for index_l in range(STREAMS_IN):
        total = coef(0, index_l) * grad_streams[0]
        for stream in range(1, 4):
            total = total + coef(stream, index_l) * grad_streams[stream]
        per_layer.append(total)
    per_layer[-1] = per_layer[-1] + grad_last
    stack_grad = jnp.stack(per_layer, axis=1).astype(jnp.bfloat16)

    wide = jnp.concatenate(
        [mix_up_part, jnp.stack(gain_rows), jnp.stack(bias_rows), gain_mix_row[None]]
    )
    narrow = jnp.concatenate([down_mix_part, static_row[None], jnp.zeros((8, 36), jnp.float32)])
    small = jnp.concatenate([wide, jnp.pad(narrow, ((0, 0), (0, 92)))], axis=1)
    for axis_name, perm in (
        ("replica", CORE_SWAP),
        ("replica", X_SWAP),
        ("fsdp", Y_SWAP),
        ("fsdp", Z_SWAP_NEAR),
        ("fsdp", Z_SWAP_FAR),
    ):
        small = small + lax.ppermute(small, axis_name, perm)
    mix_up_grad = lax.dynamic_slice(small, (0, 128 * fsdp_index), (36, 128)).T
    shape = (micro_total, local_seqs, SEQ)
    return (
        layer_output.reshape(shape + (width,)),
        coef_flat.reshape(shape + (4, STREAMS_IN)),
        stack_grad.reshape(shape + (STREAMS_IN, width)),
        small[44, :width],
        mix_up_grad,
        small[:36, width : width + 36],
        small[36, width : width + 36].reshape(4, STREAMS_IN),
        small[36:40, :width],
        small[40:44, :width],
        projection_full_grad,
        out_full_grad,
        up_full_grad,
        down_full_grad,
    )


def solution(mesh):
    fits = mesh.shape["fsdp"] == 8 and mesh.shape["replica"] == 4
    body = on_device_tensor if fits else on_device
    return jax.shard_map(
        body,
        mesh=mesh,
        in_specs=(
            P(None, ("fsdp", "replica"), None, None, None),
            P(None, ("fsdp", "replica"), None, None),
            P(None, ("fsdp", "replica")),
            P(None, ("fsdp", "replica")),
            P(),
            P("fsdp", None),
            P(),
            P(),
            P(),
            P(),
            P(None, "fsdp", None),
            P("fsdp", None),
            P("fsdp", None),
            P("fsdp", None),
        ),
        out_specs=(
            P(None, ("fsdp", "replica"), None, None),
            P(None, ("fsdp", "replica"), None, None, None),
            P(None, ("fsdp", "replica"), None, None, None),
            P(),
            P("fsdp", None),
            P(),
            P(),
            P(),
            P(),
            P(None, "fsdp", None),
            P("fsdp", None),
            P("fsdp", None),
            P("fsdp", None),
        ),
        check_vma=False,
    )
```

```python
import math

import jax
import jax.numpy as jnp
import numpy as np
from jax import lax
from jax.experimental import pallas as pl
from jax.experimental.pallas import tpu as pltpu
from jax.sharding import PartitionSpec as P

HEADS = 16
HEAD_DIM = 64
ROTARY = 16
STREAMS_IN = 9
SEQ = 64
PIC = 32


EPSILON = 1e-05
ROOT_HALF = 0.7071067811865476
NORMAL_PEAK = 0.3989422804014327
HIGHEST = lax.Precision.HIGHEST


def as_sent(value):

    def short(part):
        return part.astype(jnp.bfloat16) if part.dtype == jnp.float32 else part

    return jax.tree.map(short, value)


def gelu_value(values):
    return 0.5 * values * (1.0 + lax.erf(values * ROOT_HALF))


def gelu_slope(values):
    return 0.5 * (1.0 + lax.erf(values * ROOT_HALF)) + values * NORMAL_PEAK * jnp.exp(
        -0.5 * values * values
    )


def matmul(left_side, right_side):
    return jnp.dot(left_side, right_side, preferred_element_type=jnp.float32)


def outer_sum(left_side, right_side):
    return lax.dot_general(
        left_side, right_side, (((0,), (0,)), ((), ())), preferred_element_type=jnp.float32
    )


def back_product(left_side, right_side):
    return lax.dot_general(
        left_side, right_side, (((1,), (1,)), ((), ())), preferred_element_type=jnp.float32
    )


def rotary_tables():
    half_rot = ROTARY // 2
    inverse = jnp.exp(-math.log(10000.0) * (2.0 * jnp.arange(half_rot, dtype=jnp.float32) / ROTARY))
    angles = jnp.arange(SEQ, dtype=jnp.float32)[:, None] * inverse[None, :]
    return (jnp.cos(angles)[:, None, :], jnp.sin(angles)[:, None, :])


def rotate(values, cos_table, sin_table):
    half_rot = ROTARY // 2
    first_half = values[..., :half_rot]
    second = values[..., half_rot:ROTARY]
    return jnp.concatenate(
        [
            first_half * cos_table - second * sin_table,
            second * cos_table + first_half * sin_table,
            values[..., ROTARY:],
        ],
        axis=-1,
    )


def allowed_mask(starts, splits):
    positions = jnp.arange(SEQ, dtype=jnp.int32)
    second_doc = positions[None, :] >= splits[:, None]
    picture = (positions[None, :] >= starts[:, None]) & (positions[None, :] < starts[:, None] + PIC)
    same_doc = second_doc[:, :, None] == second_doc[:, None, :]
    causal = positions[:, None] >= positions[None, :]
    both_pic = picture[:, :, None] & picture[:, None, :]
    return same_doc & (causal[None] | both_pic)


def masked_scores(queries, key_rot, allowed):
    scores = jnp.einsum(
        "nqhe,nkhe->nhqk", queries, key_rot, preferred_element_type=jnp.float32
    ) * HEAD_DIM ** (-0.5)
    return jnp.where(allowed[:, None], scores, -1e30)


def on_device(
    layer_stack,
    out_cotangent,
    pic_start,
    doc_split,
    mix_gain,
    mix_up,
    mix_down,
    mix_static,
    norm_gain,
    norm_bias,
    query_key_value,
    out_weight,
    up_weight,
    down_weight,
):
    micro_total = layer_stack.shape[0]
    local_seqs = layer_stack.shape[1]
    model_width = layer_stack.shape[-1]
    groups = [(0, micro_total)]
    cos_table, sin_table = rotary_tables()
    output_list = []
    coef_list = []
    grad_list = []
    shard_total = None
    small_total = None
    for first_micro, micro_count in groups:
        seq_count = micro_count * local_seqs
        row_count = seq_count * SEQ
        head_shape = (seq_count, SEQ, HEADS, HEAD_DIM)
        flat_stack = layer_stack[first_micro : first_micro + micro_count].reshape(
            row_count, STREAMS_IN, model_width
        )
        grad_rows = out_cotangent[first_micro : first_micro + micro_count].reshape(
            row_count, model_width
        )
        starts = pic_start[first_micro : first_micro + micro_count].reshape(seq_count)
        splits = doc_split[first_micro : first_micro + micro_count].reshape(seq_count)
        allowed = allowed_mask(starts, splits)
        mix_up_full, projection_full, out_full = (
            lax.all_gather(mix_up, "fsdp", axis=0, tiled=True),
            lax.all_gather(query_key_value, "fsdp", axis=1, tiled=True),
            lax.all_gather(out_weight, "fsdp", axis=0, tiled=True),
        )
        up_full, down_full = (
            lax.all_gather(up_weight, "fsdp", axis=0, tiled=True),
            lax.all_gather(down_weight, "fsdp", axis=0, tiled=True),
        )
        last_layer = flat_stack[:, STREAMS_IN - 1, :].astype(jnp.float32)
        rms_scale = lax.rsqrt(jnp.mean(last_layer * last_layer, axis=-1, keepdims=True) + EPSILON)
        mixed_in = (last_layer * rms_scale * mix_gain).astype(jnp.bfloat16)
        hidden_pre = matmul(mixed_in, mix_up_full)
        hidden_mix = gelu_value(hidden_pre).astype(jnp.bfloat16)
        hidden_wide = hidden_mix.astype(jnp.float32)
        coef_flat = jnp.dot(hidden_wide, mix_down, precision=HIGHEST) + mix_static.reshape(-1)
        coef_rows = coef_flat.reshape(row_count, 4, STREAMS_IN)
        streams = coef_rows[:, :, 0, None] * flat_stack[:, None, 0, :].astype(jnp.float32)
        for layer_index in range(1, STREAMS_IN):
            streams = streams + coef_rows[:, :, layer_index, None] * flat_stack[
                :, None, layer_index, :
            ].astype(jnp.float32)
        center = streams - jnp.mean(streams, axis=-1, keepdims=True)
        inv_std = lax.rsqrt(jnp.mean(center * center, axis=-1, keepdims=True) + EPSILON)
        scaled = center * inv_std
        normed = (scaled * norm_gain + norm_bias).astype(jnp.bfloat16)
        query_lin = matmul(normed[:, 0], projection_full[0])
        key_lin = matmul(normed[:, 1], projection_full[1])
        value_lin = matmul(normed[:, 2], projection_full[2])
        queries = rotate(query_lin.reshape(head_shape), cos_table, sin_table).astype(jnp.bfloat16)
        key_rot = rotate(key_lin.reshape(head_shape), cos_table, sin_table).astype(jnp.bfloat16)
        values = value_lin.astype(jnp.bfloat16).reshape(head_shape)
        scores = masked_scores(queries, key_rot, allowed)
        row_top = jnp.max(scores, axis=-1, keepdims=True)
        exponent = jnp.exp(scores - row_top)
        row_total = jnp.sum(exponent, axis=-1, keepdims=True)
        soft_probs = exponent / row_total
        log_total = row_top + jnp.log(row_total)
        attended = (
            jnp.einsum(
                "nhqk,nkhe->nqhe",
                soft_probs.astype(jnp.bfloat16),
                values,
                preferred_element_type=jnp.float32,
            )
            .astype(jnp.bfloat16)
            .reshape(row_count, model_width)
        )
        attn_out = matmul(attended, out_full)
        up_pre = matmul(normed[:, 3], up_full)
        gated_act = gelu_value(up_pre).astype(jnp.bfloat16)
        feed_out = matmul(gated_act, down_full)
        output_list.append((streams[:, 3] + attn_out + feed_out).astype(jnp.bfloat16))
        coef_list.append(coef_rows)
        mix_up_back, projection_back, out_back = (
            lax.all_gather(mix_up, "fsdp", axis=0, tiled=True),
            lax.all_gather(query_key_value, "fsdp", axis=1, tiled=True),
            lax.all_gather(out_weight, "fsdp", axis=0, tiled=True),
        )
        up_back, down_back = (
            lax.all_gather(up_weight, "fsdp", axis=0, tiled=True),
            lax.all_gather(down_weight, "fsdp", axis=0, tiled=True),
        )
        grad_down = outer_sum(gated_act, grad_rows)
        grad_gated = back_product(grad_rows, down_back)
        grad_up_pre = (grad_gated * gelu_slope(up_pre)).astype(jnp.bfloat16)
        grad_up = outer_sum(normed[:, 3], grad_up_pre)
        grad_norm_feed = back_product(grad_up_pre, up_back)
        feed_shards = (
            lax.psum_scatter(
                grad_up.astype(jnp.bfloat16), "fsdp", scatter_dimension=0, tiled=True
            ).astype(jnp.float32),
            lax.psum_scatter(
                grad_down.astype(jnp.bfloat16), "fsdp", scatter_dimension=0, tiled=True
            ).astype(jnp.float32),
        )
        grad_out_weight = outer_sum(attended, grad_rows)
        grad_attended = back_product(grad_rows, out_back).astype(jnp.bfloat16).reshape(head_shape)
        scores_again = masked_scores(queries, key_rot, allowed)
        probs_again = jnp.exp(scores_again - log_total)
        grad_probs = jnp.einsum(
            "nqhe,nkhe->nhqk", grad_attended, values, preferred_element_type=jnp.float32
        )
        grad_value = (
            jnp.einsum(
                "nhqk,nqhe->nkhe",
                probs_again.astype(jnp.bfloat16),
                grad_attended,
                preferred_element_type=jnp.float32,
            )
            .astype(jnp.bfloat16)
            .reshape(row_count, model_width)
        )
        delta_rows = jnp.sum(probs_again * grad_probs, axis=-1, keepdims=True)
        grad_scores = (probs_again * (grad_probs - delta_rows)).astype(jnp.bfloat16)
        score_scale = HEAD_DIM ** (-0.5)
        grad_query_rot = (
            jnp.einsum("nhqk,nkhe->nqhe", grad_scores, key_rot, preferred_element_type=jnp.float32)
            * score_scale
        )
        grad_key_rot = (
            jnp.einsum("nhqk,nqhe->nkhe", grad_scores, queries, preferred_element_type=jnp.float32)
            * score_scale
        )
        grad_query = (
            rotate(grad_query_rot, cos_table, -sin_table)
            .astype(jnp.bfloat16)
            .reshape(row_count, model_width)
        )
        grad_key = (
            rotate(grad_key_rot, cos_table, -sin_table)
            .astype(jnp.bfloat16)
            .reshape(row_count, model_width)
        )
        grad_linear = (grad_query, grad_key, grad_value)
        grad_projection = jnp.stack(
            [outer_sum(normed[:, stream], grad_linear[stream]) for stream in range(3)]
        )
        grad_normed = jnp.stack(
            [back_product(grad_linear[stream], projection_back[stream]) for stream in range(3)]
            + [grad_norm_feed],
            axis=1,
        )
        gain_grad = jnp.sum(grad_normed * scaled, axis=0)
        bias_grad = jnp.sum(grad_normed, axis=0)
        grad_scaled = grad_normed * norm_gain
        grad_streams = inv_std * (
            grad_scaled
            - jnp.mean(grad_scaled, axis=-1, keepdims=True)
            - scaled * jnp.mean(grad_scaled * scaled, axis=-1, keepdims=True)
        )
        grad_streams = grad_streams + jnp.concatenate(
            [
                jnp.zeros((row_count, 3, model_width), jnp.float32),
                grad_rows[:, None, :].astype(jnp.float32),
            ],
            axis=1,
        )
        grad_coef = jnp.stack(
            [
                jnp.sum(
                    grad_streams * flat_stack[:, None, layer_index, :].astype(jnp.float32), axis=-1
                )
                for layer_index in range(STREAMS_IN)
            ],
            axis=-1,
        )
        grad_coef_flat = grad_coef.reshape(row_count, 4 * STREAMS_IN)
        static_grad = jnp.sum(grad_coef_flat, axis=0).reshape(4, STREAMS_IN)
        down_mix_grad = jnp.dot(hidden_wide.T, grad_coef_flat, precision=HIGHEST)
        grad_hidden = (
            jnp.dot(grad_coef_flat, mix_down.T, precision=HIGHEST) * gelu_slope(hidden_pre)
        ).astype(jnp.bfloat16)
        grad_mix_up = outer_sum(mixed_in, grad_hidden)
        grad_mixed = back_product(grad_hidden, mix_up_back)
        gain_mix_grad = jnp.sum(grad_mixed * last_layer * rms_scale, axis=0)
        weighted = grad_mixed * mix_gain
        grad_last = rms_scale * (
            weighted
            - last_layer
            * rms_scale
            * rms_scale
            * jnp.mean(weighted * last_layer, axis=-1, keepdims=True)
        )
        per_layer = [
            jnp.sum(coef_rows[:, :, layer_index, None] * grad_streams, axis=1)
            for layer_index in range(STREAMS_IN)
        ]
        per_layer[STREAMS_IN - 1] = per_layer[STREAMS_IN - 1] + grad_last
        grad_list.append(jnp.stack(per_layer, axis=1).astype(jnp.bfloat16))
        attention_shards = (
            lax.psum_scatter(
                grad_mix_up.astype(jnp.bfloat16), "fsdp", scatter_dimension=0, tiled=True
            ).astype(jnp.float32),
            lax.psum_scatter(
                grad_projection.astype(jnp.bfloat16), "fsdp", scatter_dimension=1, tiled=True
            ).astype(jnp.float32),
            lax.psum_scatter(
                grad_out_weight.astype(jnp.bfloat16), "fsdp", scatter_dimension=0, tiled=True
            ).astype(jnp.float32),
        )
        shards = attention_shards + feed_shards
        shards = jax.tree.map(
            lambda part: part.astype(jnp.float32), lax.psum(as_sent(shards), "replica")
        )
        smalls = (gain_mix_grad, down_mix_grad, static_grad, gain_grad, bias_grad)
        if shard_total is None:
            shard_total = shards
            small_total = smalls
        else:
            shard_total = tuple(
                (total_item + new_item for total_item, new_item in zip(shard_total, shards))
            )
            small_total = tuple(
                (total_item + new_item for total_item, new_item in zip(small_total, smalls))
            )
    small_total = lax.psum(small_total, ("fsdp", "replica"))
    layer_output = jnp.concatenate(output_list, axis=0).reshape(
        micro_total, local_seqs, SEQ, model_width
    )
    coefficients = jnp.concatenate(coef_list, axis=0).reshape(
        micro_total, local_seqs, SEQ, 4, STREAMS_IN
    )
    stack_grad = jnp.concatenate(grad_list, axis=0).reshape(
        micro_total, local_seqs, SEQ, STREAMS_IN, model_width
    )
    return (
        layer_output,
        coefficients,
        stack_grad,
        small_total[0],
        shard_total[0],
        small_total[1],
        small_total[2],
        small_total[3],
        small_total[4],
        shard_total[1],
        shard_total[2],
        shard_total[3],
        shard_total[4],
    )


ROWS = 128
WIDTH = 1024
VMEM_FULL = pl.BlockSpec(memory_space=pltpu.VMEM)
SMEM_FULL = pl.BlockSpec(memory_space=pltpu.SMEM)
IN_PLACE = pl.BlockSpec(memory_space=pl.ANY)


def bits_swap(size, bit):
    return [(index, index ^ bit) for index in range(size)]


CORE_SWAP = bits_swap(4, 1)
X_SWAP = bits_swap(4, 2)
Y_SWAP = bits_swap(8, 1)
Z_SWAP_NEAR = bits_swap(8, 2)
Z_SWAP_FAR = bits_swap(8, 4)


def z_pairs(moves):
    return [(2 * src + col, 2 * dst + col) for src, dst in moves for col in range(2)]


def pick(cond, first, second):
    return jnp.where(cond, first, second)


def order_two(flag, own, other, axis):
    first = pick(flag == 0, own, other)
    second = pick(flag == 0, other, own)
    return jnp.concatenate([first, second], axis=axis)


def after(value, *others):
    return lax.optimization_barrier((value,) + others)[0]


def gather_fsdp(piece, z, y, front):
    up_first = lax.ppermute(piece, "fsdp", z_pairs([(0, 1), (1, 2), (2, 3)]))
    down_first = lax.ppermute(piece, "fsdp", z_pairs([(1, 0), (2, 1), (3, 2)]))
    side_own = lax.ppermute(piece, "fsdp", Y_SWAP)
    early, late = front()
    up_second = lax.ppermute(after(up_first, early), "fsdp", z_pairs([(1, 2), (2, 3)]))
    down_second = lax.ppermute(after(down_first, early), "fsdp", z_pairs([(1, 0), (2, 1)]))
    near = pick(z == 0, down_first, up_first)
    side_near = lax.ppermute(near, "fsdp", Y_SWAP)
    last = lax.ppermute(
        after(pick(z == 2, up_second, down_second), side_own),
        "fsdp",
        z_pairs([(2, 3), (1, 0)]),
    )
    second_any = pick(z < 2, down_second, up_second)
    inner = (z == 1) | (z == 2)
    middle = pick(inner, down_first, second_any)
    side_middle = lax.ppermute(after(middle, side_own), "fsdp", Y_SWAP)
    far = pick(inner, second_any, last)
    side_far = lax.ppermute(after(far, side_near, late), "fsdp", Y_SWAP)
    pieces = [piece, side_own, near, side_near, middle, side_middle, far, side_far]
    places = []
    for z_from in (z, table([1, 0, 1, 2], z), table([2, 2, 3, 1], z), table([3, 3, 0, 0], z)):
        places += [2 * z_from + y, 2 * z_from + 1 - y]
    return pieces, jnp.stack(places)


def table(values, z):
    return jnp.asarray(values, jnp.int32)[z]


def scatter_order(z, y):
    places = []
    for z_to in (table([3, 3, 0, 0], z), table([2, 2, 1, 1], z), table([1, 0, 3, 2], z), z):
        places += [2 * z_to + 1 - y, 2 * z_to + y]
    return jnp.stack(places)


def wide(value):
    return value.astype(jnp.float32)


def scatter_fsdp(chunks, z, first_wait, beside):
    def add(first, second):
        return (wide(first) + wide(second)).astype(jnp.bfloat16)

    came = []
    sums = []
    for turn in range(4):
        sent = chunks[2 * turn]
        if turn == 1:
            sent = after(sent, first_wait)
        if turn >= 2:
            sent = after(sent, came[turn - 2])
        came.append(lax.ppermute(sent, "fsdp", Y_SWAP))
        sums.append(add(chunks[2 * turn + 1], came[turn]))
    first = lax.ppermute(sums[0], "fsdp", z_pairs([(0, 1), (3, 2)]))
    up_send = add(pick(z == 0, sums[1], sums[0]), first)
    down_send = add(pick(z == 3, sums[1], sums[0]), first)
    up_one = lax.ppermute(up_send, "fsdp", z_pairs([(0, 1), (1, 2)]))
    down_one = lax.ppermute(down_send, "fsdp", z_pairs([(3, 2), (2, 1)]))
    last_wait = beside()
    up_two = lax.ppermute(
        after(add(pick(z == 1, sums[1], sums[2]), up_one), last_wait),
        "fsdp",
        z_pairs([(0, 1), (1, 2), (2, 3)]),
    )
    down_two = lax.ppermute(
        after(add(pick(z == 2, sums[1], sums[2]), down_one), last_wait),
        "fsdp",
        z_pairs([(3, 2), (2, 1), (1, 0)]),
    )
    return (wide(sums[3]) + wide(up_two) + wide(down_two)).astype(jnp.bfloat16)


def lanes_of(shape):
    return lax.broadcasted_iota(jnp.int32, shape, 1)


def rows_of(shape):
    return lax.broadcasted_iota(jnp.int32, shape, 0)


def prepare_kernel(place, projection, out_weight, up_weight, down_weight, piece):
    member, x, core = place[0], place[1], place[2]
    quarter, other = 2 * x + core, 2 * x + 1 - core
    lane = lanes_of((128, 128))
    for index in range(8):
        half = index % 2
        own = up_weight[:, pl.ds(pl.multiple_of((index * 4 + quarter) * 128, 128), 128)]
        extra = up_weight[:, pl.ds(pl.multiple_of(((index ^ 1) * 4 + other) * 128, 128), 128)]
        taken = (lane >= 96) & (core == half)
        piece[index // 2, :, half * 128 : half * 128 + 128] = jnp.where(
            taken, wide(extra), wide(own)
        ).astype(jnp.bfloat16)
    for stream in range(3):
        for twin in range(2):
            tiles = [
                wide(
                    projection[
                        stream,
                        :,
                        pl.ds(pl.multiple_of((2 * twin + low) * 256 + core * 128, 128), 128),
                    ]
                )
                for low in range(2)
            ]
            first = jnp.where(x == 0, tiles[0], pltpu.roll(tiles[0], 64, 1))
            second = jnp.where(x == 0, pltpu.roll(tiles[1], 64, 1), tiles[1])
            piece[4 + stream, :, twin * 128 : twin * 128 + 128] = jnp.where(
                lane < 64, first, second
            ).astype(jnp.bfloat16)
    own_row = pl.multiple_of(quarter * 128, 128)
    other_row = pl.multiple_of(other * 128, 128)
    head_row = pl.multiple_of(x * 64, 64)
    for block in range(4):
        cols = slice(block * 256, block * 256 + 256)
        piece[7 + block, 0:96] = down_weight[pl.ds(own_row, 96), cols]

        @pl.when(member % 2 == core)
        def _():
            piece[7 + block, 96:128] = out_weight[pl.ds(head_row, 32), cols]
            piece[11, block * 32 : block * 32 + 32] = out_weight[pl.ds(head_row + 32, 32), cols]

        @pl.when(member % 2 != core)
        def _():
            piece[7 + block, 96:128] = down_weight[pl.ds(own_row + 96, 32), cols]
            piece[11, block * 32 : block * 32 + 32] = down_weight[pl.ds(other_row + 96, 32), cols]


def front_kernel(
    bounds,
    stack,
    cotangent,
    mix_gain,
    mix_up,
    mix_down,
    mix_static,
    norm_gain,
    norm_bias,
    packet,
    scaled_out,
    stats,
    stream_out,
    streams,
):
    seqs = stack.shape[0]
    for seq in range(seqs):
        last = wide(stack[seq, STREAMS_IN - 1])
        rms = lax.rsqrt(jnp.mean(last * last, axis=-1, keepdims=True) + EPSILON)
        mixed_in = (last * rms * mix_gain[...]).astype(jnp.bfloat16)
        hidden_pre = back_product(mixed_in, mix_up[...])
        hidden = wide(gelu_value(hidden_pre).astype(jnp.bfloat16))
        coef = jnp.dot(
            hidden, mix_down[...], precision=HIGHEST, preferred_element_type=jnp.float32
        )
        coef = coef + mix_static[...]
        at = slice(seq * SEQ, seq * SEQ + SEQ)
        stats[0, at, 0:36] = coef
        stats[1, at, 0:36] = hidden_pre
        stats[2, at, 4:5] = rms
        packet[4 * ROWS + seq * SEQ : 4 * ROWS + seq * SEQ + SEQ] = cotangent[at]

        def mix(step, carry):
            row = pl.multiple_of(step // 2 * 16, 16)
            col = pl.multiple_of(step % 2 * 512, 512)
            rows_coef = stats[0, pl.ds(seq * SEQ + row, 16), :]
            totals = [None] * 4
            for layer in range(STREAMS_IN):
                value = wide(stack[seq, layer, pl.ds(row, 16), pl.ds(col, 512)])
                for stream in range(4):
                    at_coef = stream * STREAMS_IN + layer
                    term = rows_coef[:, at_coef : at_coef + 1] * value
                    totals[stream] = term if layer == 0 else totals[stream] + term
            for stream in range(4):
                streams[stream, pl.ds(seq * SEQ + row, 16), pl.ds(col, 512)] = totals[stream]
            return carry

        lax.fori_loop(0, 8, mix, 0)

    def norm(step, carry):
        row = pl.multiple_of(step * 16, 16)
        for stream in range(4):
            value = streams[stream, pl.ds(row, 16), :]
            center = value - jnp.mean(value, axis=-1, keepdims=True)
            inverse = lax.rsqrt(jnp.mean(center * center, axis=-1, keepdims=True) + EPSILON)
            scaled = center * inverse
            stats[2, pl.ds(row, 16), stream : stream + 1] = inverse
            scaled_out[stream, pl.ds(row, 16), :] = scaled
            packet[pl.ds(stream * ROWS + row, 16), :] = (
                scaled * norm_gain[stream : stream + 1, :] + norm_bias[stream : stream + 1, :]
            ).astype(jnp.bfloat16)
            if stream == 3:
                stream_out[pl.ds(row, 16), :] = value
        return carry

    lax.fori_loop(0, seqs * SEQ // 16, norm, 0)
    packet[5 * ROWS :] = jnp.zeros((16, WIDTH), jnp.bfloat16)
    row = rows_of((16, 128))
    marks = jnp.zeros((16, 128), jnp.float32)
    for place in range(2 * seqs):
        marks = jnp.where(row == place, wide(bounds[place]), marks)
    packet[5 * ROWS :, 0:128] = marks.astype(jnp.bfloat16)


def main_kernel(
    place,
    origin,
    target,
    rope,
    packet0,
    packet1,
    packet2,
    packet3,
    piece0,
    piece1,
    piece2,
    piece3,
    piece4,
    piece5,
    piece6,
    piece7,
    chunk0,
    chunk1,
    chunk2,
    chunk3,
    chunk4,
    chunk5,
    chunk6,
    chunk7,
    keep,
    send,
    acts,
    marks,
    up_all,
    lin_all,
    down_all,
    out_all,
    linear,
    low_lin,
    parts,
    out_total,
    norm_total,
    sems,
    piece_sems,
    chunk_sems,
):
    core = place[2]
    packets = (packet0, packet1, packet2, packet3)
    pieces = (piece0, piece1, piece2, piece3, piece4, piece5, piece6, piece7)
    chunks = (chunk0, chunk1, chunk2, chunk3, chunk4, chunk5, chunk6, chunk7)
    copies = []
    for block in range(4):
        for unit in range(5):
            copies.append(
                pltpu.make_async_copy(
                    packets[block].at[pl.ds(unit * ROWS, ROWS)],
                    acts.at[unit, pl.ds(block * ROWS, ROWS)],
                    sems.at[block, unit],
                )
            )
        copies.append(
            pltpu.make_async_copy(
                packets[block].at[pl.ds(5 * ROWS, 16)], marks.at[block], sems.at[block, 5]
            )
        )
    for index in range(8):
        rows = pl.ds(pl.multiple_of(origin[index] * 128, 128), 128)
        piece = pieces[index]
        copies.append(
            pltpu.make_async_copy(
                piece.at[pl.ds(4, 3)], lin_all.at[:, rows], piece_sems.at[index, 0]
            )
        )
        copies.append(
            pltpu.make_async_copy(
                piece.at[pl.ds(0, 4)], up_all.at[:, rows], piece_sems.at[index, 1]
            )
        )
        copies.append(
            pltpu.make_async_copy(
                piece.at[pl.ds(7, 5)], down_all.at[origin[index]], piece_sems.at[index, 2]
            )
        )
    for copy in copies:
        copy.start()
    for copy in copies:
        copy.wait()
    for pair in range(4):
        even = 2 * pair + core
        odd = 2 * pair + 1 - core
        for block in range(4):
            band = slice(block * 32, block * 32 + 32)
            out_all[block, pair * 64 : pair * 64 + 32] = down_all[even, block, 96:128]
            out_all[block, pair * 64 + 32 : pair * 64 + 64] = down_all[even, 4, band]
            down_all[even, block, 96:128] = down_all[odd, 4, band]

    for stream in range(3):
        linear[stream] = matmul(acts[stream], lin_all[stream])
    total = None
    for block in range(4):
        term = back_product(acts[4, :, block * 256 : block * 256 + 256], out_all[block])
        total = term if total is None else total + term
    low_lin[3] = total.astype(jnp.bfloat16)
    cos_table = rope[0]
    sin_left = rope[1]
    sin_right = rope[2]

    def turn(value, sign):
        return (
            value * cos_table
            + pltpu.roll(value, 120, 1) * (sign * sin_left)
            + pltpu.roll(value, 8, 1) * (sign * sin_right)
        )

    def units(block, carry):
        row = rows_of((ROWS, ROWS))
        lane = lanes_of((ROWS, ROWS))
        bound = wide(marks[block])

        def both(first, second):
            by_lane = jnp.where(lane < SEQ, first, second)
            by_row = jnp.where(row < SEQ, first, second)
            return by_row, by_lane

        start_q, start_k = both(bound[0:1, 0:128], bound[1:2, 0:128])
        split_q, split_k = both(bound[2:3, 0:128], bound[3:4, 0:128])
        at_q = wide(row % SEQ)
        at_k = wide(lane % SEQ)
        same = (row // SEQ == lane // SEQ) & ((at_q >= split_q) == (at_k >= split_k))
        pic_q = (at_q >= start_q) & (at_q < start_q + PIC)
        pic_k = (at_k >= start_k) & (at_k < start_k + PIC)
        allowed = same & ((at_q >= at_k) | (pic_q & pic_k))
        span = pl.ds(pl.multiple_of(block * ROWS, ROWS), ROWS)
        for twin in range(2):
            cols = slice(twin * 128, twin * 128 + 128)
            query = turn(linear[0, span, cols], 1.0)
            key_wide = turn(linear[1, span, cols], 1.0)
            query_low = query.astype(jnp.bfloat16)
            key_low = key_wide.astype(jnp.bfloat16)
            value_low = linear[2, span, cols].astype(jnp.bfloat16)
            grad_att = low_lin[3, span, cols]
            grad_wide = wide(grad_att)
            got = []
            for head in range(2):
                inside = (lane // 64) == head
                query_head = jnp.where(inside, query, 0.0).astype(jnp.bfloat16)
                grad_head = jnp.where(inside, grad_wide, 0.0).astype(jnp.bfloat16)
                scores = back_product(query_head, key_low) * HEAD_DIM ** (-0.5)
                scores = jnp.where(allowed, scores, -1e30)
                exponent = jnp.exp(scores - jnp.max(scores, axis=-1, keepdims=True))
                probs = exponent / jnp.sum(exponent, axis=-1, keepdims=True)
                probs_low = probs.astype(jnp.bfloat16)
                attended = matmul(probs_low, value_low)
                grad_probs = back_product(grad_head, value_low)
                grad_value = outer_sum(probs_low, grad_att)
                delta = jnp.sum(probs * grad_probs, axis=-1, keepdims=True)
                grad_scores = (probs * (grad_probs - delta)).astype(jnp.bfloat16)
                grad_query = matmul(grad_scores, key_low)
                grad_key = outer_sum(grad_scores, query_low)
                got.append((attended, grad_query, grad_key, grad_value))
            merged = [jnp.where(lane < 64, low, high) for low, high in zip(*got)]
            scale = HEAD_DIM ** (-0.5)
            low_lin[4, span, cols] = merged[0].astype(jnp.bfloat16)
            low_lin[0, span, cols] = turn(merged[1] * scale, -1.0).astype(jnp.bfloat16)
            low_lin[1, span, cols] = turn(merged[2] * scale, -1.0).astype(jnp.bfloat16)
            low_lin[2, span, cols] = merged[3].astype(jnp.bfloat16)
        return carry

    lax.fori_loop(0, 4, units, 0)

    def put(unit, value):
        low = value.astype(jnp.bfloat16)
        for block in range(2):
            keep[block, unit] = low[block * ROWS : block * ROWS + ROWS]
            send[block, unit] = low[(2 + block) * ROWS : (3 + block) * ROWS]

    for block in range(4):
        cols = slice(block * 256, block * 256 + 256)
        out_total[:, cols] = matmul(low_lin[4], out_all[block])
        grad = outer_sum(low_lin[4], acts[4, :, cols]).astype(jnp.bfloat16)
        for pair in range(4):
            even = 2 * pair + core
            parts[even, 7 + block, 96:128] = grad[pair * 64 : pair * 64 + 32]
            parts[even, 11, block * 32 : block * 32 + 32] = grad[pair * 64 + 32 : pair * 64 + 64]
    for stream in range(3):
        grad = outer_sum(acts[stream], low_lin[stream]).astype(jnp.bfloat16)
        for index in range(8):
            parts[index, 4 + stream] = grad[index * 128 : index * 128 + 128]
        put(stream, back_product(low_lin[stream], lin_all[stream]))

    norm_total[...] = jnp.zeros_like(norm_total)

    def hidden(pair, carry):
        up_pre = matmul(acts[3], up_all[pair])
        bell = 0.5 * (1.0 + lax.erf(up_pre * ROOT_HALF))
        gated = (up_pre * bell).astype(jnp.bfloat16)
        slope = bell + up_pre * NORMAL_PEAK * jnp.exp(-0.5 * up_pre * up_pre)
        grad_gated = None
        for block in range(4):
            cols = slice(block * 256, block * 256 + 256)
            rows_down = jnp.concatenate(
                [down_all[2 * pair, block], down_all[2 * pair + 1, block]], axis=0
            )
            term = back_product(acts[4, :, cols], rows_down)
            grad_gated = term if grad_gated is None else grad_gated + term
            out_total[:, cols] += matmul(gated, rows_down)
        grad_pre = (grad_gated * slope).astype(jnp.bfloat16)
        norm_total[...] += back_product(grad_pre, up_all[pair])
        grad = outer_sum(acts[3], grad_pre).astype(jnp.bfloat16)
        for index in range(8):
            parts[index, pair] = grad[index * 128 : index * 128 + 128]
        for block in range(4):
            cols = slice(block * 256, block * 256 + 256)
            grad = outer_sum(gated, acts[4, :, cols]).astype(jnp.bfloat16)
            even, odd = 2 * pair + core, 2 * pair + 1 - core
            for half in range(2):
                parts[2 * pair + half, 7 + block, 0:96] = grad[half * 128 : half * 128 + 96]

                @pl.when(core == half)
                def _():
                    parts[odd, 11, block * 32 : block * 32 + 32] = grad[
                        half * 128 + 96 : half * 128 + 128
                    ]

                @pl.when(core != half)
                def _():
                    parts[odd, 7 + block, 96:128] = grad[half * 128 + 96 : half * 128 + 128]

        return carry

    lax.fori_loop(0, 4, hidden, 0)
    sent = [
        pltpu.make_async_copy(parts.at[target[index]], chunks[index], chunk_sems.at[index])
        for index in range(8)
    ]
    for copy in sent:
        copy.start()
    put(3, norm_total[...])
    put(4, out_total[...])
    for copy in sent:
        copy.wait()


def back_kernel(
    stack,
    cotangent,
    scaled,
    stats,
    stream_in,
    keep,
    came,
    across,
    mix_gain,
    mix_up,
    mix_down,
    norm_gain,
    layer_output,
    stack_grad,
    small,
    grads,
    sums,
    coef_grad,
):
    seqs = stack.shape[0]
    sums[...] = jnp.zeros_like(sums)
    lane = lanes_of((16, 128))

    def unit(step, carry):
        row = pl.multiple_of(step * 16, 16)
        span = pl.ds(row, 16)

        def result(index):
            return wide(keep[0, index, span]) + wide(came[0, index, span]) + wide(across[index, span])

        layer_output[span] = (stream_in[span] + result(4)).astype(jnp.bfloat16)
        for stream in range(4):
            item = result(stream)
            scale = scaled[stream, span]
            moved = item * scale
            sums[stream] += moved[:8] + moved[8:]
            sums[4 + stream] += item[:8] + item[8:]
            weighted = item * norm_gain[stream : stream + 1]
            mean = jnp.mean(weighted, axis=-1, keepdims=True)
            slant = jnp.mean(weighted * scale, axis=-1, keepdims=True)
            grad = stats[2, span, stream : stream + 1] * (weighted - mean - scale * slant)
            if stream == 3:
                grad = grad + wide(cotangent[span])
            grads[stream, span] = grad
        return carry

    lax.fori_loop(0, seqs * SEQ // 16, unit, 0)
    for seq in range(seqs):

        def coefs(step, carry):
            row = pl.multiple_of(step * 16, 16)
            span = pl.ds(seq * SEQ + row, 16)
            found = jnp.zeros((16, 128), jnp.float32)
            for layer in range(STREAMS_IN):
                value = wide(stack[seq, layer, pl.ds(row, 16), :])
                for stream in range(4):
                    got = jnp.sum(grads[stream, span] * value, axis=-1, keepdims=True)
                    found = jnp.where(lane == stream * STREAMS_IN + layer, got, found)
            coef_grad[span] = found
            return carry

        lax.fori_loop(0, SEQ // 16, coefs, 0)
    grad_coef = coef_grad[:, 0:36]
    hidden_pre = stats[1, :, 0:36]
    hidden_low = gelu_value(hidden_pre).astype(jnp.bfloat16)
    small[...] = jnp.zeros_like(small)
    small[0:36, WIDTH : WIDTH + 36] = lax.dot_general(
        wide(hidden_low),
        grad_coef,
        (((0,), (0,)), ((), ())),
        precision=HIGHEST,
        preferred_element_type=jnp.float32,
    )
    small[36:37, WIDTH : WIDTH + 36] = jnp.sum(grad_coef, axis=0, keepdims=True)
    grad_hidden = (
        lax.dot_general(
            grad_coef,
            mix_down[...],
            (((1,), (1,)), ((), ())),
            precision=HIGHEST,
            preferred_element_type=jnp.float32,
        )
        * gelu_slope(hidden_pre)
    ).astype(jnp.bfloat16)
    gain_row = jnp.zeros((8, WIDTH), jnp.float32)
    up_part = jnp.zeros((36, WIDTH), jnp.float32)
    for seq in range(seqs):
        at = slice(seq * SEQ, seq * SEQ + SEQ)
        last = wide(stack[seq, STREAMS_IN - 1])
        rms = stats[2, at, 4:5]
        mixed_in = (last * rms * mix_gain[...]).astype(jnp.bfloat16)
        up_part = up_part + outer_sum(grad_hidden[at], mixed_in)
        grad_mixed = matmul(grad_hidden[at], mix_up[...])
        along = grad_mixed * last * rms
        for place in range(SEQ // 8):
            gain_row = gain_row + along[place * 8 : place * 8 + 8]
        weighted = grad_mixed * mix_gain[...]
        mean = jnp.mean(weighted * last, axis=-1, keepdims=True)
        grads[4, at] = rms * (weighted - last * (rms * rms * mean))

        def layers(step, carry):
            row = pl.multiple_of(step // 2 * 16, 16)
            cols = pl.ds(pl.multiple_of(step % 2 * 512, 512), 512)
            span = pl.ds(seq * SEQ + row, 16)
            rows_coef = stats[0, span, :]
            parts = [grads[stream, span, cols] for stream in range(4)]
            for layer in range(STREAMS_IN):
                total = None
                for stream in range(4):
                    at_coef = stream * STREAMS_IN + layer
                    term = rows_coef[:, at_coef : at_coef + 1] * parts[stream]
                    total = term if total is None else total + term
                if layer == STREAMS_IN - 1:
                    total = total + grads[4, span, cols]
                stack_grad[seq, layer, pl.ds(row, 16), cols] = total.astype(jnp.bfloat16)
            return carry

        lax.fori_loop(0, 8, layers, 0)
    small[0:36, 0:WIDTH] = up_part
    for place in range(8):
        small[36 + place : 37 + place, 0:WIDTH] = jnp.sum(sums[place], axis=0, keepdims=True)
    small[44:45, 0:WIDTH] = jnp.sum(gain_row, axis=0, keepdims=True)


def place_kernel(place, shard0, shard1, shard2, shard3, projection, out_grad, up_grad, down_grad):
    member, x, core = place[0], place[1], place[2]
    shards = (shard0, shard1, shard2, shard3)
    lane = lanes_of((128, 128))
    for back in range(4):
        from_x = x if back % 2 == 0 else 1 - x
        from_core = core if back < 2 else 1 - core
        quarter = 2 * from_x + from_core
        own, twin = shards[back], shards[back ^ 2]
        for index in range(8):
            half = index % 2
            mine = wide(own[index // 2, :, half * 128 : half * 128 + 128])
            half_b = 1 - half
            lent = wide(twin[index // 2, :, half_b * 128 : half_b * 128 + 128])
            col = pl.multiple_of((index * 4 + quarter) * 128, 128)
            up_grad[:, pl.ds(col, 128)] = jnp.where(
                (lane >= 96) & (from_core == half), lent, mine
            )
        row = pl.multiple_of(quarter * 128, 128)
        for block in range(4):
            cols = slice(block * 256, block * 256 + 256)
            down_grad[pl.ds(row, 96), cols] = wide(own[7 + block, 0:96])

            @pl.when(member % 2 == from_core)
            def _():
                head_row = pl.multiple_of(from_x * 64, 64)
                out_grad[pl.ds(head_row, 32), cols] = wide(own[7 + block, 96:128])
                out_grad[pl.ds(head_row + 32, 32), cols] = wide(
                    own[11, block * 32 : block * 32 + 32]
                )
                down_grad[pl.ds(row + 96, 32), cols] = wide(
                    twin[11, block * 32 : block * 32 + 32]
                )

            @pl.when(member % 2 != from_core)
            def _():
                down_grad[pl.ds(row + 96, 32), cols] = wide(own[7 + block, 96:128])

    for back in (0, 2):
        from_core = core if back < 2 else 1 - core
        for stream in range(3):
            for twin in range(2):
                tile = slice(twin * 128, twin * 128 + 128)
                mine = wide(shards[back][4 + stream, :, tile])
                across = wide(shards[back + 1][4 + stream, :, tile])
                even = jnp.where(x == 0, mine, across)
                odd = jnp.where(x == 0, across, mine)
                first = jnp.where(lane < 64, even, pltpu.roll(odd, 64, 1))
                second = jnp.where(lane < 64, pltpu.roll(even, 64, 1), odd)
                for low, value in ((0, first), (1, second)):
                    col = pl.multiple_of((2 * twin + low) * 256 + from_core * 128, 128)
                    projection[stream, :, pl.ds(col, 128)] = value


def call(kernel, outs, specs, out_specs, args, scratch=(), cost=None, vmem=60 << 20):
    return pl.pallas_call(
        kernel,
        out_shape=outs,
        in_specs=specs,
        out_specs=out_specs,
        scratch_shapes=list(scratch),
        compiler_params=pltpu.CompilerParams(vmem_limit_bytes=vmem),
        cost_estimate=cost,
    )(*args)


def shape_of(shape, dtype=jnp.bfloat16):
    return jax.ShapeDtypeStruct(shape, dtype)


def rope_tables():
    half_rot = ROTARY // 2
    step = 10000.0 ** (-2.0 * np.arange(half_rot) / ROTARY)
    angles = np.arange(SEQ)[:, None] * step[None, :]
    cos_table = np.ones((SEQ, HEAD_DIM))
    left = np.zeros((SEQ, HEAD_DIM))
    right = np.zeros((SEQ, HEAD_DIM))
    cos_table[:, :half_rot] = np.cos(angles)
    cos_table[:, half_rot:ROTARY] = np.cos(angles)
    left[:, :half_rot] = -np.sin(angles)
    right[:, half_rot:ROTARY] = np.sin(angles)
    return np.stack([np.tile(item, (2, 2)) for item in (cos_table, left, right)]).astype(np.float32)


def on_device_tensor(
    layer_stack,
    out_cotangent,
    pic_start,
    doc_split,
    mix_gain,
    mix_up,
    mix_down,
    mix_static,
    norm_gain,
    norm_bias,
    query_key_value,
    out_weight,
    up_weight,
    down_weight,
):
    fsdp_index = lax.axis_index("fsdp")
    z, y = fsdp_index // 2, fsdp_index % 2
    member = lax.axis_index("replica")
    x, core = member // 2, member % 2
    place = jnp.stack([fsdp_index, x, core]).astype(jnp.int32)
    micro_total, local_seqs, _, _, width = layer_stack.shape
    seqs = micro_total * local_seqs
    stack = jnp.transpose(layer_stack, (0, 1, 3, 2, 4)).reshape(seqs, STREAMS_IN, SEQ, width)
    cotangent = out_cotangent.reshape(ROWS, width)
    gain_row = mix_gain.reshape(1, width)

    up_one = mix_up.T
    up_two = order_two(y, up_one, lax.ppermute(up_one, "fsdp", Y_SWAP), 1)
    up_four = order_two(z % 2, up_two, lax.ppermute(up_two, "fsdp", Z_SWAP_NEAR), 1)
    mix_up_full = order_two(z // 2, up_four, lax.ppermute(up_four, "fsdp", Z_SWAP_FAR), 1)

    piece = call(
        prepare_kernel,
        shape_of((12, 128, 256)),
        [SMEM_FULL] + [VMEM_FULL] * 4,
        VMEM_FULL,
        (place, query_key_value, out_weight, up_weight, down_weight),
    )
    piece = after(piece, mix_up_full)
    bounds = jnp.concatenate([pic_start.reshape(seqs), doc_split.reshape(seqs)])
    kept = {}

    def front():
        packet, *kept["rest"] = call(
            front_kernel,
            (
                shape_of((5 * ROWS + 16, width)),
                shape_of((4, ROWS, width), jnp.float32),
                shape_of((3, ROWS, 128), jnp.float32),
                shape_of((ROWS, width), jnp.float32),
            ),
            [SMEM_FULL] + [VMEM_FULL] * 8,
            (VMEM_FULL,) * 4,
            (
                bounds,
                stack,
                cotangent,
                gain_row,
                mix_up_full,
                mix_down,
                mix_static.reshape(1, 36),
                norm_gain,
                norm_bias,
            ),
            scratch=[pltpu.VMEM((4, ROWS, width), jnp.float32)],
            cost=pl.CostEstimate(flops=30 << 20, bytes_accessed=24 << 20, transcendentals=0),
        )
        across = lax.ppermute(packet, "replica", X_SWAP)
        beside = lax.ppermute(packet, "replica", CORE_SWAP)
        beside_across = lax.ppermute(across, "replica", CORE_SWAP)
        kept["packets"] = (packet, across, beside, beside_across)
        return packet, across

    pieces, origin = gather_fsdp(piece, z, y, front)
    packets = kept["packets"]
    scaled, stats, stream_last = kept["rest"]

    target = scatter_order(z, y)
    results = call(
        main_kernel,
        (shape_of((12, 128, 256)),) * 8 + (shape_of((2, 5, ROWS, width)),) * 2,
        [SMEM_FULL] * 3 + [VMEM_FULL] + [IN_PLACE] * 12,
        (IN_PLACE,) * 8 + (VMEM_FULL,) * 2,
        (place, origin, target, jnp.asarray(rope_tables())) + packets + tuple(pieces),
        scratch=[
            pltpu.VMEM((5, 4 * ROWS, width), jnp.bfloat16),
            pltpu.VMEM((4, 16, width), jnp.bfloat16),
            pltpu.VMEM((4, width, 256), jnp.bfloat16),
            pltpu.VMEM((3, width, 256), jnp.bfloat16),
            pltpu.VMEM((8, 5, 128, 256), jnp.bfloat16),
            pltpu.VMEM((4, 256, 256), jnp.bfloat16),
            pltpu.VMEM((3, 4 * ROWS, 256), jnp.float32),
            pltpu.VMEM((5, 4 * ROWS, 256), jnp.bfloat16),
            pltpu.VMEM((8, 12, 128, 256), jnp.bfloat16),
            pltpu.VMEM((4 * ROWS, width), jnp.float32),
            pltpu.VMEM((4 * ROWS, width), jnp.float32),
            pltpu.SemaphoreType.DMA((4, 6)),
            pltpu.SemaphoreType.DMA((8, 3)),
            pltpu.SemaphoreType.DMA((8,)),
        ],
        cost=pl.CostEstimate(flops=9 << 30, bytes_accessed=24 << 20, transcendentals=0),
    )
    chunks, keep, send = results[:8], results[8], results[9]

    came = lax.ppermute(send, "replica", CORE_SWAP)
    sum_across = (wide(keep[1]) + wide(came[1])).astype(jnp.bfloat16)
    came_across = lax.ppermute(sum_across, "replica", X_SWAP)

    first_half = pl.BlockSpec((1, 5, ROWS, width), lambda step: (0, 0, 0, 0))

    def whole(shape):
        return pl.BlockSpec(shape, lambda step: (0,) * len(shape))

    def back():
        kept["back"] = pl.pallas_call(
            back_kernel,
            grid=(1,),
            out_shape=(
                shape_of((ROWS, width)),
                shape_of((seqs, STREAMS_IN, SEQ, width)),
                shape_of((48, width + 128), jnp.float32),
            ),
            in_specs=[
                whole((seqs, STREAMS_IN, SEQ, width)),
                whole((ROWS, width)),
                whole((4, ROWS, width)),
                whole((3, ROWS, 128)),
                whole((ROWS, width)),
                first_half,
                first_half,
                whole((5, ROWS, width)),
                whole((1, width)),
                whole((36, width)),
                whole((36, 36)),
                whole((4, width)),
            ],
            out_specs=(
                whole((ROWS, width)),
                whole((seqs, STREAMS_IN, SEQ, width)),
                whole((48, width + 128)),
            ),
            scratch_shapes=[
                pltpu.VMEM((5, ROWS, width), jnp.float32),
                pltpu.VMEM((8, 8, width), jnp.float32),
                pltpu.VMEM((ROWS, 128), jnp.float32),
            ],
            compiler_params=pltpu.CompilerParams(vmem_limit_bytes=56 << 20),
            cost_estimate=pl.CostEstimate(flops=60 << 20, bytes_accessed=36 << 20, transcendentals=0),
        )(
            stack,
            cotangent,
            scaled,
            stats,
            stream_last,
            keep,
            came,
            came_across,
            gain_row,
            mix_up_full,
            mix_down,
            norm_gain,
        )
        return kept["back"][2]

    shard = scatter_fsdp(chunks, z, sum_across, back)
    layer_output, stack_grad, small = kept["back"]

    shard_across = lax.ppermute(shard, "replica", X_SWAP)
    shard_beside = lax.ppermute(shard, "replica", CORE_SWAP)
    shard_both = lax.ppermute(shard_across, "replica", CORE_SWAP)
    projection_grad, out_grad, up_grad, down_grad = call(
        place_kernel,
        (
            shape_of((3, 128, width), jnp.float32),
            shape_of((128, width), jnp.float32),
            shape_of((128, 4 * width), jnp.float32),
            shape_of((512, width), jnp.float32),
        ),
        [SMEM_FULL] + [VMEM_FULL] * 4,
        (VMEM_FULL,) * 4,
        (place, shard, shard_across, shard_beside, shard_both),
    )

    for axis_name, perm in (
        ("replica", CORE_SWAP),
        ("replica", X_SWAP),
        ("fsdp", Y_SWAP),
        ("fsdp", Z_SWAP_NEAR),
        ("fsdp", Z_SWAP_FAR),
    ):
        small = small + lax.ppermute(small, axis_name, perm)
    mix_up_grad = lax.dynamic_slice(small, (0, 128 * fsdp_index), (36, 128)).T
    shape = (micro_total, local_seqs, SEQ)
    stack_grad = stack_grad.reshape(micro_total, local_seqs, STREAMS_IN, SEQ, width)
    return (
        layer_output.reshape(shape + (width,)),
        stats[0, :, :36].reshape(shape + (4, STREAMS_IN)),
        jnp.transpose(stack_grad, (0, 1, 3, 2, 4)),
        small[44, :width],
        mix_up_grad,
        small[:36, width : width + 36],
        small[36, width : width + 36].reshape(4, STREAMS_IN),
        small[36:40, :width],
        small[40:44, :width],
        projection_grad,
        out_grad,
        up_grad,
        down_grad,
    )


def solution(mesh):
    fits = mesh.shape["fsdp"] == 8 and mesh.shape["replica"] == 4
    body = on_device_tensor if fits else on_device
    return jax.shard_map(
        body,
        mesh=mesh,
        in_specs=(
            P(None, ("fsdp", "replica"), None, None, None),
            P(None, ("fsdp", "replica"), None, None),
            P(None, ("fsdp", "replica")),
            P(None, ("fsdp", "replica")),
            P(),
            P("fsdp", None),
            P(),
            P(),
            P(),
            P(),
            P(None, "fsdp", None),
            P("fsdp", None),
            P("fsdp", None),
            P("fsdp", None),
        ),
        out_specs=(
            P(None, ("fsdp", "replica"), None, None),
            P(None, ("fsdp", "replica"), None, None, None),
            P(None, ("fsdp", "replica"), None, None, None),
            P(),
            P("fsdp", None),
            P(),
            P(),
            P(),
            P(),
            P(None, "fsdp", None),
            P("fsdp", None),
            P("fsdp", None),
            P("fsdp", None),
        ),
        check_vma=False,
    )
```

```python
import math

import jax
import jax.numpy as jnp
import numpy as np
from jax import lax
from jax.experimental import pallas as pl
from jax.experimental.pallas import tpu as pltpu
from jax.sharding import PartitionSpec as P

HEADS = 16
HEAD_DIM = 64
ROTARY = 16
STREAMS_IN = 9
SEQ = 64
PIC = 32


EPSILON = 1e-05
ROOT_HALF = 0.7071067811865476
NORMAL_PEAK = 0.3989422804014327
HIGHEST = lax.Precision.HIGHEST


def as_sent(value):

    def short(part):
        return part.astype(jnp.bfloat16) if part.dtype == jnp.float32 else part

    return jax.tree.map(short, value)


def gelu_value(values):
    return 0.5 * values * (1.0 + lax.erf(values * ROOT_HALF))


def gelu_slope(values):
    return 0.5 * (1.0 + lax.erf(values * ROOT_HALF)) + values * NORMAL_PEAK * jnp.exp(
        -0.5 * values * values
    )


def matmul(left_side, right_side):
    return jnp.dot(left_side, right_side, preferred_element_type=jnp.float32)


def outer_sum(left_side, right_side):
    return lax.dot_general(
        left_side, right_side, (((0,), (0,)), ((), ())), preferred_element_type=jnp.float32
    )


def back_product(left_side, right_side):
    return lax.dot_general(
        left_side, right_side, (((1,), (1,)), ((), ())), preferred_element_type=jnp.float32
    )


def rotary_tables():
    half_rot = ROTARY // 2
    inverse = jnp.exp(-math.log(10000.0) * (2.0 * jnp.arange(half_rot, dtype=jnp.float32) / ROTARY))
    angles = jnp.arange(SEQ, dtype=jnp.float32)[:, None] * inverse[None, :]
    return (jnp.cos(angles)[:, None, :], jnp.sin(angles)[:, None, :])


def rotate(values, cos_table, sin_table):
    half_rot = ROTARY // 2
    first_half = values[..., :half_rot]
    second = values[..., half_rot:ROTARY]
    return jnp.concatenate(
        [
            first_half * cos_table - second * sin_table,
            second * cos_table + first_half * sin_table,
            values[..., ROTARY:],
        ],
        axis=-1,
    )


def allowed_mask(starts, splits):
    positions = jnp.arange(SEQ, dtype=jnp.int32)
    second_doc = positions[None, :] >= splits[:, None]
    picture = (positions[None, :] >= starts[:, None]) & (positions[None, :] < starts[:, None] + PIC)
    same_doc = second_doc[:, :, None] == second_doc[:, None, :]
    causal = positions[:, None] >= positions[None, :]
    both_pic = picture[:, :, None] & picture[:, None, :]
    return same_doc & (causal[None] | both_pic)


def masked_scores(queries, key_rot, allowed):
    scores = jnp.einsum(
        "nqhe,nkhe->nhqk", queries, key_rot, preferred_element_type=jnp.float32
    ) * HEAD_DIM ** (-0.5)
    return jnp.where(allowed[:, None], scores, -1e30)


def on_device(
    layer_stack,
    out_cotangent,
    pic_start,
    doc_split,
    mix_gain,
    mix_up,
    mix_down,
    mix_static,
    norm_gain,
    norm_bias,
    query_key_value,
    out_weight,
    up_weight,
    down_weight,
):
    micro_total = layer_stack.shape[0]
    local_seqs = layer_stack.shape[1]
    model_width = layer_stack.shape[-1]
    groups = [(0, micro_total)]
    cos_table, sin_table = rotary_tables()
    output_list = []
    coef_list = []
    grad_list = []
    shard_total = None
    small_total = None
    for first_micro, micro_count in groups:
        seq_count = micro_count * local_seqs
        row_count = seq_count * SEQ
        head_shape = (seq_count, SEQ, HEADS, HEAD_DIM)
        flat_stack = layer_stack[first_micro : first_micro + micro_count].reshape(
            row_count, STREAMS_IN, model_width
        )
        grad_rows = out_cotangent[first_micro : first_micro + micro_count].reshape(
            row_count, model_width
        )
        starts = pic_start[first_micro : first_micro + micro_count].reshape(seq_count)
        splits = doc_split[first_micro : first_micro + micro_count].reshape(seq_count)
        allowed = allowed_mask(starts, splits)
        mix_up_full, projection_full, out_full = (
            lax.all_gather(mix_up, "fsdp", axis=0, tiled=True),
            lax.all_gather(query_key_value, "fsdp", axis=1, tiled=True),
            lax.all_gather(out_weight, "fsdp", axis=0, tiled=True),
        )
        up_full, down_full = (
            lax.all_gather(up_weight, "fsdp", axis=0, tiled=True),
            lax.all_gather(down_weight, "fsdp", axis=0, tiled=True),
        )
        last_layer = flat_stack[:, STREAMS_IN - 1, :].astype(jnp.float32)
        rms_scale = lax.rsqrt(jnp.mean(last_layer * last_layer, axis=-1, keepdims=True) + EPSILON)
        mixed_in = (last_layer * rms_scale * mix_gain).astype(jnp.bfloat16)
        hidden_pre = matmul(mixed_in, mix_up_full)
        hidden_mix = gelu_value(hidden_pre).astype(jnp.bfloat16)
        hidden_wide = hidden_mix.astype(jnp.float32)
        coef_flat = jnp.dot(hidden_wide, mix_down, precision=HIGHEST) + mix_static.reshape(-1)
        coef_rows = coef_flat.reshape(row_count, 4, STREAMS_IN)
        streams = coef_rows[:, :, 0, None] * flat_stack[:, None, 0, :].astype(jnp.float32)
        for layer_index in range(1, STREAMS_IN):
            streams = streams + coef_rows[:, :, layer_index, None] * flat_stack[
                :, None, layer_index, :
            ].astype(jnp.float32)
        center = streams - jnp.mean(streams, axis=-1, keepdims=True)
        inv_std = lax.rsqrt(jnp.mean(center * center, axis=-1, keepdims=True) + EPSILON)
        scaled = center * inv_std
        normed = (scaled * norm_gain + norm_bias).astype(jnp.bfloat16)
        query_lin = matmul(normed[:, 0], projection_full[0])
        key_lin = matmul(normed[:, 1], projection_full[1])
        value_lin = matmul(normed[:, 2], projection_full[2])
        queries = rotate(query_lin.reshape(head_shape), cos_table, sin_table).astype(jnp.bfloat16)
        key_rot = rotate(key_lin.reshape(head_shape), cos_table, sin_table).astype(jnp.bfloat16)
        values = value_lin.astype(jnp.bfloat16).reshape(head_shape)
        scores = masked_scores(queries, key_rot, allowed)
        row_top = jnp.max(scores, axis=-1, keepdims=True)
        exponent = jnp.exp(scores - row_top)
        row_total = jnp.sum(exponent, axis=-1, keepdims=True)
        soft_probs = exponent / row_total
        log_total = row_top + jnp.log(row_total)
        attended = (
            jnp.einsum(
                "nhqk,nkhe->nqhe",
                soft_probs.astype(jnp.bfloat16),
                values,
                preferred_element_type=jnp.float32,
            )
            .astype(jnp.bfloat16)
            .reshape(row_count, model_width)
        )
        attn_out = matmul(attended, out_full)
        up_pre = matmul(normed[:, 3], up_full)
        gated_act = gelu_value(up_pre).astype(jnp.bfloat16)
        feed_out = matmul(gated_act, down_full)
        output_list.append((streams[:, 3] + attn_out + feed_out).astype(jnp.bfloat16))
        coef_list.append(coef_rows)
        mix_up_back, projection_back, out_back = (
            lax.all_gather(mix_up, "fsdp", axis=0, tiled=True),
            lax.all_gather(query_key_value, "fsdp", axis=1, tiled=True),
            lax.all_gather(out_weight, "fsdp", axis=0, tiled=True),
        )
        up_back, down_back = (
            lax.all_gather(up_weight, "fsdp", axis=0, tiled=True),
            lax.all_gather(down_weight, "fsdp", axis=0, tiled=True),
        )
        grad_down = outer_sum(gated_act, grad_rows)
        grad_gated = back_product(grad_rows, down_back)
        grad_up_pre = (grad_gated * gelu_slope(up_pre)).astype(jnp.bfloat16)
        grad_up = outer_sum(normed[:, 3], grad_up_pre)
        grad_norm_feed = back_product(grad_up_pre, up_back)
        feed_shards = (
            lax.psum_scatter(
                grad_up.astype(jnp.bfloat16), "fsdp", scatter_dimension=0, tiled=True
            ).astype(jnp.float32),
            lax.psum_scatter(
                grad_down.astype(jnp.bfloat16), "fsdp", scatter_dimension=0, tiled=True
            ).astype(jnp.float32),
        )
        grad_out_weight = outer_sum(attended, grad_rows)
        grad_attended = back_product(grad_rows, out_back).astype(jnp.bfloat16).reshape(head_shape)
        scores_again = masked_scores(queries, key_rot, allowed)
        probs_again = jnp.exp(scores_again - log_total)
        grad_probs = jnp.einsum(
            "nqhe,nkhe->nhqk", grad_attended, values, preferred_element_type=jnp.float32
        )
        grad_value = (
            jnp.einsum(
                "nhqk,nqhe->nkhe",
                probs_again.astype(jnp.bfloat16),
                grad_attended,
                preferred_element_type=jnp.float32,
            )
            .astype(jnp.bfloat16)
            .reshape(row_count, model_width)
        )
        delta_rows = jnp.sum(probs_again * grad_probs, axis=-1, keepdims=True)
        grad_scores = (probs_again * (grad_probs - delta_rows)).astype(jnp.bfloat16)
        score_scale = HEAD_DIM ** (-0.5)
        grad_query_rot = (
            jnp.einsum("nhqk,nkhe->nqhe", grad_scores, key_rot, preferred_element_type=jnp.float32)
            * score_scale
        )
        grad_key_rot = (
            jnp.einsum("nhqk,nqhe->nkhe", grad_scores, queries, preferred_element_type=jnp.float32)
            * score_scale
        )
        grad_query = (
            rotate(grad_query_rot, cos_table, -sin_table)
            .astype(jnp.bfloat16)
            .reshape(row_count, model_width)
        )
        grad_key = (
            rotate(grad_key_rot, cos_table, -sin_table)
            .astype(jnp.bfloat16)
            .reshape(row_count, model_width)
        )
        grad_linear = (grad_query, grad_key, grad_value)
        grad_projection = jnp.stack(
            [outer_sum(normed[:, stream], grad_linear[stream]) for stream in range(3)]
        )
        grad_normed = jnp.stack(
            [back_product(grad_linear[stream], projection_back[stream]) for stream in range(3)]
            + [grad_norm_feed],
            axis=1,
        )
        gain_grad = jnp.sum(grad_normed * scaled, axis=0)
        bias_grad = jnp.sum(grad_normed, axis=0)
        grad_scaled = grad_normed * norm_gain
        grad_streams = inv_std * (
            grad_scaled
            - jnp.mean(grad_scaled, axis=-1, keepdims=True)
            - scaled * jnp.mean(grad_scaled * scaled, axis=-1, keepdims=True)
        )
        grad_streams = grad_streams + jnp.concatenate(
            [
                jnp.zeros((row_count, 3, model_width), jnp.float32),
                grad_rows[:, None, :].astype(jnp.float32),
            ],
            axis=1,
        )
        grad_coef = jnp.stack(
            [
                jnp.sum(
                    grad_streams * flat_stack[:, None, layer_index, :].astype(jnp.float32), axis=-1
                )
                for layer_index in range(STREAMS_IN)
            ],
            axis=-1,
        )
        grad_coef_flat = grad_coef.reshape(row_count, 4 * STREAMS_IN)
        static_grad = jnp.sum(grad_coef_flat, axis=0).reshape(4, STREAMS_IN)
        down_mix_grad = jnp.dot(hidden_wide.T, grad_coef_flat, precision=HIGHEST)
        grad_hidden = (
            jnp.dot(grad_coef_flat, mix_down.T, precision=HIGHEST) * gelu_slope(hidden_pre)
        ).astype(jnp.bfloat16)
        grad_mix_up = outer_sum(mixed_in, grad_hidden)
        grad_mixed = back_product(grad_hidden, mix_up_back)
        gain_mix_grad = jnp.sum(grad_mixed * last_layer * rms_scale, axis=0)
        weighted = grad_mixed * mix_gain
        grad_last = rms_scale * (
            weighted
            - last_layer
            * rms_scale
            * rms_scale
            * jnp.mean(weighted * last_layer, axis=-1, keepdims=True)
        )
        per_layer = [
            jnp.sum(coef_rows[:, :, layer_index, None] * grad_streams, axis=1)
            for layer_index in range(STREAMS_IN)
        ]
        per_layer[STREAMS_IN - 1] = per_layer[STREAMS_IN - 1] + grad_last
        grad_list.append(jnp.stack(per_layer, axis=1).astype(jnp.bfloat16))
        attention_shards = (
            lax.psum_scatter(
                grad_mix_up.astype(jnp.bfloat16), "fsdp", scatter_dimension=0, tiled=True
            ).astype(jnp.float32),
            lax.psum_scatter(
                grad_projection.astype(jnp.bfloat16), "fsdp", scatter_dimension=1, tiled=True
            ).astype(jnp.float32),
            lax.psum_scatter(
                grad_out_weight.astype(jnp.bfloat16), "fsdp", scatter_dimension=0, tiled=True
            ).astype(jnp.float32),
        )
        shards = attention_shards + feed_shards
        shards = jax.tree.map(
            lambda part: part.astype(jnp.float32), lax.psum(as_sent(shards), "replica")
        )
        smalls = (gain_mix_grad, down_mix_grad, static_grad, gain_grad, bias_grad)
        if shard_total is None:
            shard_total = shards
            small_total = smalls
        else:
            shard_total = tuple(
                (total_item + new_item for total_item, new_item in zip(shard_total, shards))
            )
            small_total = tuple(
                (total_item + new_item for total_item, new_item in zip(small_total, smalls))
            )
    small_total = lax.psum(small_total, ("fsdp", "replica"))
    layer_output = jnp.concatenate(output_list, axis=0).reshape(
        micro_total, local_seqs, SEQ, model_width
    )
    coefficients = jnp.concatenate(coef_list, axis=0).reshape(
        micro_total, local_seqs, SEQ, 4, STREAMS_IN
    )
    stack_grad = jnp.concatenate(grad_list, axis=0).reshape(
        micro_total, local_seqs, SEQ, STREAMS_IN, model_width
    )
    return (
        layer_output,
        coefficients,
        stack_grad,
        small_total[0],
        shard_total[0],
        small_total[1],
        small_total[2],
        small_total[3],
        small_total[4],
        shard_total[1],
        shard_total[2],
        shard_total[3],
        shard_total[4],
    )


ROWS = 128
WIDTH = 1024
VMEM_FULL = pl.BlockSpec(memory_space=pltpu.VMEM)
SMEM_FULL = pl.BlockSpec(memory_space=pltpu.SMEM)
IN_PLACE = pl.BlockSpec(memory_space=pl.ANY)


def bits_swap(size, bit):
    return [(index, index ^ bit) for index in range(size)]


CORE_SWAP = bits_swap(4, 1)
X_SWAP = bits_swap(4, 2)
Y_SWAP = bits_swap(8, 1)
Z_SWAP_NEAR = bits_swap(8, 2)
Z_SWAP_FAR = bits_swap(8, 4)


def z_pairs(moves):
    return [(2 * src + col, 2 * dst + col) for src, dst in moves for col in range(2)]


def pick(cond, first, second):
    return jnp.where(cond, first, second)


def order_two(flag, own, other, axis):
    first = pick(flag == 0, own, other)
    second = pick(flag == 0, other, own)
    return jnp.concatenate([first, second], axis=axis)


def after(value, *others):
    return lax.optimization_barrier((value,) + others)[0]


Z_NEAR = z_pairs([(0, 1), (1, 0), (2, 3), (3, 2)])
Z_MIDDLE = z_pairs([(0, 0), (1, 2), (2, 1), (3, 3)])


def fsdp_move(value, pairs):
    return lax.ppermute(value, "fsdp", pairs)


def gather_fsdp(piece, z, front):
    inner = (z == 1) | (z == 2)
    near = fsdp_move(piece, Z_NEAR)
    middle = fsdp_move(piece, Z_MIDDLE)
    side_own = fsdp_move(piece, Y_SWAP)
    early, late = front()
    side_near = fsdp_move(near, Y_SWAP)
    middle_near = fsdp_move(after(near, early, side_own), Z_MIDDLE)
    near_middle = fsdp_move(after(middle, early, side_own), Z_NEAR)
    third = pick(inner, middle, near_middle)
    near_twice = fsdp_move(after(middle_near, side_near, third), Z_NEAR)
    side_third = fsdp_move(after(third, late), Y_SWAP)
    last = pick(inner, middle_near, near_twice)
    side_last = fsdp_move(after(last, side_third), Y_SWAP)
    return [piece, side_own, near, side_near, third, side_third, last, side_last]


def position():
    member, partner = lax.axis_index("fsdp"), lax.axis_index("replica")
    return member // 2, member % 2, partner // 2, partner % 2


def table(values, z):
    found = jnp.int32(values[0])
    for index in range(1, 4):
        found = jnp.where(z == index, jnp.int32(values[index]), found)
    return found


def gather_order(z, y):
    places = []
    for z_from in (z, table([1, 0, 3, 2], z), table([2, 2, 1, 1], z), table([3, 3, 0, 0], z)):
        places += [2 * z_from + y, 2 * z_from + 1 - y]
    return places


def scatter_order(z, y):
    places = []
    for z_to in (table([3, 3, 0, 0], z), table([2, 2, 1, 1], z), table([1, 0, 3, 2], z), z):
        places += [2 * z_to + 1 - y, 2 * z_to + y]
    return places


def wide(value):
    return value.astype(jnp.float32)


def scatter_fsdp(chunks, z, first_wait, second_wait, beside):
    inner = (z == 1) | (z == 2)

    def add(first, second):
        return (wide(first) + wide(second)).astype(jnp.bfloat16)

    came = []
    sums = []
    for turn in range(4):
        sent = chunks[2 * turn]
        if turn >= 2:
            sent = after(sent, came[turn - 2])
        came.append(fsdp_move(sent, Y_SWAP))
        held = chunks[2 * turn + 1]
        sums.append(add(after(held, first_wait) if turn == 0 else held, came[turn]))
    far = fsdp_move(sums[0], Z_NEAR)
    far = fsdp_move(after(add(sums[0], far), second_wait), Z_MIDDLE)
    second = fsdp_move(after(sums[1], second_wait), Z_NEAR)
    last_wait = beside()
    last = add(sums[2], jnp.where(inner, wide(far), 0.0))
    last = fsdp_move(after(last, last_wait), Z_NEAR)
    second = fsdp_move(after(add(sums[1], second), last_wait), Z_MIDDLE)
    total = wide(sums[3]) + wide(last) + jnp.where(inner, wide(second), 0.0)
    return total.astype(jnp.bfloat16)


def lanes_of(shape):
    return lax.broadcasted_iota(jnp.int32, shape, 1)


def rows_of(shape):
    return lax.broadcasted_iota(jnp.int32, shape, 0)


def prepare_kernel(projection, out_weight, up_weight, down_weight, piece):
    _, member_parity, x, core = position()
    quarter, other = 2 * x + core, 2 * x + 1 - core
    lane = lanes_of((128, 128))
    for index in range(8):
        half = index % 2
        own = up_weight[:, pl.ds(pl.multiple_of((index * 4 + quarter) * 128, 128), 128)]
        extra = up_weight[:, pl.ds(pl.multiple_of(((index ^ 1) * 4 + other) * 128, 128), 128)]
        taken = (lane >= 96) & (core == half)
        piece[index // 2, :, half * 128 : half * 128 + 128] = jnp.where(
            taken, wide(extra), wide(own)
        ).astype(jnp.bfloat16)
    for stream in range(3):
        for twin in range(2):
            tiles = [
                wide(
                    projection[
                        stream,
                        :,
                        pl.ds(pl.multiple_of((2 * twin + low) * 256 + core * 128, 128), 128),
                    ]
                )
                for low in range(2)
            ]
            first = jnp.where(x == 0, tiles[0], pltpu.roll(tiles[0], 64, 1))
            second = jnp.where(x == 0, pltpu.roll(tiles[1], 64, 1), tiles[1])
            piece[4 + stream, :, twin * 128 : twin * 128 + 128] = jnp.where(
                lane < 64, first, second
            ).astype(jnp.bfloat16)
    own_row = pl.multiple_of(quarter * 128, 128)
    other_row = pl.multiple_of(other * 128, 128)
    head_row = pl.multiple_of(x * 64, 64)
    for block in range(4):
        cols = slice(block * 256, block * 256 + 256)
        piece[7 + block, 0:96] = down_weight[pl.ds(own_row, 96), cols]

        @pl.when(member_parity == core)
        def _():
            piece[7 + block, 96:128] = out_weight[pl.ds(head_row, 32), cols]
            piece[11, block * 32 : block * 32 + 32] = out_weight[pl.ds(head_row + 32, 32), cols]

        @pl.when(member_parity != core)
        def _():
            piece[7 + block, 96:128] = down_weight[pl.ds(own_row + 96, 32), cols]
            piece[11, block * 32 : block * 32 + 32] = down_weight[pl.ds(other_row + 96, 32), cols]


def front_kernel(
    bounds,
    stack,
    cotangent,
    mix_gain,
    up_own,
    up_one,
    up_two,
    up_three,
    mix_down,
    mix_static,
    norm_gain,
    norm_bias,
    packet,
    scaled_out,
    stats,
    stream_out,
    mix_up,
    streams,
):
    seqs = stack.shape[0]
    z, y, _, _ = position()
    for step, part in enumerate((up_own, up_one, up_two, up_three)):
        z_from = (z + step) % 4
        for half, col in enumerate((y, 1 - y)):
            lanes = pl.ds(pl.multiple_of((2 * z_from + col) * 128, 128), 128)
            mix_up[:, lanes] = part[:, half * 128 : half * 128 + 128]
    for seq in range(seqs):
        last = wide(stack[seq, STREAMS_IN - 1])
        rms = lax.rsqrt(jnp.mean(last * last, axis=-1, keepdims=True) + EPSILON)
        mixed_in = (last * rms * mix_gain[...]).astype(jnp.bfloat16)
        hidden_pre = back_product(mixed_in, mix_up[...])
        hidden = wide(gelu_value(hidden_pre).astype(jnp.bfloat16))
        coef = jnp.dot(
            hidden, mix_down[...], precision=HIGHEST, preferred_element_type=jnp.float32
        )
        coef = coef + mix_static[...]
        at = slice(seq * SEQ, seq * SEQ + SEQ)
        stats[0, at, 0:36] = coef
        stats[1, at, 0:36] = hidden_pre
        stats[2, at, 4:5] = rms
        packet[4 * ROWS + seq * SEQ : 4 * ROWS + seq * SEQ + SEQ] = cotangent[at]

        def mix(step, carry):
            row = pl.multiple_of(step // 2 * 16, 16)
            col = pl.multiple_of(step % 2 * 512, 512)
            rows_coef = stats[0, pl.ds(seq * SEQ + row, 16), :]
            totals = [None] * 4
            for layer in range(STREAMS_IN):
                value = wide(stack[seq, layer, pl.ds(row, 16), pl.ds(col, 512)])
                for stream in range(4):
                    at_coef = stream * STREAMS_IN + layer
                    term = rows_coef[:, at_coef : at_coef + 1] * value
                    totals[stream] = term if layer == 0 else totals[stream] + term
            for stream in range(4):
                streams[stream, pl.ds(seq * SEQ + row, 16), pl.ds(col, 512)] = totals[stream]
            return carry

        lax.fori_loop(0, 8, mix, 0)

    def norm(step, carry):
        row = pl.multiple_of(step * 16, 16)
        for stream in range(4):
            value = streams[stream, pl.ds(row, 16), :]
            center = value - jnp.mean(value, axis=-1, keepdims=True)
            inverse = lax.rsqrt(jnp.mean(center * center, axis=-1, keepdims=True) + EPSILON)
            scaled = center * inverse
            stats[2, pl.ds(row, 16), stream : stream + 1] = inverse
            scaled_out[stream, pl.ds(row, 16), :] = scaled
            packet[pl.ds(stream * ROWS + row, 16), :] = (
                scaled * norm_gain[stream : stream + 1, :] + norm_bias[stream : stream + 1, :]
            ).astype(jnp.bfloat16)
            if stream == 3:
                stream_out[pl.ds(row, 16), :] = value
        return carry

    lax.fori_loop(0, seqs * SEQ // 16, norm, 0)
    packet[5 * ROWS :] = jnp.zeros((16, WIDTH), jnp.bfloat16)
    row = rows_of((16, 128))
    marks = jnp.zeros((16, 128), jnp.float32)
    for place in range(2 * seqs):
        marks = jnp.where(row == place, wide(bounds[place]), marks)
    packet[5 * ROWS :, 0:128] = marks.astype(jnp.bfloat16)


def main_kernel(
    rope,
    packet0,
    packet1,
    packet2,
    packet3,
    piece0,
    piece1,
    piece2,
    piece3,
    piece4,
    piece5,
    piece6,
    piece7,
    chunk0,
    chunk1,
    chunk2,
    chunk3,
    chunk4,
    chunk5,
    chunk6,
    chunk7,
    keep,
    send,
    acts,
    marks,
    up_all,
    lin_all,
    rhs_all,
    spare,
    lhs_all,
    grad_pre,
    linear,
    grad_att,
    grad_lin,
    parts,
    tokens,
    packet_sems,
    piece_sems,
    chunk_sems,
    token_sems,
):
    z, y, _, core = position()
    origin = gather_order(z, y)
    target = scatter_order(z, y)
    packets = (packet0, packet1, packet2, packet3)
    pieces = (piece0, piece1, piece2, piece3, piece4, piece5, piece6, piece7)
    chunks = (chunk0, chunk1, chunk2, chunk3, chunk4, chunk5, chunk6, chunk7)
    member_rows = [pl.ds(pl.multiple_of(place * 128, 128), 128) for place in origin]

    def unit_copies(unit):
        return [
            pltpu.make_async_copy(
                packets[block].at[pl.ds(unit * ROWS, ROWS)],
                acts.at[unit, pl.ds(block * ROWS, ROWS)],
                packet_sems.at[block, unit],
            )
            for block in range(4)
        ]

    first = unit_copies(0) + unit_copies(1) + unit_copies(2)
    for index in range(8):
        first.append(
            pltpu.make_async_copy(
                pieces[index].at[pl.ds(4, 3)],
                lin_all.at[:, member_rows[index]],
                piece_sems.at[index, 0],
            )
        )
    second = unit_copies(4)
    for block in range(4):
        second.append(
            pltpu.make_async_copy(
                packets[block].at[pl.ds(5 * ROWS, 16)], marks.at[block], packet_sems.at[block, 5]
            )
        )
    for index in range(8):
        for block in range(4):
            second.append(
                pltpu.make_async_copy(
                    pieces[index].at[7 + block],
                    rhs_all.at[member_rows[index], pl.ds(block * 256, 256)],
                    piece_sems.at[index, 1 + block],
                )
            )
        second.append(
            pltpu.make_async_copy(
                pieces[index].at[11], spare.at[origin[index]], piece_sems.at[index, 5]
            )
        )
    third = unit_copies(3)
    for index in range(8):
        for block in range(4):
            third.append(
                pltpu.make_async_copy(
                    pieces[index].at[block],
                    up_all.at[member_rows[index], pl.ds(block * 256, 256)],
                    piece_sems.at[index, 6 + block],
                )
            )
    for copy in first + second + third:
        copy.start()
    for copy in first:
        copy.wait()
    for stream in range(3):
        linear[stream] = matmul(acts[stream], lin_all[stream])
    for copy in second:
        copy.wait()
    for pair in range(4):
        even = 2 * pair + core
        odd = 2 * pair + 1 - core
        tail = pl.ds(pl.multiple_of(even * 128 + 96, 32), 32)
        first_rows = slice(WIDTH + pair * 64, WIDTH + pair * 64 + 32)
        last_rows = slice(WIDTH + pair * 64 + 32, WIDTH + pair * 64 + 64)
        for block in range(4):
            band = slice(block * 32, block * 32 + 32)
            cols = slice(block * 256, block * 256 + 256)
            rhs_all[first_rows, cols] = rhs_all[tail, cols]
            rhs_all[last_rows, cols] = spare[even, band]
            rhs_all[tail, cols] = spare[odd, band]

    grad_att[...] = back_product(acts[4], rhs_all[WIDTH:, :]).astype(jnp.bfloat16)
    cos_table = rope[0]
    sin_left = rope[1]
    sin_right = rope[2]
    scale = HEAD_DIM ** (-0.5)

    def turn(value, sign):
        return (
            value * cos_table
            + pltpu.roll(value, 120, 1) * (sign * sin_left)
            + pltpu.roll(value, 8, 1) * (sign * sin_right)
        )

    def units(block, carry):
        row = rows_of((ROWS, ROWS))
        lane = lanes_of((ROWS, ROWS))
        bound = wide(marks[block])

        def both(low, high):
            return jnp.where(row < SEQ, low, high), jnp.where(lane < SEQ, low, high)

        start_q, start_k = both(bound[0:1, 0:128], bound[1:2, 0:128])
        split_q, split_k = both(bound[2:3, 0:128], bound[3:4, 0:128])
        at_q = wide(row % SEQ)
        at_k = wide(lane % SEQ)
        same = (row // SEQ == lane // SEQ) & ((at_q >= split_q) == (at_k >= split_k))
        pic_q = (at_q >= start_q) & (at_q < start_q + PIC)
        pic_k = (at_k >= start_k) & (at_k < start_k + PIC)
        penalty = jnp.where(same & ((at_q >= at_k) | (pic_q & pic_k)), 0.0, -1e30)
        span = pl.ds(pl.multiple_of(block * ROWS, ROWS), ROWS)
        twins = [slice(twin * 128, twin * 128 + 128) for twin in range(2)]
        heads = [(twin, head) for twin in range(2) for head in range(2)]
        query = [turn(linear[0, span, cols], 1.0) for cols in twins]
        query_low = [item.astype(jnp.bfloat16) for item in query]
        key_low = [turn(linear[1, span, cols], 1.0).astype(jnp.bfloat16) for cols in twins]
        value_low = [linear[2, span, cols].astype(jnp.bfloat16) for cols in twins]
        grad_low = [grad_att[span, cols] for cols in twins]

        def only(item, head):
            return jnp.where(lane // 64 == head, wide(item), 0.0).astype(jnp.bfloat16)

        scores = [
            back_product(only(query[twin], head), key_low[twin]) * scale + penalty
            for twin, head in heads
        ]
        grad_probs = [
            back_product(only(grad_low[twin], head), value_low[twin]) for twin, head in heads
        ]
        exponent = [jnp.exp(item - jnp.max(item, axis=-1, keepdims=True)) for item in scores]
        probs = [item / jnp.sum(item, axis=-1, keepdims=True) for item in exponent]
        probs_low = [item.astype(jnp.bfloat16) for item in probs]
        grad_scores = [
            (prob * (grad - jnp.sum(prob * grad, axis=-1, keepdims=True))).astype(jnp.bfloat16)
            for prob, grad in zip(probs, grad_probs)
        ]
        attended = [matmul(probs_low[i], value_low[heads[i][0]]) for i in range(4)]
        grad_value = [outer_sum(probs_low[i], grad_low[heads[i][0]]) for i in range(4)]
        grad_query = [matmul(grad_scores[i], key_low[heads[i][0]]) for i in range(4)]
        grad_key = [outer_sum(grad_scores[i], query_low[heads[i][0]]) for i in range(4)]

        def merge(items, twin):
            return jnp.where(lane < 64, items[2 * twin], items[2 * twin + 1])

        for twin, cols in enumerate(twins):
            side = slice(WIDTH + twin * 128, WIDTH + twin * 128 + 128)
            lhs_all[span, side] = merge(attended, twin).astype(jnp.bfloat16)
            grad_lin[0, span, cols] = turn(merge(grad_query, twin) * scale, -1.0).astype(
                jnp.bfloat16
            )
            grad_lin[1, span, cols] = turn(merge(grad_key, twin) * scale, -1.0).astype(
                jnp.bfloat16
            )
            grad_lin[2, span, cols] = merge(grad_value, twin).astype(jnp.bfloat16)
        return carry

    lax.fori_loop(0, 4, units, 0)

    for copy in third:
        copy.wait()

    def hidden(pair, carry):
        cols = pl.ds(pl.multiple_of(pair * 256, 256), 256)
        up_pre = matmul(acts[3], up_all[:, cols])
        bell = 0.5 * (1.0 + lax.erf(up_pre * ROOT_HALF))
        slope = bell + up_pre * NORMAL_PEAK * jnp.exp(-0.5 * up_pre * up_pre)
        lhs_all[:, cols] = (up_pre * bell).astype(jnp.bfloat16)
        grad_gated = back_product(acts[4], rhs_all[cols, :])
        grad_pre[:, cols] = (grad_gated * slope).astype(jnp.bfloat16)
        return carry

    lax.fori_loop(0, 4, hidden, 0)

    def weights(index, carry):
        cols = pl.ds(pl.multiple_of(index * 128, 128), 128)
        grad = outer_sum(acts[3, :, cols], grad_pre[...]).astype(jnp.bfloat16)
        for block in range(4):
            parts[index, block] = grad[:, block * 256 : block * 256 + 256]
        for stream in range(3):
            parts[index, 4 + stream] = outer_sum(acts[stream, :, cols], grad_lin[stream]).astype(
                jnp.bfloat16
            )
        grad = outer_sum(lhs_all[:, cols], acts[4]).astype(jnp.bfloat16)
        other = index + 1 - 2 * (index % 2)
        for block in range(4):
            part = grad[:, block * 256 : block * 256 + 256]
            parts[index, 7 + block, 0:96] = part[0:96]

            @pl.when(index % 2 == core)
            def _():
                parts[other, 11, block * 32 : block * 32 + 32] = part[96:128]

            @pl.when(index % 2 != core)
            def _():
                parts[index, 7 + block, 96:128] = part[96:128]

        return carry

    lax.fori_loop(0, 8, weights, 0)
    grad = outer_sum(lhs_all[:, WIDTH:], acts[4]).astype(jnp.bfloat16)
    for block in range(4):
        part = grad[:, block * 256 : block * 256 + 256]
        for pair in range(4):
            even = 2 * pair + core
            parts[even, 7 + block, 96:128] = part[pair * 64 : pair * 64 + 32]
            parts[even, 11, block * 32 : block * 32 + 32] = part[pair * 64 + 32 : pair * 64 + 64]
    sent = [
        pltpu.make_async_copy(parts.at[target[index]], chunks[index], chunk_sems.at[index])
        for index in range(8)
    ]
    for copy in sent:
        copy.start()

    def put(unit, cols, value):
        low = value.astype(jnp.bfloat16)
        for half in range(2):
            for block in range(2):
                at = (2 * half + block) * ROWS
                tokens[half, block, unit, :, cols] = low[at : at + ROWS]

    def ship(unit):
        for half, ref in enumerate((keep, send)):
            copy = pltpu.make_async_copy(
                tokens.at[half, :, unit], ref.at[:, unit], token_sems.at[half, unit]
            )
            copy.start()
            sent.append(copy)

    for stream in range(3):
        put(stream, slice(0, WIDTH), back_product(grad_lin[stream], lin_all[stream]))
        ship(stream)

    def feed(block, carry):
        cols = pl.ds(pl.multiple_of(block * 256, 256), 256)
        put(3, cols, back_product(grad_pre[...], up_all[cols, :]))
        put(4, cols, matmul(lhs_all[...], rhs_all[:, cols]))
        return carry

    lax.fori_loop(0, 4, feed, 0)
    ship(3)
    ship(4)
    for copy in sent:
        copy.wait()


def back_kernel(
    stack,
    cotangent,
    scaled,
    stats,
    stream_in,
    keep,
    came,
    across,
    mix_gain,
    mix_up,
    mix_down,
    norm_gain,
    layer_output,
    stack_grad,
    small_own,
    small_other,
    coefficients,
    grads,
    sums,
    coef_grad,
    small,
):
    seqs = stack.shape[0]
    sums[...] = jnp.zeros_like(sums)
    lane = lanes_of((16, 128))

    def unit(step, carry):
        row = pl.multiple_of(step * 16, 16)
        span = pl.ds(row, 16)

        def result(index):
            return wide(keep[0, index, span]) + wide(came[0, index, span]) + wide(across[index, span])

        layer_output[span] = (stream_in[span] + result(4)).astype(jnp.bfloat16)
        for stream in range(4):
            item = result(stream)
            scale = scaled[stream, span]
            moved = item * scale
            sums[stream] += moved[:8] + moved[8:]
            sums[4 + stream] += item[:8] + item[8:]
            weighted = item * norm_gain[stream : stream + 1]
            mean = jnp.mean(weighted, axis=-1, keepdims=True)
            slant = jnp.mean(weighted * scale, axis=-1, keepdims=True)
            grad = stats[2, span, stream : stream + 1] * (weighted - mean - scale * slant)
            if stream == 3:
                grad = grad + wide(cotangent[span])
            grads[stream, span] = grad
        return carry

    lax.fori_loop(0, seqs * SEQ // 16, unit, 0)
    for seq in range(seqs):

        def coefs(step, carry):
            row = pl.multiple_of(step * 16, 16)
            span = pl.ds(seq * SEQ + row, 16)
            found = jnp.zeros((16, 128), jnp.float32)
            for layer in range(STREAMS_IN):
                value = wide(stack[seq, layer, pl.ds(row, 16), :])
                for stream in range(4):
                    got = jnp.sum(grads[stream, span] * value, axis=-1, keepdims=True)
                    found = jnp.where(lane == stream * STREAMS_IN + layer, got, found)
            coef_grad[span] = found
            return carry

        lax.fori_loop(0, SEQ // 16, coefs, 0)
    grad_coef = coef_grad[:, 0:36]
    hidden_pre = stats[1, :, 0:36]
    hidden_low = gelu_value(hidden_pre).astype(jnp.bfloat16)
    for seq in range(seqs):
        turned = stats[0, seq * SEQ : seq * SEQ + SEQ, :].T
        for stream in range(4):
            for layer in range(STREAMS_IN):
                at = stream * STREAMS_IN + layer
                coefficients[seq, layer, stream : stream + 1] = turned[at : at + 1]
    small[...] = jnp.zeros_like(small)
    small[0:36, WIDTH : WIDTH + 36] = lax.dot_general(
        wide(hidden_low),
        grad_coef,
        (((0,), (0,)), ((), ())),
        precision=HIGHEST,
        preferred_element_type=jnp.float32,
    )
    small[36:37, WIDTH : WIDTH + 36] = jnp.sum(grad_coef, axis=0, keepdims=True)
    grad_hidden = (
        lax.dot_general(
            grad_coef,
            mix_down[...],
            (((1,), (1,)), ((), ())),
            precision=HIGHEST,
            preferred_element_type=jnp.float32,
        )
        * gelu_slope(hidden_pre)
    ).astype(jnp.bfloat16)
    gain_row = jnp.zeros((8, WIDTH), jnp.float32)
    up_part = jnp.zeros((36, WIDTH), jnp.float32)
    for seq in range(seqs):
        at = slice(seq * SEQ, seq * SEQ + SEQ)
        last = wide(stack[seq, STREAMS_IN - 1])
        rms = stats[2, at, 4:5]
        mixed_in = (last * rms * mix_gain[...]).astype(jnp.bfloat16)
        up_part = up_part + outer_sum(grad_hidden[at], mixed_in)
        grad_mixed = matmul(grad_hidden[at], mix_up[...])
        along = grad_mixed * last * rms
        for place in range(SEQ // 8):
            gain_row = gain_row + along[place * 8 : place * 8 + 8]
        weighted = grad_mixed * mix_gain[...]
        mean = jnp.mean(weighted * last, axis=-1, keepdims=True)
        grads[4, at] = rms * (weighted - last * (rms * rms * mean))

        def layers(step, carry):
            row = pl.multiple_of(step // 2 * 16, 16)
            cols = pl.ds(pl.multiple_of(step % 2 * 512, 512), 512)
            span = pl.ds(seq * SEQ + row, 16)
            rows_coef = stats[0, span, :]
            parts = [grads[stream, span, cols] for stream in range(4)]
            for layer in range(STREAMS_IN):
                total = None
                for stream in range(4):
                    at_coef = stream * STREAMS_IN + layer
                    term = rows_coef[:, at_coef : at_coef + 1] * parts[stream]
                    total = term if total is None else total + term
                if layer == STREAMS_IN - 1:
                    total = total + grads[4, span, cols]
                stack_grad[seq, layer, pl.ds(row, 16), cols] = total.astype(jnp.bfloat16)
            return carry

        lax.fori_loop(0, 8, layers, 0)
    small[0:36, 0:WIDTH] = up_part
    for place in range(8):
        small[36 + place : 37 + place, 0:WIDTH] = jnp.sum(sums[place], axis=0, keepdims=True)
    small[44:45, 0:WIDTH] = jnp.sum(gain_row, axis=0, keepdims=True)
    _, _, _, core = position()
    small_own[...] = small[pl.ds(pl.multiple_of(core * 24, 8), 24), :]
    small_other[...] = small[pl.ds(pl.multiple_of(24 - core * 24, 8), 24), :]


def place_kernel(
    shard0,
    shard1,
    shard2,
    shard3,
    small_own,
    small_other,
    projection,
    out_grad,
    up_grad,
    down_grad,
    mix_gain_grad,
    mix_up_grad,
    mix_down_grad,
    mix_static_grad,
    gain_grad,
    bias_grad,
    small,
):
    z, member_parity, x, core = position()
    small[pl.ds(pl.multiple_of(core * 24, 8), 24), :] = small_own[...]
    small[pl.ds(pl.multiple_of(24 - core * 24, 8), 24), :] = small_other[...]
    lanes = pl.ds(pl.multiple_of((2 * z + member_parity) * 128, 128), 128)
    mix_up_grad[...] = small[0:36, lanes]
    gain_grad[...] = small[36:40, 0:WIDTH]
    bias_grad[...] = small[40:44, 0:WIDTH]
    mix_gain_grad[...] = small[44:45, 0:WIDTH]
    mix_down_grad[...] = small[0:36, WIDTH : WIDTH + 36]
    for stream in range(4):
        at = WIDTH + stream * STREAMS_IN
        mix_static_grad[stream : stream + 1] = small[36:37, at : at + STREAMS_IN]
    shards = (shard0, shard1, shard2, shard3)
    lane = lanes_of((128, 128))
    for back in range(4):
        from_x = x if back % 2 == 0 else 1 - x
        from_core = core if back < 2 else 1 - core
        quarter = 2 * from_x + from_core
        own, twin = shards[back], shards[back ^ 2]
        for index in range(8):
            half = index % 2
            mine = wide(own[index // 2, :, half * 128 : half * 128 + 128])
            half_b = 1 - half
            lent = wide(twin[index // 2, :, half_b * 128 : half_b * 128 + 128])
            col = pl.multiple_of((index * 4 + quarter) * 128, 128)
            up_grad[:, pl.ds(col, 128)] = jnp.where(
                (lane >= 96) & (from_core == half), lent, mine
            )
        row = pl.multiple_of(quarter * 128, 128)
        for block in range(4):
            cols = slice(block * 256, block * 256 + 256)
            down_grad[pl.ds(row, 96), cols] = wide(own[7 + block, 0:96])

            @pl.when(member_parity == from_core)
            def _():
                head_row = pl.multiple_of(from_x * 64, 64)
                out_grad[pl.ds(head_row, 32), cols] = wide(own[7 + block, 96:128])
                out_grad[pl.ds(head_row + 32, 32), cols] = wide(
                    own[11, block * 32 : block * 32 + 32]
                )
                down_grad[pl.ds(row + 96, 32), cols] = wide(
                    twin[11, block * 32 : block * 32 + 32]
                )

            @pl.when(member_parity != from_core)
            def _():
                down_grad[pl.ds(row + 96, 32), cols] = wide(own[7 + block, 96:128])

    for back in (0, 2):
        from_core = core if back < 2 else 1 - core
        for stream in range(3):
            for twin in range(2):
                tile = slice(twin * 128, twin * 128 + 128)
                mine = wide(shards[back][4 + stream, :, tile])
                across = wide(shards[back + 1][4 + stream, :, tile])
                even = jnp.where(x == 0, mine, across)
                odd = jnp.where(x == 0, across, mine)
                first = jnp.where(lane < 64, even, pltpu.roll(odd, 64, 1))
                second = jnp.where(lane < 64, pltpu.roll(even, 64, 1), odd)
                for low, value in ((0, first), (1, second)):
                    col = pl.multiple_of((2 * twin + low) * 256 + from_core * 128, 128)
                    projection[stream, :, pl.ds(col, 128)] = value


def call(kernel, outs, specs, out_specs, args, scratch=(), cost=None, vmem=60 << 20):
    return pl.pallas_call(
        kernel,
        out_shape=outs,
        in_specs=specs,
        out_specs=out_specs,
        scratch_shapes=list(scratch),
        compiler_params=pltpu.CompilerParams(vmem_limit_bytes=vmem),
        cost_estimate=cost,
    )(*args)


def shape_of(shape, dtype=jnp.bfloat16):
    return jax.ShapeDtypeStruct(shape, dtype)


def rope_tables():
    half_rot = ROTARY // 2
    step = 10000.0 ** (-2.0 * np.arange(half_rot) / ROTARY)
    angles = np.arange(SEQ)[:, None] * step[None, :]
    cos_table = np.ones((SEQ, HEAD_DIM))
    left = np.zeros((SEQ, HEAD_DIM))
    right = np.zeros((SEQ, HEAD_DIM))
    cos_table[:, :half_rot] = np.cos(angles)
    cos_table[:, half_rot:ROTARY] = np.cos(angles)
    left[:, :half_rot] = -np.sin(angles)
    right[:, half_rot:ROTARY] = np.sin(angles)
    return np.stack([np.tile(item, (2, 2)) for item in (cos_table, left, right)]).astype(np.float32)


def on_device_tensor(
    layer_stack,
    out_cotangent,
    pic_start,
    doc_split,
    mix_gain,
    mix_up,
    mix_down,
    mix_static,
    norm_gain,
    norm_bias,
    query_key_value,
    out_weight,
    up_weight,
    down_weight,
):
    z, y, _, _ = position()
    micro_total, local_seqs, _, _, width = layer_stack.shape
    seqs = micro_total * local_seqs
    stack = jnp.transpose(layer_stack, (0, 1, 3, 2, 4)).reshape(seqs, STREAMS_IN, SEQ, width)
    cotangent = out_cotangent.reshape(ROWS, width)
    gain_row = mix_gain.reshape(1, width)

    piece = call(
        prepare_kernel,
        shape_of((12, 128, 256)),
        [VMEM_FULL] * 4,
        VMEM_FULL,
        (query_key_value, out_weight, up_weight, down_weight),
    )
    up_own = mix_up.T
    up_pair = jnp.concatenate([up_own, after(lax.ppermute(up_own, "fsdp", Y_SWAP), piece)], axis=1)
    ups = [up_pair] + [
        lax.ppermute(up_pair, "fsdp", z_pairs([((step + to) % 4, to) for to in range(4)]))
        for step in (1, 2, 3)
    ]
    piece = after(piece, *ups)
    bounds = jnp.concatenate([pic_start.reshape(seqs), doc_split.reshape(seqs)])
    kept = {}

    def front():
        packet, *kept["rest"] = call(
            front_kernel,
            (
                shape_of((5 * ROWS + 16, width)),
                shape_of((4, ROWS, width), jnp.float32),
                shape_of((3, ROWS, 128), jnp.float32),
                shape_of((ROWS, width), jnp.float32),
                shape_of((36, width)),
            ),
            [SMEM_FULL] + [VMEM_FULL] * 11,
            (VMEM_FULL,) * 5,
            (
                bounds,
                stack,
                cotangent,
                gain_row,
                *ups,
                mix_down,
                mix_static.reshape(1, 36),
                norm_gain,
                norm_bias,
            ),
            scratch=[pltpu.VMEM((4, ROWS, width), jnp.float32)],
        )
        across = lax.ppermute(packet, "replica", X_SWAP)
        beside = lax.ppermute(packet, "replica", CORE_SWAP)
        beside_across = lax.ppermute(across, "replica", CORE_SWAP)
        kept["packets"] = (packet, across, beside, beside_across)
        return packet, across

    pieces = gather_fsdp(piece, z, front)
    packets = kept["packets"]
    scaled, stats, stream_last, mix_up_full = kept["rest"]

    results = call(
        main_kernel,
        (shape_of((12, 128, 256)),) * 8 + (shape_of((2, 5, ROWS, width)),) * 2,
        [VMEM_FULL] + [IN_PLACE] * 12,
        (IN_PLACE,) * 10,
        (jnp.asarray(rope_tables()),) + packets + tuple(pieces),
        scratch=[
            pltpu.VMEM((5, 4 * ROWS, width), jnp.bfloat16),
            pltpu.VMEM((4, 16, width), jnp.bfloat16),
            pltpu.VMEM((width, width), jnp.bfloat16),
            pltpu.VMEM((3, width, 256), jnp.bfloat16),
            pltpu.VMEM((width + 256, width), jnp.bfloat16),
            pltpu.VMEM((8, 128, 256), jnp.bfloat16),
            pltpu.VMEM((4 * ROWS, width + 256), jnp.bfloat16),
            pltpu.VMEM((4 * ROWS, width), jnp.bfloat16),
            pltpu.VMEM((3, 4 * ROWS, 256), jnp.float32),
            pltpu.VMEM((4 * ROWS, 256), jnp.bfloat16),
            pltpu.VMEM((3, 4 * ROWS, 256), jnp.bfloat16),
            pltpu.VMEM((8, 12, 128, 256), jnp.bfloat16),
            pltpu.VMEM((2, 2, 5, ROWS, width), jnp.bfloat16),
            pltpu.SemaphoreType.DMA((4, 6)),
            pltpu.SemaphoreType.DMA((8, 10)),
            pltpu.SemaphoreType.DMA((8,)),
            pltpu.SemaphoreType.DMA((2, 5)),
        ],
    )
    chunks, keep, send = results[:8], results[8], results[9]

    came = lax.ppermute(send, "replica", CORE_SWAP)
    sum_across = (wide(keep[1]) + wide(came[1])).astype(jnp.bfloat16)
    came_across = lax.ppermute(sum_across, "replica", X_SWAP)

    first_half = pl.BlockSpec((1, 5, ROWS, width), lambda step: (0, 0, 0, 0))

    def whole(shape):
        return pl.BlockSpec(shape, lambda step: (0,) * len(shape))

    def back():
        kept["back"] = pl.pallas_call(
            back_kernel,
            grid=(1,),
            out_shape=(
                shape_of((ROWS, width)),
                shape_of((seqs, STREAMS_IN, SEQ, width)),
                shape_of((24, width + 128), jnp.float32),
                shape_of((24, width + 128), jnp.float32),
                shape_of((seqs, STREAMS_IN, 4, SEQ), jnp.float32),
            ),
            in_specs=[
                whole((seqs, STREAMS_IN, SEQ, width)),
                whole((ROWS, width)),
                whole((4, ROWS, width)),
                whole((3, ROWS, 128)),
                whole((ROWS, width)),
                first_half,
                first_half,
                whole((5, ROWS, width)),
                whole((1, width)),
                whole((36, width)),
                whole((36, 36)),
                whole((4, width)),
            ],
            out_specs=(
                whole((ROWS, width)),
                whole((seqs, STREAMS_IN, SEQ, width)),
                whole((24, width + 128)),
                whole((24, width + 128)),
                whole((seqs, STREAMS_IN, 4, SEQ)),
            ),
            scratch_shapes=[
                pltpu.VMEM((5, ROWS, width), jnp.float32),
                pltpu.VMEM((8, 8, width), jnp.float32),
                pltpu.VMEM((ROWS, 128), jnp.float32),
                pltpu.VMEM((48, width + 128), jnp.float32),
            ],
            compiler_params=pltpu.CompilerParams(vmem_limit_bytes=56 << 20),
        )(
            stack,
            cotangent,
            scaled,
            stats,
            stream_last,
            keep,
            came,
            came_across,
            gain_row,
            mix_up_full,
            mix_down,
            norm_gain,
        )
        return kept["back"][2]

    shard = scatter_fsdp(chunks, z, sum_across, came_across, back)
    layer_output, stack_grad, small, small_other, coefficients = kept["back"]

    small = small + lax.ppermute(small_other, "replica", CORE_SWAP)
    small = small + lax.ppermute(small, "replica", X_SWAP)
    shard = after(shard, small)
    shard_across = lax.ppermute(shard, "replica", X_SWAP)
    shard_beside = lax.ppermute(shard, "replica", CORE_SWAP)
    for perm in (Y_SWAP, Z_SWAP_NEAR, Z_SWAP_FAR):
        small = small + lax.ppermute(small, "fsdp", perm)
    small_beside = lax.ppermute(small, "replica", CORE_SWAP)
    shard_both = lax.ppermute(after(shard_across, small), "replica", CORE_SWAP)
    owned = call(
        place_kernel,
        (
            shape_of((3, 128, width), jnp.float32),
            shape_of((128, width), jnp.float32),
            shape_of((128, 4 * width), jnp.float32),
            shape_of((512, width), jnp.float32),
            shape_of((1, width), jnp.float32),
            shape_of((36, 128), jnp.float32),
            shape_of((36, 36), jnp.float32),
            shape_of((4, STREAMS_IN), jnp.float32),
            shape_of((4, width), jnp.float32),
            shape_of((4, width), jnp.float32),
        ),
        [VMEM_FULL] * 6,
        (VMEM_FULL,) * 10,
        (shard, shard_across, shard_beside, shard_both, small, small_beside),
        scratch=[pltpu.VMEM((48, width + 128), jnp.float32)],
    )
    projection_grad, out_grad, up_grad, down_grad, *small_grads = owned
    shape = (micro_total, local_seqs, SEQ)
    stack_grad = stack_grad.reshape(micro_total, local_seqs, STREAMS_IN, SEQ, width)
    coefficients = coefficients.reshape(micro_total, local_seqs, STREAMS_IN, 4, SEQ)
    return (
        layer_output.reshape(shape + (width,)),
        jnp.transpose(coefficients, (0, 1, 4, 3, 2)),
        jnp.transpose(stack_grad, (0, 1, 3, 2, 4)),
        small_grads[0].reshape(width),
        small_grads[1].T,
        small_grads[2],
        small_grads[3],
        small_grads[4],
        small_grads[5],
        projection_grad,
        out_grad,
        up_grad,
        down_grad,
    )


def solution(mesh):
    fits = mesh.shape["fsdp"] == 8 and mesh.shape["replica"] == 4
    body = on_device_tensor if fits else on_device
    return jax.shard_map(
        body,
        mesh=mesh,
        in_specs=(
            P(None, ("fsdp", "replica"), None, None, None),
            P(None, ("fsdp", "replica"), None, None),
            P(None, ("fsdp", "replica")),
            P(None, ("fsdp", "replica")),
            P(),
            P("fsdp", None),
            P(),
            P(),
            P(),
            P(),
            P(None, "fsdp", None),
            P("fsdp", None),
            P("fsdp", None),
            P("fsdp", None),
        ),
        out_specs=(
            P(None, ("fsdp", "replica"), None, None),
            P(None, ("fsdp", "replica"), None, None, None),
            P(None, ("fsdp", "replica"), None, None, None),
            P(),
            P("fsdp", None),
            P(),
            P(),
            P(),
            P(),
            P(None, "fsdp", None),
            P("fsdp", None),
            P("fsdp", None),
            P("fsdp", None),
        ),
        check_vma=False,
    )
```

```python
import math

import jax
import jax.numpy as jnp
import numpy as np
from jax import lax
from jax.experimental import pallas as pl
from jax.experimental.pallas import tpu as pltpu
from jax.sharding import PartitionSpec as P

HEADS = 16
HEAD_DIM = 64
ROTARY = 16
STREAMS_IN = 9
SEQ = 64
PIC = 32


EPSILON = 1e-05
ROOT_HALF = 0.7071067811865476
NORMAL_PEAK = 0.3989422804014327
HIGHEST = lax.Precision.HIGHEST


def as_sent(value):

    def short(part):
        return part.astype(jnp.bfloat16) if part.dtype == jnp.float32 else part

    return jax.tree.map(short, value)


def gelu_value(values):
    return 0.5 * values * (1.0 + lax.erf(values * ROOT_HALF))


def gelu_slope(values):
    return 0.5 * (1.0 + lax.erf(values * ROOT_HALF)) + values * NORMAL_PEAK * jnp.exp(
        -0.5 * values * values
    )


def matmul(left_side, right_side):
    return jnp.dot(left_side, right_side, preferred_element_type=jnp.float32)


def outer_sum(left_side, right_side):
    return lax.dot_general(
        left_side, right_side, (((0,), (0,)), ((), ())), preferred_element_type=jnp.float32
    )


def back_product(left_side, right_side):
    return lax.dot_general(
        left_side, right_side, (((1,), (1,)), ((), ())), preferred_element_type=jnp.float32
    )


def rotary_tables():
    half_rot = ROTARY // 2
    inverse = jnp.exp(-math.log(10000.0) * (2.0 * jnp.arange(half_rot, dtype=jnp.float32) / ROTARY))
    angles = jnp.arange(SEQ, dtype=jnp.float32)[:, None] * inverse[None, :]
    return (jnp.cos(angles)[:, None, :], jnp.sin(angles)[:, None, :])


def rotate(values, cos_table, sin_table):
    half_rot = ROTARY // 2
    first_half = values[..., :half_rot]
    second = values[..., half_rot:ROTARY]
    return jnp.concatenate(
        [
            first_half * cos_table - second * sin_table,
            second * cos_table + first_half * sin_table,
            values[..., ROTARY:],
        ],
        axis=-1,
    )


def allowed_mask(starts, splits):
    positions = jnp.arange(SEQ, dtype=jnp.int32)
    second_doc = positions[None, :] >= splits[:, None]
    picture = (positions[None, :] >= starts[:, None]) & (positions[None, :] < starts[:, None] + PIC)
    same_doc = second_doc[:, :, None] == second_doc[:, None, :]
    causal = positions[:, None] >= positions[None, :]
    both_pic = picture[:, :, None] & picture[:, None, :]
    return same_doc & (causal[None] | both_pic)


def masked_scores(queries, key_rot, allowed):
    scores = jnp.einsum(
        "nqhe,nkhe->nhqk", queries, key_rot, preferred_element_type=jnp.float32
    ) * HEAD_DIM ** (-0.5)
    return jnp.where(allowed[:, None], scores, -1e30)


def on_device(
    layer_stack,
    out_cotangent,
    pic_start,
    doc_split,
    mix_gain,
    mix_up,
    mix_down,
    mix_static,
    norm_gain,
    norm_bias,
    query_key_value,
    out_weight,
    up_weight,
    down_weight,
):
    micro_total = layer_stack.shape[0]
    local_seqs = layer_stack.shape[1]
    model_width = layer_stack.shape[-1]
    groups = [(0, micro_total)]
    cos_table, sin_table = rotary_tables()
    output_list = []
    coef_list = []
    grad_list = []
    shard_total = None
    small_total = None
    for first_micro, micro_count in groups:
        seq_count = micro_count * local_seqs
        row_count = seq_count * SEQ
        head_shape = (seq_count, SEQ, HEADS, HEAD_DIM)
        flat_stack = layer_stack[first_micro : first_micro + micro_count].reshape(
            row_count, STREAMS_IN, model_width
        )
        grad_rows = out_cotangent[first_micro : first_micro + micro_count].reshape(
            row_count, model_width
        )
        starts = pic_start[first_micro : first_micro + micro_count].reshape(seq_count)
        splits = doc_split[first_micro : first_micro + micro_count].reshape(seq_count)
        allowed = allowed_mask(starts, splits)
        mix_up_full, projection_full, out_full = (
            lax.all_gather(mix_up, "fsdp", axis=0, tiled=True),
            lax.all_gather(query_key_value, "fsdp", axis=1, tiled=True),
            lax.all_gather(out_weight, "fsdp", axis=0, tiled=True),
        )
        up_full, down_full = (
            lax.all_gather(up_weight, "fsdp", axis=0, tiled=True),
            lax.all_gather(down_weight, "fsdp", axis=0, tiled=True),
        )
        last_layer = flat_stack[:, STREAMS_IN - 1, :].astype(jnp.float32)
        rms_scale = lax.rsqrt(jnp.mean(last_layer * last_layer, axis=-1, keepdims=True) + EPSILON)
        mixed_in = (last_layer * rms_scale * mix_gain).astype(jnp.bfloat16)
        hidden_pre = matmul(mixed_in, mix_up_full)
        hidden_mix = gelu_value(hidden_pre).astype(jnp.bfloat16)
        hidden_wide = hidden_mix.astype(jnp.float32)
        coef_flat = jnp.dot(hidden_wide, mix_down, precision=HIGHEST) + mix_static.reshape(-1)
        coef_rows = coef_flat.reshape(row_count, 4, STREAMS_IN)
        streams = coef_rows[:, :, 0, None] * flat_stack[:, None, 0, :].astype(jnp.float32)
        for layer_index in range(1, STREAMS_IN):
            streams = streams + coef_rows[:, :, layer_index, None] * flat_stack[
                :, None, layer_index, :
            ].astype(jnp.float32)
        center = streams - jnp.mean(streams, axis=-1, keepdims=True)
        inv_std = lax.rsqrt(jnp.mean(center * center, axis=-1, keepdims=True) + EPSILON)
        scaled = center * inv_std
        normed = (scaled * norm_gain + norm_bias).astype(jnp.bfloat16)
        query_lin = matmul(normed[:, 0], projection_full[0])
        key_lin = matmul(normed[:, 1], projection_full[1])
        value_lin = matmul(normed[:, 2], projection_full[2])
        queries = rotate(query_lin.reshape(head_shape), cos_table, sin_table).astype(jnp.bfloat16)
        key_rot = rotate(key_lin.reshape(head_shape), cos_table, sin_table).astype(jnp.bfloat16)
        values = value_lin.astype(jnp.bfloat16).reshape(head_shape)
        scores = masked_scores(queries, key_rot, allowed)
        row_top = jnp.max(scores, axis=-1, keepdims=True)
        exponent = jnp.exp(scores - row_top)
        row_total = jnp.sum(exponent, axis=-1, keepdims=True)
        soft_probs = exponent / row_total
        log_total = row_top + jnp.log(row_total)
        attended = (
            jnp.einsum(
                "nhqk,nkhe->nqhe",
                soft_probs.astype(jnp.bfloat16),
                values,
                preferred_element_type=jnp.float32,
            )
            .astype(jnp.bfloat16)
            .reshape(row_count, model_width)
        )
        attn_out = matmul(attended, out_full)
        up_pre = matmul(normed[:, 3], up_full)
        gated_act = gelu_value(up_pre).astype(jnp.bfloat16)
        feed_out = matmul(gated_act, down_full)
        output_list.append((streams[:, 3] + attn_out + feed_out).astype(jnp.bfloat16))
        coef_list.append(coef_rows)
        mix_up_back, projection_back, out_back = (
            lax.all_gather(mix_up, "fsdp", axis=0, tiled=True),
            lax.all_gather(query_key_value, "fsdp", axis=1, tiled=True),
            lax.all_gather(out_weight, "fsdp", axis=0, tiled=True),
        )
        up_back, down_back = (
            lax.all_gather(up_weight, "fsdp", axis=0, tiled=True),
            lax.all_gather(down_weight, "fsdp", axis=0, tiled=True),
        )
        grad_down = outer_sum(gated_act, grad_rows)
        grad_gated = back_product(grad_rows, down_back)
        grad_up_pre = (grad_gated * gelu_slope(up_pre)).astype(jnp.bfloat16)
        grad_up = outer_sum(normed[:, 3], grad_up_pre)
        grad_norm_feed = back_product(grad_up_pre, up_back)
        feed_shards = (
            lax.psum_scatter(
                grad_up.astype(jnp.bfloat16), "fsdp", scatter_dimension=0, tiled=True
            ).astype(jnp.float32),
            lax.psum_scatter(
                grad_down.astype(jnp.bfloat16), "fsdp", scatter_dimension=0, tiled=True
            ).astype(jnp.float32),
        )
        grad_out_weight = outer_sum(attended, grad_rows)
        grad_attended = back_product(grad_rows, out_back).astype(jnp.bfloat16).reshape(head_shape)
        scores_again = masked_scores(queries, key_rot, allowed)
        probs_again = jnp.exp(scores_again - log_total)
        grad_probs = jnp.einsum(
            "nqhe,nkhe->nhqk", grad_attended, values, preferred_element_type=jnp.float32
        )
        grad_value = (
            jnp.einsum(
                "nhqk,nqhe->nkhe",
                probs_again.astype(jnp.bfloat16),
                grad_attended,
                preferred_element_type=jnp.float32,
            )
            .astype(jnp.bfloat16)
            .reshape(row_count, model_width)
        )
        delta_rows = jnp.sum(probs_again * grad_probs, axis=-1, keepdims=True)
        grad_scores = (probs_again * (grad_probs - delta_rows)).astype(jnp.bfloat16)
        score_scale = HEAD_DIM ** (-0.5)
        grad_query_rot = (
            jnp.einsum("nhqk,nkhe->nqhe", grad_scores, key_rot, preferred_element_type=jnp.float32)
            * score_scale
        )
        grad_key_rot = (
            jnp.einsum("nhqk,nqhe->nkhe", grad_scores, queries, preferred_element_type=jnp.float32)
            * score_scale
        )
        grad_query = (
            rotate(grad_query_rot, cos_table, -sin_table)
            .astype(jnp.bfloat16)
            .reshape(row_count, model_width)
        )
        grad_key = (
            rotate(grad_key_rot, cos_table, -sin_table)
            .astype(jnp.bfloat16)
            .reshape(row_count, model_width)
        )
        grad_linear = (grad_query, grad_key, grad_value)
        grad_projection = jnp.stack(
            [outer_sum(normed[:, stream], grad_linear[stream]) for stream in range(3)]
        )
        grad_normed = jnp.stack(
            [back_product(grad_linear[stream], projection_back[stream]) for stream in range(3)]
            + [grad_norm_feed],
            axis=1,
        )
        gain_grad = jnp.sum(grad_normed * scaled, axis=0)
        bias_grad = jnp.sum(grad_normed, axis=0)
        grad_scaled = grad_normed * norm_gain
        grad_streams = inv_std * (
            grad_scaled
            - jnp.mean(grad_scaled, axis=-1, keepdims=True)
            - scaled * jnp.mean(grad_scaled * scaled, axis=-1, keepdims=True)
        )
        grad_streams = grad_streams + jnp.concatenate(
            [
                jnp.zeros((row_count, 3, model_width), jnp.float32),
                grad_rows[:, None, :].astype(jnp.float32),
            ],
            axis=1,
        )
        grad_coef = jnp.stack(
            [
                jnp.sum(
                    grad_streams * flat_stack[:, None, layer_index, :].astype(jnp.float32), axis=-1
                )
                for layer_index in range(STREAMS_IN)
            ],
            axis=-1,
        )
        grad_coef_flat = grad_coef.reshape(row_count, 4 * STREAMS_IN)
        static_grad = jnp.sum(grad_coef_flat, axis=0).reshape(4, STREAMS_IN)
        down_mix_grad = jnp.dot(hidden_wide.T, grad_coef_flat, precision=HIGHEST)
        grad_hidden = (
            jnp.dot(grad_coef_flat, mix_down.T, precision=HIGHEST) * gelu_slope(hidden_pre)
        ).astype(jnp.bfloat16)
        grad_mix_up = outer_sum(mixed_in, grad_hidden)
        grad_mixed = back_product(grad_hidden, mix_up_back)
        gain_mix_grad = jnp.sum(grad_mixed * last_layer * rms_scale, axis=0)
        weighted = grad_mixed * mix_gain
        grad_last = rms_scale * (
            weighted
            - last_layer
            * rms_scale
            * rms_scale
            * jnp.mean(weighted * last_layer, axis=-1, keepdims=True)
        )
        per_layer = [
            jnp.sum(coef_rows[:, :, layer_index, None] * grad_streams, axis=1)
            for layer_index in range(STREAMS_IN)
        ]
        per_layer[STREAMS_IN - 1] = per_layer[STREAMS_IN - 1] + grad_last
        grad_list.append(jnp.stack(per_layer, axis=1).astype(jnp.bfloat16))
        attention_shards = (
            lax.psum_scatter(
                grad_mix_up.astype(jnp.bfloat16), "fsdp", scatter_dimension=0, tiled=True
            ).astype(jnp.float32),
            lax.psum_scatter(
                grad_projection.astype(jnp.bfloat16), "fsdp", scatter_dimension=1, tiled=True
            ).astype(jnp.float32),
            lax.psum_scatter(
                grad_out_weight.astype(jnp.bfloat16), "fsdp", scatter_dimension=0, tiled=True
            ).astype(jnp.float32),
        )
        shards = attention_shards + feed_shards
        shards = jax.tree.map(
            lambda part: part.astype(jnp.float32), lax.psum(as_sent(shards), "replica")
        )
        smalls = (gain_mix_grad, down_mix_grad, static_grad, gain_grad, bias_grad)
        if shard_total is None:
            shard_total = shards
            small_total = smalls
        else:
            shard_total = tuple(
                (total_item + new_item for total_item, new_item in zip(shard_total, shards))
            )
            small_total = tuple(
                (total_item + new_item for total_item, new_item in zip(small_total, smalls))
            )
    small_total = lax.psum(small_total, ("fsdp", "replica"))
    layer_output = jnp.concatenate(output_list, axis=0).reshape(
        micro_total, local_seqs, SEQ, model_width
    )
    coefficients = jnp.concatenate(coef_list, axis=0).reshape(
        micro_total, local_seqs, SEQ, 4, STREAMS_IN
    )
    stack_grad = jnp.concatenate(grad_list, axis=0).reshape(
        micro_total, local_seqs, SEQ, STREAMS_IN, model_width
    )
    return (
        layer_output,
        coefficients,
        stack_grad,
        small_total[0],
        shard_total[0],
        small_total[1],
        small_total[2],
        small_total[3],
        small_total[4],
        shard_total[1],
        shard_total[2],
        shard_total[3],
        shard_total[4],
    )


ROWS = 128
WIDTH = 1024
VMEM_FULL = pl.BlockSpec(memory_space=pltpu.VMEM)
SMEM_FULL = pl.BlockSpec(memory_space=pltpu.SMEM)
IN_PLACE = pl.BlockSpec(memory_space=pl.ANY)


def bits_swap(size, bit):
    return [(index, index ^ bit) for index in range(size)]


CORE_SWAP = bits_swap(4, 1)
X_SWAP = bits_swap(4, 2)
Y_SWAP = bits_swap(8, 1)
Z_SWAP_NEAR = bits_swap(8, 2)
Z_SWAP_FAR = bits_swap(8, 4)


def z_pairs(moves):
    return [(2 * src + col, 2 * dst + col) for src, dst in moves for col in range(2)]


def pick(cond, first, second):
    return jnp.where(cond, first, second)


def order_two(flag, own, other, axis):
    first = pick(flag == 0, own, other)
    second = pick(flag == 0, other, own)
    return jnp.concatenate([first, second], axis=axis)


def after(value, *others):
    return lax.optimization_barrier((value,) + others)[0]


Z_NEAR = z_pairs([(0, 1), (1, 0), (2, 3), (3, 2)])
Z_MIDDLE = [
    (index, (index ^ 1) if index // 8 in (0, 3) else (24 - index // 8 * 8 + index % 8))
    for index in range(32)
]


def fsdp_move(value, pairs):
    return lax.ppermute(value, "fsdp" if len(pairs) == 8 else ("fsdp", "replica"), pairs)


PART = 7


def gather_fsdp(piece, z, front):
    inner = (z == 1) | (z == 2)
    near = fsdp_move(piece, Z_NEAR)
    middle = fsdp_move(piece, Z_MIDDLE)
    side = fsdp_move(piece, Y_SWAP)
    early, late = front()
    middle_near = fsdp_move(after(near, *early, side), Z_MIDDLE)
    turned = fsdp_move(after(pick(inner, middle, side), *early), Z_NEAR)
    side_two = fsdp_move(pick(inner, middle, near), Y_SWAP)
    third = pick(inner, middle_near, turned)
    near_twice = fsdp_move(after(middle_near, side_two, third), Z_NEAR)
    side_three = fsdp_move(third, Y_SWAP)
    over_z = fsdp_move(side_three[:PART], Z_NEAR)
    over_y = fsdp_move(after(near_twice[PART:], side_three, *late), Y_SWAP)
    return [
        piece,
        side,
        near,
        middle,
        middle_near,
        turned,
        near_twice,
        side_two,
        side_three,
        over_z,
        over_y,
    ]


def position():
    member, partner = lax.axis_index("fsdp"), lax.axis_index("replica")
    return member // 2, member % 2, partner // 2, partner % 2


def table(values, z):
    found = jnp.int32(values[0])
    for index in range(1, 4):
        found = jnp.where(z == index, jnp.int32(values[index]), found)
    return found


def gather_order(z, y):
    places = []
    for z_from in (z, table([1, 0, 3, 2], z), table([2, 2, 1, 1], z), table([3, 3, 0, 0], z)):
        places += [2 * z_from + y, 2 * z_from + 1 - y]
    return places


def scatter_order(z, y):
    others = (table([3, 0, 3, 0], z), table([2, 3, 0, 1], z), table([1, 2, 1, 2], z), z)
    own = (table([3, 3, 0, 0], z), table([2, 2, 1, 1], z), table([1, 0, 3, 2], z), z)
    return [2 * z_to + 1 - y for z_to in others] + [2 * z_to + y for z_to in own]


def wide(value):
    return value.astype(jnp.float32)


def scatter_fsdp(chunks, z, first_wait, beside):
    inner = (z == 1) | (z == 2)
    side_low, side_high, side_one, side_two, side_own, last, third, near, own = chunks

    def low(value):
        return value.astype(jnp.bfloat16)

    def only(cond, value):
        return jnp.where(cond, wide(value), 0.0)

    over_y = fsdp_move(side_high, Y_SWAP)
    over_z = fsdp_move(side_low, Z_NEAR)
    over_z = jnp.pad(only(inner, over_z), ((0, 12 - PART), (0, 0), (0, 0)))
    back_one = fsdp_move(low(wide(after(side_one, first_wait)) + over_z), Y_SWAP)
    over_y = jnp.pad(wide(over_y), ((PART, 0), (0, 0), (0, 0)))
    back_far = fsdp_move(low(wide(last) + over_y), Z_NEAR)
    back_two = fsdp_move(after(side_two, first_wait), Y_SWAP)
    to_middle = low(wide(last) + wide(back_one) + wide(back_far))
    to_near = low(
        jnp.where(
            inner,
            wide(jnp.concatenate([side_low, side_high])),
            wide(third) + wide(back_one),
        )
    )
    middle_one = fsdp_move(to_middle, Z_MIDDLE)
    near_one = fsdp_move(to_near, Z_NEAR)
    back_own = fsdp_move(low(wide(side_own) + only(z % 3 == 0, near_one)), Y_SWAP)
    to_near = low(wide(near) + jnp.where(inner, wide(middle_one), wide(back_two)))
    to_middle = low(wide(third) + wide(back_two) + wide(near_one))
    to_near, to_middle, _ = lax.optimization_barrier((to_near, to_middle, beside()))
    near_two = fsdp_move(to_near, Z_NEAR)
    middle_two = fsdp_move(to_middle, Z_MIDDLE)
    return low(wide(own) + wide(back_own) + wide(near_two) + only(inner, middle_two))


def lanes_of(shape):
    return lax.broadcasted_iota(jnp.int32, shape, 1)


def rows_of(shape):
    return lax.broadcasted_iota(jnp.int32, shape, 0)


def prepare_kernel(projection, out_weight, up_weight, down_weight, piece):
    _, member_parity, x, core = position()
    quarter, other = 2 * x + core, 2 * x + 1 - core
    lane = lanes_of((128, 128))
    for index in range(8):
        half = index % 2
        own = up_weight[:, pl.ds(pl.multiple_of((index * 4 + quarter) * 128, 128), 128)]
        extra = up_weight[:, pl.ds(pl.multiple_of(((index ^ 1) * 4 + other) * 128, 128), 128)]
        taken = (lane >= 96) & (core == half)
        piece[index // 2, :, half * 128 : half * 128 + 128] = jnp.where(
            taken, wide(extra), wide(own)
        ).astype(jnp.bfloat16)
    for stream in range(3):
        for twin in range(2):
            tiles = [
                wide(
                    projection[
                        stream,
                        :,
                        pl.ds(pl.multiple_of((2 * twin + low) * 256 + core * 128, 128), 128),
                    ]
                )
                for low in range(2)
            ]
            first = jnp.where(x == 0, tiles[0], pltpu.roll(tiles[0], 64, 1))
            second = jnp.where(x == 0, pltpu.roll(tiles[1], 64, 1), tiles[1])
            piece[4 + stream, :, twin * 128 : twin * 128 + 128] = jnp.where(
                lane < 64, first, second
            ).astype(jnp.bfloat16)
    own_row = pl.multiple_of(quarter * 128, 128)
    other_row = pl.multiple_of(other * 128, 128)
    head_row = pl.multiple_of(x * 64, 64)
    for block in range(4):
        cols = slice(block * 256, block * 256 + 256)
        piece[7 + block, 0:96] = down_weight[pl.ds(own_row, 96), cols]

        @pl.when(member_parity == core)
        def _():
            piece[7 + block, 96:128] = out_weight[pl.ds(head_row, 32), cols]
            piece[11, block * 32 : block * 32 + 32] = out_weight[pl.ds(head_row + 32, 32), cols]

        @pl.when(member_parity != core)
        def _():
            piece[7 + block, 96:128] = down_weight[pl.ds(own_row + 96, 32), cols]
            piece[11, block * 32 : block * 32 + 32] = down_weight[pl.ds(other_row + 96, 32), cols]


def front_kernel(
    bounds,
    stack,
    mix_gain,
    up_own,
    up_one,
    up_two,
    up_three,
    mix_down,
    mix_static,
    norm_gain,
    norm_bias,
    packet,
    scaled_out,
    stats,
    stream_out,
    mix_up,
    streams,
):
    seqs = stack.shape[0]
    z, y, _, _ = position()
    for step, part in enumerate((up_own, up_one, up_two, up_three)):
        z_from = (z + step) % 4
        for half, col in enumerate((y, 1 - y)):
            lanes = pl.ds(pl.multiple_of((2 * z_from + col) * 128, 128), 128)
            mix_up[:, lanes] = part[:, half * 128 : half * 128 + 128]
    for seq in range(seqs):
        last = wide(stack[seq, STREAMS_IN - 1])
        rms = lax.rsqrt(jnp.mean(last * last, axis=-1, keepdims=True) + EPSILON)
        mixed_in = (last * rms * mix_gain[...]).astype(jnp.bfloat16)
        hidden_pre = back_product(mixed_in, mix_up[...])
        hidden = wide(gelu_value(hidden_pre).astype(jnp.bfloat16))
        coef = jnp.dot(
            hidden, mix_down[...], precision=HIGHEST, preferred_element_type=jnp.float32
        )
        coef = coef + mix_static[...]
        at = slice(seq * SEQ, seq * SEQ + SEQ)
        stats[0, at, 0:36] = coef
        stats[1, at, 0:36] = hidden_pre
        stats[2, at, 4:5] = rms

        def mix(step, carry):
            row = pl.multiple_of(step // 2 * 16, 16)
            col = pl.multiple_of(step % 2 * 512, 512)
            rows_coef = stats[0, pl.ds(seq * SEQ + row, 16), :]
            totals = [None] * 4
            for layer in range(STREAMS_IN):
                value = wide(stack[seq, layer, pl.ds(row, 16), pl.ds(col, 512)])
                for stream in range(4):
                    at_coef = stream * STREAMS_IN + layer
                    term = rows_coef[:, at_coef : at_coef + 1] * value
                    totals[stream] = term if layer == 0 else totals[stream] + term
            for stream in range(4):
                streams[stream, pl.ds(seq * SEQ + row, 16), pl.ds(col, 512)] = totals[stream]
            return carry

        lax.fori_loop(0, 8, mix, 0)

    def norm(step, carry):
        row = pl.multiple_of(step * 16, 16)
        for stream in range(4):
            value = streams[stream, pl.ds(row, 16), :]
            center = value - jnp.mean(value, axis=-1, keepdims=True)
            inverse = lax.rsqrt(jnp.mean(center * center, axis=-1, keepdims=True) + EPSILON)
            scaled = center * inverse
            stats[2, pl.ds(row, 16), stream : stream + 1] = inverse
            scaled_out[stream, pl.ds(row, 16), :] = scaled
            packet[pl.ds(stream * ROWS + row, 16), :] = (
                scaled * norm_gain[stream : stream + 1, :] + norm_bias[stream : stream + 1, :]
            ).astype(jnp.bfloat16)
            if stream == 3:
                stream_out[pl.ds(row, 16), :] = value
        return carry

    lax.fori_loop(0, seqs * SEQ // 16, norm, 0)
    packet[4 * ROWS :] = jnp.zeros((16, WIDTH), jnp.bfloat16)
    row = rows_of((16, 128))
    marks = jnp.zeros((16, 128), jnp.float32)
    for place in range(2 * seqs):
        marks = jnp.where(row == place, wide(bounds[place]), marks)
    packet[4 * ROWS :, 0:128] = marks.astype(jnp.bfloat16)


def main_kernel(
    rope,
    packet0,
    packet1,
    packet2,
    packet3,
    cotangent0,
    cotangent1,
    cotangent2,
    cotangent3,
    piece0,
    piece1,
    piece2,
    piece3,
    piece4,
    piece5,
    piece6,
    piece7,
    piece8,
    piece9,
    piece10,
    chunk_low,
    chunk_high,
    chunk1,
    chunk2,
    chunk3,
    chunk4,
    chunk5,
    chunk6,
    chunk7,
    keep,
    send,
    acts,
    marks,
    up_all,
    lin_all,
    rhs_all,
    spare,
    lhs_all,
    grad_pre,
    linear,
    grad_att,
    grad_lin,
    parts,
    tokens,
    packet_sems,
    piece_sems,
    chunk_sems,
    token_sems,
):
    z, y, _, core = position()
    origin = gather_order(z, y)
    target = scatter_order(z, y)
    packets = (packet0, packet1, packet2, packet3)
    cotangents = (cotangent0, cotangent1, cotangent2, cotangent3)
    piece, side, near, middle, middle_near, turned = piece0, piece1, piece2, piece3, piece4, piece5
    near_twice, side_two, side_three, over_z, over_y = piece6, piece7, piece8, piece9, piece10
    inner = (z == 1) | (z == 2)
    sources = (
        (piece, piece),
        (side, side),
        (near, near),
        (turned, side_two),
        (middle, turned),
        (side_two, side_three),
        (middle_near, near_twice),
        (side_three, None),
    )
    chunks = (chunk1, chunk2, chunk3, chunk4, chunk5, chunk6, chunk7)
    member_rows = [pl.ds(pl.multiple_of(place * 128, 128), 128) for place in origin]

    def unit_copies(unit):
        return [
            pltpu.make_async_copy(
                packets[block].at[pl.ds(unit * ROWS, ROWS)],
                acts.at[unit, pl.ds(block * ROWS, ROWS)],
                packet_sems.at[block, unit],
            )
            for block in range(4)
        ]

    def piece_copies(index, ref, tail_ref):
        rows = member_rows[index]
        down = 7 if tail_ref is ref else 0
        found = [
            pltpu.make_async_copy(
                ref.at[pl.ds(4, 3)], lin_all.at[:, rows], piece_sems.at[index, 0]
            )
        ]
        for block in range(4):
            cols = pl.ds(block * 256, 256)
            found.append(
                pltpu.make_async_copy(
                    tail_ref.at[down + block], rhs_all.at[rows, cols], piece_sems.at[index, 1 + block]
                )
            )
        found.append(
            pltpu.make_async_copy(
                tail_ref.at[down + 4], spare.at[origin[index]], piece_sems.at[index, 5]
            )
        )
        for block in range(4):
            found.append(
                pltpu.make_async_copy(
                    ref.at[block],
                    up_all.at[rows, pl.ds(block * 256, 256)],
                    piece_sems.at[index, 6 + block],
                )
            )
        return found

    first = unit_copies(0) + unit_copies(1) + unit_copies(2)
    second = [
        pltpu.make_async_copy(
            cotangents[block],
            acts.at[4, pl.ds(block * ROWS, ROWS)],
            packet_sems.at[block, 4],
        )
        for block in range(4)
    ]
    for block in range(4):
        second.append(
            pltpu.make_async_copy(
                packets[block].at[pl.ds(4 * ROWS, 16)], marks.at[block], packet_sems.at[block, 5]
            )
        )
    third = unit_copies(3)
    for copy in first + second + third:
        copy.start()
    for index, (for_inner, for_ends) in enumerate(sources):
        copies = piece_copies(index, for_inner, for_inner)
        first.append(copies[0])
        second += copies[1:6]
        third += copies[6:]
        if for_inner is for_ends:
            for copy in copies:
                copy.start()
            continue
        ends = (
            piece_copies(index, over_z, over_y)
            if for_ends is None
            else piece_copies(index, for_ends, for_ends)
        )

        @pl.when(inner)
        def _():
            for copy in copies:
                copy.start()

        @pl.when(jnp.logical_not(inner))
        def _():
            for copy in ends:
                copy.start()

    for copy in first:
        copy.wait()
    for stream in range(3):
        linear[stream] = matmul(acts[stream], lin_all[stream])
    for copy in second:
        copy.wait()
    for pair in range(4):
        even = 2 * pair + core
        odd = 2 * pair + 1 - core
        tail = pl.ds(pl.multiple_of(even * 128 + 96, 32), 32)
        first_rows = slice(WIDTH + pair * 64, WIDTH + pair * 64 + 32)
        last_rows = slice(WIDTH + pair * 64 + 32, WIDTH + pair * 64 + 64)
        for block in range(4):
            band = slice(block * 32, block * 32 + 32)
            cols = slice(block * 256, block * 256 + 256)
            rhs_all[first_rows, cols] = rhs_all[tail, cols]
            rhs_all[last_rows, cols] = spare[even, band]
            rhs_all[tail, cols] = spare[odd, band]

    grad_att[...] = back_product(acts[4], rhs_all[WIDTH:, :]).astype(jnp.bfloat16)
    cos_table = rope[0]
    sin_left = rope[1]
    sin_right = rope[2]
    scale = HEAD_DIM ** (-0.5)

    def turn(value, sign):
        return (
            value * cos_table
            + pltpu.roll(value, 120, 1) * (sign * sin_left)
            + pltpu.roll(value, 8, 1) * (sign * sin_right)
        )

    def units(block, carry):
        row = rows_of((ROWS, ROWS))
        lane = lanes_of((ROWS, ROWS))
        bound = wide(marks[block])

        def both(low, high):
            return jnp.where(row < SEQ, low, high), jnp.where(lane < SEQ, low, high)

        start_q, start_k = both(bound[0:1, 0:128], bound[1:2, 0:128])
        split_q, split_k = both(bound[2:3, 0:128], bound[3:4, 0:128])
        at_q = wide(row % SEQ)
        at_k = wide(lane % SEQ)
        same = (row // SEQ == lane // SEQ) & ((at_q >= split_q) == (at_k >= split_k))
        pic_q = (at_q >= start_q) & (at_q < start_q + PIC)
        pic_k = (at_k >= start_k) & (at_k < start_k + PIC)
        penalty = jnp.where(same & ((at_q >= at_k) | (pic_q & pic_k)), 0.0, -1e30)
        span = pl.ds(pl.multiple_of(block * ROWS, ROWS), ROWS)
        twins = [slice(twin * 128, twin * 128 + 128) for twin in range(2)]
        heads = [(twin, head) for twin in range(2) for head in range(2)]
        query = [turn(linear[0, span, cols], 1.0) for cols in twins]
        query_low = [item.astype(jnp.bfloat16) for item in query]
        key_low = [turn(linear[1, span, cols], 1.0).astype(jnp.bfloat16) for cols in twins]
        value_low = [linear[2, span, cols].astype(jnp.bfloat16) for cols in twins]
        grad_low = [grad_att[span, cols] for cols in twins]

        def only(item, head):
            return jnp.where(lane // 64 == head, wide(item), 0.0).astype(jnp.bfloat16)

        scores = [
            back_product(only(query[twin], head), key_low[twin]) * scale + penalty
            for twin, head in heads
        ]
        grad_probs = [
            back_product(only(grad_low[twin], head), value_low[twin]) for twin, head in heads
        ]
        exponent = [jnp.exp(item - jnp.max(item, axis=-1, keepdims=True)) for item in scores]
        probs = [item / jnp.sum(item, axis=-1, keepdims=True) for item in exponent]
        probs_low = [item.astype(jnp.bfloat16) for item in probs]
        grad_scores = [
            (prob * (grad - jnp.sum(prob * grad, axis=-1, keepdims=True))).astype(jnp.bfloat16)
            for prob, grad in zip(probs, grad_probs)
        ]
        attended = [matmul(probs_low[i], value_low[heads[i][0]]) for i in range(4)]
        grad_value = [outer_sum(probs_low[i], grad_low[heads[i][0]]) for i in range(4)]
        grad_query = [matmul(grad_scores[i], key_low[heads[i][0]]) for i in range(4)]
        grad_key = [outer_sum(grad_scores[i], query_low[heads[i][0]]) for i in range(4)]

        def merge(items, twin):
            return jnp.where(lane < 64, items[2 * twin], items[2 * twin + 1])

        for twin, cols in enumerate(twins):
            side = slice(WIDTH + twin * 128, WIDTH + twin * 128 + 128)
            lhs_all[span, side] = merge(attended, twin).astype(jnp.bfloat16)
            grad_lin[0, span, cols] = turn(merge(grad_query, twin) * scale, -1.0).astype(
                jnp.bfloat16
            )
            grad_lin[1, span, cols] = turn(merge(grad_key, twin) * scale, -1.0).astype(
                jnp.bfloat16
            )
            grad_lin[2, span, cols] = merge(grad_value, twin).astype(jnp.bfloat16)
        return carry

    lax.fori_loop(0, 4, units, 0)

    for copy in third:
        copy.wait()

    def hidden(pair, carry):
        cols = pl.ds(pl.multiple_of(pair * 256, 256), 256)
        up_pre = matmul(acts[3], up_all[:, cols])
        bell = 0.5 * (1.0 + lax.erf(up_pre * ROOT_HALF))
        slope = bell + up_pre * NORMAL_PEAK * jnp.exp(-0.5 * up_pre * up_pre)
        lhs_all[:, cols] = (up_pre * bell).astype(jnp.bfloat16)
        grad_gated = back_product(acts[4], rhs_all[cols, :])
        grad_pre[:, cols] = (grad_gated * slope).astype(jnp.bfloat16)
        return carry

    lax.fori_loop(0, 4, hidden, 0)

    def weights(index, carry):
        cols = pl.ds(pl.multiple_of(index * 128, 128), 128)
        grad = outer_sum(acts[3, :, cols], grad_pre[...]).astype(jnp.bfloat16)
        for block in range(4):
            parts[index, block] = grad[:, block * 256 : block * 256 + 256]
        for stream in range(3):
            parts[index, 4 + stream] = outer_sum(acts[stream, :, cols], grad_lin[stream]).astype(
                jnp.bfloat16
            )
        grad = outer_sum(lhs_all[:, cols], acts[4]).astype(jnp.bfloat16)
        other = index + 1 - 2 * (index % 2)
        for block in range(4):
            part = grad[:, block * 256 : block * 256 + 256]
            parts[index, 7 + block, 0:96] = part[0:96]

            @pl.when(index % 2 == core)
            def _():
                parts[other, 11, block * 32 : block * 32 + 32] = part[96:128]

            @pl.when(index % 2 != core)
            def _():
                parts[index, 7 + block, 96:128] = part[96:128]

        return carry

    lax.fori_loop(0, 8, weights, 0)
    grad = outer_sum(lhs_all[:, WIDTH:], acts[4]).astype(jnp.bfloat16)
    for block in range(4):
        part = grad[:, block * 256 : block * 256 + 256]
        for pair in range(4):
            even = 2 * pair + core
            parts[even, 7 + block, 96:128] = part[pair * 64 : pair * 64 + 32]
            parts[even, 11, block * 32 : block * 32 + 32] = part[pair * 64 + 32 : pair * 64 + 64]
    sent = [
        pltpu.make_async_copy(
            parts.at[target[0], pl.ds(0, PART)], chunk_low, chunk_sems.at[0]
        ),
        pltpu.make_async_copy(
            parts.at[target[0], pl.ds(PART, 12 - PART)], chunk_high, chunk_sems.at[8]
        ),
    ] + [
        pltpu.make_async_copy(parts.at[target[index]], chunks[index - 1], chunk_sems.at[index])
        for index in range(1, 8)
    ]
    for copy in sent:
        copy.start()

    def put(unit, cols, value):
        low = value.astype(jnp.bfloat16)
        for half in range(2):
            for block in range(2):
                at = (2 * half + block) * ROWS
                tokens[half, block, unit, :, cols] = low[at : at + ROWS]

    def ship(unit):
        for half, ref in enumerate((keep, send)):
            copy = pltpu.make_async_copy(
                tokens.at[half, :, unit], ref.at[:, unit], token_sems.at[half, unit]
            )
            copy.start()
            sent.append(copy)

    for stream in range(3):
        put(stream, slice(0, WIDTH), back_product(grad_lin[stream], lin_all[stream]))
        ship(stream)

    def feed(block, carry):
        cols = pl.ds(pl.multiple_of(block * 256, 256), 256)
        put(3, cols, back_product(grad_pre[...], up_all[cols, :]))
        put(4, cols, matmul(lhs_all[...], rhs_all[:, cols]))
        return carry

    lax.fori_loop(0, 4, feed, 0)
    ship(3)
    ship(4)
    for copy in sent:
        copy.wait()


def back_kernel(
    stack,
    cotangent,
    scaled,
    stats,
    keep,
    came,
    across,
    mix_gain,
    mix_up,
    mix_down,
    norm_gain,
    stack_grad,
    small_own,
    small_other,
    coefficients,
    grads,
    sums,
    coef_grad,
    small,
):
    seqs = stack.shape[0]
    sums[...] = jnp.zeros_like(sums)
    lane = lanes_of((16, 128))

    def unit(step, carry):
        row = pl.multiple_of(step * 16, 16)
        span = pl.ds(row, 16)

        def result(index):
            return wide(keep[0, index, span]) + wide(came[0, index, span]) + wide(across[index, span])

        for stream in range(4):
            item = result(stream)
            scale = scaled[stream, span]
            moved = item * scale
            sums[stream] += moved[:8] + moved[8:]
            sums[4 + stream] += item[:8] + item[8:]
            weighted = item * norm_gain[stream : stream + 1]
            mean = jnp.mean(weighted, axis=-1, keepdims=True)
            slant = jnp.mean(weighted * scale, axis=-1, keepdims=True)
            grad = stats[2, span, stream : stream + 1] * (weighted - mean - scale * slant)
            if stream == 3:
                grad = grad + wide(cotangent[span])
            grads[stream, span] = grad
        return carry

    lax.fori_loop(0, seqs * SEQ // 16, unit, 0)
    for seq in range(seqs):

        def coefs(step, carry):
            row = pl.multiple_of(step * 16, 16)
            span = pl.ds(seq * SEQ + row, 16)
            found = jnp.zeros((16, 128), jnp.float32)
            for layer in range(STREAMS_IN):
                value = wide(stack[seq, layer, pl.ds(row, 16), :])
                for stream in range(4):
                    got = jnp.sum(grads[stream, span] * value, axis=-1, keepdims=True)
                    found = jnp.where(lane == stream * STREAMS_IN + layer, got, found)
            coef_grad[span] = found
            return carry

        lax.fori_loop(0, SEQ // 16, coefs, 0)
    grad_coef = coef_grad[:, 0:36]
    hidden_pre = stats[1, :, 0:36]
    hidden_low = gelu_value(hidden_pre).astype(jnp.bfloat16)
    for seq in range(seqs):
        turned = stats[0, seq * SEQ : seq * SEQ + SEQ, :].T
        for stream in range(4):
            for layer in range(STREAMS_IN):
                at = stream * STREAMS_IN + layer
                coefficients[seq, layer, stream : stream + 1] = turned[at : at + 1]
    small[...] = jnp.zeros_like(small)
    small[0:36, WIDTH : WIDTH + 36] = lax.dot_general(
        wide(hidden_low),
        grad_coef,
        (((0,), (0,)), ((), ())),
        precision=HIGHEST,
        preferred_element_type=jnp.float32,
    )
    small[36:37, WIDTH : WIDTH + 36] = jnp.sum(grad_coef, axis=0, keepdims=True)
    grad_hidden = (
        lax.dot_general(
            grad_coef,
            mix_down[...],
            (((1,), (1,)), ((), ())),
            precision=HIGHEST,
            preferred_element_type=jnp.float32,
        )
        * gelu_slope(hidden_pre)
    ).astype(jnp.bfloat16)
    gain_row = jnp.zeros((8, WIDTH), jnp.float32)
    up_part = jnp.zeros((36, WIDTH), jnp.float32)
    for seq in range(seqs):
        at = slice(seq * SEQ, seq * SEQ + SEQ)
        last = wide(stack[seq, STREAMS_IN - 1])
        rms = stats[2, at, 4:5]
        mixed_in = (last * rms * mix_gain[...]).astype(jnp.bfloat16)
        up_part = up_part + outer_sum(grad_hidden[at], mixed_in)
        grad_mixed = matmul(grad_hidden[at], mix_up[...])
        along = grad_mixed * last * rms
        for place in range(SEQ // 8):
            gain_row = gain_row + along[place * 8 : place * 8 + 8]
        weighted = grad_mixed * mix_gain[...]
        mean = jnp.mean(weighted * last, axis=-1, keepdims=True)
        grads[4, at] = rms * (weighted - last * (rms * rms * mean))

        def layers(step, carry):
            row = pl.multiple_of(step // 2 * 16, 16)
            cols = pl.ds(pl.multiple_of(step % 2 * 512, 512), 512)
            span = pl.ds(seq * SEQ + row, 16)
            rows_coef = stats[0, span, :]
            parts = [grads[stream, span, cols] for stream in range(4)]
            for layer in range(STREAMS_IN):
                total = None
                for stream in range(4):
                    at_coef = stream * STREAMS_IN + layer
                    term = rows_coef[:, at_coef : at_coef + 1] * parts[stream]
                    total = term if total is None else total + term
                if layer == STREAMS_IN - 1:
                    total = total + grads[4, span, cols]
                stack_grad[seq, layer, pl.ds(row, 16), cols] = total.astype(jnp.bfloat16)
            return carry

        lax.fori_loop(0, 8, layers, 0)
    small[0:36, 0:WIDTH] = up_part
    for place in range(8):
        small[36 + place : 37 + place, 0:WIDTH] = jnp.sum(sums[place], axis=0, keepdims=True)
    small[44:45, 0:WIDTH] = jnp.sum(gain_row, axis=0, keepdims=True)
    _, _, _, core = position()
    small_own[...] = small[pl.ds(pl.multiple_of(core * 24, 8), 24), :]
    small_other[...] = small[pl.ds(pl.multiple_of(24 - core * 24, 8), 24), :]


def place_kernel(
    shard0,
    shard1,
    shard2,
    shard3,
    small_own,
    small_other,
    projection,
    out_grad,
    up_grad,
    down_grad,
    mix_gain_grad,
    mix_up_grad,
    mix_down_grad,
    mix_static_grad,
    gain_grad,
    bias_grad,
    small,
):
    z, member_parity, x, core = position()
    small[pl.ds(pl.multiple_of(core * 24, 8), 24), :] = small_own[...]
    small[pl.ds(pl.multiple_of(24 - core * 24, 8), 24), :] = small_other[...]
    lanes = pl.ds(pl.multiple_of((2 * z + member_parity) * 128, 128), 128)
    mix_up_grad[...] = small[0:36, lanes]
    gain_grad[...] = small[36:40, 0:WIDTH]
    bias_grad[...] = small[40:44, 0:WIDTH]
    mix_gain_grad[...] = small[44:45, 0:WIDTH]
    mix_down_grad[...] = small[0:36, WIDTH : WIDTH + 36]
    for stream in range(4):
        at = WIDTH + stream * STREAMS_IN
        mix_static_grad[stream : stream + 1] = small[36:37, at : at + STREAMS_IN]
    shards = (shard0, shard1, shard2, shard3)
    lane = lanes_of((128, 128))
    for back in range(4):
        from_x = x if back % 2 == 0 else 1 - x
        from_core = core if back < 2 else 1 - core
        quarter = 2 * from_x + from_core
        own, twin = shards[back], shards[back ^ 2]
        for index in range(8):
            half = index % 2
            mine = wide(own[index // 2, :, half * 128 : half * 128 + 128])
            half_b = 1 - half
            lent = wide(twin[index // 2, :, half_b * 128 : half_b * 128 + 128])
            col = pl.multiple_of((index * 4 + quarter) * 128, 128)
            up_grad[:, pl.ds(col, 128)] = jnp.where(
                (lane >= 96) & (from_core == half), lent, mine
            )
        row = pl.multiple_of(quarter * 128, 128)
        for block in range(4):
            cols = slice(block * 256, block * 256 + 256)
            down_grad[pl.ds(row, 96), cols] = wide(own[7 + block, 0:96])

            @pl.when(member_parity == from_core)
            def _():
                head_row = pl.multiple_of(from_x * 64, 64)
                out_grad[pl.ds(head_row, 32), cols] = wide(own[7 + block, 96:128])
                out_grad[pl.ds(head_row + 32, 32), cols] = wide(
                    own[11, block * 32 : block * 32 + 32]
                )
                down_grad[pl.ds(row + 96, 32), cols] = wide(
                    twin[11, block * 32 : block * 32 + 32]
                )

            @pl.when(member_parity != from_core)
            def _():
                down_grad[pl.ds(row + 96, 32), cols] = wide(own[7 + block, 96:128])

    for back in (0, 2):
        from_core = core if back < 2 else 1 - core
        for stream in range(3):
            for twin in range(2):
                tile = slice(twin * 128, twin * 128 + 128)
                mine = wide(shards[back][4 + stream, :, tile])
                across = wide(shards[back + 1][4 + stream, :, tile])
                even = jnp.where(x == 0, mine, across)
                odd = jnp.where(x == 0, across, mine)
                first = jnp.where(lane < 64, even, pltpu.roll(odd, 64, 1))
                second = jnp.where(lane < 64, pltpu.roll(even, 64, 1), odd)
                for low, value in ((0, first), (1, second)):
                    col = pl.multiple_of((2 * twin + low) * 256 + from_core * 128, 128)
                    projection[stream, :, pl.ds(col, 128)] = value


def call(kernel, outs, specs, out_specs, args, scratch=(), cost=None, vmem=60 << 20):
    return pl.pallas_call(
        kernel,
        out_shape=outs,
        in_specs=specs,
        out_specs=out_specs,
        scratch_shapes=list(scratch),
        compiler_params=pltpu.CompilerParams(vmem_limit_bytes=vmem),
        cost_estimate=cost,
    )(*args)


def shape_of(shape, dtype=jnp.bfloat16):
    return jax.ShapeDtypeStruct(shape, dtype)


def rope_tables():
    half_rot = ROTARY // 2
    step = 10000.0 ** (-2.0 * np.arange(half_rot) / ROTARY)
    angles = np.arange(SEQ)[:, None] * step[None, :]
    cos_table = np.ones((SEQ, HEAD_DIM))
    left = np.zeros((SEQ, HEAD_DIM))
    right = np.zeros((SEQ, HEAD_DIM))
    cos_table[:, :half_rot] = np.cos(angles)
    cos_table[:, half_rot:ROTARY] = np.cos(angles)
    left[:, :half_rot] = -np.sin(angles)
    right[:, half_rot:ROTARY] = np.sin(angles)
    return np.stack([np.tile(item, (2, 2)) for item in (cos_table, left, right)]).astype(np.float32)


def on_device_tensor(
    layer_stack,
    out_cotangent,
    pic_start,
    doc_split,
    mix_gain,
    mix_up,
    mix_down,
    mix_static,
    norm_gain,
    norm_bias,
    query_key_value,
    out_weight,
    up_weight,
    down_weight,
):
    z, y, _, _ = position()
    micro_total, local_seqs, _, _, width = layer_stack.shape
    seqs = micro_total * local_seqs
    stack = jnp.transpose(layer_stack, (0, 1, 3, 2, 4)).reshape(seqs, STREAMS_IN, SEQ, width)
    cotangent = out_cotangent.reshape(ROWS, width)
    gain_row = mix_gain.reshape(1, width)

    piece = call(
        prepare_kernel,
        shape_of((12, 128, 256)),
        [VMEM_FULL] * 4,
        VMEM_FULL,
        (query_key_value, out_weight, up_weight, down_weight),
    )
    up_own = mix_up.T
    up_pair = jnp.concatenate([up_own, after(lax.ppermute(up_own, "fsdp", Y_SWAP), piece)], axis=1)
    ups = [up_pair] + [
        lax.ppermute(up_pair, "fsdp", z_pairs([((step + to) % 4, to) for to in range(4)]))
        for step in (1, 2, 3)
    ]
    piece = after(piece, *ups)
    bounds = jnp.concatenate([pic_start.reshape(seqs), doc_split.reshape(seqs)])
    kept = {}
    grad_across = lax.ppermute(cotangent, "replica", X_SWAP)
    grad_packets = (
        cotangent,
        grad_across,
        lax.ppermute(cotangent, "replica", CORE_SWAP),
        lax.ppermute(grad_across, "replica", CORE_SWAP),
    )

    def front():
        packet, *kept["rest"] = call(
            front_kernel,
            (
                shape_of((4 * ROWS + 16, width)),
                shape_of((4, ROWS, width), jnp.float32),
                shape_of((3, ROWS, 128), jnp.float32),
                shape_of((ROWS, width), jnp.float32),
                shape_of((36, width)),
            ),
            [SMEM_FULL] + [VMEM_FULL] * 10,
            (VMEM_FULL,) * 5,
            (
                bounds,
                stack,
                gain_row,
                *ups,
                mix_down,
                mix_static.reshape(1, 36),
                norm_gain,
                norm_bias,
            ),
            scratch=[pltpu.VMEM((4, ROWS, width), jnp.float32)],
        )
        across = lax.ppermute(packet, "replica", X_SWAP)
        beside = lax.ppermute(packet, "replica", CORE_SWAP)
        beside_across = lax.ppermute(across, "replica", CORE_SWAP)
        kept["packets"] = (packet, across, beside, beside_across)
        return (packet, grad_across), (across,)

    pieces = gather_fsdp(piece, z, front)
    packets = kept["packets"]
    scaled, stats, stream_last, mix_up_full = kept["rest"]

    results = call(
        main_kernel,
        (shape_of((PART, 128, 256)), shape_of((12 - PART, 128, 256)))
        + (shape_of((12, 128, 256)),) * 7
        + (shape_of((2, 5, ROWS, width)),) * 2,
        [VMEM_FULL] + [IN_PLACE] * 19,
        (IN_PLACE,) * 11,
        (jnp.asarray(rope_tables()),) + packets + grad_packets + tuple(pieces),
        scratch=[
            pltpu.VMEM((5, 4 * ROWS, width), jnp.bfloat16),
            pltpu.VMEM((4, 16, width), jnp.bfloat16),
            pltpu.VMEM((width, width), jnp.bfloat16),
            pltpu.VMEM((3, width, 256), jnp.bfloat16),
            pltpu.VMEM((width + 256, width), jnp.bfloat16),
            pltpu.VMEM((8, 128, 256), jnp.bfloat16),
            pltpu.VMEM((4 * ROWS, width + 256), jnp.bfloat16),
            pltpu.VMEM((4 * ROWS, width), jnp.bfloat16),
            pltpu.VMEM((3, 4 * ROWS, 256), jnp.float32),
            pltpu.VMEM((4 * ROWS, 256), jnp.bfloat16),
            pltpu.VMEM((3, 4 * ROWS, 256), jnp.bfloat16),
            pltpu.VMEM((8, 12, 128, 256), jnp.bfloat16),
            pltpu.VMEM((2, 2, 5, ROWS, width), jnp.bfloat16),
            pltpu.SemaphoreType.DMA((4, 6)),
            pltpu.SemaphoreType.DMA((8, 10)),
            pltpu.SemaphoreType.DMA((9,)),
            pltpu.SemaphoreType.DMA((2, 5)),
        ],
    )
    chunks, keep, send = results[:9], results[9], results[10]

    came = lax.ppermute(send, "replica", CORE_SWAP)
    sum_across = (wide(keep[1, :4]) + wide(came[1, :4])).astype(jnp.bfloat16)
    came_across = lax.ppermute(sum_across, "replica", X_SWAP)
    out_across = (wide(keep[1, 4]) + wide(came[1, 4])).astype(jnp.bfloat16)
    out_across = lax.ppermute(after(out_across, came_across), "replica", X_SWAP)
    layer_output = (
        stream_last + wide(keep[0, 4]) + wide(came[0, 4]) + wide(out_across)
    ).astype(jnp.bfloat16)

    first_half = pl.BlockSpec((1, 4, ROWS, width), lambda step: (0, 0, 0, 0))

    def whole(shape):
        return pl.BlockSpec(shape, lambda step: (0,) * len(shape))

    def back():
        kept["back"] = pl.pallas_call(
            back_kernel,
            grid=(1,),
            out_shape=(
                shape_of((seqs, STREAMS_IN, SEQ, width)),
                shape_of((24, width + 128), jnp.float32),
                shape_of((24, width + 128), jnp.float32),
                shape_of((seqs, STREAMS_IN, 4, SEQ), jnp.float32),
            ),
            in_specs=[
                whole((seqs, STREAMS_IN, SEQ, width)),
                whole((ROWS, width)),
                whole((4, ROWS, width)),
                whole((3, ROWS, 128)),
                first_half,
                first_half,
                whole((4, ROWS, width)),
                whole((1, width)),
                whole((36, width)),
                whole((36, 36)),
                whole((4, width)),
            ],
            out_specs=(
                whole((seqs, STREAMS_IN, SEQ, width)),
                whole((24, width + 128)),
                whole((24, width + 128)),
                whole((seqs, STREAMS_IN, 4, SEQ)),
            ),
            scratch_shapes=[
                pltpu.VMEM((5, ROWS, width), jnp.float32),
                pltpu.VMEM((8, 8, width), jnp.float32),
                pltpu.VMEM((ROWS, 128), jnp.float32),
                pltpu.VMEM((48, width + 128), jnp.float32),
            ],
            compiler_params=pltpu.CompilerParams(vmem_limit_bytes=56 << 20),
        )(
            stack,
            cotangent,
            scaled,
            stats,
            keep,
            came,
            came_across,
            gain_row,
            mix_up_full,
            mix_down,
            norm_gain,
        )
        return kept["back"][1]

    shard = scatter_fsdp(chunks, z, sum_across, back)
    stack_grad, small, small_other, coefficients = kept["back"]

    small = small + lax.ppermute(small_other, "replica", CORE_SWAP)
    small = small + lax.ppermute(small, "replica", X_SWAP)
    shard = after(shard, small, out_across)
    shard_across = lax.ppermute(shard, "replica", X_SWAP)
    shard_beside = lax.ppermute(shard, "replica", CORE_SWAP)
    for perm in (Y_SWAP, Z_SWAP_NEAR, Z_SWAP_FAR):
        small = small + lax.ppermute(small, "fsdp", perm)
    small_beside = lax.ppermute(small, "replica", CORE_SWAP)
    shard_both = lax.ppermute(after(shard_across, small), "replica", CORE_SWAP)
    owned = call(
        place_kernel,
        (
            shape_of((3, 128, width), jnp.float32),
            shape_of((128, width), jnp.float32),
            shape_of((128, 4 * width), jnp.float32),
            shape_of((512, width), jnp.float32),
            shape_of((1, width), jnp.float32),
            shape_of((36, 128), jnp.float32),
            shape_of((36, 36), jnp.float32),
            shape_of((4, STREAMS_IN), jnp.float32),
            shape_of((4, width), jnp.float32),
            shape_of((4, width), jnp.float32),
        ),
        [VMEM_FULL] * 6,
        (VMEM_FULL,) * 10,
        (shard, shard_across, shard_beside, shard_both, small, small_beside),
        scratch=[pltpu.VMEM((48, width + 128), jnp.float32)],
    )
    projection_grad, out_grad, up_grad, down_grad, *small_grads = owned
    shape = (micro_total, local_seqs, SEQ)
    stack_grad = stack_grad.reshape(micro_total, local_seqs, STREAMS_IN, SEQ, width)
    coefficients = coefficients.reshape(micro_total, local_seqs, STREAMS_IN, 4, SEQ)
    return (
        layer_output.reshape(shape + (width,)),
        jnp.transpose(coefficients, (0, 1, 4, 3, 2)),
        jnp.transpose(stack_grad, (0, 1, 3, 2, 4)),
        small_grads[0].reshape(width),
        small_grads[1].T,
        small_grads[2],
        small_grads[3],
        small_grads[4],
        small_grads[5],
        projection_grad,
        out_grad,
        up_grad,
        down_grad,
    )


def solution(mesh):
    fits = mesh.shape["fsdp"] == 8 and mesh.shape["replica"] == 4
    body = on_device_tensor if fits else on_device
    return jax.shard_map(
        body,
        mesh=mesh,
        in_specs=(
            P(None, ("fsdp", "replica"), None, None, None),
            P(None, ("fsdp", "replica"), None, None),
            P(None, ("fsdp", "replica")),
            P(None, ("fsdp", "replica")),
            P(),
            P("fsdp", None),
            P(),
            P(),
            P(),
            P(),
            P(None, "fsdp", None),
            P("fsdp", None),
            P("fsdp", None),
            P("fsdp", None),
        ),
        out_specs=(
            P(None, ("fsdp", "replica"), None, None),
            P(None, ("fsdp", "replica"), None, None, None),
            P(None, ("fsdp", "replica"), None, None, None),
            P(),
            P("fsdp", None),
            P(),
            P(),
            P(),
            P(),
            P(None, "fsdp", None),
            P("fsdp", None),
            P("fsdp", None),
            P("fsdp", None),
        ),
        check_vma=False,
    )
```

```python
import math

import jax
import jax.numpy as jnp
import numpy as np
from jax import lax
from jax.experimental import pallas as pl
from jax.experimental.pallas import tpu as pltpu
from jax.sharding import PartitionSpec as P

HEADS = 16
HEAD_DIM = 64
ROTARY = 16
STREAMS_IN = 9
SEQ = 64
PIC = 32


EPSILON = 1e-05
ROOT_HALF = 0.7071067811865476
NORMAL_PEAK = 0.3989422804014327
HIGHEST = lax.Precision.HIGHEST


def as_sent(value):

    def short(part):
        return part.astype(jnp.bfloat16) if part.dtype == jnp.float32 else part

    return jax.tree.map(short, value)


def gelu_value(values):
    return 0.5 * values * (1.0 + lax.erf(values * ROOT_HALF))


def gelu_slope(values):
    return 0.5 * (1.0 + lax.erf(values * ROOT_HALF)) + values * NORMAL_PEAK * jnp.exp(
        -0.5 * values * values
    )


def matmul(left_side, right_side):
    return jnp.dot(left_side, right_side, preferred_element_type=jnp.float32)


def outer_sum(left_side, right_side):
    return lax.dot_general(
        left_side, right_side, (((0,), (0,)), ((), ())), preferred_element_type=jnp.float32
    )


def back_product(left_side, right_side):
    return lax.dot_general(
        left_side, right_side, (((1,), (1,)), ((), ())), preferred_element_type=jnp.float32
    )


def rotary_tables():
    half_rot = ROTARY // 2
    inverse = jnp.exp(-math.log(10000.0) * (2.0 * jnp.arange(half_rot, dtype=jnp.float32) / ROTARY))
    angles = jnp.arange(SEQ, dtype=jnp.float32)[:, None] * inverse[None, :]
    return (jnp.cos(angles)[:, None, :], jnp.sin(angles)[:, None, :])


def rotate(values, cos_table, sin_table):
    half_rot = ROTARY // 2
    first_half = values[..., :half_rot]
    second = values[..., half_rot:ROTARY]
    return jnp.concatenate(
        [
            first_half * cos_table - second * sin_table,
            second * cos_table + first_half * sin_table,
            values[..., ROTARY:],
        ],
        axis=-1,
    )


def allowed_mask(starts, splits):
    positions = jnp.arange(SEQ, dtype=jnp.int32)
    second_doc = positions[None, :] >= splits[:, None]
    picture = (positions[None, :] >= starts[:, None]) & (positions[None, :] < starts[:, None] + PIC)
    same_doc = second_doc[:, :, None] == second_doc[:, None, :]
    causal = positions[:, None] >= positions[None, :]
    both_pic = picture[:, :, None] & picture[:, None, :]
    return same_doc & (causal[None] | both_pic)


def masked_scores(queries, key_rot, allowed):
    scores = jnp.einsum(
        "nqhe,nkhe->nhqk", queries, key_rot, preferred_element_type=jnp.float32
    ) * HEAD_DIM ** (-0.5)
    return jnp.where(allowed[:, None], scores, -1e30)


def on_device(
    layer_stack,
    out_cotangent,
    pic_start,
    doc_split,
    mix_gain,
    mix_up,
    mix_down,
    mix_static,
    norm_gain,
    norm_bias,
    query_key_value,
    out_weight,
    up_weight,
    down_weight,
):
    micro_total = layer_stack.shape[0]
    local_seqs = layer_stack.shape[1]
    model_width = layer_stack.shape[-1]
    groups = [(0, micro_total)]
    cos_table, sin_table = rotary_tables()
    output_list = []
    coef_list = []
    grad_list = []
    shard_total = None
    small_total = None
    for first_micro, micro_count in groups:
        seq_count = micro_count * local_seqs
        row_count = seq_count * SEQ
        head_shape = (seq_count, SEQ, HEADS, HEAD_DIM)
        flat_stack = layer_stack[first_micro : first_micro + micro_count].reshape(
            row_count, STREAMS_IN, model_width
        )
        grad_rows = out_cotangent[first_micro : first_micro + micro_count].reshape(
            row_count, model_width
        )
        starts = pic_start[first_micro : first_micro + micro_count].reshape(seq_count)
        splits = doc_split[first_micro : first_micro + micro_count].reshape(seq_count)
        allowed = allowed_mask(starts, splits)
        mix_up_full, projection_full, out_full = (
            lax.all_gather(mix_up, "fsdp", axis=0, tiled=True),
            lax.all_gather(query_key_value, "fsdp", axis=1, tiled=True),
            lax.all_gather(out_weight, "fsdp", axis=0, tiled=True),
        )
        up_full, down_full = (
            lax.all_gather(up_weight, "fsdp", axis=0, tiled=True),
            lax.all_gather(down_weight, "fsdp", axis=0, tiled=True),
        )
        last_layer = flat_stack[:, STREAMS_IN - 1, :].astype(jnp.float32)
        rms_scale = lax.rsqrt(jnp.mean(last_layer * last_layer, axis=-1, keepdims=True) + EPSILON)
        mixed_in = (last_layer * rms_scale * mix_gain).astype(jnp.bfloat16)
        hidden_pre = matmul(mixed_in, mix_up_full)
        hidden_mix = gelu_value(hidden_pre).astype(jnp.bfloat16)
        hidden_wide = hidden_mix.astype(jnp.float32)
        coef_flat = jnp.dot(hidden_wide, mix_down, precision=HIGHEST) + mix_static.reshape(-1)
        coef_rows = coef_flat.reshape(row_count, 4, STREAMS_IN)
        streams = coef_rows[:, :, 0, None] * flat_stack[:, None, 0, :].astype(jnp.float32)
        for layer_index in range(1, STREAMS_IN):
            streams = streams + coef_rows[:, :, layer_index, None] * flat_stack[
                :, None, layer_index, :
            ].astype(jnp.float32)
        center = streams - jnp.mean(streams, axis=-1, keepdims=True)
        inv_std = lax.rsqrt(jnp.mean(center * center, axis=-1, keepdims=True) + EPSILON)
        scaled = center * inv_std
        normed = (scaled * norm_gain + norm_bias).astype(jnp.bfloat16)
        query_lin = matmul(normed[:, 0], projection_full[0])
        key_lin = matmul(normed[:, 1], projection_full[1])
        value_lin = matmul(normed[:, 2], projection_full[2])
        queries = rotate(query_lin.reshape(head_shape), cos_table, sin_table).astype(jnp.bfloat16)
        key_rot = rotate(key_lin.reshape(head_shape), cos_table, sin_table).astype(jnp.bfloat16)
        values = value_lin.astype(jnp.bfloat16).reshape(head_shape)
        scores = masked_scores(queries, key_rot, allowed)
        row_top = jnp.max(scores, axis=-1, keepdims=True)
        exponent = jnp.exp(scores - row_top)
        row_total = jnp.sum(exponent, axis=-1, keepdims=True)
        soft_probs = exponent / row_total
        log_total = row_top + jnp.log(row_total)
        attended = (
            jnp.einsum(
                "nhqk,nkhe->nqhe",
                soft_probs.astype(jnp.bfloat16),
                values,
                preferred_element_type=jnp.float32,
            )
            .astype(jnp.bfloat16)
            .reshape(row_count, model_width)
        )
        attn_out = matmul(attended, out_full)
        up_pre = matmul(normed[:, 3], up_full)
        gated_act = gelu_value(up_pre).astype(jnp.bfloat16)
        feed_out = matmul(gated_act, down_full)
        output_list.append((streams[:, 3] + attn_out + feed_out).astype(jnp.bfloat16))
        coef_list.append(coef_rows)
        mix_up_back, projection_back, out_back = (
            lax.all_gather(mix_up, "fsdp", axis=0, tiled=True),
            lax.all_gather(query_key_value, "fsdp", axis=1, tiled=True),
            lax.all_gather(out_weight, "fsdp", axis=0, tiled=True),
        )
        up_back, down_back = (
            lax.all_gather(up_weight, "fsdp", axis=0, tiled=True),
            lax.all_gather(down_weight, "fsdp", axis=0, tiled=True),
        )
        grad_down = outer_sum(gated_act, grad_rows)
        grad_gated = back_product(grad_rows, down_back)
        grad_up_pre = (grad_gated * gelu_slope(up_pre)).astype(jnp.bfloat16)
        grad_up = outer_sum(normed[:, 3], grad_up_pre)
        grad_norm_feed = back_product(grad_up_pre, up_back)
        feed_shards = (
            lax.psum_scatter(
                grad_up.astype(jnp.bfloat16), "fsdp", scatter_dimension=0, tiled=True
            ).astype(jnp.float32),
            lax.psum_scatter(
                grad_down.astype(jnp.bfloat16), "fsdp", scatter_dimension=0, tiled=True
            ).astype(jnp.float32),
        )
        grad_out_weight = outer_sum(attended, grad_rows)
        grad_attended = back_product(grad_rows, out_back).astype(jnp.bfloat16).reshape(head_shape)
        scores_again = masked_scores(queries, key_rot, allowed)
        probs_again = jnp.exp(scores_again - log_total)
        grad_probs = jnp.einsum(
            "nqhe,nkhe->nhqk", grad_attended, values, preferred_element_type=jnp.float32
        )
        grad_value = (
            jnp.einsum(
                "nhqk,nqhe->nkhe",
                probs_again.astype(jnp.bfloat16),
                grad_attended,
                preferred_element_type=jnp.float32,
            )
            .astype(jnp.bfloat16)
            .reshape(row_count, model_width)
        )
        delta_rows = jnp.sum(probs_again * grad_probs, axis=-1, keepdims=True)
        grad_scores = (probs_again * (grad_probs - delta_rows)).astype(jnp.bfloat16)
        score_scale = HEAD_DIM ** (-0.5)
        grad_query_rot = (
            jnp.einsum("nhqk,nkhe->nqhe", grad_scores, key_rot, preferred_element_type=jnp.float32)
            * score_scale
        )
        grad_key_rot = (
            jnp.einsum("nhqk,nqhe->nkhe", grad_scores, queries, preferred_element_type=jnp.float32)
            * score_scale
        )
        grad_query = (
            rotate(grad_query_rot, cos_table, -sin_table)
            .astype(jnp.bfloat16)
            .reshape(row_count, model_width)
        )
        grad_key = (
            rotate(grad_key_rot, cos_table, -sin_table)
            .astype(jnp.bfloat16)
            .reshape(row_count, model_width)
        )
        grad_linear = (grad_query, grad_key, grad_value)
        grad_projection = jnp.stack(
            [outer_sum(normed[:, stream], grad_linear[stream]) for stream in range(3)]
        )
        grad_normed = jnp.stack(
            [back_product(grad_linear[stream], projection_back[stream]) for stream in range(3)]
            + [grad_norm_feed],
            axis=1,
        )
        gain_grad = jnp.sum(grad_normed * scaled, axis=0)
        bias_grad = jnp.sum(grad_normed, axis=0)
        grad_scaled = grad_normed * norm_gain
        grad_streams = inv_std * (
            grad_scaled
            - jnp.mean(grad_scaled, axis=-1, keepdims=True)
            - scaled * jnp.mean(grad_scaled * scaled, axis=-1, keepdims=True)
        )
        grad_streams = grad_streams + jnp.concatenate(
            [
                jnp.zeros((row_count, 3, model_width), jnp.float32),
                grad_rows[:, None, :].astype(jnp.float32),
            ],
            axis=1,
        )
        grad_coef = jnp.stack(
            [
                jnp.sum(
                    grad_streams * flat_stack[:, None, layer_index, :].astype(jnp.float32), axis=-1
                )
                for layer_index in range(STREAMS_IN)
            ],
            axis=-1,
        )
        grad_coef_flat = grad_coef.reshape(row_count, 4 * STREAMS_IN)
        static_grad = jnp.sum(grad_coef_flat, axis=0).reshape(4, STREAMS_IN)
        down_mix_grad = jnp.dot(hidden_wide.T, grad_coef_flat, precision=HIGHEST)
        grad_hidden = (
            jnp.dot(grad_coef_flat, mix_down.T, precision=HIGHEST) * gelu_slope(hidden_pre)
        ).astype(jnp.bfloat16)
        grad_mix_up = outer_sum(mixed_in, grad_hidden)
        grad_mixed = back_product(grad_hidden, mix_up_back)
        gain_mix_grad = jnp.sum(grad_mixed * last_layer * rms_scale, axis=0)
        weighted = grad_mixed * mix_gain
        grad_last = rms_scale * (
            weighted
            - last_layer
            * rms_scale
            * rms_scale
            * jnp.mean(weighted * last_layer, axis=-1, keepdims=True)
        )
        per_layer = [
            jnp.sum(coef_rows[:, :, layer_index, None] * grad_streams, axis=1)
            for layer_index in range(STREAMS_IN)
        ]
        per_layer[STREAMS_IN - 1] = per_layer[STREAMS_IN - 1] + grad_last
        grad_list.append(jnp.stack(per_layer, axis=1).astype(jnp.bfloat16))
        attention_shards = (
            lax.psum_scatter(
                grad_mix_up.astype(jnp.bfloat16), "fsdp", scatter_dimension=0, tiled=True
            ).astype(jnp.float32),
            lax.psum_scatter(
                grad_projection.astype(jnp.bfloat16), "fsdp", scatter_dimension=1, tiled=True
            ).astype(jnp.float32),
            lax.psum_scatter(
                grad_out_weight.astype(jnp.bfloat16), "fsdp", scatter_dimension=0, tiled=True
            ).astype(jnp.float32),
        )
        shards = attention_shards + feed_shards
        shards = jax.tree.map(
            lambda part: part.astype(jnp.float32), lax.psum(as_sent(shards), "replica")
        )
        smalls = (gain_mix_grad, down_mix_grad, static_grad, gain_grad, bias_grad)
        if shard_total is None:
            shard_total = shards
            small_total = smalls
        else:
            shard_total = tuple(
                (total_item + new_item for total_item, new_item in zip(shard_total, shards))
            )
            small_total = tuple(
                (total_item + new_item for total_item, new_item in zip(small_total, smalls))
            )
    small_total = lax.psum(small_total, ("fsdp", "replica"))
    layer_output = jnp.concatenate(output_list, axis=0).reshape(
        micro_total, local_seqs, SEQ, model_width
    )
    coefficients = jnp.concatenate(coef_list, axis=0).reshape(
        micro_total, local_seqs, SEQ, 4, STREAMS_IN
    )
    stack_grad = jnp.concatenate(grad_list, axis=0).reshape(
        micro_total, local_seqs, SEQ, STREAMS_IN, model_width
    )
    return (
        layer_output,
        coefficients,
        stack_grad,
        small_total[0],
        shard_total[0],
        small_total[1],
        small_total[2],
        small_total[3],
        small_total[4],
        shard_total[1],
        shard_total[2],
        shard_total[3],
        shard_total[4],
    )


ROWS = 128
WIDTH = 1024
VMEM_FULL = pl.BlockSpec(memory_space=pltpu.VMEM)
SMEM_FULL = pl.BlockSpec(memory_space=pltpu.SMEM)
IN_PLACE = pl.BlockSpec(memory_space=pl.ANY)


def bits_swap(size, bit):
    return [(index, index ^ bit) for index in range(size)]


CORE_SWAP = bits_swap(4, 1)
X_SWAP = bits_swap(4, 2)
Y_SWAP = bits_swap(8, 1)
Z_SWAP_NEAR = bits_swap(8, 2)
Z_SWAP_FAR = bits_swap(8, 4)


def z_pairs(moves):
    return [(2 * src + col, 2 * dst + col) for src, dst in moves for col in range(2)]


def pick(cond, first, second):
    return jnp.where(cond, first, second)


def order_two(flag, own, other, axis):
    first = pick(flag == 0, own, other)
    second = pick(flag == 0, other, own)
    return jnp.concatenate([first, second], axis=axis)


def after(value, *others):
    return lax.optimization_barrier((value,) + others)[0]


Z_NEAR = z_pairs([(0, 1), (1, 0), (2, 3), (3, 2)])
Z_MIDDLE = [
    (index, (index ^ 1) if index // 8 in (0, 3) else (24 - index // 8 * 8 + index % 8))
    for index in range(32)
]


def fsdp_move(value, pairs):
    return lax.ppermute(value, "fsdp" if len(pairs) == 8 else ("fsdp", "replica"), pairs)


PART = 7


def gather_fsdp(piece, z, front):
    inner = (z == 1) | (z == 2)
    near = fsdp_move(piece, Z_NEAR)
    middle = fsdp_move(piece, Z_MIDDLE)
    side = fsdp_move(piece, Y_SWAP)
    early, late = front()
    middle_near = fsdp_move(after(near, *early, side), Z_MIDDLE)
    turned = fsdp_move(after(pick(inner, middle, side), *early), Z_NEAR)
    side_two = fsdp_move(pick(inner, middle, near), Y_SWAP)
    third = pick(inner, middle_near, turned)
    near_twice = fsdp_move(after(middle_near, side_two, third), Z_NEAR)
    side_three = fsdp_move(third, Y_SWAP)
    over_z = fsdp_move(side_three[:PART], Z_NEAR)
    over_y = fsdp_move(after(near_twice[PART:], side_three, *late), Y_SWAP)
    return [
        piece,
        side,
        near,
        middle,
        middle_near,
        turned,
        near_twice,
        side_two,
        side_three,
        over_z,
        over_y,
    ]


def position():
    member, partner = lax.axis_index("fsdp"), lax.axis_index("replica")
    return member // 2, member % 2, partner // 2, partner % 2


def table(values, z):
    found = jnp.int32(values[0])
    for index in range(1, 4):
        found = jnp.where(z == index, jnp.int32(values[index]), found)
    return found


def gather_order(z, y):
    places = []
    for z_from in (z, table([1, 0, 3, 2], z), table([2, 2, 1, 1], z), table([3, 3, 0, 0], z)):
        places += [2 * z_from + y, 2 * z_from + 1 - y]
    return places


def scatter_order(z, y):
    others = (table([3, 0, 3, 0], z), table([2, 3, 0, 1], z), table([1, 2, 1, 2], z), z)
    own = (table([3, 3, 0, 0], z), table([2, 2, 1, 1], z), table([1, 0, 3, 2], z), z)
    return [2 * z_to + 1 - y for z_to in others] + [2 * z_to + y for z_to in own]


def wide(value):
    return value.astype(jnp.float32)


def scatter_fsdp(chunks, z, first_wait, beside):
    inner = (z == 1) | (z == 2)
    side_low, side_high, side_one, side_two, side_own, last, third, near, own = chunks

    def low(value):
        return value.astype(jnp.bfloat16)

    def only(cond, value):
        return jnp.where(cond, wide(value), 0.0)

    over_z = fsdp_move(side_high, Z_NEAR)
    over_y = fsdp_move(side_low, Y_SWAP)
    over_z = jnp.pad(only(inner, over_z), ((PART, 0), (0, 0), (0, 0)))
    back_one = fsdp_move(low(wide(side_one) + over_z), Y_SWAP)
    over_y = jnp.pad(wide(over_y), ((0, 12 - PART), (0, 0), (0, 0)))
    back_far = fsdp_move(low(wide(after(last, first_wait)) + over_y), Z_NEAR)
    back_two = fsdp_move(after(side_two, first_wait), Y_SWAP)
    to_middle = low(wide(last) + wide(back_one) + wide(back_far))
    to_near = low(
        jnp.where(
            inner,
            wide(jnp.concatenate([side_low, side_high])),
            wide(third) + wide(back_one),
        )
    )
    middle_one = fsdp_move(to_middle, Z_MIDDLE)
    near_one = fsdp_move(to_near, Z_NEAR)
    back_own = fsdp_move(low(wide(side_own) + only(z % 3 == 0, near_one)), Y_SWAP)
    to_near = low(wide(near) + jnp.where(inner, wide(middle_one), wide(back_two)))
    to_middle = low(wide(third) + wide(back_two) + wide(near_one))
    to_near, to_middle, _ = lax.optimization_barrier((to_near, to_middle, beside()))
    near_two = fsdp_move(to_near, Z_NEAR)
    middle_two = fsdp_move(to_middle, Z_MIDDLE)
    return low(wide(own) + wide(back_own) + wide(near_two) + only(inner, middle_two))


def lanes_of(shape):
    return lax.broadcasted_iota(jnp.int32, shape, 1)


def rows_of(shape):
    return lax.broadcasted_iota(jnp.int32, shape, 0)


def prepare_kernel(projection, out_weight, up_weight, down_weight, piece):
    _, member_parity, x, core = position()
    quarter, other = 2 * x + core, 2 * x + 1 - core
    lane = lanes_of((128, 128))
    for index in range(8):
        half = index % 2
        own = up_weight[:, pl.ds(pl.multiple_of((index * 4 + quarter) * 128, 128), 128)]
        extra = up_weight[:, pl.ds(pl.multiple_of(((index ^ 1) * 4 + other) * 128, 128), 128)]
        taken = (lane >= 96) & (core == half)
        piece[index // 2, :, half * 128 : half * 128 + 128] = jnp.where(
            taken, wide(extra), wide(own)
        ).astype(jnp.bfloat16)
    for stream in range(3):
        for twin in range(2):
            tiles = [
                wide(
                    projection[
                        stream,
                        :,
                        pl.ds(pl.multiple_of((2 * twin + low) * 256 + core * 128, 128), 128),
                    ]
                )
                for low in range(2)
            ]
            first = jnp.where(x == 0, tiles[0], pltpu.roll(tiles[0], 64, 1))
            second = jnp.where(x == 0, pltpu.roll(tiles[1], 64, 1), tiles[1])
            piece[4 + stream, :, twin * 128 : twin * 128 + 128] = jnp.where(
                lane < 64, first, second
            ).astype(jnp.bfloat16)
    own_row = pl.multiple_of(quarter * 128, 128)
    other_row = pl.multiple_of(other * 128, 128)
    head_row = pl.multiple_of(x * 64, 64)
    for block in range(4):
        cols = slice(block * 256, block * 256 + 256)
        piece[7 + block, 0:96] = down_weight[pl.ds(own_row, 96), cols]

        @pl.when(member_parity == core)
        def _():
            piece[7 + block, 96:128] = out_weight[pl.ds(head_row, 32), cols]
            piece[11, block * 32 : block * 32 + 32] = out_weight[pl.ds(head_row + 32, 32), cols]

        @pl.when(member_parity != core)
        def _():
            piece[7 + block, 96:128] = down_weight[pl.ds(own_row + 96, 32), cols]
            piece[11, block * 32 : block * 32 + 32] = down_weight[pl.ds(other_row + 96, 32), cols]


def front_kernel(
    bounds,
    stack,
    mix_gain,
    up_own,
    up_one,
    up_two,
    up_three,
    mix_down,
    mix_static,
    norm_gain,
    norm_bias,
    packet,
    scaled_out,
    stats,
    stream_out,
    mix_up,
    streams,
):
    seqs = stack.shape[0]
    z, y, _, _ = position()
    for step, part in enumerate((up_own, up_one, up_two, up_three)):
        z_from = (z + step) % 4
        for half, col in enumerate((y, 1 - y)):
            lanes = pl.ds(pl.multiple_of((2 * z_from + col) * 128, 128), 128)
            mix_up[:, lanes] = part[:, half * 128 : half * 128 + 128]
    for seq in range(seqs):
        last = wide(stack[seq, STREAMS_IN - 1])
        rms = lax.rsqrt(jnp.mean(last * last, axis=-1, keepdims=True) + EPSILON)
        mixed_in = (last * rms * mix_gain[...]).astype(jnp.bfloat16)
        hidden_pre = back_product(mixed_in, mix_up[...])
        hidden = wide(gelu_value(hidden_pre).astype(jnp.bfloat16))
        coef = jnp.dot(
            hidden, mix_down[...], precision=HIGHEST, preferred_element_type=jnp.float32
        )
        coef = coef + mix_static[...]
        at = slice(seq * SEQ, seq * SEQ + SEQ)
        stats[0, at, 0:36] = coef
        stats[1, at, 0:36] = hidden_pre
        stats[2, at, 4:5] = rms

        def mix(step, carry):
            row = pl.multiple_of(step // 2 * 16, 16)
            col = pl.multiple_of(step % 2 * 512, 512)
            rows_coef = stats[0, pl.ds(seq * SEQ + row, 16), :]
            totals = [None] * 4
            for layer in range(STREAMS_IN):
                value = wide(stack[seq, layer, pl.ds(row, 16), pl.ds(col, 512)])
                for stream in range(4):
                    at_coef = stream * STREAMS_IN + layer
                    term = rows_coef[:, at_coef : at_coef + 1] * value
                    totals[stream] = term if layer == 0 else totals[stream] + term
            for stream in range(4):
                streams[stream, pl.ds(seq * SEQ + row, 16), pl.ds(col, 512)] = totals[stream]
            return carry

        lax.fori_loop(0, 8, mix, 0)

    def norm(step, carry):
        row = pl.multiple_of(step * 16, 16)
        for stream in range(4):
            value = streams[stream, pl.ds(row, 16), :]
            center = value - jnp.mean(value, axis=-1, keepdims=True)
            inverse = lax.rsqrt(jnp.mean(center * center, axis=-1, keepdims=True) + EPSILON)
            scaled = center * inverse
            stats[2, pl.ds(row, 16), stream : stream + 1] = inverse
            scaled_out[stream, pl.ds(row, 16), :] = scaled
            packet[pl.ds(stream * ROWS + row, 16), :] = (
                scaled * norm_gain[stream : stream + 1, :] + norm_bias[stream : stream + 1, :]
            ).astype(jnp.bfloat16)
            if stream == 3:
                stream_out[pl.ds(row, 16), :] = value
        return carry

    lax.fori_loop(0, seqs * SEQ // 16, norm, 0)
    packet[4 * ROWS :] = jnp.zeros((16, WIDTH), jnp.bfloat16)
    row = rows_of((16, 128))
    marks = jnp.zeros((16, 128), jnp.float32)
    for place in range(2 * seqs):
        marks = jnp.where(row == place, wide(bounds[place]), marks)
    packet[4 * ROWS :, 0:128] = marks.astype(jnp.bfloat16)


def main_kernel(
    rope,
    packet0,
    packet1,
    packet2,
    packet3,
    cotangent0,
    cotangent1,
    cotangent2,
    cotangent3,
    piece0,
    piece1,
    piece2,
    piece3,
    piece4,
    piece5,
    piece6,
    piece7,
    piece8,
    piece9,
    piece10,
    chunk_low,
    chunk_high,
    chunk1,
    chunk2,
    chunk3,
    chunk4,
    chunk5,
    chunk6,
    chunk7,
    keep_own,
    keep_far,
    send_norm,
    keep_out,
    send_out,
    acts,
    marks,
    up_all,
    lin_all,
    down_all,
    out_rows,
    lhs_all,
    grad_pre,
    linear,
    grad_att,
    grad_lin,
    parts,
    tokens,
    packet_sems,
    piece_sems,
    chunk_sems,
    token_sems,
):
    z, y, _, core = position()
    origin = gather_order(z, y)
    target = scatter_order(z, y)
    packets = (packet0, packet1, packet2, packet3)
    cotangents = (cotangent0, cotangent1, cotangent2, cotangent3)
    piece, side, near, middle, middle_near, turned = piece0, piece1, piece2, piece3, piece4, piece5
    near_twice, side_two, side_three, over_z, over_y = piece6, piece7, piece8, piece9, piece10
    inner = (z == 1) | (z == 2)
    sources = (
        (piece, piece),
        (side, side),
        (near, near),
        (turned, side_two),
        (middle, turned),
        (side_two, side_three),
        (middle_near, near_twice),
        (side_three, None),
    )
    chunks = (chunk1, chunk2, chunk3, chunk4, chunk5, chunk6, chunk7)
    member_rows = [pl.ds(pl.multiple_of(place * 128, 128), 128) for place in origin]

    def unit_copies(unit):
        return [
            pltpu.make_async_copy(
                packets[block].at[pl.ds(unit * ROWS, ROWS)],
                acts.at[unit, pl.ds(block * ROWS, ROWS)],
                packet_sems.at[block, unit],
            )
            for block in range(4)
        ]

    def piece_copies(index, ref, tail_ref):
        rows = member_rows[index]
        down = 7 if tail_ref is ref else 0
        return [
            pltpu.make_async_copy(
                ref.at[pl.ds(4, 3)], lin_all.at[:, rows], piece_sems.at[index, 0]
            ),
            pltpu.make_async_copy(
                tail_ref.at[pl.ds(down, 5)], down_all.at[origin[index]], piece_sems.at[index, 1]
            ),
            pltpu.make_async_copy(
                ref.at[pl.ds(0, 4)], up_all.at[:, rows], piece_sems.at[index, 2]
            ),
        ]

    first = unit_copies(0) + unit_copies(1) + unit_copies(2)
    second = [
        pltpu.make_async_copy(
            cotangents[block],
            acts.at[4, pl.ds(block * ROWS, ROWS)],
            packet_sems.at[block, 4],
        )
        for block in range(4)
    ]
    for block in range(4):
        second.append(
            pltpu.make_async_copy(
                packets[block].at[pl.ds(4 * ROWS, 16)], marks.at[block], packet_sems.at[block, 5]
            )
        )
    third = unit_copies(3)
    for copy in first + second + third:
        copy.start()
    for index, (for_inner, for_ends) in enumerate(sources):
        copies = piece_copies(index, for_inner, for_inner)
        first.append(copies[0])
        second.append(copies[1])
        third.append(copies[2])
        if for_inner is for_ends:
            for copy in copies:
                copy.start()
            continue
        ends = (
            piece_copies(index, over_z, over_y)
            if for_ends is None
            else piece_copies(index, for_ends, for_ends)
        )

        @pl.when(inner)
        def _():
            for copy in copies:
                copy.start()

        @pl.when(jnp.logical_not(inner))
        def _():
            for copy in ends:
                copy.start()

    for copy in first:
        copy.wait()
    for stream in range(3):
        linear[stream] = matmul(acts[stream], lin_all[stream])
    for copy in second:
        copy.wait()
    for pair in range(4):
        even = 2 * pair + core
        odd = 2 * pair + 1 - core
        for block in range(4):
            band = slice(block * 32, block * 32 + 32)
            cols = slice(block * 256, block * 256 + 256)
            out_rows[pair * 64 : pair * 64 + 32, cols] = down_all[even, block, 96:128]
            out_rows[pair * 64 + 32 : pair * 64 + 64, cols] = down_all[even, 4, band]
            down_all[even, block, 96:128] = down_all[odd, 4, band]

    grad_att[...] = back_product(acts[4], out_rows[...]).astype(jnp.bfloat16)
    cos_table = rope[0]
    sin_left = rope[1]
    sin_right = rope[2]
    scale = HEAD_DIM ** (-0.5)

    def turn(value, sign):
        return (
            value * cos_table
            + pltpu.roll(value, 120, 1) * (sign * sin_left)
            + pltpu.roll(value, 8, 1) * (sign * sin_right)
        )

    def units(block, carry):
        row = rows_of((ROWS, ROWS))
        lane = lanes_of((ROWS, ROWS))
        bound = wide(marks[block])

        def both(low, high):
            return jnp.where(row < SEQ, low, high), jnp.where(lane < SEQ, low, high)

        start_q, start_k = both(bound[0:1, 0:128], bound[1:2, 0:128])
        split_q, split_k = both(bound[2:3, 0:128], bound[3:4, 0:128])
        at_q = wide(row % SEQ)
        at_k = wide(lane % SEQ)
        same = (row // SEQ == lane // SEQ) & ((at_q >= split_q) == (at_k >= split_k))
        pic_q = (at_q >= start_q) & (at_q < start_q + PIC)
        pic_k = (at_k >= start_k) & (at_k < start_k + PIC)
        penalty = jnp.where(same & ((at_q >= at_k) | (pic_q & pic_k)), 0.0, -1e30)
        span = pl.ds(pl.multiple_of(block * ROWS, ROWS), ROWS)
        twins = [slice(twin * 128, twin * 128 + 128) for twin in range(2)]
        heads = [(twin, head) for twin in range(2) for head in range(2)]
        query = [turn(linear[0, span, cols], 1.0) for cols in twins]
        query_low = [item.astype(jnp.bfloat16) for item in query]
        key_low = [turn(linear[1, span, cols], 1.0).astype(jnp.bfloat16) for cols in twins]
        value_low = [linear[2, span, cols].astype(jnp.bfloat16) for cols in twins]
        grad_low = [grad_att[span, cols] for cols in twins]

        def only(item, head):
            return jnp.where(lane // 64 == head, wide(item), 0.0).astype(jnp.bfloat16)

        scores = [
            back_product(only(query[twin], head), key_low[twin]) * scale + penalty
            for twin, head in heads
        ]
        grad_probs = [
            back_product(only(grad_low[twin], head), value_low[twin]) for twin, head in heads
        ]
        exponent = [jnp.exp(item - jnp.max(item, axis=-1, keepdims=True)) for item in scores]
        probs = [item / jnp.sum(item, axis=-1, keepdims=True) for item in exponent]
        probs_low = [item.astype(jnp.bfloat16) for item in probs]
        grad_scores = [
            (prob * (grad - jnp.sum(prob * grad, axis=-1, keepdims=True))).astype(jnp.bfloat16)
            for prob, grad in zip(probs, grad_probs)
        ]
        attended = [matmul(probs_low[i], value_low[heads[i][0]]) for i in range(4)]
        grad_value = [outer_sum(probs_low[i], grad_low[heads[i][0]]) for i in range(4)]
        grad_query = [matmul(grad_scores[i], key_low[heads[i][0]]) for i in range(4)]
        grad_key = [outer_sum(grad_scores[i], query_low[heads[i][0]]) for i in range(4)]

        def merge(items, twin):
            return jnp.where(lane < 64, items[2 * twin], items[2 * twin + 1])

        for twin, cols in enumerate(twins):
            side = slice(WIDTH + twin * 128, WIDTH + twin * 128 + 128)
            lhs_all[span, side] = merge(attended, twin).astype(jnp.bfloat16)
            grad_lin[0, span, cols] = turn(merge(grad_query, twin) * scale, -1.0).astype(
                jnp.bfloat16
            )
            grad_lin[1, span, cols] = turn(merge(grad_key, twin) * scale, -1.0).astype(
                jnp.bfloat16
            )
            grad_lin[2, span, cols] = merge(grad_value, twin).astype(jnp.bfloat16)
        return carry

    lax.fori_loop(0, 4, units, 0)

    for copy in third:
        copy.wait()

    def hidden(pair, carry):
        cols = pl.ds(pl.multiple_of(pair * 256, 256), 256)
        up_pre = matmul(acts[3], up_all[pair])
        bell = 0.5 * (1.0 + lax.erf(up_pre * ROOT_HALF))
        slope = bell + up_pre * NORMAL_PEAK * jnp.exp(-0.5 * up_pre * up_pre)
        lhs_all[:, cols] = (up_pre * bell).astype(jnp.bfloat16)
        rows_down = jnp.concatenate(
            [
                jnp.concatenate([down_all[2 * pair + half, block] for block in range(4)], axis=1)
                for half in range(2)
            ]
        )
        grad_gated = back_product(acts[4], rows_down)
        grad_pre[:, cols] = (grad_gated * slope).astype(jnp.bfloat16)
        return carry

    lax.fori_loop(0, 4, hidden, 0)

    def weights(index, carry):
        cols = pl.ds(pl.multiple_of(index * 128, 128), 128)
        grad = outer_sum(acts[3, :, cols], grad_pre[...]).astype(jnp.bfloat16)
        for block in range(4):
            parts[index, block] = grad[:, block * 256 : block * 256 + 256]
        for stream in range(3):
            parts[index, 4 + stream] = outer_sum(acts[stream, :, cols], grad_lin[stream]).astype(
                jnp.bfloat16
            )
        grad = outer_sum(lhs_all[:, cols], acts[4]).astype(jnp.bfloat16)
        other = index + 1 - 2 * (index % 2)
        for block in range(4):
            part = grad[:, block * 256 : block * 256 + 256]
            parts[index, 7 + block, 0:96] = part[0:96]

            @pl.when(index % 2 == core)
            def _():
                parts[other, 11, block * 32 : block * 32 + 32] = part[96:128]

            @pl.when(index % 2 != core)
            def _():
                parts[index, 7 + block, 96:128] = part[96:128]

        return carry

    lax.fori_loop(0, 8, weights, 0)
    grad = outer_sum(lhs_all[:, WIDTH:], acts[4]).astype(jnp.bfloat16)
    for block in range(4):
        part = grad[:, block * 256 : block * 256 + 256]
        for pair in range(4):
            even = 2 * pair + core
            parts[even, 7 + block, 96:128] = part[pair * 64 : pair * 64 + 32]
            parts[even, 11, block * 32 : block * 32 + 32] = part[pair * 64 + 32 : pair * 64 + 64]
    sent = [
        pltpu.make_async_copy(
            parts.at[target[0], pl.ds(0, PART)], chunk_low, chunk_sems.at[0]
        ),
        pltpu.make_async_copy(
            parts.at[target[0], pl.ds(PART, 12 - PART)], chunk_high, chunk_sems.at[8]
        ),
    ] + [
        pltpu.make_async_copy(parts.at[target[index]], chunks[index - 1], chunk_sems.at[index])
        for index in range(1, 8)
    ]
    for copy in sent:
        copy.start()

    def put(unit, cols, value):
        low = value.astype(jnp.bfloat16)
        for half in range(2):
            for block in range(2):
                at = (2 * half + block) * ROWS
                tokens[half, block, unit, :, cols] = low[at : at + ROWS]

    def ship(unit):
        if unit < 4:
            routes = (
                (tokens.at[0, 0, unit], keep_own.at[unit]),
                (tokens.at[0, 1, unit], keep_far.at[unit]),
                (tokens.at[1, :, unit], send_norm.at[:, unit]),
            )
        else:
            routes = ((tokens.at[0, :, unit], keep_out), (tokens.at[1, :, unit], send_out))
        for place, (source, goal) in enumerate(routes):
            copy = pltpu.make_async_copy(source, goal, token_sems.at[place, unit])
            copy.start()
            sent.append(copy)

    for stream in range(3):
        put(stream, slice(0, WIDTH), back_product(grad_lin[stream], lin_all[stream]))
        ship(stream)

    def feed(block, carry):
        cols = pl.ds(pl.multiple_of(block * 256, 256), 256)
        rows_up = jnp.concatenate([up_all[part, cols] for part in range(4)], axis=1)
        put(3, cols, back_product(grad_pre[...], rows_up))
        right = [down_all[index, block] for index in range(8)] + [out_rows[:, cols]]
        put(4, cols, matmul(lhs_all[...], jnp.concatenate(right)))
        return carry

    lax.fori_loop(0, 4, feed, 0)
    ship(3)
    ship(4)
    for copy in sent:
        copy.wait()


def back_kernel(
    stack,
    cotangent,
    scaled,
    stats,
    keep,
    came,
    across,
    mix_gain,
    mix_up,
    mix_down,
    norm_gain,
    stack_grad,
    small_own,
    small_other,
    coefficients,
    grads,
    sums,
    coef_grad,
    small,
):
    seqs = stack.shape[0]
    sums[...] = jnp.zeros_like(sums)
    lane = lanes_of((16, 128))

    def unit(step, carry):
        row = pl.multiple_of(step * 16, 16)
        span = pl.ds(row, 16)

        def result(index):
            return wide(keep[index, span]) + wide(came[0, index, span]) + wide(across[index, span])

        for stream in range(4):
            item = result(stream)
            scale = scaled[stream, span]
            moved = item * scale
            sums[stream] += moved[:8] + moved[8:]
            sums[4 + stream] += item[:8] + item[8:]
            weighted = item * norm_gain[stream : stream + 1]
            mean = jnp.mean(weighted, axis=-1, keepdims=True)
            slant = jnp.mean(weighted * scale, axis=-1, keepdims=True)
            grad = stats[2, span, stream : stream + 1] * (weighted - mean - scale * slant)
            if stream == 3:
                grad = grad + wide(cotangent[span])
            grads[stream, span] = grad
        return carry

    lax.fori_loop(0, seqs * SEQ // 16, unit, 0)
    for seq in range(seqs):

        def coefs(step, carry):
            row = pl.multiple_of(step * 16, 16)
            span = pl.ds(seq * SEQ + row, 16)
            found = jnp.zeros((16, 128), jnp.float32)
            for layer in range(STREAMS_IN):
                value = wide(stack[seq, layer, pl.ds(row, 16), :])
                for stream in range(4):
                    got = jnp.sum(grads[stream, span] * value, axis=-1, keepdims=True)
                    found = jnp.where(lane == stream * STREAMS_IN + layer, got, found)
            coef_grad[span] = found
            return carry

        lax.fori_loop(0, SEQ // 16, coefs, 0)
    grad_coef = coef_grad[:, 0:36]
    hidden_pre = stats[1, :, 0:36]
    hidden_low = gelu_value(hidden_pre).astype(jnp.bfloat16)
    for seq in range(seqs):
        turned = stats[0, seq * SEQ : seq * SEQ + SEQ, :].T
        for stream in range(4):
            for layer in range(STREAMS_IN):
                at = stream * STREAMS_IN + layer
                coefficients[seq, layer, stream : stream + 1] = turned[at : at + 1]
    small[...] = jnp.zeros_like(small)
    small[0:36, WIDTH : WIDTH + 36] = lax.dot_general(
        wide(hidden_low),
        grad_coef,
        (((0,), (0,)), ((), ())),
        precision=HIGHEST,
        preferred_element_type=jnp.float32,
    )
    small[36:37, WIDTH : WIDTH + 36] = jnp.sum(grad_coef, axis=0, keepdims=True)
    grad_hidden = (
        lax.dot_general(
            grad_coef,
            mix_down[...],
            (((1,), (1,)), ((), ())),
            precision=HIGHEST,
            preferred_element_type=jnp.float32,
        )
        * gelu_slope(hidden_pre)
    ).astype(jnp.bfloat16)
    gain_row = jnp.zeros((8, WIDTH), jnp.float32)
    up_part = jnp.zeros((36, WIDTH), jnp.float32)
    for seq in range(seqs):
        at = slice(seq * SEQ, seq * SEQ + SEQ)
        last = wide(stack[seq, STREAMS_IN - 1])
        rms = stats[2, at, 4:5]
        mixed_in = (last * rms * mix_gain[...]).astype(jnp.bfloat16)
        up_part = up_part + outer_sum(grad_hidden[at], mixed_in)
        grad_mixed = matmul(grad_hidden[at], mix_up[...])
        along = grad_mixed * last * rms
        for place in range(SEQ // 8):
            gain_row = gain_row + along[place * 8 : place * 8 + 8]
        weighted = grad_mixed * mix_gain[...]
        mean = jnp.mean(weighted * last, axis=-1, keepdims=True)
        grads[4, at] = rms * (weighted - last * (rms * rms * mean))

        def layers(step, carry):
            row = pl.multiple_of(step // 2 * 16, 16)
            cols = pl.ds(pl.multiple_of(step % 2 * 512, 512), 512)
            span = pl.ds(seq * SEQ + row, 16)
            rows_coef = stats[0, span, :]
            parts = [grads[stream, span, cols] for stream in range(4)]
            for layer in range(STREAMS_IN):
                total = None
                for stream in range(4):
                    at_coef = stream * STREAMS_IN + layer
                    term = rows_coef[:, at_coef : at_coef + 1] * parts[stream]
                    total = term if total is None else total + term
                if layer == STREAMS_IN - 1:
                    total = total + grads[4, span, cols]
                stack_grad[seq, layer, pl.ds(row, 16), cols] = total.astype(jnp.bfloat16)
            return carry

        lax.fori_loop(0, 8, layers, 0)
    small[0:36, 0:WIDTH] = up_part
    for place in range(8):
        small[36 + place : 37 + place, 0:WIDTH] = jnp.sum(sums[place], axis=0, keepdims=True)
    small[44:45, 0:WIDTH] = jnp.sum(gain_row, axis=0, keepdims=True)
    _, _, _, core = position()
    small_own[...] = small[pl.ds(pl.multiple_of(core * 24, 8), 24), :]
    small_other[...] = small[pl.ds(pl.multiple_of(24 - core * 24, 8), 24), :]


def place_kernel(
    shard0,
    shard1,
    shard2,
    shard3,
    small_own,
    small_other,
    projection,
    out_grad,
    up_grad,
    down_grad,
    mix_gain_grad,
    mix_up_grad,
    mix_down_grad,
    mix_static_grad,
    gain_grad,
    bias_grad,
    small,
):
    z, member_parity, x, core = position()
    small[pl.ds(pl.multiple_of(core * 24, 8), 24), :] = small_own[...]
    small[pl.ds(pl.multiple_of(24 - core * 24, 8), 24), :] = small_other[...]
    lanes = pl.ds(pl.multiple_of((2 * z + member_parity) * 128, 128), 128)
    mix_up_grad[...] = small[0:36, lanes]
    gain_grad[...] = small[36:40, 0:WIDTH]
    bias_grad[...] = small[40:44, 0:WIDTH]
    mix_gain_grad[...] = small[44:45, 0:WIDTH]
    mix_down_grad[...] = small[0:36, WIDTH : WIDTH + 36]
    for stream in range(4):
        at = WIDTH + stream * STREAMS_IN
        mix_static_grad[stream : stream + 1] = small[36:37, at : at + STREAMS_IN]
    shards = (shard0, shard1, shard2, shard3)
    lane = lanes_of((128, 128))
    for back in range(4):
        from_x = x if back % 2 == 0 else 1 - x
        from_core = core if back < 2 else 1 - core
        quarter = 2 * from_x + from_core
        own, twin = shards[back], shards[back ^ 2]
        for index in range(8):
            half = index % 2
            mine = wide(own[index // 2, :, half * 128 : half * 128 + 128])
            half_b = 1 - half
            lent = wide(twin[index // 2, :, half_b * 128 : half_b * 128 + 128])
            col = pl.multiple_of((index * 4 + quarter) * 128, 128)
            up_grad[:, pl.ds(col, 128)] = jnp.where(
                (lane >= 96) & (from_core == half), lent, mine
            )
        row = pl.multiple_of(quarter * 128, 128)
        for block in range(4):
            cols = slice(block * 256, block * 256 + 256)
            down_grad[pl.ds(row, 96), cols] = wide(own[7 + block, 0:96])

            @pl.when(member_parity == from_core)
            def _():
                head_row = pl.multiple_of(from_x * 64, 64)
                out_grad[pl.ds(head_row, 32), cols] = wide(own[7 + block, 96:128])
                out_grad[pl.ds(head_row + 32, 32), cols] = wide(
                    own[11, block * 32 : block * 32 + 32]
                )
                down_grad[pl.ds(row + 96, 32), cols] = wide(
                    twin[11, block * 32 : block * 32 + 32]
                )

            @pl.when(member_parity != from_core)
            def _():
                down_grad[pl.ds(row + 96, 32), cols] = wide(own[7 + block, 96:128])

    for back in (0, 2):
        from_core = core if back < 2 else 1 - core
        for stream in range(3):
            for twin in range(2):
                tile = slice(twin * 128, twin * 128 + 128)
                mine = wide(shards[back][4 + stream, :, tile])
                across = wide(shards[back + 1][4 + stream, :, tile])
                even = jnp.where(x == 0, mine, across)
                odd = jnp.where(x == 0, across, mine)
                first = jnp.where(lane < 64, even, pltpu.roll(odd, 64, 1))
                second = jnp.where(lane < 64, pltpu.roll(even, 64, 1), odd)
                for low, value in ((0, first), (1, second)):
                    col = pl.multiple_of((2 * twin + low) * 256 + from_core * 128, 128)
                    projection[stream, :, pl.ds(col, 128)] = value


def call(kernel, outs, specs, out_specs, args, scratch=(), cost=None, vmem=60 << 20):
    return pl.pallas_call(
        kernel,
        out_shape=outs,
        in_specs=specs,
        out_specs=out_specs,
        scratch_shapes=list(scratch),
        compiler_params=pltpu.CompilerParams(vmem_limit_bytes=vmem),
        cost_estimate=cost,
    )(*args)


def shape_of(shape, dtype=jnp.bfloat16):
    return jax.ShapeDtypeStruct(shape, dtype)


def rope_tables():
    half_rot = ROTARY // 2
    step = 10000.0 ** (-2.0 * np.arange(half_rot) / ROTARY)
    angles = np.arange(SEQ)[:, None] * step[None, :]
    cos_table = np.ones((SEQ, HEAD_DIM))
    left = np.zeros((SEQ, HEAD_DIM))
    right = np.zeros((SEQ, HEAD_DIM))
    cos_table[:, :half_rot] = np.cos(angles)
    cos_table[:, half_rot:ROTARY] = np.cos(angles)
    left[:, :half_rot] = -np.sin(angles)
    right[:, half_rot:ROTARY] = np.sin(angles)
    return np.stack([np.tile(item, (2, 2)) for item in (cos_table, left, right)]).astype(np.float32)


def on_device_tensor(
    layer_stack,
    out_cotangent,
    pic_start,
    doc_split,
    mix_gain,
    mix_up,
    mix_down,
    mix_static,
    norm_gain,
    norm_bias,
    query_key_value,
    out_weight,
    up_weight,
    down_weight,
):
    z, y, _, _ = position()
    micro_total, local_seqs, _, _, width = layer_stack.shape
    seqs = micro_total * local_seqs
    stack = jnp.transpose(layer_stack, (0, 1, 3, 2, 4)).reshape(seqs, STREAMS_IN, SEQ, width)
    cotangent = out_cotangent.reshape(ROWS, width)
    gain_row = mix_gain.reshape(1, width)

    piece = call(
        prepare_kernel,
        shape_of((12, 128, 256)),
        [VMEM_FULL] * 4,
        VMEM_FULL,
        (query_key_value, out_weight, up_weight, down_weight),
    )
    up_own = mix_up.T
    up_pair = jnp.concatenate([up_own, after(lax.ppermute(up_own, "fsdp", Y_SWAP), piece)], axis=1)
    ups = [up_pair] + [
        lax.ppermute(up_pair, "fsdp", z_pairs([((step + to) % 4, to) for to in range(4)]))
        for step in (1, 2, 3)
    ]
    piece = after(piece, *ups)
    bounds = jnp.concatenate([pic_start.reshape(seqs), doc_split.reshape(seqs)])
    kept = {}
    grad_across = lax.ppermute(cotangent, "replica", X_SWAP)
    grad_packets = (
        cotangent,
        grad_across,
        lax.ppermute(cotangent, "replica", CORE_SWAP),
        lax.ppermute(grad_across, "replica", CORE_SWAP),
    )

    def front():
        packet, *kept["rest"] = call(
            front_kernel,
            (
                shape_of((4 * ROWS + 16, width)),
                shape_of((4, ROWS, width), jnp.float32),
                shape_of((3, ROWS, 128), jnp.float32),
                shape_of((ROWS, width), jnp.float32),
                shape_of((36, width)),
            ),
            [SMEM_FULL] + [VMEM_FULL] * 10,
            (VMEM_FULL,) * 5,
            (
                bounds,
                stack,
                gain_row,
                *ups,
                mix_down,
                mix_static.reshape(1, 36),
                norm_gain,
                norm_bias,
            ),
            scratch=[pltpu.VMEM((4, ROWS, width), jnp.float32)],
        )
        across = lax.ppermute(packet, "replica", X_SWAP)
        beside = lax.ppermute(packet, "replica", CORE_SWAP)
        beside_across = lax.ppermute(across, "replica", CORE_SWAP)
        kept["packets"] = (packet, across, beside, beside_across)
        return (packet, grad_across), (across,)

    pieces = gather_fsdp(piece, z, front)
    packets = kept["packets"]
    scaled, stats, stream_last, mix_up_full = kept["rest"]

    results = call(
        main_kernel,
        (shape_of((PART, 128, 256)), shape_of((12 - PART, 128, 256)))
        + (shape_of((12, 128, 256)),) * 7
        + (shape_of((4, ROWS, width)),) * 2
        + (shape_of((2, 4, ROWS, width)),)
        + (shape_of((2, ROWS, width)),) * 2,
        [VMEM_FULL] + [IN_PLACE] * 19,
        (IN_PLACE,) * 14,
        (jnp.asarray(rope_tables()),) + packets + grad_packets + tuple(pieces),
        scratch=[
            pltpu.VMEM((5, 4 * ROWS, width), jnp.bfloat16),
            pltpu.VMEM((4, 16, width), jnp.bfloat16),
            pltpu.VMEM((4, width, 256), jnp.bfloat16),
            pltpu.VMEM((3, width, 256), jnp.bfloat16),
            pltpu.VMEM((8, 5, 128, 256), jnp.bfloat16),
            pltpu.VMEM((256, width), jnp.bfloat16),
            pltpu.VMEM((4 * ROWS, width + 256), jnp.bfloat16),
            pltpu.VMEM((4 * ROWS, width), jnp.bfloat16),
            pltpu.VMEM((3, 4 * ROWS, 256), jnp.float32),
            pltpu.VMEM((4 * ROWS, 256), jnp.bfloat16),
            pltpu.VMEM((3, 4 * ROWS, 256), jnp.bfloat16),
            pltpu.VMEM((8, 12, 128, 256), jnp.bfloat16),
            pltpu.VMEM((2, 2, 5, ROWS, width), jnp.bfloat16),
            pltpu.SemaphoreType.DMA((4, 6)),
            pltpu.SemaphoreType.DMA((8, 3)),
            pltpu.SemaphoreType.DMA((9,)),
            pltpu.SemaphoreType.DMA((3, 5)),
        ],
    )
    chunks = results[:9]
    keep_own, keep_far, send_norm, keep_out, send_out = results[9:]

    came = lax.ppermute(send_norm, "replica", CORE_SWAP)
    sum_across = (wide(keep_far) + wide(came[1])).astype(jnp.bfloat16)
    came_across = lax.ppermute(sum_across, "replica", X_SWAP)
    out_came = lax.ppermute(after(send_out, sum_across), "replica", CORE_SWAP)
    out_across = (wide(keep_out[1]) + wide(out_came[1])).astype(jnp.bfloat16)
    out_across = lax.ppermute(after(out_across, came_across), "replica", X_SWAP)
    layer_output = (
        stream_last + wide(keep_out[0]) + wide(out_came[0]) + wide(out_across)
    ).astype(jnp.bfloat16)

    first_half = pl.BlockSpec((1, 4, ROWS, width), lambda step: (0, 0, 0, 0))

    def whole(shape):
        return pl.BlockSpec(shape, lambda step: (0,) * len(shape))

    def back():
        kept["back"] = pl.pallas_call(
            back_kernel,
            grid=(1,),
            out_shape=(
                shape_of((seqs, STREAMS_IN, SEQ, width)),
                shape_of((24, width + 128), jnp.float32),
                shape_of((24, width + 128), jnp.float32),
                shape_of((seqs, STREAMS_IN, 4, SEQ), jnp.float32),
            ),
            in_specs=[
                whole((seqs, STREAMS_IN, SEQ, width)),
                whole((ROWS, width)),
                whole((4, ROWS, width)),
                whole((3, ROWS, 128)),
                whole((4, ROWS, width)),
                first_half,
                whole((4, ROWS, width)),
                whole((1, width)),
                whole((36, width)),
                whole((36, 36)),
                whole((4, width)),
            ],
            out_specs=(
                whole((seqs, STREAMS_IN, SEQ, width)),
                whole((24, width + 128)),
                whole((24, width + 128)),
                whole((seqs, STREAMS_IN, 4, SEQ)),
            ),
            scratch_shapes=[
                pltpu.VMEM((5, ROWS, width), jnp.float32),
                pltpu.VMEM((8, 8, width), jnp.float32),
                pltpu.VMEM((ROWS, 128), jnp.float32),
                pltpu.VMEM((48, width + 128), jnp.float32),
            ],
            compiler_params=pltpu.CompilerParams(vmem_limit_bytes=56 << 20),
        )(
            stack,
            cotangent,
            scaled,
            stats,
            keep_own,
            came,
            came_across,
            gain_row,
            mix_up_full,
            mix_down,
            norm_gain,
        )
        return kept["back"][1]

    shard = scatter_fsdp(chunks, z, sum_across, back)
    stack_grad, small, small_other, coefficients = kept["back"]

    small = small + lax.ppermute(small_other, "replica", CORE_SWAP)
    small = small + lax.ppermute(small, "replica", X_SWAP)
    shard = after(shard, small, out_across)
    shard_across = lax.ppermute(shard, "replica", X_SWAP)
    shard_beside = lax.ppermute(shard, "replica", CORE_SWAP)
    for perm in (Y_SWAP, Z_SWAP_NEAR, Z_SWAP_FAR):
        small = small + lax.ppermute(small, "fsdp", perm)
    small_beside = lax.ppermute(small, "replica", CORE_SWAP)
    shard_both = lax.ppermute(after(shard_across, small), "replica", CORE_SWAP)
    owned = call(
        place_kernel,
        (
            shape_of((3, 128, width), jnp.float32),
            shape_of((128, width), jnp.float32),
            shape_of((128, 4 * width), jnp.float32),
            shape_of((512, width), jnp.float32),
            shape_of((1, width), jnp.float32),
            shape_of((36, 128), jnp.float32),
            shape_of((36, 36), jnp.float32),
            shape_of((4, STREAMS_IN), jnp.float32),
            shape_of((4, width), jnp.float32),
            shape_of((4, width), jnp.float32),
        ),
        [VMEM_FULL] * 6,
        (VMEM_FULL,) * 10,
        (shard, shard_across, shard_beside, shard_both, small, small_beside),
        scratch=[pltpu.VMEM((48, width + 128), jnp.float32)],
    )
    projection_grad, out_grad, up_grad, down_grad, *small_grads = owned
    shape = (micro_total, local_seqs, SEQ)
    stack_grad = stack_grad.reshape(micro_total, local_seqs, STREAMS_IN, SEQ, width)
    coefficients = coefficients.reshape(micro_total, local_seqs, STREAMS_IN, 4, SEQ)
    return (
        layer_output.reshape(shape + (width,)),
        jnp.transpose(coefficients, (0, 1, 4, 3, 2)),
        jnp.transpose(stack_grad, (0, 1, 3, 2, 4)),
        small_grads[0].reshape(width),
        small_grads[1].T,
        small_grads[2],
        small_grads[3],
        small_grads[4],
        small_grads[5],
        projection_grad,
        out_grad,
        up_grad,
        down_grad,
    )


def solution(mesh):
    fits = mesh.shape["fsdp"] == 8 and mesh.shape["replica"] == 4
    body = on_device_tensor if fits else on_device
    return jax.shard_map(
        body,
        mesh=mesh,
        in_specs=(
            P(None, ("fsdp", "replica"), None, None, None),
            P(None, ("fsdp", "replica"), None, None),
            P(None, ("fsdp", "replica")),
            P(None, ("fsdp", "replica")),
            P(),
            P("fsdp", None),
            P(),
            P(),
            P(),
            P(),
            P(None, "fsdp", None),
            P("fsdp", None),
            P("fsdp", None),
            P("fsdp", None),
        ),
        out_specs=(
            P(None, ("fsdp", "replica"), None, None),
            P(None, ("fsdp", "replica"), None, None, None),
            P(None, ("fsdp", "replica"), None, None, None),
            P(),
            P("fsdp", None),
            P(),
            P(),
            P(),
            P(),
            P(None, "fsdp", None),
            P("fsdp", None),
            P("fsdp", None),
            P("fsdp", None),
        ),
        check_vma=False,
    )
```

```python
import math

import jax
import jax.numpy as jnp
import numpy as np
from jax import lax
from jax.experimental import pallas as pl
from jax.experimental.pallas import tpu as pltpu
from jax.sharding import PartitionSpec as P

HEADS = 16
HEAD_DIM = 64
ROTARY = 16
STREAMS_IN = 9
SEQ = 64
PIC = 32


EPSILON = 1e-05
ROOT_HALF = 0.7071067811865476
NORMAL_PEAK = 0.3989422804014327
HIGHEST = lax.Precision.HIGHEST


def as_sent(value):

    def short(part):
        return part.astype(jnp.bfloat16) if part.dtype == jnp.float32 else part

    return jax.tree.map(short, value)


def gelu_value(values):
    return 0.5 * values * (1.0 + lax.erf(values * ROOT_HALF))


def gelu_slope(values):
    return 0.5 * (1.0 + lax.erf(values * ROOT_HALF)) + values * NORMAL_PEAK * jnp.exp(
        -0.5 * values * values
    )


def matmul(left_side, right_side):
    return jnp.dot(left_side, right_side, preferred_element_type=jnp.float32)


def outer_sum(left_side, right_side):
    return lax.dot_general(
        left_side, right_side, (((0,), (0,)), ((), ())), preferred_element_type=jnp.float32
    )


def back_product(left_side, right_side):
    return lax.dot_general(
        left_side, right_side, (((1,), (1,)), ((), ())), preferred_element_type=jnp.float32
    )


def rotary_tables():
    half_rot = ROTARY // 2
    inverse = jnp.exp(-math.log(10000.0) * (2.0 * jnp.arange(half_rot, dtype=jnp.float32) / ROTARY))
    angles = jnp.arange(SEQ, dtype=jnp.float32)[:, None] * inverse[None, :]
    return (jnp.cos(angles)[:, None, :], jnp.sin(angles)[:, None, :])


def rotate(values, cos_table, sin_table):
    half_rot = ROTARY // 2
    first_half = values[..., :half_rot]
    second = values[..., half_rot:ROTARY]
    return jnp.concatenate(
        [
            first_half * cos_table - second * sin_table,
            second * cos_table + first_half * sin_table,
            values[..., ROTARY:],
        ],
        axis=-1,
    )


def allowed_mask(starts, splits):
    positions = jnp.arange(SEQ, dtype=jnp.int32)
    second_doc = positions[None, :] >= splits[:, None]
    picture = (positions[None, :] >= starts[:, None]) & (positions[None, :] < starts[:, None] + PIC)
    same_doc = second_doc[:, :, None] == second_doc[:, None, :]
    causal = positions[:, None] >= positions[None, :]
    both_pic = picture[:, :, None] & picture[:, None, :]
    return same_doc & (causal[None] | both_pic)


def masked_scores(queries, key_rot, allowed):
    scores = jnp.einsum(
        "nqhe,nkhe->nhqk", queries, key_rot, preferred_element_type=jnp.float32
    ) * HEAD_DIM ** (-0.5)
    return jnp.where(allowed[:, None], scores, -1e30)


def on_device(
    layer_stack,
    out_cotangent,
    pic_start,
    doc_split,
    mix_gain,
    mix_up,
    mix_down,
    mix_static,
    norm_gain,
    norm_bias,
    query_key_value,
    out_weight,
    up_weight,
    down_weight,
):
    micro_total = layer_stack.shape[0]
    local_seqs = layer_stack.shape[1]
    model_width = layer_stack.shape[-1]
    groups = [(0, micro_total)]
    cos_table, sin_table = rotary_tables()
    output_list = []
    coef_list = []
    grad_list = []
    shard_total = None
    small_total = None
    for first_micro, micro_count in groups:
        seq_count = micro_count * local_seqs
        row_count = seq_count * SEQ
        head_shape = (seq_count, SEQ, HEADS, HEAD_DIM)
        flat_stack = layer_stack[first_micro : first_micro + micro_count].reshape(
            row_count, STREAMS_IN, model_width
        )
        grad_rows = out_cotangent[first_micro : first_micro + micro_count].reshape(
            row_count, model_width
        )
        starts = pic_start[first_micro : first_micro + micro_count].reshape(seq_count)
        splits = doc_split[first_micro : first_micro + micro_count].reshape(seq_count)
        allowed = allowed_mask(starts, splits)
        mix_up_full, projection_full, out_full = (
            lax.all_gather(mix_up, "fsdp", axis=0, tiled=True),
            lax.all_gather(query_key_value, "fsdp", axis=1, tiled=True),
            lax.all_gather(out_weight, "fsdp", axis=0, tiled=True),
        )
        up_full, down_full = (
            lax.all_gather(up_weight, "fsdp", axis=0, tiled=True),
            lax.all_gather(down_weight, "fsdp", axis=0, tiled=True),
        )
        last_layer = flat_stack[:, STREAMS_IN - 1, :].astype(jnp.float32)
        rms_scale = lax.rsqrt(jnp.mean(last_layer * last_layer, axis=-1, keepdims=True) + EPSILON)
        mixed_in = (last_layer * rms_scale * mix_gain).astype(jnp.bfloat16)
        hidden_pre = matmul(mixed_in, mix_up_full)
        hidden_mix = gelu_value(hidden_pre).astype(jnp.bfloat16)
        hidden_wide = hidden_mix.astype(jnp.float32)
        coef_flat = jnp.dot(hidden_wide, mix_down, precision=HIGHEST) + mix_static.reshape(-1)
        coef_rows = coef_flat.reshape(row_count, 4, STREAMS_IN)
        streams = coef_rows[:, :, 0, None] * flat_stack[:, None, 0, :].astype(jnp.float32)
        for layer_index in range(1, STREAMS_IN):
            streams = streams + coef_rows[:, :, layer_index, None] * flat_stack[
                :, None, layer_index, :
            ].astype(jnp.float32)
        center = streams - jnp.mean(streams, axis=-1, keepdims=True)
        inv_std = lax.rsqrt(jnp.mean(center * center, axis=-1, keepdims=True) + EPSILON)
        scaled = center * inv_std
        normed = (scaled * norm_gain + norm_bias).astype(jnp.bfloat16)
        query_lin = matmul(normed[:, 0], projection_full[0])
        key_lin = matmul(normed[:, 1], projection_full[1])
        value_lin = matmul(normed[:, 2], projection_full[2])
        queries = rotate(query_lin.reshape(head_shape), cos_table, sin_table).astype(jnp.bfloat16)
        key_rot = rotate(key_lin.reshape(head_shape), cos_table, sin_table).astype(jnp.bfloat16)
        values = value_lin.astype(jnp.bfloat16).reshape(head_shape)
        scores = masked_scores(queries, key_rot, allowed)
        row_top = jnp.max(scores, axis=-1, keepdims=True)
        exponent = jnp.exp(scores - row_top)
        row_total = jnp.sum(exponent, axis=-1, keepdims=True)
        soft_probs = exponent / row_total
        log_total = row_top + jnp.log(row_total)
        attended = (
            jnp.einsum(
                "nhqk,nkhe->nqhe",
                soft_probs.astype(jnp.bfloat16),
                values,
                preferred_element_type=jnp.float32,
            )
            .astype(jnp.bfloat16)
            .reshape(row_count, model_width)
        )
        attn_out = matmul(attended, out_full)
        up_pre = matmul(normed[:, 3], up_full)
        gated_act = gelu_value(up_pre).astype(jnp.bfloat16)
        feed_out = matmul(gated_act, down_full)
        output_list.append((streams[:, 3] + attn_out + feed_out).astype(jnp.bfloat16))
        coef_list.append(coef_rows)
        mix_up_back, projection_back, out_back = (
            lax.all_gather(mix_up, "fsdp", axis=0, tiled=True),
            lax.all_gather(query_key_value, "fsdp", axis=1, tiled=True),
            lax.all_gather(out_weight, "fsdp", axis=0, tiled=True),
        )
        up_back, down_back = (
            lax.all_gather(up_weight, "fsdp", axis=0, tiled=True),
            lax.all_gather(down_weight, "fsdp", axis=0, tiled=True),
        )
        grad_down = outer_sum(gated_act, grad_rows)
        grad_gated = back_product(grad_rows, down_back)
        grad_up_pre = (grad_gated * gelu_slope(up_pre)).astype(jnp.bfloat16)
        grad_up = outer_sum(normed[:, 3], grad_up_pre)
        grad_norm_feed = back_product(grad_up_pre, up_back)
        feed_shards = (
            lax.psum_scatter(
                grad_up.astype(jnp.bfloat16), "fsdp", scatter_dimension=0, tiled=True
            ).astype(jnp.float32),
            lax.psum_scatter(
                grad_down.astype(jnp.bfloat16), "fsdp", scatter_dimension=0, tiled=True
            ).astype(jnp.float32),
        )
        grad_out_weight = outer_sum(attended, grad_rows)
        grad_attended = back_product(grad_rows, out_back).astype(jnp.bfloat16).reshape(head_shape)
        scores_again = masked_scores(queries, key_rot, allowed)
        probs_again = jnp.exp(scores_again - log_total)
        grad_probs = jnp.einsum(
            "nqhe,nkhe->nhqk", grad_attended, values, preferred_element_type=jnp.float32
        )
        grad_value = (
            jnp.einsum(
                "nhqk,nqhe->nkhe",
                probs_again.astype(jnp.bfloat16),
                grad_attended,
                preferred_element_type=jnp.float32,
            )
            .astype(jnp.bfloat16)
            .reshape(row_count, model_width)
        )
        delta_rows = jnp.sum(probs_again * grad_probs, axis=-1, keepdims=True)
        grad_scores = (probs_again * (grad_probs - delta_rows)).astype(jnp.bfloat16)
        score_scale = HEAD_DIM ** (-0.5)
        grad_query_rot = (
            jnp.einsum("nhqk,nkhe->nqhe", grad_scores, key_rot, preferred_element_type=jnp.float32)
            * score_scale
        )
        grad_key_rot = (
            jnp.einsum("nhqk,nqhe->nkhe", grad_scores, queries, preferred_element_type=jnp.float32)
            * score_scale
        )
        grad_query = (
            rotate(grad_query_rot, cos_table, -sin_table)
            .astype(jnp.bfloat16)
            .reshape(row_count, model_width)
        )
        grad_key = (
            rotate(grad_key_rot, cos_table, -sin_table)
            .astype(jnp.bfloat16)
            .reshape(row_count, model_width)
        )
        grad_linear = (grad_query, grad_key, grad_value)
        grad_projection = jnp.stack(
            [outer_sum(normed[:, stream], grad_linear[stream]) for stream in range(3)]
        )
        grad_normed = jnp.stack(
            [back_product(grad_linear[stream], projection_back[stream]) for stream in range(3)]
            + [grad_norm_feed],
            axis=1,
        )
        gain_grad = jnp.sum(grad_normed * scaled, axis=0)
        bias_grad = jnp.sum(grad_normed, axis=0)
        grad_scaled = grad_normed * norm_gain
        grad_streams = inv_std * (
            grad_scaled
            - jnp.mean(grad_scaled, axis=-1, keepdims=True)
            - scaled * jnp.mean(grad_scaled * scaled, axis=-1, keepdims=True)
        )
        grad_streams = grad_streams + jnp.concatenate(
            [
                jnp.zeros((row_count, 3, model_width), jnp.float32),
                grad_rows[:, None, :].astype(jnp.float32),
            ],
            axis=1,
        )
        grad_coef = jnp.stack(
            [
                jnp.sum(
                    grad_streams * flat_stack[:, None, layer_index, :].astype(jnp.float32), axis=-1
                )
                for layer_index in range(STREAMS_IN)
            ],
            axis=-1,
        )
        grad_coef_flat = grad_coef.reshape(row_count, 4 * STREAMS_IN)
        static_grad = jnp.sum(grad_coef_flat, axis=0).reshape(4, STREAMS_IN)
        down_mix_grad = jnp.dot(hidden_wide.T, grad_coef_flat, precision=HIGHEST)
        grad_hidden = (
            jnp.dot(grad_coef_flat, mix_down.T, precision=HIGHEST) * gelu_slope(hidden_pre)
        ).astype(jnp.bfloat16)
        grad_mix_up = outer_sum(mixed_in, grad_hidden)
        grad_mixed = back_product(grad_hidden, mix_up_back)
        gain_mix_grad = jnp.sum(grad_mixed * last_layer * rms_scale, axis=0)
        weighted = grad_mixed * mix_gain
        grad_last = rms_scale * (
            weighted
            - last_layer
            * rms_scale
            * rms_scale
            * jnp.mean(weighted * last_layer, axis=-1, keepdims=True)
        )
        per_layer = [
            jnp.sum(coef_rows[:, :, layer_index, None] * grad_streams, axis=1)
            for layer_index in range(STREAMS_IN)
        ]
        per_layer[STREAMS_IN - 1] = per_layer[STREAMS_IN - 1] + grad_last
        grad_list.append(jnp.stack(per_layer, axis=1).astype(jnp.bfloat16))
        attention_shards = (
            lax.psum_scatter(
                grad_mix_up.astype(jnp.bfloat16), "fsdp", scatter_dimension=0, tiled=True
            ).astype(jnp.float32),
            lax.psum_scatter(
                grad_projection.astype(jnp.bfloat16), "fsdp", scatter_dimension=1, tiled=True
            ).astype(jnp.float32),
            lax.psum_scatter(
                grad_out_weight.astype(jnp.bfloat16), "fsdp", scatter_dimension=0, tiled=True
            ).astype(jnp.float32),
        )
        shards = attention_shards + feed_shards
        shards = jax.tree.map(
            lambda part: part.astype(jnp.float32), lax.psum(as_sent(shards), "replica")
        )
        smalls = (gain_mix_grad, down_mix_grad, static_grad, gain_grad, bias_grad)
        if shard_total is None:
            shard_total = shards
            small_total = smalls
        else:
            shard_total = tuple(
                (total_item + new_item for total_item, new_item in zip(shard_total, shards))
            )
            small_total = tuple(
                (total_item + new_item for total_item, new_item in zip(small_total, smalls))
            )
    small_total = lax.psum(small_total, ("fsdp", "replica"))
    layer_output = jnp.concatenate(output_list, axis=0).reshape(
        micro_total, local_seqs, SEQ, model_width
    )
    coefficients = jnp.concatenate(coef_list, axis=0).reshape(
        micro_total, local_seqs, SEQ, 4, STREAMS_IN
    )
    stack_grad = jnp.concatenate(grad_list, axis=0).reshape(
        micro_total, local_seqs, SEQ, STREAMS_IN, model_width
    )
    return (
        layer_output,
        coefficients,
        stack_grad,
        small_total[0],
        shard_total[0],
        small_total[1],
        small_total[2],
        small_total[3],
        small_total[4],
        shard_total[1],
        shard_total[2],
        shard_total[3],
        shard_total[4],
    )


ROWS = 128
WIDTH = 1024
VMEM_FULL = pl.BlockSpec(memory_space=pltpu.VMEM)
SMEM_FULL = pl.BlockSpec(memory_space=pltpu.SMEM)
IN_PLACE = pl.BlockSpec(memory_space=pl.ANY)


def bits_swap(size, bit):
    return [(index, index ^ bit) for index in range(size)]


CORE_SWAP = bits_swap(4, 1)
X_SWAP = bits_swap(4, 2)
Y_SWAP = bits_swap(8, 1)
Z_SWAP_NEAR = bits_swap(8, 2)
Z_SWAP_FAR = bits_swap(8, 4)


def z_pairs(moves):
    return [(2 * src + col, 2 * dst + col) for src, dst in moves for col in range(2)]


def pick(cond, first, second):
    return jnp.where(cond, first, second)


def order_two(flag, own, other, axis):
    first = pick(flag == 0, own, other)
    second = pick(flag == 0, other, own)
    return jnp.concatenate([first, second], axis=axis)


def after(value, *others):
    return lax.optimization_barrier((value,) + others)[0]


Z_NEAR = z_pairs([(0, 1), (1, 0), (2, 3), (3, 2)])
Z_MIDDLE = [
    (index, (index ^ 1) if index // 8 in (0, 3) else (24 - index // 8 * 8 + index % 8))
    for index in range(32)
]


def fsdp_move(value, pairs):
    return lax.ppermute(value, "fsdp" if len(pairs) == 8 else ("fsdp", "replica"), pairs)


PART = 7


def gather_fsdp(piece, z, front):
    inner = (z == 1) | (z == 2)
    near = fsdp_move(piece, Z_NEAR)
    middle = fsdp_move(piece, Z_MIDDLE)
    side = fsdp_move(piece, Y_SWAP)
    early, late = front()
    middle_near = fsdp_move(after(near, *early, side), Z_MIDDLE)
    turned = fsdp_move(after(pick(inner, middle, side), *early), Z_NEAR)
    side_two = fsdp_move(pick(inner, middle, near), Y_SWAP)
    third = pick(inner, middle_near, turned)
    near_twice = fsdp_move(after(middle_near, side_two, third), Z_NEAR)
    side_three = fsdp_move(third, Y_SWAP)
    over_z = fsdp_move(side_three[:PART], Z_NEAR)
    over_y = fsdp_move(after(near_twice[PART:], side_three, *late), Y_SWAP)
    return [
        piece,
        side,
        near,
        middle,
        middle_near,
        turned,
        near_twice,
        side_two,
        side_three,
        over_z,
        over_y,
    ]


def position():
    member, partner = lax.axis_index("fsdp"), lax.axis_index("replica")
    return member // 2, member % 2, partner // 2, partner % 2


def table(values, z):
    found = jnp.int32(values[0])
    for index in range(1, 4):
        found = jnp.where(z == index, jnp.int32(values[index]), found)
    return found


def gather_order(z, y):
    places = []
    for z_from in (z, table([1, 0, 3, 2], z), table([2, 2, 1, 1], z), table([3, 3, 0, 0], z)):
        places += [2 * z_from + y, 2 * z_from + 1 - y]
    return places


def scatter_order(z, y):
    others = (table([3, 0, 3, 0], z), table([2, 3, 0, 1], z), table([1, 2, 1, 2], z), z)
    own = (table([3, 3, 0, 0], z), table([2, 2, 1, 1], z), table([1, 0, 3, 2], z), z)
    return [2 * z_to + 1 - y for z_to in others] + [2 * z_to + y for z_to in own]


def wide(value):
    return value.astype(jnp.float32)


def scatter_fsdp(chunks, z, first_wait, beside):
    inner = (z == 1) | (z == 2)
    side_low, side_high, side_one, side_two, side_own, last, third, near, own = chunks

    def low(value):
        return value.astype(jnp.bfloat16)

    def only(cond, value):
        return jnp.where(cond, wide(value), 0.0)

    over_z = fsdp_move(side_high, Z_NEAR)
    over_y = fsdp_move(side_low, Y_SWAP)
    over_z = jnp.pad(only(inner, over_z), ((PART, 0), (0, 0), (0, 0)))
    back_one = fsdp_move(low(wide(side_one) + over_z), Y_SWAP)
    over_y = jnp.pad(wide(over_y), ((0, 12 - PART), (0, 0), (0, 0)))
    back_far = fsdp_move(low(wide(after(last, first_wait)) + over_y), Z_NEAR)
    back_two = fsdp_move(after(side_two, first_wait), Y_SWAP)
    to_middle = low(wide(last) + wide(back_one) + wide(back_far))
    to_near = low(
        jnp.where(
            inner,
            wide(jnp.concatenate([side_low, side_high])),
            wide(third) + wide(back_one),
        )
    )
    middle_one = fsdp_move(to_middle, Z_MIDDLE)
    near_one = fsdp_move(to_near, Z_NEAR)
    back_own = fsdp_move(low(wide(side_own) + only(z % 3 == 0, near_one)), Y_SWAP)
    to_near = low(wide(near) + jnp.where(inner, wide(middle_one), wide(back_two)))
    to_middle = low(wide(third) + wide(back_two) + wide(near_one))
    to_near, to_middle, _ = lax.optimization_barrier((to_near, to_middle, beside()))
    near_two = fsdp_move(to_near, Z_NEAR)
    middle_two = fsdp_move(to_middle, Z_MIDDLE)
    return low(wide(own) + wide(back_own) + wide(near_two) + only(inner, middle_two))


def lanes_of(shape):
    return lax.broadcasted_iota(jnp.int32, shape, 1)


def rows_of(shape):
    return lax.broadcasted_iota(jnp.int32, shape, 0)


def prepare_kernel(projection, out_weight, up_weight, down_weight, piece):
    _, member_parity, x, core = position()
    quarter, other = 2 * x + core, 2 * x + 1 - core
    lane = lanes_of((128, 128))
    for index in range(8):
        half = index % 2
        own = up_weight[:, pl.ds(pl.multiple_of((index * 4 + quarter) * 128, 128), 128)]
        extra = up_weight[:, pl.ds(pl.multiple_of(((index ^ 1) * 4 + other) * 128, 128), 128)]
        taken = (lane >= 96) & (core == half)
        piece[index // 2, :, half * 128 : half * 128 + 128] = jnp.where(
            taken, wide(extra), wide(own)
        ).astype(jnp.bfloat16)
    for stream in range(3):
        for twin in range(2):
            tiles = [
                wide(
                    projection[
                        stream,
                        :,
                        pl.ds(pl.multiple_of((2 * twin + low) * 256 + core * 128, 128), 128),
                    ]
                )
                for low in range(2)
            ]
            first = jnp.where(x == 0, tiles[0], pltpu.roll(tiles[0], 64, 1))
            second = jnp.where(x == 0, pltpu.roll(tiles[1], 64, 1), tiles[1])
            piece[4 + stream, :, twin * 128 : twin * 128 + 128] = jnp.where(
                lane < 64, first, second
            ).astype(jnp.bfloat16)
    own_row = pl.multiple_of(quarter * 128, 128)
    other_row = pl.multiple_of(other * 128, 128)
    head_row = pl.multiple_of(x * 64, 64)
    for block in range(4):
        cols = slice(block * 256, block * 256 + 256)
        piece[7 + block, 0:96] = down_weight[pl.ds(own_row, 96), cols]

        @pl.when(member_parity == core)
        def _():
            piece[7 + block, 96:128] = out_weight[pl.ds(head_row, 32), cols]
            piece[11, block * 32 : block * 32 + 32] = out_weight[pl.ds(head_row + 32, 32), cols]

        @pl.when(member_parity != core)
        def _():
            piece[7 + block, 96:128] = down_weight[pl.ds(own_row + 96, 32), cols]
            piece[11, block * 32 : block * 32 + 32] = down_weight[pl.ds(other_row + 96, 32), cols]


def front_kernel(
    bounds,
    stack,
    mix_gain,
    up_own,
    up_one,
    up_two,
    up_three,
    mix_down,
    mix_static,
    norm_gain,
    norm_bias,
    packet,
    scaled_out,
    stats,
    stream_out,
    mix_up,
    streams,
):
    seqs = stack.shape[0]
    z, y, _, _ = position()
    for step, part in enumerate((up_own, up_one, up_two, up_three)):
        z_from = (z + step) % 4
        for half, col in enumerate((y, 1 - y)):
            lanes = pl.ds(pl.multiple_of((2 * z_from + col) * 128, 128), 128)
            mix_up[:, lanes] = part[:, half * 128 : half * 128 + 128]
    for seq in range(seqs):
        last = wide(stack[seq, STREAMS_IN - 1])
        rms = lax.rsqrt(jnp.mean(last * last, axis=-1, keepdims=True) + EPSILON)
        mixed_in = (last * rms * mix_gain[...]).astype(jnp.bfloat16)
        hidden_pre = back_product(mixed_in, mix_up[...])
        hidden = wide(gelu_value(hidden_pre).astype(jnp.bfloat16))
        coef = jnp.dot(
            hidden, mix_down[...], precision=HIGHEST, preferred_element_type=jnp.float32
        )
        coef = coef + mix_static[...]
        at = slice(seq * SEQ, seq * SEQ + SEQ)
        stats[0, at, 0:36] = coef
        stats[1, at, 0:36] = hidden_pre
        stats[2, at, 4:5] = rms

        def mix(step, carry):
            row = pl.multiple_of(step // 2 * 16, 16)
            col = pl.multiple_of(step % 2 * 512, 512)
            rows_coef = stats[0, pl.ds(seq * SEQ + row, 16), :]
            totals = [None] * 4
            for layer in range(STREAMS_IN):
                value = wide(stack[seq, layer, pl.ds(row, 16), pl.ds(col, 512)])
                for stream in range(4):
                    at_coef = stream * STREAMS_IN + layer
                    term = rows_coef[:, at_coef : at_coef + 1] * value
                    totals[stream] = term if layer == 0 else totals[stream] + term
            for stream in range(4):
                streams[stream, pl.ds(seq * SEQ + row, 16), pl.ds(col, 512)] = totals[stream]
            return carry

        lax.fori_loop(0, 8, mix, 0)

    def norm(step, carry):
        row = pl.multiple_of(step * 16, 16)
        for stream in range(4):
            value = streams[stream, pl.ds(row, 16), :]
            center = value - jnp.mean(value, axis=-1, keepdims=True)
            inverse = lax.rsqrt(jnp.mean(center * center, axis=-1, keepdims=True) + EPSILON)
            scaled = center * inverse
            stats[2, pl.ds(row, 16), stream : stream + 1] = inverse
            scaled_out[stream, pl.ds(row, 16), :] = scaled
            packet[pl.ds(stream * ROWS + row, 16), :] = (
                scaled * norm_gain[stream : stream + 1, :] + norm_bias[stream : stream + 1, :]
            ).astype(jnp.bfloat16)
            if stream == 3:
                stream_out[pl.ds(row, 16), :] = value
        return carry

    lax.fori_loop(0, seqs * SEQ // 16, norm, 0)
    packet[4 * ROWS :] = jnp.zeros((16, WIDTH), jnp.bfloat16)
    row = rows_of((16, 128))
    marks = jnp.zeros((16, 128), jnp.float32)
    for place in range(2 * seqs):
        marks = jnp.where(row == place, wide(bounds[place]), marks)
    packet[4 * ROWS :, 0:128] = marks.astype(jnp.bfloat16)


def main_kernel(
    rope,
    packet0,
    packet1,
    packet2,
    packet3,
    cotangent0,
    cotangent1,
    cotangent2,
    cotangent3,
    piece0,
    piece1,
    piece2,
    piece3,
    piece4,
    piece5,
    piece6,
    piece7,
    piece8,
    piece9,
    piece10,
    chunk_low,
    chunk_high,
    chunk1,
    chunk2,
    chunk3,
    chunk4,
    chunk5,
    chunk6,
    chunk7,
    keep_own,
    keep_far,
    send_norm,
    keep_out,
    send_out,
    acts,
    marks,
    up_all,
    lin_all,
    down_all,
    out_rows,
    lhs_all,
    grad_pre,
    linear,
    grad_att,
    grad_lin,
    parts,
    tokens,
    packet_sems,
    piece_sems,
    chunk_sems,
    token_sems,
):
    z, y, _, core = position()
    origin = gather_order(z, y)
    target = scatter_order(z, y)
    packets = (packet0, packet1, packet2, packet3)
    cotangents = (cotangent0, cotangent1, cotangent2, cotangent3)
    piece, side, near, middle, middle_near, turned = piece0, piece1, piece2, piece3, piece4, piece5
    near_twice, side_two, side_three, over_z, over_y = piece6, piece7, piece8, piece9, piece10
    inner = (z == 1) | (z == 2)
    sources = (
        (piece, piece),
        (side, side),
        (near, near),
        (turned, side_two),
        (middle, turned),
        (side_two, side_three),
        (middle_near, near_twice),
        (side_three, None),
    )
    chunks = (chunk1, chunk2, chunk3, chunk4, chunk5, chunk6, chunk7)
    member_rows = [pl.ds(pl.multiple_of(place * 128, 128), 128) for place in origin]

    def unit_copies(unit):
        return [
            pltpu.make_async_copy(
                packets[block].at[pl.ds(unit * ROWS, ROWS)],
                acts.at[unit, pl.ds(block * ROWS, ROWS)],
                packet_sems.at[block, unit],
            )
            for block in range(4)
        ]

    def piece_copies(index, ref, tail_ref):
        rows = member_rows[index]
        down = 7 if tail_ref is ref else 0
        return [
            pltpu.make_async_copy(
                ref.at[pl.ds(4, 3)], lin_all.at[:, rows], piece_sems.at[index, 0]
            ),
            pltpu.make_async_copy(
                tail_ref.at[pl.ds(down, 5)], down_all.at[origin[index]], piece_sems.at[index, 1]
            ),
            pltpu.make_async_copy(
                ref.at[pl.ds(0, 4)], up_all.at[:, rows], piece_sems.at[index, 2]
            ),
        ]

    first = unit_copies(0) + unit_copies(1) + unit_copies(2)
    second = [
        pltpu.make_async_copy(
            cotangents[block],
            acts.at[4, pl.ds(block * ROWS, ROWS)],
            packet_sems.at[block, 4],
        )
        for block in range(4)
    ]
    for block in range(4):
        second.append(
            pltpu.make_async_copy(
                packets[block].at[pl.ds(4 * ROWS, 16)], marks.at[block], packet_sems.at[block, 5]
            )
        )
    third = unit_copies(3)
    for copy in first + second + third:
        copy.start()
    for index, (for_inner, for_ends) in enumerate(sources):
        copies = piece_copies(index, for_inner, for_inner)
        first.append(copies[0])
        second.append(copies[1])
        third.append(copies[2])
        if for_inner is for_ends:
            for copy in copies:
                copy.start()
            continue
        ends = (
            piece_copies(index, over_z, over_y)
            if for_ends is None
            else piece_copies(index, for_ends, for_ends)
        )

        @pl.when(inner)
        def _():
            for copy in copies:
                copy.start()

        @pl.when(jnp.logical_not(inner))
        def _():
            for copy in ends:
                copy.start()

    for copy in first:
        copy.wait()
    for stream in range(3):
        linear[stream] = matmul(acts[stream], lin_all[stream])
    for copy in second:
        copy.wait()
    for pair in range(4):
        even = 2 * pair + core
        odd = 2 * pair + 1 - core
        for block in range(4):
            band = slice(block * 32, block * 32 + 32)
            cols = slice(block * 256, block * 256 + 256)
            out_rows[pair * 64 : pair * 64 + 32, cols] = down_all[even, block, 96:128]
            out_rows[pair * 64 + 32 : pair * 64 + 64, cols] = down_all[even, 4, band]
            down_all[even, block, 96:128] = down_all[odd, 4, band]

    grad_att[...] = back_product(acts[4], out_rows[...]).astype(jnp.bfloat16)
    cos_table = rope[0]
    sin_left = rope[1]
    sin_right = rope[2]
    scale = HEAD_DIM ** (-0.5)

    def turn(value, sign):
        return (
            value * cos_table
            + pltpu.roll(value, 120, 1) * (sign * sin_left)
            + pltpu.roll(value, 8, 1) * (sign * sin_right)
        )

    def units(block, carry):
        row = rows_of((ROWS, ROWS))
        lane = lanes_of((ROWS, ROWS))
        bound = wide(marks[block])

        def both(low, high):
            return jnp.where(row < SEQ, low, high), jnp.where(lane < SEQ, low, high)

        start_q, start_k = both(bound[0:1, 0:128], bound[1:2, 0:128])
        split_q, split_k = both(bound[2:3, 0:128], bound[3:4, 0:128])
        at_q = wide(row % SEQ)
        at_k = wide(lane % SEQ)
        same = (row // SEQ == lane // SEQ) & ((at_q >= split_q) == (at_k >= split_k))
        pic_q = (at_q >= start_q) & (at_q < start_q + PIC)
        pic_k = (at_k >= start_k) & (at_k < start_k + PIC)
        penalty = jnp.where(same & ((at_q >= at_k) | (pic_q & pic_k)), 0.0, -1e30)
        span = pl.ds(pl.multiple_of(block * ROWS, ROWS), ROWS)
        twins = [slice(twin * 128, twin * 128 + 128) for twin in range(2)]
        heads = [(twin, head) for twin in range(2) for head in range(2)]
        query = [turn(linear[0, span, cols], 1.0) for cols in twins]
        query_low = [item.astype(jnp.bfloat16) for item in query]
        key_low = [turn(linear[1, span, cols], 1.0).astype(jnp.bfloat16) for cols in twins]
        value_low = [linear[2, span, cols].astype(jnp.bfloat16) for cols in twins]
        grad_low = [grad_att[span, cols] for cols in twins]

        def only(item, head):
            return jnp.where(lane // 64 == head, wide(item), 0.0).astype(jnp.bfloat16)

        scores = [
            back_product(only(query[twin], head), key_low[twin]) * scale + penalty
            for twin, head in heads
        ]
        grad_probs = [
            back_product(only(grad_low[twin], head), value_low[twin]) for twin, head in heads
        ]
        exponent = [jnp.exp(item - jnp.max(item, axis=-1, keepdims=True)) for item in scores]
        probs = [item / jnp.sum(item, axis=-1, keepdims=True) for item in exponent]
        probs_low = [item.astype(jnp.bfloat16) for item in probs]
        grad_scores = [
            (prob * (grad - jnp.sum(prob * grad, axis=-1, keepdims=True))).astype(jnp.bfloat16)
            for prob, grad in zip(probs, grad_probs)
        ]
        attended = [matmul(probs_low[i], value_low[heads[i][0]]) for i in range(4)]
        grad_value = [outer_sum(probs_low[i], grad_low[heads[i][0]]) for i in range(4)]
        grad_query = [matmul(grad_scores[i], key_low[heads[i][0]]) for i in range(4)]
        grad_key = [outer_sum(grad_scores[i], query_low[heads[i][0]]) for i in range(4)]

        def merge(items, twin):
            return jnp.where(lane < 64, items[2 * twin], items[2 * twin + 1])

        for twin, cols in enumerate(twins):
            side = slice(WIDTH + twin * 128, WIDTH + twin * 128 + 128)
            lhs_all[span, side] = merge(attended, twin).astype(jnp.bfloat16)
            grad_lin[0, span, cols] = turn(merge(grad_query, twin) * scale, -1.0).astype(
                jnp.bfloat16
            )
            grad_lin[1, span, cols] = turn(merge(grad_key, twin) * scale, -1.0).astype(
                jnp.bfloat16
            )
            grad_lin[2, span, cols] = merge(grad_value, twin).astype(jnp.bfloat16)
        return carry

    lax.fori_loop(0, 4, units, 0)

    for copy in third:
        copy.wait()

    def hidden(pair, carry):
        cols = pl.ds(pl.multiple_of(pair * 256, 256), 256)
        up_pre = matmul(acts[3], up_all[pair])
        bell = 0.5 * (1.0 + lax.erf(up_pre * ROOT_HALF))
        slope = bell + up_pre * NORMAL_PEAK * jnp.exp(-0.5 * up_pre * up_pre)
        lhs_all[:, cols] = (up_pre * bell).astype(jnp.bfloat16)
        rows_down = jnp.concatenate(
            [
                jnp.concatenate([down_all[2 * pair + half, block] for block in range(4)], axis=1)
                for half in range(2)
            ]
        )
        grad_gated = back_product(acts[4], rows_down)
        grad_pre[:, cols] = (grad_gated * slope).astype(jnp.bfloat16)
        return carry

    lax.fori_loop(0, 4, hidden, 0)

    def weights(index, carry):
        cols = pl.ds(pl.multiple_of(index * 128, 128), 128)
        grad = outer_sum(acts[3, :, cols], grad_pre[...]).astype(jnp.bfloat16)
        for block in range(4):
            parts[index, block] = grad[:, block * 256 : block * 256 + 256]
        for stream in range(3):
            parts[index, 4 + stream] = outer_sum(acts[stream, :, cols], grad_lin[stream]).astype(
                jnp.bfloat16
            )
        grad = outer_sum(lhs_all[:, cols], acts[4]).astype(jnp.bfloat16)
        other = index + 1 - 2 * (index % 2)
        for block in range(4):
            part = grad[:, block * 256 : block * 256 + 256]
            parts[index, 7 + block, 0:96] = part[0:96]

            @pl.when(index % 2 == core)
            def _():
                parts[other, 11, block * 32 : block * 32 + 32] = part[96:128]

            @pl.when(index % 2 != core)
            def _():
                parts[index, 7 + block, 96:128] = part[96:128]

        return carry

    lax.fori_loop(0, 8, weights, 0)
    grad = outer_sum(lhs_all[:, WIDTH:], acts[4]).astype(jnp.bfloat16)
    for block in range(4):
        part = grad[:, block * 256 : block * 256 + 256]
        for pair in range(4):
            even = 2 * pair + core
            parts[even, 7 + block, 96:128] = part[pair * 64 : pair * 64 + 32]
            parts[even, 11, block * 32 : block * 32 + 32] = part[pair * 64 + 32 : pair * 64 + 64]
    sent = [
        pltpu.make_async_copy(
            parts.at[target[0], pl.ds(0, PART)], chunk_low, chunk_sems.at[0]
        ),
        pltpu.make_async_copy(
            parts.at[target[0], pl.ds(PART, 12 - PART)], chunk_high, chunk_sems.at[8]
        ),
    ] + [
        pltpu.make_async_copy(parts.at[target[index]], chunks[index - 1], chunk_sems.at[index])
        for index in range(1, 8)
    ]
    for copy in sent:
        copy.start()

    def put(unit, cols, value):
        low = value.astype(jnp.bfloat16)
        for half in range(2):
            for block in range(2):
                at = (2 * half + block) * ROWS
                tokens[half, block, unit, :, cols] = low[at : at + ROWS]

    def ship(unit):
        if unit < 4:
            routes = (
                (tokens.at[0, 0, unit], keep_own.at[unit]),
                (tokens.at[0, 1, unit], keep_far.at[unit]),
                (tokens.at[1, :, unit], send_norm.at[:, unit]),
            )
        else:
            routes = ((tokens.at[0, :, unit], keep_out), (tokens.at[1, :, unit], send_out))
        for place, (source, goal) in enumerate(routes):
            copy = pltpu.make_async_copy(source, goal, token_sems.at[place, unit])
            copy.start()
            sent.append(copy)

    for stream in range(3):
        put(stream, slice(0, WIDTH), back_product(grad_lin[stream], lin_all[stream]))
        ship(stream)

    def feed(block, carry):
        cols = pl.ds(pl.multiple_of(block * 256, 256), 256)
        rows_up = jnp.concatenate([up_all[part, cols] for part in range(4)], axis=1)
        put(3, cols, back_product(grad_pre[...], rows_up))
        right = [down_all[index, block] for index in range(8)] + [out_rows[:, cols]]
        put(4, cols, matmul(lhs_all[...], jnp.concatenate(right)))
        return carry

    lax.fori_loop(0, 4, feed, 0)
    ship(3)
    ship(4)
    for copy in sent:
        copy.wait()


def back_kernel(
    stack,
    cotangent,
    scaled,
    stats,
    keep,
    came,
    across,
    mix_gain,
    mix_up,
    mix_down,
    norm_gain,
    stack_grad,
    small_own,
    small_other,
    coefficients,
    grads,
    sums,
    coef_grad,
    small,
):
    seqs = stack.shape[0]
    sums[...] = jnp.zeros_like(sums)
    lane = lanes_of((16, 128))

    def unit(step, carry):
        row = pl.multiple_of(step * 16, 16)
        span = pl.ds(row, 16)

        def result(index):
            return wide(keep[index, span]) + wide(came[0, index, span]) + wide(across[index, span])

        for stream in range(4):
            item = result(stream)
            scale = scaled[stream, span]
            moved = item * scale
            sums[stream] += moved[:8] + moved[8:]
            sums[4 + stream] += item[:8] + item[8:]
            weighted = item * norm_gain[stream : stream + 1]
            mean = jnp.mean(weighted, axis=-1, keepdims=True)
            slant = jnp.mean(weighted * scale, axis=-1, keepdims=True)
            grad = stats[2, span, stream : stream + 1] * (weighted - mean - scale * slant)
            if stream == 3:
                grad = grad + wide(cotangent[span])
            grads[stream, span] = grad
        return carry

    lax.fori_loop(0, seqs * SEQ // 16, unit, 0)
    for seq in range(seqs):

        def coefs(step, carry):
            row = pl.multiple_of(step * 16, 16)
            span = pl.ds(seq * SEQ + row, 16)
            found = jnp.zeros((16, 128), jnp.float32)
            for layer in range(STREAMS_IN):
                value = wide(stack[seq, layer, pl.ds(row, 16), :])
                for stream in range(4):
                    got = jnp.sum(grads[stream, span] * value, axis=-1, keepdims=True)
                    found = jnp.where(lane == stream * STREAMS_IN + layer, got, found)
            coef_grad[span] = found
            return carry

        lax.fori_loop(0, SEQ // 16, coefs, 0)
    grad_coef = coef_grad[:, 0:36]
    hidden_pre = stats[1, :, 0:36]
    hidden_low = gelu_value(hidden_pre).astype(jnp.bfloat16)
    for seq in range(seqs):
        turned = stats[0, seq * SEQ : seq * SEQ + SEQ, :].T
        for stream in range(4):
            for layer in range(STREAMS_IN):
                at = stream * STREAMS_IN + layer
                coefficients[seq, layer, stream : stream + 1] = turned[at : at + 1]
    small[...] = jnp.zeros_like(small)
    small[0:36, WIDTH : WIDTH + 36] = lax.dot_general(
        wide(hidden_low),
        grad_coef,
        (((0,), (0,)), ((), ())),
        precision=HIGHEST,
        preferred_element_type=jnp.float32,
    )
    small[36:37, WIDTH : WIDTH + 36] = jnp.sum(grad_coef, axis=0, keepdims=True)
    grad_hidden = (
        lax.dot_general(
            grad_coef,
            mix_down[...],
            (((1,), (1,)), ((), ())),
            precision=HIGHEST,
            preferred_element_type=jnp.float32,
        )
        * gelu_slope(hidden_pre)
    ).astype(jnp.bfloat16)
    gain_row = jnp.zeros((8, WIDTH), jnp.float32)
    up_part = jnp.zeros((36, WIDTH), jnp.float32)
    for seq in range(seqs):
        at = slice(seq * SEQ, seq * SEQ + SEQ)
        last = wide(stack[seq, STREAMS_IN - 1])
        rms = stats[2, at, 4:5]
        mixed_in = (last * rms * mix_gain[...]).astype(jnp.bfloat16)
        up_part = up_part + outer_sum(grad_hidden[at], mixed_in)
        grad_mixed = matmul(grad_hidden[at], mix_up[...])
        along = grad_mixed * last * rms
        for place in range(SEQ // 8):
            gain_row = gain_row + along[place * 8 : place * 8 + 8]
        weighted = grad_mixed * mix_gain[...]
        mean = jnp.mean(weighted * last, axis=-1, keepdims=True)
        grads[4, at] = rms * (weighted - last * (rms * rms * mean))

        def layers(step, carry):
            row = pl.multiple_of(step // 2 * 16, 16)
            cols = pl.ds(pl.multiple_of(step % 2 * 512, 512), 512)
            span = pl.ds(seq * SEQ + row, 16)
            rows_coef = stats[0, span, :]
            parts = [grads[stream, span, cols] for stream in range(4)]
            for layer in range(STREAMS_IN):
                total = None
                for stream in range(4):
                    at_coef = stream * STREAMS_IN + layer
                    term = rows_coef[:, at_coef : at_coef + 1] * parts[stream]
                    total = term if total is None else total + term
                if layer == STREAMS_IN - 1:
                    total = total + grads[4, span, cols]
                stack_grad[seq, layer, pl.ds(row, 16), cols] = total.astype(jnp.bfloat16)
            return carry

        lax.fori_loop(0, 8, layers, 0)
    small[0:36, 0:WIDTH] = up_part
    for place in range(8):
        small[36 + place : 37 + place, 0:WIDTH] = jnp.sum(sums[place], axis=0, keepdims=True)
    small[44:45, 0:WIDTH] = jnp.sum(gain_row, axis=0, keepdims=True)
    _, _, _, core = position()
    small_own[...] = small[pl.ds(pl.multiple_of(core * 24, 8), 24), :]
    small_other[...] = small[pl.ds(pl.multiple_of(24 - core * 24, 8), 24), :]


def place_kernel(
    shard0,
    shard1,
    shard2,
    shard3,
    small_own,
    small_other,
    projection,
    out_grad,
    up_grad,
    down_grad,
    mix_gain_grad,
    mix_up_grad,
    mix_down_grad,
    mix_static_grad,
    gain_grad,
    bias_grad,
    small,
):
    z, member_parity, x, core = position()
    small[pl.ds(pl.multiple_of(core * 24, 8), 24), :] = small_own[...]
    small[pl.ds(pl.multiple_of(24 - core * 24, 8), 24), :] = small_other[...]
    lanes = pl.ds(pl.multiple_of((2 * z + member_parity) * 128, 128), 128)
    mix_up_grad[...] = small[0:36, lanes]
    gain_grad[...] = small[36:40, 0:WIDTH]
    bias_grad[...] = small[40:44, 0:WIDTH]
    mix_gain_grad[...] = small[44:45, 0:WIDTH]
    mix_down_grad[...] = small[0:36, WIDTH : WIDTH + 36]
    for stream in range(4):
        at = WIDTH + stream * STREAMS_IN
        mix_static_grad[stream : stream + 1] = small[36:37, at : at + STREAMS_IN]
    shards = (shard0, shard1, shard2, shard3)
    lane = lanes_of((128, 128))
    for back in range(4):
        from_x = x if back % 2 == 0 else 1 - x
        from_core = core if back < 2 else 1 - core
        quarter = 2 * from_x + from_core
        own, twin = shards[back], shards[back ^ 2]
        for index in range(8):
            half = index % 2
            mine = wide(own[index // 2, :, half * 128 : half * 128 + 128])
            half_b = 1 - half
            lent = wide(twin[index // 2, :, half_b * 128 : half_b * 128 + 128])
            col = pl.multiple_of((index * 4 + quarter) * 128, 128)
            up_grad[:, pl.ds(col, 128)] = jnp.where(
                (lane >= 96) & (from_core == half), lent, mine
            )
        row = pl.multiple_of(quarter * 128, 128)
        for block in range(4):
            cols = slice(block * 256, block * 256 + 256)
            down_grad[pl.ds(row, 96), cols] = wide(own[7 + block, 0:96])

            @pl.when(member_parity == from_core)
            def _():
                head_row = pl.multiple_of(from_x * 64, 64)
                out_grad[pl.ds(head_row, 32), cols] = wide(own[7 + block, 96:128])
                out_grad[pl.ds(head_row + 32, 32), cols] = wide(
                    own[11, block * 32 : block * 32 + 32]
                )
                down_grad[pl.ds(row + 96, 32), cols] = wide(
                    twin[11, block * 32 : block * 32 + 32]
                )

            @pl.when(member_parity != from_core)
            def _():
                down_grad[pl.ds(row + 96, 32), cols] = wide(own[7 + block, 96:128])

    for back in (0, 2):
        from_core = core if back < 2 else 1 - core
        for stream in range(3):
            for twin in range(2):
                tile = slice(twin * 128, twin * 128 + 128)
                mine = wide(shards[back][4 + stream, :, tile])
                across = wide(shards[back + 1][4 + stream, :, tile])
                even = jnp.where(x == 0, mine, across)
                odd = jnp.where(x == 0, across, mine)
                first = jnp.where(lane < 64, even, pltpu.roll(odd, 64, 1))
                second = jnp.where(lane < 64, pltpu.roll(even, 64, 1), odd)
                for low, value in ((0, first), (1, second)):
                    col = pl.multiple_of((2 * twin + low) * 256 + from_core * 128, 128)
                    projection[stream, :, pl.ds(col, 128)] = value


def call(kernel, outs, specs, out_specs, args, scratch=(), cost=None, vmem=60 << 20):
    return pl.pallas_call(
        kernel,
        out_shape=outs,
        in_specs=specs,
        out_specs=out_specs,
        scratch_shapes=list(scratch),
        compiler_params=pltpu.CompilerParams(vmem_limit_bytes=vmem),
        cost_estimate=cost,
    )(*args)


def shape_of(shape, dtype=jnp.bfloat16):
    return jax.ShapeDtypeStruct(shape, dtype)


def rope_tables():
    half_rot = ROTARY // 2
    step = 10000.0 ** (-2.0 * np.arange(half_rot) / ROTARY)
    angles = np.arange(SEQ)[:, None] * step[None, :]
    cos_table = np.ones((SEQ, HEAD_DIM))
    left = np.zeros((SEQ, HEAD_DIM))
    right = np.zeros((SEQ, HEAD_DIM))
    cos_table[:, :half_rot] = np.cos(angles)
    cos_table[:, half_rot:ROTARY] = np.cos(angles)
    left[:, :half_rot] = -np.sin(angles)
    right[:, half_rot:ROTARY] = np.sin(angles)
    return np.stack([np.tile(item, (2, 2)) for item in (cos_table, left, right)]).astype(np.float32)


def on_device_tensor(
    layer_stack,
    out_cotangent,
    pic_start,
    doc_split,
    mix_gain,
    mix_up,
    mix_down,
    mix_static,
    norm_gain,
    norm_bias,
    query_key_value,
    out_weight,
    up_weight,
    down_weight,
):
    z, y, _, _ = position()
    micro_total, local_seqs, _, _, width = layer_stack.shape
    seqs = micro_total * local_seqs
    stack = jnp.transpose(layer_stack, (0, 1, 3, 2, 4)).reshape(seqs, STREAMS_IN, SEQ, width)
    cotangent = out_cotangent.reshape(ROWS, width)
    gain_row = mix_gain.reshape(1, width)

    piece = call(
        prepare_kernel,
        shape_of((12, 128, 256)),
        [VMEM_FULL] * 4,
        VMEM_FULL,
        (query_key_value, out_weight, up_weight, down_weight),
        vmem=60 << 20,
    )
    up_own = mix_up.T
    up_pair = jnp.concatenate([up_own, after(lax.ppermute(up_own, "fsdp", Y_SWAP), piece)], axis=1)
    ups = [up_pair] + [
        lax.ppermute(up_pair, "fsdp", z_pairs([((step + to) % 4, to) for to in range(4)]))
        for step in (1, 2, 3)
    ]
    piece = after(piece, *ups)
    bounds = jnp.concatenate([pic_start.reshape(seqs), doc_split.reshape(seqs)])
    kept = {}
    grad_across = lax.ppermute(cotangent, "replica", X_SWAP)
    grad_packets = (
        cotangent,
        grad_across,
        lax.ppermute(cotangent, "replica", CORE_SWAP),
        lax.ppermute(grad_across, "replica", CORE_SWAP),
    )

    def front():
        packet, *kept["rest"] = call(
            front_kernel,
            (
                shape_of((4 * ROWS + 16, width)),
                shape_of((4, ROWS, width), jnp.float32),
                shape_of((3, ROWS, 128), jnp.float32),
                shape_of((ROWS, width), jnp.float32),
                shape_of((36, width)),
            ),
            [SMEM_FULL] + [VMEM_FULL] * 10,
            (VMEM_FULL,) * 5,
            (
                bounds,
                stack,
                gain_row,
                *ups,
                mix_down,
                mix_static.reshape(1, 36),
                norm_gain,
                norm_bias,
            ),
            scratch=[pltpu.VMEM((4, ROWS, width), jnp.float32)],
            vmem=36 << 20,
        )
        across = lax.ppermute(packet, "replica", X_SWAP)
        beside = lax.ppermute(packet, "replica", CORE_SWAP)
        beside_across = lax.ppermute(across, "replica", CORE_SWAP)
        kept["packets"] = (packet, across, beside, beside_across)
        return (packet, grad_across), (across,)

    pieces = gather_fsdp(piece, z, front)
    packets = kept["packets"]
    scaled, stats, stream_last, mix_up_full = kept["rest"]

    results = call(
        main_kernel,
        (shape_of((PART, 128, 256)), shape_of((12 - PART, 128, 256)))
        + (shape_of((12, 128, 256)),) * 7
        + (shape_of((4, ROWS, width)),) * 2
        + (shape_of((2, 4, ROWS, width)),)
        + (shape_of((2, ROWS, width)),) * 2,
        [VMEM_FULL] + [IN_PLACE] * 19,
        (IN_PLACE,) * 14,
        (jnp.asarray(rope_tables()),) + packets + grad_packets + tuple(pieces),
        scratch=[
            pltpu.VMEM((5, 4 * ROWS, width), jnp.bfloat16),
            pltpu.VMEM((4, 16, width), jnp.bfloat16),
            pltpu.VMEM((4, width, 256), jnp.bfloat16),
            pltpu.VMEM((3, width, 256), jnp.bfloat16),
            pltpu.VMEM((8, 5, 128, 256), jnp.bfloat16),
            pltpu.VMEM((256, width), jnp.bfloat16),
            pltpu.VMEM((4 * ROWS, width + 256), jnp.bfloat16),
            pltpu.VMEM((4 * ROWS, width), jnp.bfloat16),
            pltpu.VMEM((3, 4 * ROWS, 256), jnp.float32),
            pltpu.VMEM((4 * ROWS, 256), jnp.bfloat16),
            pltpu.VMEM((3, 4 * ROWS, 256), jnp.bfloat16),
            pltpu.VMEM((8, 12, 128, 256), jnp.bfloat16),
            pltpu.VMEM((2, 2, 5, ROWS, width), jnp.bfloat16),
            pltpu.SemaphoreType.DMA((4, 6)),
            pltpu.SemaphoreType.DMA((8, 3)),
            pltpu.SemaphoreType.DMA((9,)),
            pltpu.SemaphoreType.DMA((3, 5)),
        ],
        vmem=38 << 20,
    )
    chunks = results[:9]
    keep_own, keep_far, send_norm, keep_out, send_out = results[9:]

    came = lax.ppermute(send_norm, "replica", CORE_SWAP)
    sum_across = (wide(keep_far) + wide(came[1])).astype(jnp.bfloat16)
    came_across = lax.ppermute(sum_across, "replica", X_SWAP)
    out_came = lax.ppermute(after(send_out, sum_across), "replica", CORE_SWAP)
    out_across = (wide(keep_out[1]) + wide(out_came[1])).astype(jnp.bfloat16)
    out_across = lax.ppermute(after(out_across, came_across), "replica", X_SWAP)
    layer_output = (
        stream_last + wide(keep_out[0]) + wide(out_came[0]) + wide(out_across)
    ).astype(jnp.bfloat16)

    first_half = pl.BlockSpec((1, 4, ROWS, width), lambda step: (0, 0, 0, 0))

    def whole(shape):
        return pl.BlockSpec(shape, lambda step: (0,) * len(shape))

    def back():
        kept["back"] = pl.pallas_call(
            back_kernel,
            grid=(1,),
            out_shape=(
                shape_of((seqs, STREAMS_IN, SEQ, width)),
                shape_of((24, width + 128), jnp.float32),
                shape_of((24, width + 128), jnp.float32),
                shape_of((seqs, STREAMS_IN, 4, SEQ), jnp.float32),
            ),
            in_specs=[
                whole((seqs, STREAMS_IN, SEQ, width)),
                whole((ROWS, width)),
                whole((4, ROWS, width)),
                whole((3, ROWS, 128)),
                whole((4, ROWS, width)),
                first_half,
                whole((4, ROWS, width)),
                whole((1, width)),
                whole((36, width)),
                whole((36, 36)),
                whole((4, width)),
            ],
            out_specs=(
                whole((seqs, STREAMS_IN, SEQ, width)),
                whole((24, width + 128)),
                whole((24, width + 128)),
                whole((seqs, STREAMS_IN, 4, SEQ)),
            ),
            scratch_shapes=[
                pltpu.VMEM((5, ROWS, width), jnp.float32),
                pltpu.VMEM((8, 8, width), jnp.float32),
                pltpu.VMEM((ROWS, 128), jnp.float32),
                pltpu.VMEM((48, width + 128), jnp.float32),
            ],
            compiler_params=pltpu.CompilerParams(vmem_limit_bytes=56 << 20),
        )(
            stack,
            cotangent,
            scaled,
            stats,
            keep_own,
            came,
            came_across,
            gain_row,
            mix_up_full,
            mix_down,
            norm_gain,
        )
        return kept["back"][1]

    shard = scatter_fsdp(chunks, z, sum_across, back)
    stack_grad, small, small_other, coefficients = kept["back"]

    small = small + lax.ppermute(small_other, "replica", CORE_SWAP)
    small = small + lax.ppermute(small, "replica", X_SWAP)
    shard = after(shard, small, out_across)
    shard_across = lax.ppermute(shard, "replica", X_SWAP)
    shard_beside = lax.ppermute(shard, "replica", CORE_SWAP)
    for perm in (Y_SWAP, Z_SWAP_NEAR, Z_SWAP_FAR):
        small = small + lax.ppermute(small, "fsdp", perm)
    small_beside = lax.ppermute(small, "replica", CORE_SWAP)
    shard_both = lax.ppermute(after(shard_across, small), "replica", CORE_SWAP)
    owned = call(
        place_kernel,
        (
            shape_of((3, 128, width), jnp.float32),
            shape_of((128, width), jnp.float32),
            shape_of((128, 4 * width), jnp.float32),
            shape_of((512, width), jnp.float32),
            shape_of((1, width), jnp.float32),
            shape_of((36, 128), jnp.float32),
            shape_of((36, 36), jnp.float32),
            shape_of((4, STREAMS_IN), jnp.float32),
            shape_of((4, width), jnp.float32),
            shape_of((4, width), jnp.float32),
        ),
        [VMEM_FULL] * 6,
        (VMEM_FULL,) * 10,
        (shard, shard_across, shard_beside, shard_both, small, small_beside),
        scratch=[pltpu.VMEM((48, width + 128), jnp.float32)],
        vmem=14 << 20,
    )
    projection_grad, out_grad, up_grad, down_grad, *small_grads = owned
    shape = (micro_total, local_seqs, SEQ)
    stack_grad = stack_grad.reshape(micro_total, local_seqs, STREAMS_IN, SEQ, width)
    coefficients = coefficients.reshape(micro_total, local_seqs, STREAMS_IN, 4, SEQ)
    return (
        layer_output.reshape(shape + (width,)),
        jnp.transpose(coefficients, (0, 1, 4, 3, 2)),
        jnp.transpose(stack_grad, (0, 1, 3, 2, 4)),
        small_grads[0].reshape(width),
        small_grads[1].T,
        small_grads[2],
        small_grads[3],
        small_grads[4],
        small_grads[5],
        projection_grad,
        out_grad,
        up_grad,
        down_grad,
    )


def solution(mesh):
    fits = mesh.shape["fsdp"] == 8 and mesh.shape["replica"] == 4
    body = on_device_tensor if fits else on_device
    return jax.shard_map(
        body,
        mesh=mesh,
        in_specs=(
            P(None, ("fsdp", "replica"), None, None, None),
            P(None, ("fsdp", "replica"), None, None),
            P(None, ("fsdp", "replica")),
            P(None, ("fsdp", "replica")),
            P(),
            P("fsdp", None),
            P(),
            P(),
            P(),
            P(),
            P(None, "fsdp", None),
            P("fsdp", None),
            P("fsdp", None),
            P("fsdp", None),
        ),
        out_specs=(
            P(None, ("fsdp", "replica"), None, None),
            P(None, ("fsdp", "replica"), None, None, None),
            P(None, ("fsdp", "replica"), None, None, None),
            P(),
            P("fsdp", None),
            P(),
            P(),
            P(),
            P(),
            P(None, "fsdp", None),
            P("fsdp", None),
            P("fsdp", None),
            P("fsdp", None),
        ),
        check_vma=False,
    )
```

```python
import math

import jax
import jax.numpy as jnp
import numpy as np
from jax import lax
from jax.experimental import pallas as pl
from jax.experimental.pallas import tpu as pltpu
from jax.sharding import PartitionSpec as P

HEADS = 16
HEAD_DIM = 64
ROTARY = 16
STREAMS_IN = 9
SEQ = 64
PIC = 32


EPSILON = 1e-05
ROOT_HALF = 0.7071067811865476
NORMAL_PEAK = 0.3989422804014327
HIGHEST = lax.Precision.HIGHEST


def as_sent(value):

    def short(part):
        return part.astype(jnp.bfloat16) if part.dtype == jnp.float32 else part

    return jax.tree.map(short, value)


def gelu_value(values):
    return 0.5 * values * (1.0 + lax.erf(values * ROOT_HALF))


def gelu_slope(values):
    return 0.5 * (1.0 + lax.erf(values * ROOT_HALF)) + values * NORMAL_PEAK * jnp.exp(
        -0.5 * values * values
    )


def matmul(left_side, right_side):
    return jnp.dot(left_side, right_side, preferred_element_type=jnp.float32)


def outer_sum(left_side, right_side):
    return lax.dot_general(
        left_side, right_side, (((0,), (0,)), ((), ())), preferred_element_type=jnp.float32
    )


def back_product(left_side, right_side):
    return lax.dot_general(
        left_side, right_side, (((1,), (1,)), ((), ())), preferred_element_type=jnp.float32
    )


def rotary_tables():
    half_rot = ROTARY // 2
    inverse = jnp.exp(-math.log(10000.0) * (2.0 * jnp.arange(half_rot, dtype=jnp.float32) / ROTARY))
    angles = jnp.arange(SEQ, dtype=jnp.float32)[:, None] * inverse[None, :]
    return (jnp.cos(angles)[:, None, :], jnp.sin(angles)[:, None, :])


def rotate(values, cos_table, sin_table):
    half_rot = ROTARY // 2
    first_half = values[..., :half_rot]
    second = values[..., half_rot:ROTARY]
    return jnp.concatenate(
        [
            first_half * cos_table - second * sin_table,
            second * cos_table + first_half * sin_table,
            values[..., ROTARY:],
        ],
        axis=-1,
    )


def allowed_mask(starts, splits):
    positions = jnp.arange(SEQ, dtype=jnp.int32)
    second_doc = positions[None, :] >= splits[:, None]
    picture = (positions[None, :] >= starts[:, None]) & (positions[None, :] < starts[:, None] + PIC)
    same_doc = second_doc[:, :, None] == second_doc[:, None, :]
    causal = positions[:, None] >= positions[None, :]
    both_pic = picture[:, :, None] & picture[:, None, :]
    return same_doc & (causal[None] | both_pic)


def masked_scores(queries, key_rot, allowed):
    scores = jnp.einsum(
        "nqhe,nkhe->nhqk", queries, key_rot, preferred_element_type=jnp.float32
    ) * HEAD_DIM ** (-0.5)
    return jnp.where(allowed[:, None], scores, -1e30)


def on_device(
    layer_stack,
    out_cotangent,
    pic_start,
    doc_split,
    mix_gain,
    mix_up,
    mix_down,
    mix_static,
    norm_gain,
    norm_bias,
    query_key_value,
    out_weight,
    up_weight,
    down_weight,
):
    micro_total = layer_stack.shape[0]
    local_seqs = layer_stack.shape[1]
    model_width = layer_stack.shape[-1]
    groups = [(0, micro_total)]
    cos_table, sin_table = rotary_tables()
    output_list = []
    coef_list = []
    grad_list = []
    shard_total = None
    small_total = None
    for first_micro, micro_count in groups:
        seq_count = micro_count * local_seqs
        row_count = seq_count * SEQ
        head_shape = (seq_count, SEQ, HEADS, HEAD_DIM)
        flat_stack = layer_stack[first_micro : first_micro + micro_count].reshape(
            row_count, STREAMS_IN, model_width
        )
        grad_rows = out_cotangent[first_micro : first_micro + micro_count].reshape(
            row_count, model_width
        )
        starts = pic_start[first_micro : first_micro + micro_count].reshape(seq_count)
        splits = doc_split[first_micro : first_micro + micro_count].reshape(seq_count)
        allowed = allowed_mask(starts, splits)
        mix_up_full, projection_full, out_full = (
            lax.all_gather(mix_up, "fsdp", axis=0, tiled=True),
            lax.all_gather(query_key_value, "fsdp", axis=1, tiled=True),
            lax.all_gather(out_weight, "fsdp", axis=0, tiled=True),
        )
        up_full, down_full = (
            lax.all_gather(up_weight, "fsdp", axis=0, tiled=True),
            lax.all_gather(down_weight, "fsdp", axis=0, tiled=True),
        )
        last_layer = flat_stack[:, STREAMS_IN - 1, :].astype(jnp.float32)
        rms_scale = lax.rsqrt(jnp.mean(last_layer * last_layer, axis=-1, keepdims=True) + EPSILON)
        mixed_in = (last_layer * rms_scale * mix_gain).astype(jnp.bfloat16)
        hidden_pre = matmul(mixed_in, mix_up_full)
        hidden_mix = gelu_value(hidden_pre).astype(jnp.bfloat16)
        hidden_wide = hidden_mix.astype(jnp.float32)
        coef_flat = jnp.dot(hidden_wide, mix_down, precision=HIGHEST) + mix_static.reshape(-1)
        coef_rows = coef_flat.reshape(row_count, 4, STREAMS_IN)
        streams = coef_rows[:, :, 0, None] * flat_stack[:, None, 0, :].astype(jnp.float32)
        for layer_index in range(1, STREAMS_IN):
            streams = streams + coef_rows[:, :, layer_index, None] * flat_stack[
                :, None, layer_index, :
            ].astype(jnp.float32)
        center = streams - jnp.mean(streams, axis=-1, keepdims=True)
        inv_std = lax.rsqrt(jnp.mean(center * center, axis=-1, keepdims=True) + EPSILON)
        scaled = center * inv_std
        normed = (scaled * norm_gain + norm_bias).astype(jnp.bfloat16)
        query_lin = matmul(normed[:, 0], projection_full[0])
        key_lin = matmul(normed[:, 1], projection_full[1])
        value_lin = matmul(normed[:, 2], projection_full[2])
        queries = rotate(query_lin.reshape(head_shape), cos_table, sin_table).astype(jnp.bfloat16)
        key_rot = rotate(key_lin.reshape(head_shape), cos_table, sin_table).astype(jnp.bfloat16)
        values = value_lin.astype(jnp.bfloat16).reshape(head_shape)
        scores = masked_scores(queries, key_rot, allowed)
        row_top = jnp.max(scores, axis=-1, keepdims=True)
        exponent = jnp.exp(scores - row_top)
        row_total = jnp.sum(exponent, axis=-1, keepdims=True)
        soft_probs = exponent / row_total
        log_total = row_top + jnp.log(row_total)
        attended = (
            jnp.einsum(
                "nhqk,nkhe->nqhe",
                soft_probs.astype(jnp.bfloat16),
                values,
                preferred_element_type=jnp.float32,
            )
            .astype(jnp.bfloat16)
            .reshape(row_count, model_width)
        )
        attn_out = matmul(attended, out_full)
        up_pre = matmul(normed[:, 3], up_full)
        gated_act = gelu_value(up_pre).astype(jnp.bfloat16)
        feed_out = matmul(gated_act, down_full)
        output_list.append((streams[:, 3] + attn_out + feed_out).astype(jnp.bfloat16))
        coef_list.append(coef_rows)
        mix_up_back, projection_back, out_back = (
            lax.all_gather(mix_up, "fsdp", axis=0, tiled=True),
            lax.all_gather(query_key_value, "fsdp", axis=1, tiled=True),
            lax.all_gather(out_weight, "fsdp", axis=0, tiled=True),
        )
        up_back, down_back = (
            lax.all_gather(up_weight, "fsdp", axis=0, tiled=True),
            lax.all_gather(down_weight, "fsdp", axis=0, tiled=True),
        )
        grad_down = outer_sum(gated_act, grad_rows)
        grad_gated = back_product(grad_rows, down_back)
        grad_up_pre = (grad_gated * gelu_slope(up_pre)).astype(jnp.bfloat16)
        grad_up = outer_sum(normed[:, 3], grad_up_pre)
        grad_norm_feed = back_product(grad_up_pre, up_back)
        feed_shards = (
            lax.psum_scatter(
                grad_up.astype(jnp.bfloat16), "fsdp", scatter_dimension=0, tiled=True
            ).astype(jnp.float32),
            lax.psum_scatter(
                grad_down.astype(jnp.bfloat16), "fsdp", scatter_dimension=0, tiled=True
            ).astype(jnp.float32),
        )
        grad_out_weight = outer_sum(attended, grad_rows)
        grad_attended = back_product(grad_rows, out_back).astype(jnp.bfloat16).reshape(head_shape)
        scores_again = masked_scores(queries, key_rot, allowed)
        probs_again = jnp.exp(scores_again - log_total)
        grad_probs = jnp.einsum(
            "nqhe,nkhe->nhqk", grad_attended, values, preferred_element_type=jnp.float32
        )
        grad_value = (
            jnp.einsum(
                "nhqk,nqhe->nkhe",
                probs_again.astype(jnp.bfloat16),
                grad_attended,
                preferred_element_type=jnp.float32,
            )
            .astype(jnp.bfloat16)
            .reshape(row_count, model_width)
        )
        delta_rows = jnp.sum(probs_again * grad_probs, axis=-1, keepdims=True)
        grad_scores = (probs_again * (grad_probs - delta_rows)).astype(jnp.bfloat16)
        score_scale = HEAD_DIM ** (-0.5)
        grad_query_rot = (
            jnp.einsum("nhqk,nkhe->nqhe", grad_scores, key_rot, preferred_element_type=jnp.float32)
            * score_scale
        )
        grad_key_rot = (
            jnp.einsum("nhqk,nqhe->nkhe", grad_scores, queries, preferred_element_type=jnp.float32)
            * score_scale
        )
        grad_query = (
            rotate(grad_query_rot, cos_table, -sin_table)
            .astype(jnp.bfloat16)
            .reshape(row_count, model_width)
        )
        grad_key = (
            rotate(grad_key_rot, cos_table, -sin_table)
            .astype(jnp.bfloat16)
            .reshape(row_count, model_width)
        )
        grad_linear = (grad_query, grad_key, grad_value)
        grad_projection = jnp.stack(
            [outer_sum(normed[:, stream], grad_linear[stream]) for stream in range(3)]
        )
        grad_normed = jnp.stack(
            [back_product(grad_linear[stream], projection_back[stream]) for stream in range(3)]
            + [grad_norm_feed],
            axis=1,
        )
        gain_grad = jnp.sum(grad_normed * scaled, axis=0)
        bias_grad = jnp.sum(grad_normed, axis=0)
        grad_scaled = grad_normed * norm_gain
        grad_streams = inv_std * (
            grad_scaled
            - jnp.mean(grad_scaled, axis=-1, keepdims=True)
            - scaled * jnp.mean(grad_scaled * scaled, axis=-1, keepdims=True)
        )
        grad_streams = grad_streams + jnp.concatenate(
            [
                jnp.zeros((row_count, 3, model_width), jnp.float32),
                grad_rows[:, None, :].astype(jnp.float32),
            ],
            axis=1,
        )
        grad_coef = jnp.stack(
            [
                jnp.sum(
                    grad_streams * flat_stack[:, None, layer_index, :].astype(jnp.float32), axis=-1
                )
                for layer_index in range(STREAMS_IN)
            ],
            axis=-1,
        )
        grad_coef_flat = grad_coef.reshape(row_count, 4 * STREAMS_IN)
        static_grad = jnp.sum(grad_coef_flat, axis=0).reshape(4, STREAMS_IN)
        down_mix_grad = jnp.dot(hidden_wide.T, grad_coef_flat, precision=HIGHEST)
        grad_hidden = (
            jnp.dot(grad_coef_flat, mix_down.T, precision=HIGHEST) * gelu_slope(hidden_pre)
        ).astype(jnp.bfloat16)
        grad_mix_up = outer_sum(mixed_in, grad_hidden)
        grad_mixed = back_product(grad_hidden, mix_up_back)
        gain_mix_grad = jnp.sum(grad_mixed * last_layer * rms_scale, axis=0)
        weighted = grad_mixed * mix_gain
        grad_last = rms_scale * (
            weighted
            - last_layer
            * rms_scale
            * rms_scale
            * jnp.mean(weighted * last_layer, axis=-1, keepdims=True)
        )
        per_layer = [
            jnp.sum(coef_rows[:, :, layer_index, None] * grad_streams, axis=1)
            for layer_index in range(STREAMS_IN)
        ]
        per_layer[STREAMS_IN - 1] = per_layer[STREAMS_IN - 1] + grad_last
        grad_list.append(jnp.stack(per_layer, axis=1).astype(jnp.bfloat16))
        attention_shards = (
            lax.psum_scatter(
                grad_mix_up.astype(jnp.bfloat16), "fsdp", scatter_dimension=0, tiled=True
            ).astype(jnp.float32),
            lax.psum_scatter(
                grad_projection.astype(jnp.bfloat16), "fsdp", scatter_dimension=1, tiled=True
            ).astype(jnp.float32),
            lax.psum_scatter(
                grad_out_weight.astype(jnp.bfloat16), "fsdp", scatter_dimension=0, tiled=True
            ).astype(jnp.float32),
        )
        shards = attention_shards + feed_shards
        shards = jax.tree.map(
            lambda part: part.astype(jnp.float32), lax.psum(as_sent(shards), "replica")
        )
        smalls = (gain_mix_grad, down_mix_grad, static_grad, gain_grad, bias_grad)
        if shard_total is None:
            shard_total = shards
            small_total = smalls
        else:
            shard_total = tuple(
                (total_item + new_item for total_item, new_item in zip(shard_total, shards))
            )
            small_total = tuple(
                (total_item + new_item for total_item, new_item in zip(small_total, smalls))
            )
    small_total = lax.psum(small_total, ("fsdp", "replica"))
    layer_output = jnp.concatenate(output_list, axis=0).reshape(
        micro_total, local_seqs, SEQ, model_width
    )
    coefficients = jnp.concatenate(coef_list, axis=0).reshape(
        micro_total, local_seqs, SEQ, 4, STREAMS_IN
    )
    stack_grad = jnp.concatenate(grad_list, axis=0).reshape(
        micro_total, local_seqs, SEQ, STREAMS_IN, model_width
    )
    return (
        layer_output,
        coefficients,
        stack_grad,
        small_total[0],
        shard_total[0],
        small_total[1],
        small_total[2],
        small_total[3],
        small_total[4],
        shard_total[1],
        shard_total[2],
        shard_total[3],
        shard_total[4],
    )


ROWS = 128
WIDTH = 1024
VMEM_FULL = pl.BlockSpec(memory_space=pltpu.VMEM)
SMEM_FULL = pl.BlockSpec(memory_space=pltpu.SMEM)
IN_PLACE = pl.BlockSpec(memory_space=pl.ANY)


def bits_swap(size, bit):
    return [(index, index ^ bit) for index in range(size)]


CORE_SWAP = bits_swap(4, 1)
X_SWAP = bits_swap(4, 2)
Y_SWAP = bits_swap(8, 1)
Z_SWAP_NEAR = bits_swap(8, 2)
Z_SWAP_FAR = bits_swap(8, 4)


def z_pairs(moves):
    return [(2 * src + col, 2 * dst + col) for src, dst in moves for col in range(2)]


def pick(cond, first, second):
    return jnp.where(cond, first, second)


def order_two(flag, own, other, axis):
    first = pick(flag == 0, own, other)
    second = pick(flag == 0, other, own)
    return jnp.concatenate([first, second], axis=axis)


def after(value, *others):
    return lax.optimization_barrier((value,) + others)[0]


Z_NEAR = z_pairs([(0, 1), (1, 0), (2, 3), (3, 2)])
Z_MIDDLE = [
    (index, (index ^ 1) if index // 8 in (0, 3) else (24 - index // 8 * 8 + index % 8))
    for index in range(32)
]


def fsdp_move(value, pairs):
    return lax.ppermute(value, "fsdp" if len(pairs) == 8 else ("fsdp", "replica"), pairs)


PART = 7


def gather_fsdp(piece, z, front):
    inner = (z == 1) | (z == 2)
    near = fsdp_move(piece, Z_NEAR)
    middle = fsdp_move(piece, Z_MIDDLE)
    side = fsdp_move(piece, Y_SWAP)
    early, late = front()
    middle_near = fsdp_move(after(near, *early, side), Z_MIDDLE)
    turned = fsdp_move(after(pick(inner, middle, side), *early), Z_NEAR)
    side_two = fsdp_move(pick(inner, middle, near), Y_SWAP)
    third = pick(inner, middle_near, turned)
    near_twice = fsdp_move(after(middle_near, side_two, third), Z_NEAR)
    side_three = fsdp_move(third, Y_SWAP)
    over_z = fsdp_move(side_three[:PART], Z_NEAR)
    over_y = fsdp_move(after(near_twice[PART:], side_three, *late), Y_SWAP)
    return [
        piece,
        side,
        near,
        middle,
        middle_near,
        turned,
        near_twice,
        side_two,
        side_three,
        over_z,
        over_y,
    ]


def position():
    member, partner = lax.axis_index("fsdp"), lax.axis_index("replica")
    return member // 2, member % 2, partner // 2, partner % 2


def table(values, z):
    found = jnp.int32(values[0])
    for index in range(1, 4):
        found = jnp.where(z == index, jnp.int32(values[index]), found)
    return found


def gather_order(z, y):
    places = []
    for z_from in (z, table([1, 0, 3, 2], z), table([2, 2, 1, 1], z), table([3, 3, 0, 0], z)):
        places += [2 * z_from + y, 2 * z_from + 1 - y]
    return places


def scatter_order(z, y):
    others = (table([3, 0, 3, 0], z), table([2, 3, 0, 1], z), table([1, 2, 1, 2], z), z)
    own = (table([3, 3, 0, 0], z), table([2, 2, 1, 1], z), table([1, 0, 3, 2], z), z)
    return [2 * z_to + 1 - y for z_to in others] + [2 * z_to + y for z_to in own]


def wide(value):
    return value.astype(jnp.float32)


def scatter_fsdp(chunks, z, first_wait, beside):
    inner = (z == 1) | (z == 2)
    side_low, side_high, side_one, side_two, side_own, last, third, near, own = chunks

    def low(value):
        return value.astype(jnp.bfloat16)

    def only(cond, value):
        return jnp.where(cond, wide(value), 0.0)

    over_z = fsdp_move(side_high, Z_NEAR)
    over_y = fsdp_move(side_low, Y_SWAP)
    over_z = jnp.pad(only(inner, over_z), ((PART, 0), (0, 0), (0, 0)))
    back_one = fsdp_move(low(wide(side_one) + over_z), Y_SWAP)
    over_y = jnp.pad(wide(over_y), ((0, 12 - PART), (0, 0), (0, 0)))
    back_far = fsdp_move(low(wide(after(last, first_wait)) + over_y), Z_NEAR)
    back_two = fsdp_move(after(side_two, first_wait), Y_SWAP)
    to_middle = low(wide(last) + wide(back_one) + wide(back_far))
    to_near = low(
        jnp.where(
            inner,
            wide(jnp.concatenate([side_low, side_high])),
            wide(third) + wide(back_one),
        )
    )
    middle_one = fsdp_move(to_middle, Z_MIDDLE)
    near_one = fsdp_move(to_near, Z_NEAR)
    back_own = fsdp_move(low(wide(side_own) + only(z % 3 == 0, near_one)), Y_SWAP)
    to_near = low(wide(near) + jnp.where(inner, wide(middle_one), wide(back_two)))
    to_middle = low(wide(third) + wide(back_two) + wide(near_one))
    to_near, to_middle, _ = lax.optimization_barrier((to_near, to_middle, beside()))
    near_two = fsdp_move(to_near, Z_NEAR)
    middle_two = fsdp_move(to_middle, Z_MIDDLE)
    return low(wide(own) + wide(back_own) + wide(near_two) + only(inner, middle_two))


def lanes_of(shape):
    return lax.broadcasted_iota(jnp.int32, shape, 1)


def rows_of(shape):
    return lax.broadcasted_iota(jnp.int32, shape, 0)


def prepare_kernel(projection, out_weight, up_weight, down_weight, piece):
    _, member_parity, x, core = position()
    quarter, other = 2 * x + core, 2 * x + 1 - core
    lane = lanes_of((128, 128))
    for index in range(8):
        half = index % 2
        own = up_weight[:, pl.ds(pl.multiple_of((index * 4 + quarter) * 128, 128), 128)]
        extra = up_weight[:, pl.ds(pl.multiple_of(((index ^ 1) * 4 + other) * 128, 128), 128)]
        taken = (lane >= 96) & (core == half)
        piece[index // 2, :, half * 128 : half * 128 + 128] = jnp.where(
            taken, wide(extra), wide(own)
        ).astype(jnp.bfloat16)
    for stream in range(3):
        for twin in range(2):
            tiles = [
                wide(
                    projection[
                        stream,
                        :,
                        pl.ds(pl.multiple_of((2 * twin + low) * 256 + core * 128, 128), 128),
                    ]
                )
                for low in range(2)
            ]
            first = jnp.where(x == 0, tiles[0], pltpu.roll(tiles[0], 64, 1))
            second = jnp.where(x == 0, pltpu.roll(tiles[1], 64, 1), tiles[1])
            piece[4 + stream, :, twin * 128 : twin * 128 + 128] = jnp.where(
                lane < 64, first, second
            ).astype(jnp.bfloat16)
    own_row = pl.multiple_of(quarter * 128, 128)
    other_row = pl.multiple_of(other * 128, 128)
    head_row = pl.multiple_of(x * 64, 64)
    for block in range(4):
        cols = slice(block * 256, block * 256 + 256)
        piece[7 + block, 0:96] = down_weight[pl.ds(own_row, 96), cols]

        @pl.when(member_parity == core)
        def _():
            piece[7 + block, 96:128] = out_weight[pl.ds(head_row, 32), cols]
            piece[11, block * 32 : block * 32 + 32] = out_weight[pl.ds(head_row + 32, 32), cols]

        @pl.when(member_parity != core)
        def _():
            piece[7 + block, 96:128] = down_weight[pl.ds(own_row + 96, 32), cols]
            piece[11, block * 32 : block * 32 + 32] = down_weight[pl.ds(other_row + 96, 32), cols]


def front_kernel(
    bounds,
    stack,
    mix_gain,
    up_own,
    up_one,
    up_two,
    up_three,
    mix_down,
    mix_static,
    norm_gain,
    norm_bias,
    packet,
    scaled_out,
    stats,
    stream_out,
    mix_up,
    streams,
):
    seqs = stack.shape[0]
    z, y, _, core = position()
    for step, part in ((0, up_own), (1 + 2 * core, up_one), (2, up_two), (3 - 2 * core, up_three)):
        z_from = (z + step) % 4
        for half, col in enumerate((y, 1 - y)):
            lanes = pl.ds(pl.multiple_of((2 * z_from + col) * 128, 128), 128)
            mix_up[:, lanes] = part[:, half * 128 : half * 128 + 128]
    for seq in range(seqs):
        last = wide(stack[seq, STREAMS_IN - 1])
        rms = lax.rsqrt(jnp.mean(last * last, axis=-1, keepdims=True) + EPSILON)
        mixed_in = (last * rms * mix_gain[...]).astype(jnp.bfloat16)
        hidden_pre = back_product(mixed_in, mix_up[...])
        hidden = wide(gelu_value(hidden_pre).astype(jnp.bfloat16))
        coef = jnp.dot(
            hidden, mix_down[...], precision=HIGHEST, preferred_element_type=jnp.float32
        )
        coef = coef + mix_static[...]
        at = slice(seq * SEQ, seq * SEQ + SEQ)
        stats[0, at, 0:36] = coef
        stats[1, at, 0:36] = hidden_pre
        stats[2, at, 4:5] = rms

        def mix(step, carry):
            row = pl.multiple_of(step // 2 * 16, 16)
            col = pl.multiple_of(step % 2 * 512, 512)
            rows_coef = stats[0, pl.ds(seq * SEQ + row, 16), :]
            totals = [None] * 4
            for layer in range(STREAMS_IN):
                value = wide(stack[seq, layer, pl.ds(row, 16), pl.ds(col, 512)])
                for stream in range(4):
                    at_coef = stream * STREAMS_IN + layer
                    term = rows_coef[:, at_coef : at_coef + 1] * value
                    totals[stream] = term if layer == 0 else totals[stream] + term
            for stream in range(4):
                streams[stream, pl.ds(seq * SEQ + row, 16), pl.ds(col, 512)] = totals[stream]
            return carry

        lax.fori_loop(0, 8, mix, 0)

    def norm(step, carry):
        row = pl.multiple_of(step * 16, 16)
        for stream in range(4):
            value = streams[stream, pl.ds(row, 16), :]
            center = value - jnp.mean(value, axis=-1, keepdims=True)
            inverse = lax.rsqrt(jnp.mean(center * center, axis=-1, keepdims=True) + EPSILON)
            scaled = center * inverse
            stats[2, pl.ds(row, 16), stream : stream + 1] = inverse
            scaled_out[stream, pl.ds(row, 16), :] = scaled
            packet[pl.ds(stream * ROWS + row, 16), :] = (
                scaled * norm_gain[stream : stream + 1, :] + norm_bias[stream : stream + 1, :]
            ).astype(jnp.bfloat16)
            if stream == 3:
                stream_out[pl.ds(row, 16), :] = value
        return carry

    lax.fori_loop(0, seqs * SEQ // 16, norm, 0)
    packet[4 * ROWS :] = jnp.zeros((16, WIDTH), jnp.bfloat16)
    row = rows_of((16, 128))
    marks = jnp.zeros((16, 128), jnp.float32)
    for place in range(2 * seqs):
        marks = jnp.where(row == place, wide(bounds[place]), marks)
    packet[4 * ROWS :, 0:128] = marks.astype(jnp.bfloat16)


def main_kernel(
    rope,
    packet0,
    packet1,
    packet2,
    packet3,
    cotangent0,
    cotangent1,
    cotangent2,
    cotangent3,
    piece0,
    piece1,
    piece2,
    piece3,
    piece4,
    piece5,
    piece6,
    piece7,
    piece8,
    piece9,
    piece10,
    chunk_low,
    chunk_high,
    chunk1,
    chunk2,
    chunk3,
    chunk4,
    chunk5,
    chunk6,
    chunk7,
    keep_own,
    keep_far,
    send_norm,
    keep_out,
    send_out,
    acts,
    marks,
    up_all,
    lin_all,
    down_all,
    out_rows,
    lhs_all,
    grad_pre,
    linear,
    grad_att,
    grad_lin,
    parts,
    tokens,
    packet_sems,
    piece_sems,
    chunk_sems,
    token_sems,
):
    z, y, _, core = position()
    origin = gather_order(z, y)
    target = scatter_order(z, y)
    packets = (packet0, packet1, packet2, packet3)
    cotangents = (cotangent0, cotangent1, cotangent2, cotangent3)
    piece, side, near, middle, middle_near, turned = piece0, piece1, piece2, piece3, piece4, piece5
    near_twice, side_two, side_three, over_z, over_y = piece6, piece7, piece8, piece9, piece10
    inner = (z == 1) | (z == 2)
    sources = (
        (piece, piece),
        (side, side),
        (near, near),
        (turned, side_two),
        (middle, turned),
        (side_two, side_three),
        (middle_near, near_twice),
        (side_three, None),
    )
    chunks = (chunk1, chunk2, chunk3, chunk4, chunk5, chunk6, chunk7)
    member_rows = [pl.ds(pl.multiple_of(place * 128, 128), 128) for place in origin]

    def unit_copies(unit):
        return [
            pltpu.make_async_copy(
                packets[block].at[pl.ds(unit * ROWS, ROWS)],
                acts.at[unit, pl.ds(block * ROWS, ROWS)],
                packet_sems.at[block, unit],
            )
            for block in range(4)
        ]

    def piece_copies(index, ref, tail_ref):
        rows = member_rows[index]
        down = 7 if tail_ref is ref else 0
        return [
            pltpu.make_async_copy(
                ref.at[pl.ds(4, 3)], lin_all.at[:, rows], piece_sems.at[index, 0]
            ),
            pltpu.make_async_copy(
                tail_ref.at[pl.ds(down, 5)], down_all.at[origin[index]], piece_sems.at[index, 1]
            ),
            pltpu.make_async_copy(
                ref.at[pl.ds(0, 4)], up_all.at[:, rows], piece_sems.at[index, 2]
            ),
        ]

    first = unit_copies(0) + unit_copies(1) + unit_copies(2)
    second = [
        pltpu.make_async_copy(
            cotangents[block],
            acts.at[4, pl.ds(block * ROWS, ROWS)],
            packet_sems.at[block, 4],
        )
        for block in range(4)
    ]
    for block in range(4):
        second.append(
            pltpu.make_async_copy(
                packets[block].at[pl.ds(4 * ROWS, 16)], marks.at[block], packet_sems.at[block, 5]
            )
        )
    third = unit_copies(3)
    for copy in first + second + third:
        copy.start()
    for index, (for_inner, for_ends) in enumerate(sources):
        copies = piece_copies(index, for_inner, for_inner)
        first.append(copies[0])
        second.append(copies[1])
        third.append(copies[2])
        if for_inner is for_ends:
            for copy in copies:
                copy.start()
            continue
        ends = (
            piece_copies(index, over_z, over_y)
            if for_ends is None
            else piece_copies(index, for_ends, for_ends)
        )

        @pl.when(inner)
        def _():
            for copy in copies:
                copy.start()

        @pl.when(jnp.logical_not(inner))
        def _():
            for copy in ends:
                copy.start()

    for copy in first:
        copy.wait()
    for stream in range(3):
        linear[stream] = matmul(acts[stream], lin_all[stream])
    for copy in second:
        copy.wait()
    for pair in range(4):
        even = 2 * pair + core
        odd = 2 * pair + 1 - core
        for block in range(4):
            band = slice(block * 32, block * 32 + 32)
            cols = slice(block * 256, block * 256 + 256)
            out_rows[pair * 64 : pair * 64 + 32, cols] = down_all[even, block, 96:128]
            out_rows[pair * 64 + 32 : pair * 64 + 64, cols] = down_all[even, 4, band]
            down_all[even, block, 96:128] = down_all[odd, 4, band]

    grad_att[...] = back_product(acts[4], out_rows[...]).astype(jnp.bfloat16)
    cos_table = rope[0]
    sin_left = rope[1]
    sin_right = rope[2]
    scale = HEAD_DIM ** (-0.5)

    def turn(value, sign):
        return (
            value * cos_table
            + pltpu.roll(value, 120, 1) * (sign * sin_left)
            + pltpu.roll(value, 8, 1) * (sign * sin_right)
        )

    def units(block, carry):
        row = rows_of((ROWS, ROWS))
        lane = lanes_of((ROWS, ROWS))
        bound = wide(marks[block])

        def both(low, high):
            return jnp.where(row < SEQ, low, high), jnp.where(lane < SEQ, low, high)

        start_q, start_k = both(bound[0:1, 0:128], bound[1:2, 0:128])
        split_q, split_k = both(bound[2:3, 0:128], bound[3:4, 0:128])
        at_q = wide(row % SEQ)
        at_k = wide(lane % SEQ)
        same = (row // SEQ == lane // SEQ) & ((at_q >= split_q) == (at_k >= split_k))
        pic_q = (at_q >= start_q) & (at_q < start_q + PIC)
        pic_k = (at_k >= start_k) & (at_k < start_k + PIC)
        penalty = jnp.where(same & ((at_q >= at_k) | (pic_q & pic_k)), 0.0, -1e30)
        span = pl.ds(pl.multiple_of(block * ROWS, ROWS), ROWS)
        twins = [slice(twin * 128, twin * 128 + 128) for twin in range(2)]
        heads = [(twin, head) for twin in range(2) for head in range(2)]
        query = [turn(linear[0, span, cols], 1.0) for cols in twins]
        query_low = [item.astype(jnp.bfloat16) for item in query]
        key_low = [turn(linear[1, span, cols], 1.0).astype(jnp.bfloat16) for cols in twins]
        value_low = [linear[2, span, cols].astype(jnp.bfloat16) for cols in twins]
        grad_low = [grad_att[span, cols] for cols in twins]

        def only(item, head):
            return jnp.where(lane // 64 == head, wide(item), 0.0).astype(jnp.bfloat16)

        scores = [
            back_product(only(query[twin], head), key_low[twin]) * scale + penalty
            for twin, head in heads
        ]
        grad_probs = [
            back_product(only(grad_low[twin], head), value_low[twin]) for twin, head in heads
        ]
        exponent = [jnp.exp(item - jnp.max(item, axis=-1, keepdims=True)) for item in scores]
        probs = [item / jnp.sum(item, axis=-1, keepdims=True) for item in exponent]
        probs_low = [item.astype(jnp.bfloat16) for item in probs]
        grad_scores = [
            (prob * (grad - jnp.sum(prob * grad, axis=-1, keepdims=True))).astype(jnp.bfloat16)
            for prob, grad in zip(probs, grad_probs)
        ]
        attended = [matmul(probs_low[i], value_low[heads[i][0]]) for i in range(4)]
        grad_value = [outer_sum(probs_low[i], grad_low[heads[i][0]]) for i in range(4)]
        grad_query = [matmul(grad_scores[i], key_low[heads[i][0]]) for i in range(4)]
        grad_key = [outer_sum(grad_scores[i], query_low[heads[i][0]]) for i in range(4)]

        def merge(items, twin):
            return jnp.where(lane < 64, items[2 * twin], items[2 * twin + 1])

        for twin, cols in enumerate(twins):
            side = slice(WIDTH + twin * 128, WIDTH + twin * 128 + 128)
            lhs_all[span, side] = merge(attended, twin).astype(jnp.bfloat16)
            grad_lin[0, span, cols] = turn(merge(grad_query, twin) * scale, -1.0).astype(
                jnp.bfloat16
            )
            grad_lin[1, span, cols] = turn(merge(grad_key, twin) * scale, -1.0).astype(
                jnp.bfloat16
            )
            grad_lin[2, span, cols] = merge(grad_value, twin).astype(jnp.bfloat16)
        return carry

    lax.fori_loop(0, 4, units, 0)

    for copy in third:
        copy.wait()

    def hidden(pair, carry):
        cols = pl.ds(pl.multiple_of(pair * 256, 256), 256)
        up_pre = matmul(acts[3], up_all[pair])
        bell = 0.5 * (1.0 + lax.erf(up_pre * ROOT_HALF))
        slope = bell + up_pre * NORMAL_PEAK * jnp.exp(-0.5 * up_pre * up_pre)
        lhs_all[:, cols] = (up_pre * bell).astype(jnp.bfloat16)
        rows_down = jnp.concatenate(
            [
                jnp.concatenate([down_all[2 * pair + half, block] for block in range(4)], axis=1)
                for half in range(2)
            ]
        )
        grad_gated = back_product(acts[4], rows_down)
        grad_pre[:, cols] = (grad_gated * slope).astype(jnp.bfloat16)
        return carry

    lax.fori_loop(0, 4, hidden, 0)

    def weights(pair, carry):
        cols = pl.ds(pl.multiple_of(pair * 256, 256), 256)
        halves = (slice(0, 128), slice(128, 256))
        grad = outer_sum(acts[3, :, cols], grad_pre[...]).astype(jnp.bfloat16)
        for block in range(4):
            for half, rows in enumerate(halves):
                parts[2 * pair + half, block] = grad[rows, block * 256 : block * 256 + 256]
        for stream in range(3):
            grad = outer_sum(acts[stream, :, cols], grad_lin[stream]).astype(jnp.bfloat16)
            for half, rows in enumerate(halves):
                parts[2 * pair + half, 4 + stream] = grad[rows]
        grad = outer_sum(lhs_all[:, cols], acts[4]).astype(jnp.bfloat16)
        for half in range(2):
            index, other = 2 * pair + half, 2 * pair + 1 - half
            for block in range(4):
                part = grad[half * 128 : half * 128 + 128, block * 256 : block * 256 + 256]
                parts[index, 7 + block, 0:96] = part[0:96]

                @pl.when(core == half)
                def _():
                    parts[other, 11, block * 32 : block * 32 + 32] = part[96:128]

                @pl.when(core != half)
                def _():
                    parts[index, 7 + block, 96:128] = part[96:128]

        return carry

    lax.fori_loop(0, 4, weights, 0)
    grad = outer_sum(lhs_all[:, WIDTH:], acts[4]).astype(jnp.bfloat16)
    for block in range(4):
        part = grad[:, block * 256 : block * 256 + 256]
        for pair in range(4):
            even = 2 * pair + core
            parts[even, 7 + block, 96:128] = part[pair * 64 : pair * 64 + 32]
            parts[even, 11, block * 32 : block * 32 + 32] = part[pair * 64 + 32 : pair * 64 + 64]
    sent = [
        pltpu.make_async_copy(
            parts.at[target[0], pl.ds(0, PART)], chunk_low, chunk_sems.at[0]
        ),
        pltpu.make_async_copy(
            parts.at[target[0], pl.ds(PART, 12 - PART)], chunk_high, chunk_sems.at[8]
        ),
    ] + [
        pltpu.make_async_copy(parts.at[target[index]], chunks[index - 1], chunk_sems.at[index])
        for index in range(1, 8)
    ]
    for copy in sent:
        copy.start()

    def put(unit, cols, value):
        low = value.astype(jnp.bfloat16)
        for half in range(2):
            for block in range(2):
                at = (2 * half + block) * ROWS
                tokens[half, block, unit, :, cols] = low[at : at + ROWS]

    def ship(unit):
        if unit < 4:
            routes = (
                (tokens.at[0, 0, unit], keep_own.at[unit]),
                (tokens.at[0, 1, unit], keep_far.at[unit]),
                (tokens.at[1, :, unit], send_norm.at[:, unit]),
            )
        else:
            routes = ((tokens.at[0, :, unit], keep_out), (tokens.at[1, :, unit], send_out))
        for place, (source, goal) in enumerate(routes):
            copy = pltpu.make_async_copy(source, goal, token_sems.at[place, unit])
            copy.start()
            sent.append(copy)

    for stream in range(3):
        put(stream, slice(0, WIDTH), back_product(grad_lin[stream], lin_all[stream]))
        ship(stream)

    def feed(block, carry):
        cols = pl.ds(pl.multiple_of(block * 256, 256), 256)
        rows_up = jnp.concatenate([up_all[part, cols] for part in range(4)], axis=1)
        put(3, cols, back_product(grad_pre[...], rows_up))
        right = [down_all[index, block] for index in range(8)] + [out_rows[:, cols]]
        put(4, cols, matmul(lhs_all[...], jnp.concatenate(right)))
        return carry

    lax.fori_loop(0, 4, feed, 0)
    ship(3)
    ship(4)
    for copy in sent:
        copy.wait()


def back_kernel(
    stack,
    cotangent,
    scaled,
    stats,
    keep,
    came,
    across,
    mix_gain,
    mix_up,
    mix_down,
    norm_gain,
    stack_grad,
    small_own,
    small_other,
    coefficients,
    grads,
    sums,
    coef_grad,
    small,
):
    seqs = stack.shape[0]
    sums[...] = jnp.zeros_like(sums)
    lane = lanes_of((16, 128))

    def unit(step, carry):
        row = pl.multiple_of(step * 16, 16)
        span = pl.ds(row, 16)

        def result(index):
            return wide(keep[index, span]) + wide(came[0, index, span]) + wide(across[index, span])

        for stream in range(4):
            item = result(stream)
            scale = scaled[stream, span]
            moved = item * scale
            sums[stream] += moved[:8] + moved[8:]
            sums[4 + stream] += item[:8] + item[8:]
            weighted = item * norm_gain[stream : stream + 1]
            mean = jnp.mean(weighted, axis=-1, keepdims=True)
            slant = jnp.mean(weighted * scale, axis=-1, keepdims=True)
            grad = stats[2, span, stream : stream + 1] * (weighted - mean - scale * slant)
            if stream == 3:
                grad = grad + wide(cotangent[span])
            grads[stream, span] = grad
        return carry

    lax.fori_loop(0, seqs * SEQ // 16, unit, 0)
    for seq in range(seqs):

        def coefs(step, carry):
            row = pl.multiple_of(step * 16, 16)
            span = pl.ds(seq * SEQ + row, 16)
            found = jnp.zeros((16, 128), jnp.float32)
            for layer in range(STREAMS_IN):
                value = wide(stack[seq, layer, pl.ds(row, 16), :])
                for stream in range(4):
                    got = jnp.sum(grads[stream, span] * value, axis=-1, keepdims=True)
                    found = jnp.where(lane == stream * STREAMS_IN + layer, got, found)
            coef_grad[span] = found
            return carry

        lax.fori_loop(0, SEQ // 16, coefs, 0)
    grad_coef = coef_grad[:, 0:36]
    hidden_pre = stats[1, :, 0:36]
    hidden_low = gelu_value(hidden_pre).astype(jnp.bfloat16)
    for seq in range(seqs):
        turned = stats[0, seq * SEQ : seq * SEQ + SEQ, :].T
        for stream in range(4):
            for layer in range(STREAMS_IN):
                at = stream * STREAMS_IN + layer
                coefficients[seq, layer, stream : stream + 1] = turned[at : at + 1]
    small[...] = jnp.zeros_like(small)
    small[0:36, WIDTH : WIDTH + 36] = lax.dot_general(
        wide(hidden_low),
        grad_coef,
        (((0,), (0,)), ((), ())),
        precision=HIGHEST,
        preferred_element_type=jnp.float32,
    )
    small[36:37, WIDTH : WIDTH + 36] = jnp.sum(grad_coef, axis=0, keepdims=True)
    grad_hidden = (
        lax.dot_general(
            grad_coef,
            mix_down[...],
            (((1,), (1,)), ((), ())),
            precision=HIGHEST,
            preferred_element_type=jnp.float32,
        )
        * gelu_slope(hidden_pre)
    ).astype(jnp.bfloat16)
    gain_row = jnp.zeros((8, WIDTH), jnp.float32)
    up_part = jnp.zeros((36, WIDTH), jnp.float32)
    for seq in range(seqs):
        at = slice(seq * SEQ, seq * SEQ + SEQ)
        last = wide(stack[seq, STREAMS_IN - 1])
        rms = stats[2, at, 4:5]
        mixed_in = (last * rms * mix_gain[...]).astype(jnp.bfloat16)
        up_part = up_part + outer_sum(grad_hidden[at], mixed_in)
        grad_mixed = matmul(grad_hidden[at], mix_up[...])
        along = grad_mixed * last * rms
        for place in range(SEQ // 8):
            gain_row = gain_row + along[place * 8 : place * 8 + 8]
        weighted = grad_mixed * mix_gain[...]
        mean = jnp.mean(weighted * last, axis=-1, keepdims=True)
        grads[4, at] = rms * (weighted - last * (rms * rms * mean))

        def layers(step, carry):
            row = pl.multiple_of(step // 2 * 16, 16)
            cols = pl.ds(pl.multiple_of(step % 2 * 512, 512), 512)
            span = pl.ds(seq * SEQ + row, 16)
            rows_coef = stats[0, span, :]
            parts = [grads[stream, span, cols] for stream in range(4)]
            for layer in range(STREAMS_IN):
                total = None
                for stream in range(4):
                    at_coef = stream * STREAMS_IN + layer
                    term = rows_coef[:, at_coef : at_coef + 1] * parts[stream]
                    total = term if total is None else total + term
                if layer == STREAMS_IN - 1:
                    total = total + grads[4, span, cols]
                stack_grad[seq, layer, pl.ds(row, 16), cols] = total.astype(jnp.bfloat16)
            return carry

        lax.fori_loop(0, 8, layers, 0)
    small[0:36, 0:WIDTH] = up_part
    for place in range(8):
        small[36 + place : 37 + place, 0:WIDTH] = jnp.sum(sums[place], axis=0, keepdims=True)
    small[44:45, 0:WIDTH] = jnp.sum(gain_row, axis=0, keepdims=True)
    _, _, _, core = position()
    small_own[...] = small[pl.ds(pl.multiple_of(core * 24, 8), 24), :]
    small_other[...] = small[pl.ds(pl.multiple_of(24 - core * 24, 8), 24), :]


def place_kernel(
    shard0,
    shard1,
    shard2,
    shard3,
    small_own,
    small_other,
    projection,
    out_grad,
    up_grad,
    down_grad,
    mix_gain_grad,
    mix_up_grad,
    mix_down_grad,
    mix_static_grad,
    gain_grad,
    bias_grad,
    small,
):
    z, member_parity, x, core = position()
    small[pl.ds(pl.multiple_of(core * 24, 8), 24), :] = small_own[...]
    small[pl.ds(pl.multiple_of(24 - core * 24, 8), 24), :] = small_other[...]
    lanes = pl.ds(pl.multiple_of((2 * z + member_parity) * 128, 128), 128)
    mix_up_grad[...] = small[0:36, lanes]
    gain_grad[...] = small[36:40, 0:WIDTH]
    bias_grad[...] = small[40:44, 0:WIDTH]
    mix_gain_grad[...] = small[44:45, 0:WIDTH]
    mix_down_grad[...] = small[0:36, WIDTH : WIDTH + 36]
    for stream in range(4):
        at = WIDTH + stream * STREAMS_IN
        mix_static_grad[stream : stream + 1] = small[36:37, at : at + STREAMS_IN]
    shards = (shard0, shard1, shard2, shard3)
    lane = lanes_of((128, 128))
    for back in range(4):
        from_x = x if back % 2 == 0 else 1 - x
        from_core = core if back < 2 else 1 - core
        quarter = 2 * from_x + from_core
        own, twin = shards[back], shards[back ^ 2]
        for index in range(8):
            half = index % 2
            mine = wide(own[index // 2, :, half * 128 : half * 128 + 128])
            half_b = 1 - half
            lent = wide(twin[index // 2, :, half_b * 128 : half_b * 128 + 128])
            col = pl.multiple_of((index * 4 + quarter) * 128, 128)
            up_grad[:, pl.ds(col, 128)] = jnp.where(
                (lane >= 96) & (from_core == half), lent, mine
            )
        row = pl.multiple_of(quarter * 128, 128)
        for block in range(4):
            cols = slice(block * 256, block * 256 + 256)
            down_grad[pl.ds(row, 96), cols] = wide(own[7 + block, 0:96])

            @pl.when(member_parity == from_core)
            def _():
                head_row = pl.multiple_of(from_x * 64, 64)
                out_grad[pl.ds(head_row, 32), cols] = wide(own[7 + block, 96:128])
                out_grad[pl.ds(head_row + 32, 32), cols] = wide(
                    own[11, block * 32 : block * 32 + 32]
                )
                down_grad[pl.ds(row + 96, 32), cols] = wide(
                    twin[11, block * 32 : block * 32 + 32]
                )

            @pl.when(member_parity != from_core)
            def _():
                down_grad[pl.ds(row + 96, 32), cols] = wide(own[7 + block, 96:128])

    for back in (0, 2):
        from_core = core if back < 2 else 1 - core
        for stream in range(3):
            for twin in range(2):
                tile = slice(twin * 128, twin * 128 + 128)
                mine = wide(shards[back][4 + stream, :, tile])
                across = wide(shards[back + 1][4 + stream, :, tile])
                even = jnp.where(x == 0, mine, across)
                odd = jnp.where(x == 0, across, mine)
                first = jnp.where(lane < 64, even, pltpu.roll(odd, 64, 1))
                second = jnp.where(lane < 64, pltpu.roll(even, 64, 1), odd)
                for low, value in ((0, first), (1, second)):
                    col = pl.multiple_of((2 * twin + low) * 256 + from_core * 128, 128)
                    projection[stream, :, pl.ds(col, 128)] = value


def call(kernel, outs, specs, out_specs, args, scratch=(), cost=None, vmem=60 << 20):
    return pl.pallas_call(
        kernel,
        out_shape=outs,
        in_specs=specs,
        out_specs=out_specs,
        scratch_shapes=list(scratch),
        compiler_params=pltpu.CompilerParams(vmem_limit_bytes=vmem),
        cost_estimate=cost,
    )(*args)


def shape_of(shape, dtype=jnp.bfloat16):
    return jax.ShapeDtypeStruct(shape, dtype)


def rope_tables():
    half_rot = ROTARY // 2
    step = 10000.0 ** (-2.0 * np.arange(half_rot) / ROTARY)
    angles = np.arange(SEQ)[:, None] * step[None, :]
    cos_table = np.ones((SEQ, HEAD_DIM))
    left = np.zeros((SEQ, HEAD_DIM))
    right = np.zeros((SEQ, HEAD_DIM))
    cos_table[:, :half_rot] = np.cos(angles)
    cos_table[:, half_rot:ROTARY] = np.cos(angles)
    left[:, :half_rot] = -np.sin(angles)
    right[:, half_rot:ROTARY] = np.sin(angles)
    return np.stack([np.tile(item, (2, 2)) for item in (cos_table, left, right)]).astype(np.float32)


def on_device_tensor(
    layer_stack,
    out_cotangent,
    pic_start,
    doc_split,
    mix_gain,
    mix_up,
    mix_down,
    mix_static,
    norm_gain,
    norm_bias,
    query_key_value,
    out_weight,
    up_weight,
    down_weight,
):
    z, y, _, _ = position()
    micro_total, local_seqs, _, _, width = layer_stack.shape
    seqs = micro_total * local_seqs
    stack = jnp.transpose(layer_stack, (0, 1, 3, 2, 4)).reshape(seqs, STREAMS_IN, SEQ, width)
    cotangent = out_cotangent.reshape(ROWS, width)
    gain_row = mix_gain.reshape(1, width)

    piece = call(
        prepare_kernel,
        shape_of((12, 128, 256)),
        [VMEM_FULL] * 4,
        VMEM_FULL,
        (query_key_value, out_weight, up_weight, down_weight),
        vmem=60 << 20,
    )
    up_own = mix_up.T
    up_pair = jnp.concatenate([up_own, after(lax.ppermute(up_own, "fsdp", Y_SWAP), piece)], axis=1)
    up_one = fsdp_move(
        up_pair,
        [((index + 8 + index % 2 * 16) % 32, index) for index in range(32)],
    )
    up_two = fsdp_move(up_pair, Z_SWAP_FAR)
    ups = (up_pair, up_one, up_two)
    piece = after(piece, *ups)
    up_three = lax.ppermute(up_one, "replica", CORE_SWAP)
    ups += (up_three,)
    bounds = jnp.concatenate([pic_start.reshape(seqs), doc_split.reshape(seqs)])
    kept = {}
    grad_across = lax.ppermute(cotangent, "replica", X_SWAP)
    grad_packets = (
        cotangent,
        grad_across,
        lax.ppermute(cotangent, "replica", CORE_SWAP),
        lax.ppermute(grad_across, "replica", CORE_SWAP),
    )

    def front():
        packet, *kept["rest"] = call(
            front_kernel,
            (
                shape_of((4 * ROWS + 16, width)),
                shape_of((4, ROWS, width), jnp.float32),
                shape_of((3, ROWS, 128), jnp.float32),
                shape_of((ROWS, width), jnp.float32),
                shape_of((36, width)),
            ),
            [SMEM_FULL] + [VMEM_FULL] * 10,
            (VMEM_FULL,) * 5,
            (
                bounds,
                stack,
                gain_row,
                *ups,
                mix_down,
                mix_static.reshape(1, 36),
                norm_gain,
                norm_bias,
            ),
            scratch=[pltpu.VMEM((4, ROWS, width), jnp.float32)],
            vmem=36 << 20,
        )
        across = lax.ppermute(packet, "replica", X_SWAP)
        beside = lax.ppermute(packet, "replica", CORE_SWAP)
        beside_across = lax.ppermute(across, "replica", CORE_SWAP)
        kept["packets"] = (packet, across, beside, beside_across)
        return (packet, grad_across), (across,)

    pieces = gather_fsdp(piece, z, front)
    packets = kept["packets"]
    scaled, stats, stream_last, mix_up_full = kept["rest"]

    results = call(
        main_kernel,
        (shape_of((PART, 128, 256)), shape_of((12 - PART, 128, 256)))
        + (shape_of((12, 128, 256)),) * 7
        + (shape_of((4, ROWS, width)),) * 2
        + (shape_of((2, 4, ROWS, width)),)
        + (shape_of((2, ROWS, width)),) * 2,
        [VMEM_FULL] + [IN_PLACE] * 19,
        (IN_PLACE,) * 14,
        (jnp.asarray(rope_tables()),) + packets + grad_packets + tuple(pieces),
        scratch=[
            pltpu.VMEM((5, 4 * ROWS, width), jnp.bfloat16),
            pltpu.VMEM((4, 16, width), jnp.bfloat16),
            pltpu.VMEM((4, width, 256), jnp.bfloat16),
            pltpu.VMEM((3, width, 256), jnp.bfloat16),
            pltpu.VMEM((8, 5, 128, 256), jnp.bfloat16),
            pltpu.VMEM((256, width), jnp.bfloat16),
            pltpu.VMEM((4 * ROWS, width + 256), jnp.bfloat16),
            pltpu.VMEM((4 * ROWS, width), jnp.bfloat16),
            pltpu.VMEM((3, 4 * ROWS, 256), jnp.float32),
            pltpu.VMEM((4 * ROWS, 256), jnp.bfloat16),
            pltpu.VMEM((3, 4 * ROWS, 256), jnp.bfloat16),
            pltpu.VMEM((8, 12, 128, 256), jnp.bfloat16),
            pltpu.VMEM((2, 2, 5, ROWS, width), jnp.bfloat16),
            pltpu.SemaphoreType.DMA((4, 6)),
            pltpu.SemaphoreType.DMA((8, 3)),
            pltpu.SemaphoreType.DMA((9,)),
            pltpu.SemaphoreType.DMA((3, 5)),
        ],
        vmem=38 << 20,
    )
    chunks = results[:9]
    keep_own, keep_far, send_norm, keep_out, send_out = results[9:]

    came = lax.ppermute(send_norm, "replica", CORE_SWAP)
    sum_across = (wide(keep_far) + wide(came[1])).astype(jnp.bfloat16)
    came_across = lax.ppermute(sum_across, "replica", X_SWAP)
    out_came = lax.ppermute(after(send_out, sum_across), "replica", CORE_SWAP)
    out_across = (wide(keep_out[1]) + wide(out_came[1])).astype(jnp.bfloat16)
    out_across = lax.ppermute(after(out_across, came_across), "replica", X_SWAP)
    layer_output = (
        stream_last + wide(keep_out[0]) + wide(out_came[0]) + wide(out_across)
    ).astype(jnp.bfloat16)

    first_half = pl.BlockSpec((1, 4, ROWS, width), lambda step: (0, 0, 0, 0))

    def whole(shape):
        return pl.BlockSpec(shape, lambda step: (0,) * len(shape))

    def back():
        kept["back"] = pl.pallas_call(
            back_kernel,
            grid=(1,),
            out_shape=(
                shape_of((seqs, STREAMS_IN, SEQ, width)),
                shape_of((24, width + 128), jnp.float32),
                shape_of((24, width + 128), jnp.float32),
                shape_of((seqs, STREAMS_IN, 4, SEQ), jnp.float32),
            ),
            in_specs=[
                whole((seqs, STREAMS_IN, SEQ, width)),
                whole((ROWS, width)),
                whole((4, ROWS, width)),
                whole((3, ROWS, 128)),
                whole((4, ROWS, width)),
                first_half,
                whole((4, ROWS, width)),
                whole((1, width)),
                whole((36, width)),
                whole((36, 36)),
                whole((4, width)),
            ],
            out_specs=(
                whole((seqs, STREAMS_IN, SEQ, width)),
                whole((24, width + 128)),
                whole((24, width + 128)),
                whole((seqs, STREAMS_IN, 4, SEQ)),
            ),
            scratch_shapes=[
                pltpu.VMEM((5, ROWS, width), jnp.float32),
                pltpu.VMEM((8, 8, width), jnp.float32),
                pltpu.VMEM((ROWS, 128), jnp.float32),
                pltpu.VMEM((48, width + 128), jnp.float32),
            ],
            compiler_params=pltpu.CompilerParams(vmem_limit_bytes=56 << 20),
        )(
            stack,
            cotangent,
            scaled,
            stats,
            keep_own,
            came,
            came_across,
            gain_row,
            mix_up_full,
            mix_down,
            norm_gain,
        )
        return kept["back"][1]

    shard = scatter_fsdp(chunks, z, sum_across, back)
    stack_grad, small, small_other, coefficients = kept["back"]

    small = small + lax.ppermute(small_other, "replica", CORE_SWAP)
    small = small + lax.ppermute(small, "replica", X_SWAP)
    small = small + lax.ppermute(small, "fsdp", Y_SWAP)
    shard = after(shard, small, out_across)
    shard_across = lax.ppermute(shard, "replica", X_SWAP)
    shard_beside = lax.ppermute(shard, "replica", CORE_SWAP)
    for perm in (Z_SWAP_NEAR, Z_SWAP_FAR):
        small = small + lax.ppermute(small, "fsdp", perm)
    small_beside = lax.ppermute(small, "replica", CORE_SWAP)
    shard_both = lax.ppermute(after(shard_across, small), "replica", CORE_SWAP)
    owned = call(
        place_kernel,
        (
            shape_of((3, 128, width), jnp.float32),
            shape_of((128, width), jnp.float32),
            shape_of((128, 4 * width), jnp.float32),
            shape_of((512, width), jnp.float32),
            shape_of((1, width), jnp.float32),
            shape_of((36, 128), jnp.float32),
            shape_of((36, 36), jnp.float32),
            shape_of((4, STREAMS_IN), jnp.float32),
            shape_of((4, width), jnp.float32),
            shape_of((4, width), jnp.float32),
        ),
        [VMEM_FULL] * 6,
        (VMEM_FULL,) * 10,
        (shard, shard_across, shard_beside, shard_both, small, small_beside),
        scratch=[pltpu.VMEM((48, width + 128), jnp.float32)],
        vmem=14 << 20,
    )
    projection_grad, out_grad, up_grad, down_grad, *small_grads = owned
    shape = (micro_total, local_seqs, SEQ)
    stack_grad = stack_grad.reshape(micro_total, local_seqs, STREAMS_IN, SEQ, width)
    coefficients = coefficients.reshape(micro_total, local_seqs, STREAMS_IN, 4, SEQ)
    return (
        layer_output.reshape(shape + (width,)),
        jnp.transpose(coefficients, (0, 1, 4, 3, 2)),
        jnp.transpose(stack_grad, (0, 1, 3, 2, 4)),
        small_grads[0].reshape(width),
        small_grads[1].T,
        small_grads[2],
        small_grads[3],
        small_grads[4],
        small_grads[5],
        projection_grad,
        out_grad,
        up_grad,
        down_grad,
    )


def solution(mesh):
    fits = mesh.shape["fsdp"] == 8 and mesh.shape["replica"] == 4
    body = on_device_tensor if fits else on_device
    return jax.shard_map(
        body,
        mesh=mesh,
        in_specs=(
            P(None, ("fsdp", "replica"), None, None, None),
            P(None, ("fsdp", "replica"), None, None),
            P(None, ("fsdp", "replica")),
            P(None, ("fsdp", "replica")),
            P(),
            P("fsdp", None),
            P(),
            P(),
            P(),
            P(),
            P(None, "fsdp", None),
            P("fsdp", None),
            P("fsdp", None),
            P("fsdp", None),
        ),
        out_specs=(
            P(None, ("fsdp", "replica"), None, None),
            P(None, ("fsdp", "replica"), None, None, None),
            P(None, ("fsdp", "replica"), None, None, None),
            P(),
            P("fsdp", None),
            P(),
            P(),
            P(),
            P(),
            P(None, "fsdp", None),
            P("fsdp", None),
            P("fsdp", None),
            P("fsdp", None),
        ),
        check_vma=False,
    )
```

```python
import math

import jax
import jax.numpy as jnp
import numpy as np
from jax import lax
from jax.experimental import pallas as pl
from jax.experimental.pallas import tpu as pltpu
from jax.sharding import PartitionSpec as P

HEADS = 16
HEAD_DIM = 64
ROTARY = 16
STREAMS_IN = 9
SEQ = 64
PIC = 32


EPSILON = 1e-05
ROOT_HALF = 0.7071067811865476
NORMAL_PEAK = 0.3989422804014327
HIGHEST = lax.Precision.HIGHEST


def as_sent(value):

    def short(part):
        return part.astype(jnp.bfloat16) if part.dtype == jnp.float32 else part

    return jax.tree.map(short, value)


def gelu_value(values):
    return 0.5 * values * (1.0 + lax.erf(values * ROOT_HALF))


def gelu_slope(values):
    return 0.5 * (1.0 + lax.erf(values * ROOT_HALF)) + values * NORMAL_PEAK * jnp.exp(
        -0.5 * values * values
    )


def matmul(left_side, right_side):
    return jnp.dot(left_side, right_side, preferred_element_type=jnp.float32)


def outer_sum(left_side, right_side):
    return lax.dot_general(
        left_side, right_side, (((0,), (0,)), ((), ())), preferred_element_type=jnp.float32
    )


def back_product(left_side, right_side):
    return lax.dot_general(
        left_side, right_side, (((1,), (1,)), ((), ())), preferred_element_type=jnp.float32
    )


def rotary_tables():
    half_rot = ROTARY // 2
    inverse = jnp.exp(-math.log(10000.0) * (2.0 * jnp.arange(half_rot, dtype=jnp.float32) / ROTARY))
    angles = jnp.arange(SEQ, dtype=jnp.float32)[:, None] * inverse[None, :]
    return (jnp.cos(angles)[:, None, :], jnp.sin(angles)[:, None, :])


def rotate(values, cos_table, sin_table):
    half_rot = ROTARY // 2
    first_half = values[..., :half_rot]
    second = values[..., half_rot:ROTARY]
    return jnp.concatenate(
        [
            first_half * cos_table - second * sin_table,
            second * cos_table + first_half * sin_table,
            values[..., ROTARY:],
        ],
        axis=-1,
    )


def allowed_mask(starts, splits):
    positions = jnp.arange(SEQ, dtype=jnp.int32)
    second_doc = positions[None, :] >= splits[:, None]
    picture = (positions[None, :] >= starts[:, None]) & (positions[None, :] < starts[:, None] + PIC)
    same_doc = second_doc[:, :, None] == second_doc[:, None, :]
    causal = positions[:, None] >= positions[None, :]
    both_pic = picture[:, :, None] & picture[:, None, :]
    return same_doc & (causal[None] | both_pic)


def masked_scores(queries, key_rot, allowed):
    scores = jnp.einsum(
        "nqhe,nkhe->nhqk", queries, key_rot, preferred_element_type=jnp.float32
    ) * HEAD_DIM ** (-0.5)
    return jnp.where(allowed[:, None], scores, -1e30)


def on_device(
    layer_stack,
    out_cotangent,
    pic_start,
    doc_split,
    mix_gain,
    mix_up,
    mix_down,
    mix_static,
    norm_gain,
    norm_bias,
    query_key_value,
    out_weight,
    up_weight,
    down_weight,
):
    micro_total = layer_stack.shape[0]
    local_seqs = layer_stack.shape[1]
    model_width = layer_stack.shape[-1]
    groups = [(0, micro_total)]
    cos_table, sin_table = rotary_tables()
    output_list = []
    coef_list = []
    grad_list = []
    shard_total = None
    small_total = None
    for first_micro, micro_count in groups:
        seq_count = micro_count * local_seqs
        row_count = seq_count * SEQ
        head_shape = (seq_count, SEQ, HEADS, HEAD_DIM)
        flat_stack = layer_stack[first_micro : first_micro + micro_count].reshape(
            row_count, STREAMS_IN, model_width
        )
        grad_rows = out_cotangent[first_micro : first_micro + micro_count].reshape(
            row_count, model_width
        )
        starts = pic_start[first_micro : first_micro + micro_count].reshape(seq_count)
        splits = doc_split[first_micro : first_micro + micro_count].reshape(seq_count)
        allowed = allowed_mask(starts, splits)
        mix_up_full, projection_full, out_full = (
            lax.all_gather(mix_up, "fsdp", axis=0, tiled=True),
            lax.all_gather(query_key_value, "fsdp", axis=1, tiled=True),
            lax.all_gather(out_weight, "fsdp", axis=0, tiled=True),
        )
        up_full, down_full = (
            lax.all_gather(up_weight, "fsdp", axis=0, tiled=True),
            lax.all_gather(down_weight, "fsdp", axis=0, tiled=True),
        )
        last_layer = flat_stack[:, STREAMS_IN - 1, :].astype(jnp.float32)
        rms_scale = lax.rsqrt(jnp.mean(last_layer * last_layer, axis=-1, keepdims=True) + EPSILON)
        mixed_in = (last_layer * rms_scale * mix_gain).astype(jnp.bfloat16)
        hidden_pre = matmul(mixed_in, mix_up_full)
        hidden_mix = gelu_value(hidden_pre).astype(jnp.bfloat16)
        hidden_wide = hidden_mix.astype(jnp.float32)
        coef_flat = jnp.dot(hidden_wide, mix_down, precision=HIGHEST) + mix_static.reshape(-1)
        coef_rows = coef_flat.reshape(row_count, 4, STREAMS_IN)
        streams = coef_rows[:, :, 0, None] * flat_stack[:, None, 0, :].astype(jnp.float32)
        for layer_index in range(1, STREAMS_IN):
            streams = streams + coef_rows[:, :, layer_index, None] * flat_stack[
                :, None, layer_index, :
            ].astype(jnp.float32)
        center = streams - jnp.mean(streams, axis=-1, keepdims=True)
        inv_std = lax.rsqrt(jnp.mean(center * center, axis=-1, keepdims=True) + EPSILON)
        scaled = center * inv_std
        normed = (scaled * norm_gain + norm_bias).astype(jnp.bfloat16)
        query_lin = matmul(normed[:, 0], projection_full[0])
        key_lin = matmul(normed[:, 1], projection_full[1])
        value_lin = matmul(normed[:, 2], projection_full[2])
        queries = rotate(query_lin.reshape(head_shape), cos_table, sin_table).astype(jnp.bfloat16)
        key_rot = rotate(key_lin.reshape(head_shape), cos_table, sin_table).astype(jnp.bfloat16)
        values = value_lin.astype(jnp.bfloat16).reshape(head_shape)
        scores = masked_scores(queries, key_rot, allowed)
        row_top = jnp.max(scores, axis=-1, keepdims=True)
        exponent = jnp.exp(scores - row_top)
        row_total = jnp.sum(exponent, axis=-1, keepdims=True)
        soft_probs = exponent / row_total
        log_total = row_top + jnp.log(row_total)
        attended = (
            jnp.einsum(
                "nhqk,nkhe->nqhe",
                soft_probs.astype(jnp.bfloat16),
                values,
                preferred_element_type=jnp.float32,
            )
            .astype(jnp.bfloat16)
            .reshape(row_count, model_width)
        )
        attn_out = matmul(attended, out_full)
        up_pre = matmul(normed[:, 3], up_full)
        gated_act = gelu_value(up_pre).astype(jnp.bfloat16)
        feed_out = matmul(gated_act, down_full)
        output_list.append((streams[:, 3] + attn_out + feed_out).astype(jnp.bfloat16))
        coef_list.append(coef_rows)
        mix_up_back, projection_back, out_back = (
            lax.all_gather(mix_up, "fsdp", axis=0, tiled=True),
            lax.all_gather(query_key_value, "fsdp", axis=1, tiled=True),
            lax.all_gather(out_weight, "fsdp", axis=0, tiled=True),
        )
        up_back, down_back = (
            lax.all_gather(up_weight, "fsdp", axis=0, tiled=True),
            lax.all_gather(down_weight, "fsdp", axis=0, tiled=True),
        )
        grad_down = outer_sum(gated_act, grad_rows)
        grad_gated = back_product(grad_rows, down_back)
        grad_up_pre = (grad_gated * gelu_slope(up_pre)).astype(jnp.bfloat16)
        grad_up = outer_sum(normed[:, 3], grad_up_pre)
        grad_norm_feed = back_product(grad_up_pre, up_back)
        feed_shards = (
            lax.psum_scatter(
                grad_up.astype(jnp.bfloat16), "fsdp", scatter_dimension=0, tiled=True
            ).astype(jnp.float32),
            lax.psum_scatter(
                grad_down.astype(jnp.bfloat16), "fsdp", scatter_dimension=0, tiled=True
            ).astype(jnp.float32),
        )
        grad_out_weight = outer_sum(attended, grad_rows)
        grad_attended = back_product(grad_rows, out_back).astype(jnp.bfloat16).reshape(head_shape)
        scores_again = masked_scores(queries, key_rot, allowed)
        probs_again = jnp.exp(scores_again - log_total)
        grad_probs = jnp.einsum(
            "nqhe,nkhe->nhqk", grad_attended, values, preferred_element_type=jnp.float32
        )
        grad_value = (
            jnp.einsum(
                "nhqk,nqhe->nkhe",
                probs_again.astype(jnp.bfloat16),
                grad_attended,
                preferred_element_type=jnp.float32,
            )
            .astype(jnp.bfloat16)
            .reshape(row_count, model_width)
        )
        delta_rows = jnp.sum(probs_again * grad_probs, axis=-1, keepdims=True)
        grad_scores = (probs_again * (grad_probs - delta_rows)).astype(jnp.bfloat16)
        score_scale = HEAD_DIM ** (-0.5)
        grad_query_rot = (
            jnp.einsum("nhqk,nkhe->nqhe", grad_scores, key_rot, preferred_element_type=jnp.float32)
            * score_scale
        )
        grad_key_rot = (
            jnp.einsum("nhqk,nqhe->nkhe", grad_scores, queries, preferred_element_type=jnp.float32)
            * score_scale
        )
        grad_query = (
            rotate(grad_query_rot, cos_table, -sin_table)
            .astype(jnp.bfloat16)
            .reshape(row_count, model_width)
        )
        grad_key = (
            rotate(grad_key_rot, cos_table, -sin_table)
            .astype(jnp.bfloat16)
            .reshape(row_count, model_width)
        )
        grad_linear = (grad_query, grad_key, grad_value)
        grad_projection = jnp.stack(
            [outer_sum(normed[:, stream], grad_linear[stream]) for stream in range(3)]
        )
        grad_normed = jnp.stack(
            [back_product(grad_linear[stream], projection_back[stream]) for stream in range(3)]
            + [grad_norm_feed],
            axis=1,
        )
        gain_grad = jnp.sum(grad_normed * scaled, axis=0)
        bias_grad = jnp.sum(grad_normed, axis=0)
        grad_scaled = grad_normed * norm_gain
        grad_streams = inv_std * (
            grad_scaled
            - jnp.mean(grad_scaled, axis=-1, keepdims=True)
            - scaled * jnp.mean(grad_scaled * scaled, axis=-1, keepdims=True)
        )
        grad_streams = grad_streams + jnp.concatenate(
            [
                jnp.zeros((row_count, 3, model_width), jnp.float32),
                grad_rows[:, None, :].astype(jnp.float32),
            ],
            axis=1,
        )
        grad_coef = jnp.stack(
            [
                jnp.sum(
                    grad_streams * flat_stack[:, None, layer_index, :].astype(jnp.float32), axis=-1
                )
                for layer_index in range(STREAMS_IN)
            ],
            axis=-1,
        )
        grad_coef_flat = grad_coef.reshape(row_count, 4 * STREAMS_IN)
        static_grad = jnp.sum(grad_coef_flat, axis=0).reshape(4, STREAMS_IN)
        down_mix_grad = jnp.dot(hidden_wide.T, grad_coef_flat, precision=HIGHEST)
        grad_hidden = (
            jnp.dot(grad_coef_flat, mix_down.T, precision=HIGHEST) * gelu_slope(hidden_pre)
        ).astype(jnp.bfloat16)
        grad_mix_up = outer_sum(mixed_in, grad_hidden)
        grad_mixed = back_product(grad_hidden, mix_up_back)
        gain_mix_grad = jnp.sum(grad_mixed * last_layer * rms_scale, axis=0)
        weighted = grad_mixed * mix_gain
        grad_last = rms_scale * (
            weighted
            - last_layer
            * rms_scale
            * rms_scale
            * jnp.mean(weighted * last_layer, axis=-1, keepdims=True)
        )
        per_layer = [
            jnp.sum(coef_rows[:, :, layer_index, None] * grad_streams, axis=1)
            for layer_index in range(STREAMS_IN)
        ]
        per_layer[STREAMS_IN - 1] = per_layer[STREAMS_IN - 1] + grad_last
        grad_list.append(jnp.stack(per_layer, axis=1).astype(jnp.bfloat16))
        attention_shards = (
            lax.psum_scatter(
                grad_mix_up.astype(jnp.bfloat16), "fsdp", scatter_dimension=0, tiled=True
            ).astype(jnp.float32),
            lax.psum_scatter(
                grad_projection.astype(jnp.bfloat16), "fsdp", scatter_dimension=1, tiled=True
            ).astype(jnp.float32),
            lax.psum_scatter(
                grad_out_weight.astype(jnp.bfloat16), "fsdp", scatter_dimension=0, tiled=True
            ).astype(jnp.float32),
        )
        shards = attention_shards + feed_shards
        shards = jax.tree.map(
            lambda part: part.astype(jnp.float32), lax.psum(as_sent(shards), "replica")
        )
        smalls = (gain_mix_grad, down_mix_grad, static_grad, gain_grad, bias_grad)
        if shard_total is None:
            shard_total = shards
            small_total = smalls
        else:
            shard_total = tuple(
                (total_item + new_item for total_item, new_item in zip(shard_total, shards))
            )
            small_total = tuple(
                (total_item + new_item for total_item, new_item in zip(small_total, smalls))
            )
    small_total = lax.psum(small_total, ("fsdp", "replica"))
    layer_output = jnp.concatenate(output_list, axis=0).reshape(
        micro_total, local_seqs, SEQ, model_width
    )
    coefficients = jnp.concatenate(coef_list, axis=0).reshape(
        micro_total, local_seqs, SEQ, 4, STREAMS_IN
    )
    stack_grad = jnp.concatenate(grad_list, axis=0).reshape(
        micro_total, local_seqs, SEQ, STREAMS_IN, model_width
    )
    return (
        layer_output,
        coefficients,
        stack_grad,
        small_total[0],
        shard_total[0],
        small_total[1],
        small_total[2],
        small_total[3],
        small_total[4],
        shard_total[1],
        shard_total[2],
        shard_total[3],
        shard_total[4],
    )


ROWS = 128
WIDTH = 1024
VMEM_FULL = pl.BlockSpec(memory_space=pltpu.VMEM)
SMEM_FULL = pl.BlockSpec(memory_space=pltpu.SMEM)
IN_PLACE = pl.BlockSpec(memory_space=pl.ANY)


def bits_swap(size, bit):
    return [(index, index ^ bit) for index in range(size)]


CORE_SWAP = bits_swap(4, 1)
X_SWAP = bits_swap(4, 2)
Y_SWAP = bits_swap(8, 1)
Z_SWAP_NEAR = bits_swap(8, 2)
Z_SWAP_FAR = bits_swap(8, 4)


def z_pairs(moves):
    return [(2 * src + col, 2 * dst + col) for src, dst in moves for col in range(2)]


def pick(cond, first, second):
    return jnp.where(cond, first, second)


def order_two(flag, own, other, axis):
    first = pick(flag == 0, own, other)
    second = pick(flag == 0, other, own)
    return jnp.concatenate([first, second], axis=axis)


def after(value, *others):
    return lax.optimization_barrier((value,) + others)[0]


Z_NEAR = z_pairs([(0, 1), (1, 0), (2, 3), (3, 2)])
Z_MIDDLE = [
    (index, (index ^ 1) if index // 8 in (0, 3) else (24 - index // 8 * 8 + index % 8))
    for index in range(32)
]


MIDDLE_OR_SIDE = [
    (index, (index ^ 4) if index // 8 in (0, 3) else (24 - index // 8 * 8 + index % 8))
    for index in range(32)
]
SIDE_OR_CORE = [
    (index, (index ^ 1) if index // 8 in (0, 3) else (index ^ 4)) for index in range(32)
]


def fsdp_move(value, pairs):
    return lax.ppermute(value, "fsdp" if len(pairs) == 8 else ("fsdp", "replica"), pairs)


PART = 7


def gather_fsdp(piece, z, front):
    inner = (z == 1) | (z == 2)
    near = fsdp_move(piece, Z_NEAR)
    middle = fsdp_move(piece, MIDDLE_OR_SIDE)
    side = fsdp_move(piece, SIDE_OR_CORE)
    early, late = front()
    middle_near = fsdp_move(after(near, *early, side), Z_MIDDLE)
    turned = fsdp_move(after(middle, *early), Z_NEAR)
    side_two = fsdp_move(pick(inner, middle, near), Y_SWAP)
    third = pick(inner, middle_near, turned)
    near_twice = fsdp_move(after(middle_near, side_two, third), Z_NEAR)
    side_three = fsdp_move(third, Y_SWAP)
    over_z = fsdp_move(side_three[:PART], Z_NEAR)
    over_y = fsdp_move(after(near_twice[PART:], side_three, *late), Y_SWAP)
    return [
        piece,
        side,
        near,
        middle,
        middle_near,
        turned,
        near_twice,
        side_two,
        side_three,
        over_z,
        over_y,
    ]


def position():
    member, partner = lax.axis_index("fsdp"), lax.axis_index("replica")
    return member // 2, member % 2, partner // 2, partner % 2


def table(values, z):
    found = jnp.int32(values[0])
    for index in range(1, 4):
        found = jnp.where(z == index, jnp.int32(values[index]), found)
    return found


def gather_order(z, y):
    places = []
    for z_from in (z, table([1, 0, 3, 2], z), table([2, 2, 1, 1], z), table([3, 3, 0, 0], z)):
        places += [2 * z_from + y, 2 * z_from + 1 - y]
    return places


def scatter_order(z, y):
    others = (table([3, 0, 3, 0], z), table([2, 3, 0, 1], z), table([1, 2, 1, 2], z), z)
    own = (table([3, 3, 0, 0], z), table([2, 2, 1, 1], z), table([1, 0, 3, 2], z), z)
    return [2 * z_to + 1 - y for z_to in others] + [2 * z_to + y for z_to in own]


def wide(value):
    return value.astype(jnp.float32)


def scatter_fsdp(chunks, z, first_wait, beside):
    inner = (z == 1) | (z == 2)
    side_low, side_high, side_one, side_two, side_own, last, third, near, own = chunks

    def low(value):
        return value.astype(jnp.bfloat16)

    def only(cond, value):
        return jnp.where(cond, wide(value), 0.0)

    over_z = fsdp_move(side_high, Z_NEAR)
    over_y = fsdp_move(side_low, Y_SWAP)
    over_z = jnp.pad(only(inner, over_z), ((PART, 0), (0, 0), (0, 0)))
    back_one = fsdp_move(low(wide(side_one) + over_z), Y_SWAP)
    over_y = jnp.pad(wide(over_y), ((0, 12 - PART), (0, 0), (0, 0)))
    back_far = fsdp_move(low(wide(after(last, first_wait)) + over_y), Z_NEAR)
    back_two = fsdp_move(after(side_two, first_wait), Y_SWAP)
    to_middle = low(wide(last) + wide(back_one) + wide(back_far))
    to_near = low(
        jnp.where(
            inner,
            wide(jnp.concatenate([side_low, side_high])),
            wide(third) + wide(back_one),
        )
    )
    middle_one = fsdp_move(to_middle, Z_MIDDLE)
    near_one = fsdp_move(to_near, Z_NEAR)
    back_own = fsdp_move(low(wide(side_own) + only(z % 3 == 0, near_one)), Y_SWAP)
    to_near = low(wide(near) + jnp.where(inner, wide(middle_one), wide(back_two)))
    to_middle = low(wide(third) + wide(back_two) + wide(near_one))
    to_near, to_middle, _ = lax.optimization_barrier((to_near, to_middle, beside()))
    near_two = fsdp_move(to_near, Z_NEAR)
    middle_two = fsdp_move(to_middle, Z_MIDDLE)
    return low(wide(own) + wide(back_own) + wide(near_two) + only(inner, middle_two))


def lanes_of(shape):
    return lax.broadcasted_iota(jnp.int32, shape, 1)


def rows_of(shape):
    return lax.broadcasted_iota(jnp.int32, shape, 0)


def prepare_kernel(projection, out_weight, up_weight, down_weight, piece):
    _, member_parity, x, core = position()
    quarter, other = 2 * x + core, 2 * x + 1 - core
    lane = lanes_of((128, 128))
    for index in range(8):
        half = index % 2
        own = up_weight[:, pl.ds(pl.multiple_of((index * 4 + quarter) * 128, 128), 128)]
        extra = up_weight[:, pl.ds(pl.multiple_of(((index ^ 1) * 4 + other) * 128, 128), 128)]
        taken = (lane >= 96) & (core == half)
        piece[index // 2, :, half * 128 : half * 128 + 128] = jnp.where(
            taken, wide(extra), wide(own)
        ).astype(jnp.bfloat16)
    for stream in range(3):
        for twin in range(2):
            tiles = [
                wide(
                    projection[
                        stream,
                        :,
                        pl.ds(pl.multiple_of((2 * twin + low) * 256 + core * 128, 128), 128),
                    ]
                )
                for low in range(2)
            ]
            first = jnp.where(x == 0, tiles[0], pltpu.roll(tiles[0], 64, 1))
            second = jnp.where(x == 0, pltpu.roll(tiles[1], 64, 1), tiles[1])
            piece[4 + stream, :, twin * 128 : twin * 128 + 128] = jnp.where(
                lane < 64, first, second
            ).astype(jnp.bfloat16)
    own_row = pl.multiple_of(quarter * 128, 128)
    other_row = pl.multiple_of(other * 128, 128)
    head_row = pl.multiple_of(x * 64, 64)
    for block in range(4):
        cols = slice(block * 256, block * 256 + 256)
        piece[7 + block, 0:96] = down_weight[pl.ds(own_row, 96), cols]

        @pl.when(member_parity == core)
        def _():
            piece[7 + block, 96:128] = out_weight[pl.ds(head_row, 32), cols]
            piece[11, block * 32 : block * 32 + 32] = out_weight[pl.ds(head_row + 32, 32), cols]

        @pl.when(member_parity != core)
        def _():
            piece[7 + block, 96:128] = down_weight[pl.ds(own_row + 96, 32), cols]
            piece[11, block * 32 : block * 32 + 32] = down_weight[pl.ds(other_row + 96, 32), cols]


def front_kernel(
    bounds,
    stack,
    mix_gain,
    up_own,
    up_one,
    up_two,
    up_three,
    mix_down,
    mix_static,
    norm_gain,
    norm_bias,
    packet,
    scaled_out,
    stats,
    stream_out,
    mix_up,
    streams,
):
    seqs = stack.shape[0]
    z, y, _, core = position()
    for step, part in ((0, up_own), (1 + 2 * core, up_one), (2, up_two), (3 - 2 * core, up_three)):
        z_from = (z + step) % 4
        for half, col in enumerate((y, 1 - y)):
            lanes = pl.ds(pl.multiple_of((2 * z_from + col) * 128, 128), 128)
            mix_up[:, lanes] = part[:, half * 128 : half * 128 + 128]
    for seq in range(seqs):
        last = wide(stack[seq, STREAMS_IN - 1])
        rms = lax.rsqrt(jnp.mean(last * last, axis=-1, keepdims=True) + EPSILON)
        mixed_in = (last * rms * mix_gain[...]).astype(jnp.bfloat16)
        hidden_pre = back_product(mixed_in, mix_up[...])
        hidden = wide(gelu_value(hidden_pre).astype(jnp.bfloat16))
        coef = jnp.dot(
            hidden, mix_down[...], precision=HIGHEST, preferred_element_type=jnp.float32
        )
        coef = coef + mix_static[...]
        at = slice(seq * SEQ, seq * SEQ + SEQ)
        stats[0, at, 0:36] = coef
        stats[1, at, 0:36] = hidden_pre
        stats[2, at, 4:5] = rms

        def mix(step, carry):
            row = pl.multiple_of(step // 2 * 16, 16)
            col = pl.multiple_of(step % 2 * 512, 512)
            rows_coef = stats[0, pl.ds(seq * SEQ + row, 16), :]
            totals = [None] * 4
            for layer in range(STREAMS_IN):
                value = wide(stack[seq, layer, pl.ds(row, 16), pl.ds(col, 512)])
                for stream in range(4):
                    at_coef = stream * STREAMS_IN + layer
                    term = rows_coef[:, at_coef : at_coef + 1] * value
                    totals[stream] = term if layer == 0 else totals[stream] + term
            for stream in range(4):
                streams[stream, pl.ds(seq * SEQ + row, 16), pl.ds(col, 512)] = totals[stream]
            return carry

        lax.fori_loop(0, 8, mix, 0)

    def norm(step, carry):
        row = pl.multiple_of(step * 16, 16)
        for stream in range(4):
            value = streams[stream, pl.ds(row, 16), :]
            center = value - jnp.mean(value, axis=-1, keepdims=True)
            inverse = lax.rsqrt(jnp.mean(center * center, axis=-1, keepdims=True) + EPSILON)
            scaled = center * inverse
            stats[2, pl.ds(row, 16), stream : stream + 1] = inverse
            scaled_out[stream, pl.ds(row, 16), :] = scaled
            packet[pl.ds(stream * ROWS + row, 16), :] = (
                scaled * norm_gain[stream : stream + 1, :] + norm_bias[stream : stream + 1, :]
            ).astype(jnp.bfloat16)
            if stream == 3:
                stream_out[pl.ds(row, 16), :] = value
        return carry

    lax.fori_loop(0, seqs * SEQ // 16, norm, 0)
    packet[4 * ROWS :] = jnp.zeros((16, WIDTH), jnp.bfloat16)
    row = rows_of((16, 128))
    marks = jnp.zeros((16, 128), jnp.float32)
    for place in range(2 * seqs):
        marks = jnp.where(row == place, wide(bounds[place]), marks)
    packet[4 * ROWS :, 0:128] = marks.astype(jnp.bfloat16)


def main_kernel(
    rope,
    packet0,
    packet1,
    packet2,
    packet3,
    cotangent0,
    cotangent1,
    cotangent2,
    cotangent3,
    piece0,
    piece1,
    piece2,
    piece3,
    piece4,
    piece5,
    piece6,
    piece7,
    piece8,
    piece9,
    piece10,
    chunk_low,
    chunk_high,
    chunk1,
    chunk2,
    chunk3,
    chunk4,
    chunk5,
    chunk6,
    chunk7,
    keep_own,
    keep_far,
    send_norm,
    keep_out,
    send_out,
    acts,
    marks,
    up_all,
    lin_all,
    down_all,
    out_rows,
    lhs_all,
    grad_pre,
    linear,
    grad_att,
    grad_lin,
    parts,
    tokens,
    packet_sems,
    piece_sems,
    chunk_sems,
    token_sems,
):
    z, y, _, core = position()
    origin = gather_order(z, y)
    target = scatter_order(z, y)
    packets = (packet0, packet1, packet2, packet3)
    cotangents = (cotangent0, cotangent1, cotangent2, cotangent3)
    piece, side, near, middle, middle_near, turned = piece0, piece1, piece2, piece3, piece4, piece5
    near_twice, side_two, side_three, over_z, over_y = piece6, piece7, piece8, piece9, piece10
    inner = (z == 1) | (z == 2)
    sources = (
        (piece, piece),
        (side, middle),
        (near, near),
        (turned, side_two),
        (middle, turned),
        (side_two, side_three),
        (middle_near, near_twice),
        (side_three, None),
    )
    chunks = (chunk1, chunk2, chunk3, chunk4, chunk5, chunk6, chunk7)
    member_rows = [pl.ds(pl.multiple_of(place * 128, 128), 128) for place in origin]

    def unit_copies(unit):
        return [
            pltpu.make_async_copy(
                packets[block].at[pl.ds(unit * ROWS, ROWS)],
                acts.at[unit, pl.ds(block * ROWS, ROWS)],
                packet_sems.at[block, unit],
            )
            for block in range(4)
        ]

    def piece_copies(index, ref, tail_ref):
        rows = member_rows[index]
        down = 7 if tail_ref is ref else 0
        return [
            pltpu.make_async_copy(
                ref.at[pl.ds(4, 3)], lin_all.at[:, rows], piece_sems.at[index, 0]
            ),
            pltpu.make_async_copy(
                tail_ref.at[pl.ds(down, 5)], down_all.at[origin[index]], piece_sems.at[index, 1]
            ),
            pltpu.make_async_copy(
                ref.at[pl.ds(0, 4)], up_all.at[:, rows], piece_sems.at[index, 2]
            ),
        ]

    first = unit_copies(0) + unit_copies(1) + unit_copies(2)
    second = [
        pltpu.make_async_copy(
            cotangents[block],
            acts.at[4, pl.ds(block * ROWS, ROWS)],
            packet_sems.at[block, 4],
        )
        for block in range(4)
    ]
    for block in range(4):
        second.append(
            pltpu.make_async_copy(
                packets[block].at[pl.ds(4 * ROWS, 16)], marks.at[block], packet_sems.at[block, 5]
            )
        )
    third = unit_copies(3)
    for copy in first + second + third:
        copy.start()
    for index, (for_inner, for_ends) in enumerate(sources):
        copies = piece_copies(index, for_inner, for_inner)
        first.append(copies[0])
        second.append(copies[1])
        third.append(copies[2])
        if for_inner is for_ends:
            for copy in copies:
                copy.start()
            continue
        ends = (
            piece_copies(index, over_z, over_y)
            if for_ends is None
            else piece_copies(index, for_ends, for_ends)
        )

        @pl.when(inner)
        def _():
            for copy in copies:
                copy.start()

        @pl.when(jnp.logical_not(inner))
        def _():
            for copy in ends:
                copy.start()

    for copy in first:
        copy.wait()
    for stream in range(3):
        linear[stream] = matmul(acts[stream], lin_all[stream])
    for copy in second:
        copy.wait()
    for pair in range(4):
        even = 2 * pair + core
        odd = 2 * pair + 1 - core
        for block in range(4):
            band = slice(block * 32, block * 32 + 32)
            cols = slice(block * 256, block * 256 + 256)
            out_rows[pair * 64 : pair * 64 + 32, cols] = down_all[even, block, 96:128]
            out_rows[pair * 64 + 32 : pair * 64 + 64, cols] = down_all[even, 4, band]
            down_all[even, block, 96:128] = down_all[odd, 4, band]

    grad_att[...] = back_product(acts[4], out_rows[...]).astype(jnp.bfloat16)
    cos_table = rope[0]
    sin_left = rope[1]
    sin_right = rope[2]
    scale = HEAD_DIM ** (-0.5)

    def turn(value, sign):
        return (
            value * cos_table
            + pltpu.roll(value, 120, 1) * (sign * sin_left)
            + pltpu.roll(value, 8, 1) * (sign * sin_right)
        )

    def units(block, carry):
        row = rows_of((ROWS, ROWS))
        lane = lanes_of((ROWS, ROWS))
        bound = wide(marks[block])

        def both(low, high):
            return jnp.where(row < SEQ, low, high), jnp.where(lane < SEQ, low, high)

        start_q, start_k = both(bound[0:1, 0:128], bound[1:2, 0:128])
        split_q, split_k = both(bound[2:3, 0:128], bound[3:4, 0:128])
        at_q = wide(row % SEQ)
        at_k = wide(lane % SEQ)
        same = (row // SEQ == lane // SEQ) & ((at_q >= split_q) == (at_k >= split_k))
        pic_q = (at_q >= start_q) & (at_q < start_q + PIC)
        pic_k = (at_k >= start_k) & (at_k < start_k + PIC)
        penalty = jnp.where(same & ((at_q >= at_k) | (pic_q & pic_k)), 0.0, -1e30)
        span = pl.ds(pl.multiple_of(block * ROWS, ROWS), ROWS)
        twins = [slice(twin * 128, twin * 128 + 128) for twin in range(2)]
        heads = [(twin, head) for twin in range(2) for head in range(2)]
        query = [turn(linear[0, span, cols], 1.0) for cols in twins]
        query_low = [item.astype(jnp.bfloat16) for item in query]
        key_low = [turn(linear[1, span, cols], 1.0).astype(jnp.bfloat16) for cols in twins]
        value_low = [linear[2, span, cols].astype(jnp.bfloat16) for cols in twins]
        grad_low = [grad_att[span, cols] for cols in twins]

        def only(item, head):
            return jnp.where(lane // 64 == head, wide(item), 0.0).astype(jnp.bfloat16)

        scores = [
            back_product(only(query[twin], head), key_low[twin]) * scale + penalty
            for twin, head in heads
        ]
        grad_probs = [
            back_product(only(grad_low[twin], head), value_low[twin]) for twin, head in heads
        ]
        exponent = [jnp.exp(item - jnp.max(item, axis=-1, keepdims=True)) for item in scores]
        probs = [item / jnp.sum(item, axis=-1, keepdims=True) for item in exponent]
        probs_low = [item.astype(jnp.bfloat16) for item in probs]
        grad_scores = [
            (prob * (grad - jnp.sum(prob * grad, axis=-1, keepdims=True))).astype(jnp.bfloat16)
            for prob, grad in zip(probs, grad_probs)
        ]
        attended = [matmul(probs_low[i], value_low[heads[i][0]]) for i in range(4)]
        grad_value = [outer_sum(probs_low[i], grad_low[heads[i][0]]) for i in range(4)]
        grad_query = [matmul(grad_scores[i], key_low[heads[i][0]]) for i in range(4)]
        grad_key = [outer_sum(grad_scores[i], query_low[heads[i][0]]) for i in range(4)]

        def merge(items, twin):
            return jnp.where(lane < 64, items[2 * twin], items[2 * twin + 1])

        for twin, cols in enumerate(twins):
            side = slice(WIDTH + twin * 128, WIDTH + twin * 128 + 128)
            lhs_all[span, side] = merge(attended, twin).astype(jnp.bfloat16)
            grad_lin[0, span, cols] = turn(merge(grad_query, twin) * scale, -1.0).astype(
                jnp.bfloat16
            )
            grad_lin[1, span, cols] = turn(merge(grad_key, twin) * scale, -1.0).astype(
                jnp.bfloat16
            )
            grad_lin[2, span, cols] = merge(grad_value, twin).astype(jnp.bfloat16)
        return carry

    lax.fori_loop(0, 4, units, 0, unroll=2)

    for copy in third:
        copy.wait()

    def hidden(pair, carry):
        cols = pl.ds(pl.multiple_of(pair * 256, 256), 256)
        up_pre = matmul(acts[3], up_all[pair])
        bell = 0.5 * (1.0 + lax.erf(up_pre * ROOT_HALF))
        slope = bell + up_pre * NORMAL_PEAK * jnp.exp(-0.5 * up_pre * up_pre)
        lhs_all[:, cols] = (up_pre * bell).astype(jnp.bfloat16)
        rows_down = jnp.concatenate(
            [
                jnp.concatenate([down_all[2 * pair + half, block] for block in range(4)], axis=1)
                for half in range(2)
            ]
        )
        grad_gated = back_product(acts[4], rows_down)
        grad_pre[:, cols] = (grad_gated * slope).astype(jnp.bfloat16)
        return carry

    lax.fori_loop(0, 4, hidden, 0, unroll=4)

    def weights(pair, carry):
        cols = pl.ds(pl.multiple_of(pair * 256, 256), 256)
        halves = (slice(0, 128), slice(128, 256))
        grad = outer_sum(acts[3, :, cols], grad_pre[...]).astype(jnp.bfloat16)
        for block in range(4):
            for half, rows in enumerate(halves):
                parts[2 * pair + half, block] = grad[rows, block * 256 : block * 256 + 256]
        for stream in range(3):
            grad = outer_sum(acts[stream, :, cols], grad_lin[stream]).astype(jnp.bfloat16)
            for half, rows in enumerate(halves):
                parts[2 * pair + half, 4 + stream] = grad[rows]
        grad = outer_sum(lhs_all[:, cols], acts[4]).astype(jnp.bfloat16)
        for half in range(2):
            index, other = 2 * pair + half, 2 * pair + 1 - half
            for block in range(4):
                part = grad[half * 128 : half * 128 + 128, block * 256 : block * 256 + 256]
                parts[index, 7 + block, 0:96] = part[0:96]

                @pl.when(core == half)
                def _():
                    parts[other, 11, block * 32 : block * 32 + 32] = part[96:128]

                @pl.when(core != half)
                def _():
                    parts[index, 7 + block, 96:128] = part[96:128]

        return carry

    lax.fori_loop(0, 4, weights, 0, unroll=2)
    grad = outer_sum(lhs_all[:, WIDTH:], acts[4]).astype(jnp.bfloat16)
    for block in range(4):
        part = grad[:, block * 256 : block * 256 + 256]
        for pair in range(4):
            even = 2 * pair + core
            parts[even, 7 + block, 96:128] = part[pair * 64 : pair * 64 + 32]
            parts[even, 11, block * 32 : block * 32 + 32] = part[pair * 64 + 32 : pair * 64 + 64]
    sent = [
        pltpu.make_async_copy(
            parts.at[target[0], pl.ds(0, PART)], chunk_low, chunk_sems.at[0]
        ),
        pltpu.make_async_copy(
            parts.at[target[0], pl.ds(PART, 12 - PART)], chunk_high, chunk_sems.at[8]
        ),
    ] + [
        pltpu.make_async_copy(parts.at[target[index]], chunks[index - 1], chunk_sems.at[index])
        for index in range(1, 8)
    ]
    for copy in sent:
        copy.start()

    def put(unit, cols, value):
        low = value.astype(jnp.bfloat16)
        for half in range(2):
            for block in range(2):
                at = (2 * half + block) * ROWS
                tokens[half, block, unit, :, cols] = low[at : at + ROWS]

    def ship(unit):
        if unit < 4:
            routes = (
                (tokens.at[0, 0, unit], keep_own.at[unit]),
                (tokens.at[0, 1, unit], keep_far.at[unit]),
                (tokens.at[1, :, unit], send_norm.at[:, unit]),
            )
        else:
            routes = ((tokens.at[0, :, unit], keep_out), (tokens.at[1, :, unit], send_out))
        for place, (source, goal) in enumerate(routes):
            copy = pltpu.make_async_copy(source, goal, token_sems.at[place, unit])
            copy.start()
            sent.append(copy)

    for stream in range(3):
        put(stream, slice(0, WIDTH), back_product(grad_lin[stream], lin_all[stream]))
        ship(stream)

    def feed(block, carry):
        cols = pl.ds(pl.multiple_of(block * 256, 256), 256)
        rows_up = jnp.concatenate([up_all[part, cols] for part in range(4)], axis=1)
        put(3, cols, back_product(grad_pre[...], rows_up))
        right = [down_all[index, block] for index in range(8)] + [out_rows[:, cols]]
        put(4, cols, matmul(lhs_all[...], jnp.concatenate(right)))
        return carry

    lax.fori_loop(0, 4, feed, 0, unroll=2)
    ship(3)
    ship(4)
    for copy in sent:
        copy.wait()


def back_kernel(
    stack,
    cotangent,
    scaled,
    stats,
    keep,
    came,
    across,
    mix_gain,
    mix_up,
    mix_down,
    norm_gain,
    stack_grad,
    small_own,
    small_other,
    coefficients,
    grads,
    sums,
    coef_grad,
    small,
):
    seqs = stack.shape[0]
    sums[...] = jnp.zeros_like(sums)
    lane = lanes_of((16, 128))

    def unit(step, carry):
        row = pl.multiple_of(step * 16, 16)
        span = pl.ds(row, 16)

        def result(index):
            return wide(keep[index, span]) + wide(came[0, index, span]) + wide(across[index, span])

        for stream in range(4):
            item = result(stream)
            scale = scaled[stream, span]
            moved = item * scale
            sums[stream] += moved[:8] + moved[8:]
            sums[4 + stream] += item[:8] + item[8:]
            weighted = item * norm_gain[stream : stream + 1]
            mean = jnp.mean(weighted, axis=-1, keepdims=True)
            slant = jnp.mean(weighted * scale, axis=-1, keepdims=True)
            grad = stats[2, span, stream : stream + 1] * (weighted - mean - scale * slant)
            if stream == 3:
                grad = grad + wide(cotangent[span])
            grads[stream, span] = grad
        return carry

    lax.fori_loop(0, seqs * SEQ // 16, unit, 0)
    for seq in range(seqs):

        def coefs(step, carry):
            row = pl.multiple_of(step * 16, 16)
            span = pl.ds(seq * SEQ + row, 16)
            found = jnp.zeros((16, 128), jnp.float32)
            for layer in range(STREAMS_IN):
                value = wide(stack[seq, layer, pl.ds(row, 16), :])
                for stream in range(4):
                    got = jnp.sum(grads[stream, span] * value, axis=-1, keepdims=True)
                    found = jnp.where(lane == stream * STREAMS_IN + layer, got, found)
            coef_grad[span] = found
            return carry

        lax.fori_loop(0, SEQ // 16, coefs, 0)
    grad_coef = coef_grad[:, 0:36]
    hidden_pre = stats[1, :, 0:36]
    hidden_low = gelu_value(hidden_pre).astype(jnp.bfloat16)
    for seq in range(seqs):
        turned = stats[0, seq * SEQ : seq * SEQ + SEQ, :].T
        for stream in range(4):
            for layer in range(STREAMS_IN):
                at = stream * STREAMS_IN + layer
                coefficients[seq, layer, stream : stream + 1] = turned[at : at + 1]
    small[...] = jnp.zeros_like(small)
    small[0:36, WIDTH : WIDTH + 36] = lax.dot_general(
        wide(hidden_low),
        grad_coef,
        (((0,), (0,)), ((), ())),
        precision=HIGHEST,
        preferred_element_type=jnp.float32,
    )
    small[36:37, WIDTH : WIDTH + 36] = jnp.sum(grad_coef, axis=0, keepdims=True)
    grad_hidden = (
        lax.dot_general(
            grad_coef,
            mix_down[...],
            (((1,), (1,)), ((), ())),
            precision=HIGHEST,
            preferred_element_type=jnp.float32,
        )
        * gelu_slope(hidden_pre)
    ).astype(jnp.bfloat16)
    gain_row = jnp.zeros((8, WIDTH), jnp.float32)
    up_part = jnp.zeros((36, WIDTH), jnp.float32)
    for seq in range(seqs):
        at = slice(seq * SEQ, seq * SEQ + SEQ)
        last = wide(stack[seq, STREAMS_IN - 1])
        rms = stats[2, at, 4:5]
        mixed_in = (last * rms * mix_gain[...]).astype(jnp.bfloat16)
        up_part = up_part + outer_sum(grad_hidden[at], mixed_in)
        grad_mixed = matmul(grad_hidden[at], mix_up[...])
        along = grad_mixed * last * rms
        for place in range(SEQ // 8):
            gain_row = gain_row + along[place * 8 : place * 8 + 8]
        weighted = grad_mixed * mix_gain[...]
        mean = jnp.mean(weighted * last, axis=-1, keepdims=True)
        grads[4, at] = rms * (weighted - last * (rms * rms * mean))

        def layers(step, carry):
            row = pl.multiple_of(step // 2 * 16, 16)
            cols = pl.ds(pl.multiple_of(step % 2 * 512, 512), 512)
            span = pl.ds(seq * SEQ + row, 16)
            rows_coef = stats[0, span, :]
            parts = [grads[stream, span, cols] for stream in range(4)]
            for layer in range(STREAMS_IN):
                total = None
                for stream in range(4):
                    at_coef = stream * STREAMS_IN + layer
                    term = rows_coef[:, at_coef : at_coef + 1] * parts[stream]
                    total = term if total is None else total + term
                if layer == STREAMS_IN - 1:
                    total = total + grads[4, span, cols]
                stack_grad[seq, layer, pl.ds(row, 16), cols] = total.astype(jnp.bfloat16)
            return carry

        lax.fori_loop(0, 8, layers, 0)
    small[0:36, 0:WIDTH] = up_part
    for place in range(8):
        small[36 + place : 37 + place, 0:WIDTH] = jnp.sum(sums[place], axis=0, keepdims=True)
    small[44:45, 0:WIDTH] = jnp.sum(gain_row, axis=0, keepdims=True)
    _, _, _, core = position()
    small_own[...] = small[pl.ds(pl.multiple_of(core * 24, 8), 24), :]
    small_other[...] = small[pl.ds(pl.multiple_of(24 - core * 24, 8), 24), :]


def place_kernel(
    shard0,
    shard1,
    shard2,
    shard3,
    small_own,
    small_other,
    projection,
    out_grad,
    up_grad,
    down_grad,
    mix_gain_grad,
    mix_up_grad,
    mix_down_grad,
    mix_static_grad,
    gain_grad,
    bias_grad,
    small,
):
    z, member_parity, x, core = position()
    small[pl.ds(pl.multiple_of(core * 24, 8), 24), :] = small_own[...]
    small[pl.ds(pl.multiple_of(24 - core * 24, 8), 24), :] = small_other[...]
    lanes = pl.ds(pl.multiple_of((2 * z + member_parity) * 128, 128), 128)
    mix_up_grad[...] = small[0:36, lanes]
    gain_grad[...] = small[36:40, 0:WIDTH]
    bias_grad[...] = small[40:44, 0:WIDTH]
    mix_gain_grad[...] = small[44:45, 0:WIDTH]
    mix_down_grad[...] = small[0:36, WIDTH : WIDTH + 36]
    for stream in range(4):
        at = WIDTH + stream * STREAMS_IN
        mix_static_grad[stream : stream + 1] = small[36:37, at : at + STREAMS_IN]
    shards = (shard0, shard1, shard2, shard3)
    lane = lanes_of((128, 128))
    for back in range(4):
        from_x = x if back % 2 == 0 else 1 - x
        from_core = core if back < 2 else 1 - core
        quarter = 2 * from_x + from_core
        own, twin = shards[back], shards[back ^ 2]
        for index in range(8):
            half = index % 2
            mine = wide(own[index // 2, :, half * 128 : half * 128 + 128])
            half_b = 1 - half
            lent = wide(twin[index // 2, :, half_b * 128 : half_b * 128 + 128])
            col = pl.multiple_of((index * 4 + quarter) * 128, 128)
            up_grad[:, pl.ds(col, 128)] = jnp.where(
                (lane >= 96) & (from_core == half), lent, mine
            )
        row = pl.multiple_of(quarter * 128, 128)
        for block in range(4):
            cols = slice(block * 256, block * 256 + 256)
            down_grad[pl.ds(row, 96), cols] = wide(own[7 + block, 0:96])

            @pl.when(member_parity == from_core)
            def _():
                head_row = pl.multiple_of(from_x * 64, 64)
                out_grad[pl.ds(head_row, 32), cols] = wide(own[7 + block, 96:128])
                out_grad[pl.ds(head_row + 32, 32), cols] = wide(
                    own[11, block * 32 : block * 32 + 32]
                )
                down_grad[pl.ds(row + 96, 32), cols] = wide(
                    twin[11, block * 32 : block * 32 + 32]
                )

            @pl.when(member_parity != from_core)
            def _():
                down_grad[pl.ds(row + 96, 32), cols] = wide(own[7 + block, 96:128])

    for back in (0, 2):
        from_core = core if back < 2 else 1 - core
        for stream in range(3):
            for twin in range(2):
                tile = slice(twin * 128, twin * 128 + 128)
                mine = wide(shards[back][4 + stream, :, tile])
                across = wide(shards[back + 1][4 + stream, :, tile])
                even = jnp.where(x == 0, mine, across)
                odd = jnp.where(x == 0, across, mine)
                first = jnp.where(lane < 64, even, pltpu.roll(odd, 64, 1))
                second = jnp.where(lane < 64, pltpu.roll(even, 64, 1), odd)
                for low, value in ((0, first), (1, second)):
                    col = pl.multiple_of((2 * twin + low) * 256 + from_core * 128, 128)
                    projection[stream, :, pl.ds(col, 128)] = value


def call(kernel, outs, specs, out_specs, args, scratch=(), cost=None, vmem=60 << 20):
    return pl.pallas_call(
        kernel,
        out_shape=outs,
        in_specs=specs,
        out_specs=out_specs,
        scratch_shapes=list(scratch),
        compiler_params=pltpu.CompilerParams(vmem_limit_bytes=vmem),
        cost_estimate=cost,
    )(*args)


def shape_of(shape, dtype=jnp.bfloat16):
    return jax.ShapeDtypeStruct(shape, dtype)


def rope_tables():
    half_rot = ROTARY // 2
    step = 10000.0 ** (-2.0 * np.arange(half_rot) / ROTARY)
    angles = np.arange(SEQ)[:, None] * step[None, :]
    cos_table = np.ones((SEQ, HEAD_DIM))
    left = np.zeros((SEQ, HEAD_DIM))
    right = np.zeros((SEQ, HEAD_DIM))
    cos_table[:, :half_rot] = np.cos(angles)
    cos_table[:, half_rot:ROTARY] = np.cos(angles)
    left[:, :half_rot] = -np.sin(angles)
    right[:, half_rot:ROTARY] = np.sin(angles)
    return np.stack([np.tile(item, (2, 2)) for item in (cos_table, left, right)]).astype(np.float32)


def on_device_tensor(
    layer_stack,
    out_cotangent,
    pic_start,
    doc_split,
    mix_gain,
    mix_up,
    mix_down,
    mix_static,
    norm_gain,
    norm_bias,
    query_key_value,
    out_weight,
    up_weight,
    down_weight,
):
    z, y, _, _ = position()
    micro_total, local_seqs, _, _, width = layer_stack.shape
    seqs = micro_total * local_seqs
    stack = jnp.transpose(layer_stack, (0, 1, 3, 2, 4)).reshape(seqs, STREAMS_IN, SEQ, width)
    cotangent = out_cotangent.reshape(ROWS, width)
    gain_row = mix_gain.reshape(1, width)

    piece = call(
        prepare_kernel,
        shape_of((12, 128, 256)),
        [VMEM_FULL] * 4,
        VMEM_FULL,
        (query_key_value, out_weight, up_weight, down_weight),
        vmem=60 << 20,
    )
    up_own = mix_up.T
    up_pair = jnp.concatenate([up_own, after(lax.ppermute(up_own, "fsdp", Y_SWAP), piece)], axis=1)
    up_one = fsdp_move(
        up_pair,
        [((index + 8 + index % 2 * 16) % 32, index) for index in range(32)],
    )
    up_two = fsdp_move(up_pair, Z_SWAP_FAR)
    ups = (up_pair, up_one, up_two)
    piece = after(piece, *ups)
    up_three = lax.ppermute(up_one, "replica", CORE_SWAP)
    ups += (up_three,)
    bounds = jnp.concatenate([pic_start.reshape(seqs), doc_split.reshape(seqs)])
    kept = {}
    grad_across = lax.ppermute(cotangent, "replica", X_SWAP)
    grad_packets = (
        cotangent,
        grad_across,
        lax.ppermute(cotangent, "replica", CORE_SWAP),
        lax.ppermute(grad_across, "replica", CORE_SWAP),
    )

    def front():
        packet, *kept["rest"] = call(
            front_kernel,
            (
                shape_of((4 * ROWS + 16, width)),
                shape_of((4, ROWS, width), jnp.float32),
                shape_of((3, ROWS, 128), jnp.float32),
                shape_of((ROWS, width), jnp.float32),
                shape_of((36, width)),
            ),
            [SMEM_FULL] + [VMEM_FULL] * 10,
            (VMEM_FULL,) * 5,
            (
                bounds,
                stack,
                gain_row,
                *ups,
                mix_down,
                mix_static.reshape(1, 36),
                norm_gain,
                norm_bias,
            ),
            scratch=[pltpu.VMEM((4, ROWS, width), jnp.float32)],
            vmem=30 << 20,
        )
        across = lax.ppermute(packet, "replica", X_SWAP)
        beside = lax.ppermute(packet, "replica", CORE_SWAP)
        beside_across = lax.ppermute(across, "replica", CORE_SWAP)
        kept["packets"] = (packet, across, beside, beside_across)
        return (packet, grad_across), (across,)

    pieces = gather_fsdp(piece, z, front)
    packets = kept["packets"]
    scaled, stats, stream_last, mix_up_full = kept["rest"]

    results = call(
        main_kernel,
        (shape_of((PART, 128, 256)), shape_of((12 - PART, 128, 256)))
        + (shape_of((12, 128, 256)),) * 7
        + (shape_of((4, ROWS, width)),) * 2
        + (shape_of((2, 4, ROWS, width)),)
        + (shape_of((2, ROWS, width)),) * 2,
        [VMEM_FULL] + [IN_PLACE] * 19,
        (IN_PLACE,) * 14,
        (jnp.asarray(rope_tables()),) + packets + grad_packets + tuple(pieces),
        scratch=[
            pltpu.VMEM((5, 4 * ROWS, width), jnp.bfloat16),
            pltpu.VMEM((4, 16, width), jnp.bfloat16),
            pltpu.VMEM((4, width, 256), jnp.bfloat16),
            pltpu.VMEM((3, width, 256), jnp.bfloat16),
            pltpu.VMEM((8, 5, 128, 256), jnp.bfloat16),
            pltpu.VMEM((256, width), jnp.bfloat16),
            pltpu.VMEM((4 * ROWS, width + 256), jnp.bfloat16),
            pltpu.VMEM((4 * ROWS, width), jnp.bfloat16),
            pltpu.VMEM((3, 4 * ROWS, 256), jnp.float32),
            pltpu.VMEM((4 * ROWS, 256), jnp.bfloat16),
            pltpu.VMEM((3, 4 * ROWS, 256), jnp.bfloat16),
            pltpu.VMEM((8, 12, 128, 256), jnp.bfloat16),
            pltpu.VMEM((2, 2, 5, ROWS, width), jnp.bfloat16),
            pltpu.SemaphoreType.DMA((4, 6)),
            pltpu.SemaphoreType.DMA((8, 3)),
            pltpu.SemaphoreType.DMA((9,)),
            pltpu.SemaphoreType.DMA((3, 5)),
        ],
        vmem=42 << 20,
    )
    chunks = results[:9]
    keep_own, keep_far, send_norm, keep_out, send_out = results[9:]

    came = lax.ppermute(send_norm, "replica", CORE_SWAP)
    sum_across = (wide(keep_far) + wide(came[1])).astype(jnp.bfloat16)
    came_across = lax.ppermute(sum_across, "replica", X_SWAP)
    out_came = lax.ppermute(after(send_out, sum_across), "replica", CORE_SWAP)
    out_across = (wide(keep_out[1]) + wide(out_came[1])).astype(jnp.bfloat16)
    out_across = lax.ppermute(after(out_across, came_across), "replica", X_SWAP)
    layer_output = (
        stream_last + wide(keep_out[0]) + wide(out_came[0]) + wide(out_across)
    ).astype(jnp.bfloat16)

    first_half = pl.BlockSpec((1, 4, ROWS, width), lambda step: (0, 0, 0, 0))

    def whole(shape):
        return pl.BlockSpec(shape, lambda step: (0,) * len(shape))

    def back():
        kept["back"] = pl.pallas_call(
            back_kernel,
            grid=(1,),
            out_shape=(
                shape_of((seqs, STREAMS_IN, SEQ, width)),
                shape_of((24, width + 128), jnp.float32),
                shape_of((24, width + 128), jnp.float32),
                shape_of((seqs, STREAMS_IN, 4, SEQ), jnp.float32),
            ),
            in_specs=[
                whole((seqs, STREAMS_IN, SEQ, width)),
                whole((ROWS, width)),
                whole((4, ROWS, width)),
                whole((3, ROWS, 128)),
                whole((4, ROWS, width)),
                first_half,
                whole((4, ROWS, width)),
                whole((1, width)),
                whole((36, width)),
                whole((36, 36)),
                whole((4, width)),
            ],
            out_specs=(
                whole((seqs, STREAMS_IN, SEQ, width)),
                whole((24, width + 128)),
                whole((24, width + 128)),
                whole((seqs, STREAMS_IN, 4, SEQ)),
            ),
            scratch_shapes=[
                pltpu.VMEM((5, ROWS, width), jnp.float32),
                pltpu.VMEM((8, 8, width), jnp.float32),
                pltpu.VMEM((ROWS, 128), jnp.float32),
                pltpu.VMEM((48, width + 128), jnp.float32),
            ],
            compiler_params=pltpu.CompilerParams(vmem_limit_bytes=56 << 20),
        )(
            stack,
            cotangent,
            scaled,
            stats,
            keep_own,
            came,
            came_across,
            gain_row,
            mix_up_full,
            mix_down,
            norm_gain,
        )
        return kept["back"][1]

    shard = scatter_fsdp(chunks, z, sum_across, back)
    stack_grad, small, small_other, coefficients = kept["back"]

    small = small + lax.ppermute(small_other, "replica", CORE_SWAP)
    small = small + lax.ppermute(small, "replica", X_SWAP)
    small = small + lax.ppermute(small, "fsdp", Y_SWAP)
    shard = after(shard, small, out_across)
    shard_across = lax.ppermute(shard, "replica", X_SWAP)
    shard_beside = lax.ppermute(shard, "replica", CORE_SWAP)
    for perm in (Z_SWAP_NEAR, Z_SWAP_FAR):
        small = small + lax.ppermute(small, "fsdp", perm)
    small_beside = lax.ppermute(small, "replica", CORE_SWAP)
    shard_both = lax.ppermute(after(shard_across, small), "replica", CORE_SWAP)
    owned = call(
        place_kernel,
        (
            shape_of((3, 128, width), jnp.float32),
            shape_of((128, width), jnp.float32),
            shape_of((128, 4 * width), jnp.float32),
            shape_of((512, width), jnp.float32),
            shape_of((1, width), jnp.float32),
            shape_of((36, 128), jnp.float32),
            shape_of((36, 36), jnp.float32),
            shape_of((4, STREAMS_IN), jnp.float32),
            shape_of((4, width), jnp.float32),
            shape_of((4, width), jnp.float32),
        ),
        [VMEM_FULL] * 6,
        (VMEM_FULL,) * 10,
        (shard, shard_across, shard_beside, shard_both, small, small_beside),
        scratch=[pltpu.VMEM((48, width + 128), jnp.float32)],
        vmem=14 << 20,
    )
    projection_grad, out_grad, up_grad, down_grad, *small_grads = owned
    shape = (micro_total, local_seqs, SEQ)
    stack_grad = stack_grad.reshape(micro_total, local_seqs, STREAMS_IN, SEQ, width)
    coefficients = coefficients.reshape(micro_total, local_seqs, STREAMS_IN, 4, SEQ)
    return (
        layer_output.reshape(shape + (width,)),
        jnp.transpose(coefficients, (0, 1, 4, 3, 2)),
        jnp.transpose(stack_grad, (0, 1, 3, 2, 4)),
        small_grads[0].reshape(width),
        small_grads[1].T,
        small_grads[2],
        small_grads[3],
        small_grads[4],
        small_grads[5],
        projection_grad,
        out_grad,
        up_grad,
        down_grad,
    )


def solution(mesh):
    fits = mesh.shape["fsdp"] == 8 and mesh.shape["replica"] == 4
    body = on_device_tensor if fits else on_device
    return jax.shard_map(
        body,
        mesh=mesh,
        in_specs=(
            P(None, ("fsdp", "replica"), None, None, None),
            P(None, ("fsdp", "replica"), None, None),
            P(None, ("fsdp", "replica")),
            P(None, ("fsdp", "replica")),
            P(),
            P("fsdp", None),
            P(),
            P(),
            P(),
            P(),
            P(None, "fsdp", None),
            P("fsdp", None),
            P("fsdp", None),
            P("fsdp", None),
        ),
        out_specs=(
            P(None, ("fsdp", "replica"), None, None),
            P(None, ("fsdp", "replica"), None, None, None),
            P(None, ("fsdp", "replica"), None, None, None),
            P(),
            P("fsdp", None),
            P(),
            P(),
            P(),
            P(),
            P(None, "fsdp", None),
            P("fsdp", None),
            P("fsdp", None),
            P("fsdp", None),
        ),
        check_vma=False,
    )
```

```python
import math

import jax
import jax.numpy as jnp
import numpy as np
from jax import lax
from jax.experimental import pallas as pl
from jax.experimental.pallas import tpu as pltpu
from jax.sharding import PartitionSpec as P

HEADS = 16
HEAD_DIM = 64
ROTARY = 16
STREAMS_IN = 9
SEQ = 64
PIC = 32


EPSILON = 1e-05
ROOT_HALF = 0.7071067811865476
NORMAL_PEAK = 0.3989422804014327
HIGHEST = lax.Precision.HIGHEST


def as_sent(value):

    def short(part):
        return part.astype(jnp.bfloat16) if part.dtype == jnp.float32 else part

    return jax.tree.map(short, value)


def gelu_value(values):
    return 0.5 * values * (1.0 + lax.erf(values * ROOT_HALF))


def gelu_slope(values):
    return 0.5 * (1.0 + lax.erf(values * ROOT_HALF)) + values * NORMAL_PEAK * jnp.exp(
        -0.5 * values * values
    )


def matmul(left_side, right_side):
    return jnp.dot(left_side, right_side, preferred_element_type=jnp.float32)


def outer_sum(left_side, right_side):
    return lax.dot_general(
        left_side, right_side, (((0,), (0,)), ((), ())), preferred_element_type=jnp.float32
    )


def back_product(left_side, right_side):
    return lax.dot_general(
        left_side, right_side, (((1,), (1,)), ((), ())), preferred_element_type=jnp.float32
    )


def rotary_tables():
    half_rot = ROTARY // 2
    inverse = jnp.exp(-math.log(10000.0) * (2.0 * jnp.arange(half_rot, dtype=jnp.float32) / ROTARY))
    angles = jnp.arange(SEQ, dtype=jnp.float32)[:, None] * inverse[None, :]
    return (jnp.cos(angles)[:, None, :], jnp.sin(angles)[:, None, :])


def rotate(values, cos_table, sin_table):
    half_rot = ROTARY // 2
    first_half = values[..., :half_rot]
    second = values[..., half_rot:ROTARY]
    return jnp.concatenate(
        [
            first_half * cos_table - second * sin_table,
            second * cos_table + first_half * sin_table,
            values[..., ROTARY:],
        ],
        axis=-1,
    )


def allowed_mask(starts, splits):
    positions = jnp.arange(SEQ, dtype=jnp.int32)
    second_doc = positions[None, :] >= splits[:, None]
    picture = (positions[None, :] >= starts[:, None]) & (positions[None, :] < starts[:, None] + PIC)
    same_doc = second_doc[:, :, None] == second_doc[:, None, :]
    causal = positions[:, None] >= positions[None, :]
    both_pic = picture[:, :, None] & picture[:, None, :]
    return same_doc & (causal[None] | both_pic)


def masked_scores(queries, key_rot, allowed):
    scores = jnp.einsum(
        "nqhe,nkhe->nhqk", queries, key_rot, preferred_element_type=jnp.float32
    ) * HEAD_DIM ** (-0.5)
    return jnp.where(allowed[:, None], scores, -1e30)


def on_device(
    layer_stack,
    out_cotangent,
    pic_start,
    doc_split,
    mix_gain,
    mix_up,
    mix_down,
    mix_static,
    norm_gain,
    norm_bias,
    query_key_value,
    out_weight,
    up_weight,
    down_weight,
):
    micro_total = layer_stack.shape[0]
    local_seqs = layer_stack.shape[1]
    model_width = layer_stack.shape[-1]
    groups = [(0, micro_total)]
    cos_table, sin_table = rotary_tables()
    output_list = []
    coef_list = []
    grad_list = []
    shard_total = None
    small_total = None
    for first_micro, micro_count in groups:
        seq_count = micro_count * local_seqs
        row_count = seq_count * SEQ
        head_shape = (seq_count, SEQ, HEADS, HEAD_DIM)
        flat_stack = layer_stack[first_micro : first_micro + micro_count].reshape(
            row_count, STREAMS_IN, model_width
        )
        grad_rows = out_cotangent[first_micro : first_micro + micro_count].reshape(
            row_count, model_width
        )
        starts = pic_start[first_micro : first_micro + micro_count].reshape(seq_count)
        splits = doc_split[first_micro : first_micro + micro_count].reshape(seq_count)
        allowed = allowed_mask(starts, splits)
        mix_up_full, projection_full, out_full = (
            lax.all_gather(mix_up, "fsdp", axis=0, tiled=True),
            lax.all_gather(query_key_value, "fsdp", axis=1, tiled=True),
            lax.all_gather(out_weight, "fsdp", axis=0, tiled=True),
        )
        up_full, down_full = (
            lax.all_gather(up_weight, "fsdp", axis=0, tiled=True),
            lax.all_gather(down_weight, "fsdp", axis=0, tiled=True),
        )
        last_layer = flat_stack[:, STREAMS_IN - 1, :].astype(jnp.float32)
        rms_scale = lax.rsqrt(jnp.mean(last_layer * last_layer, axis=-1, keepdims=True) + EPSILON)
        mixed_in = (last_layer * rms_scale * mix_gain).astype(jnp.bfloat16)
        hidden_pre = matmul(mixed_in, mix_up_full)
        hidden_mix = gelu_value(hidden_pre).astype(jnp.bfloat16)
        hidden_wide = hidden_mix.astype(jnp.float32)
        coef_flat = jnp.dot(hidden_wide, mix_down, precision=HIGHEST) + mix_static.reshape(-1)
        coef_rows = coef_flat.reshape(row_count, 4, STREAMS_IN)
        streams = coef_rows[:, :, 0, None] * flat_stack[:, None, 0, :].astype(jnp.float32)
        for layer_index in range(1, STREAMS_IN):
            streams = streams + coef_rows[:, :, layer_index, None] * flat_stack[
                :, None, layer_index, :
            ].astype(jnp.float32)
        center = streams - jnp.mean(streams, axis=-1, keepdims=True)
        inv_std = lax.rsqrt(jnp.mean(center * center, axis=-1, keepdims=True) + EPSILON)
        scaled = center * inv_std
        normed = (scaled * norm_gain + norm_bias).astype(jnp.bfloat16)
        query_lin = matmul(normed[:, 0], projection_full[0])
        key_lin = matmul(normed[:, 1], projection_full[1])
        value_lin = matmul(normed[:, 2], projection_full[2])
        queries = rotate(query_lin.reshape(head_shape), cos_table, sin_table).astype(jnp.bfloat16)
        key_rot = rotate(key_lin.reshape(head_shape), cos_table, sin_table).astype(jnp.bfloat16)
        values = value_lin.astype(jnp.bfloat16).reshape(head_shape)
        scores = masked_scores(queries, key_rot, allowed)
        row_top = jnp.max(scores, axis=-1, keepdims=True)
        exponent = jnp.exp(scores - row_top)
        row_total = jnp.sum(exponent, axis=-1, keepdims=True)
        soft_probs = exponent / row_total
        log_total = row_top + jnp.log(row_total)
        attended = (
            jnp.einsum(
                "nhqk,nkhe->nqhe",
                soft_probs.astype(jnp.bfloat16),
                values,
                preferred_element_type=jnp.float32,
            )
            .astype(jnp.bfloat16)
            .reshape(row_count, model_width)
        )
        attn_out = matmul(attended, out_full)
        up_pre = matmul(normed[:, 3], up_full)
        gated_act = gelu_value(up_pre).astype(jnp.bfloat16)
        feed_out = matmul(gated_act, down_full)
        output_list.append((streams[:, 3] + attn_out + feed_out).astype(jnp.bfloat16))
        coef_list.append(coef_rows)
        mix_up_back, projection_back, out_back = (
            lax.all_gather(mix_up, "fsdp", axis=0, tiled=True),
            lax.all_gather(query_key_value, "fsdp", axis=1, tiled=True),
            lax.all_gather(out_weight, "fsdp", axis=0, tiled=True),
        )
        up_back, down_back = (
            lax.all_gather(up_weight, "fsdp", axis=0, tiled=True),
            lax.all_gather(down_weight, "fsdp", axis=0, tiled=True),
        )
        grad_down = outer_sum(gated_act, grad_rows)
        grad_gated = back_product(grad_rows, down_back)
        grad_up_pre = (grad_gated * gelu_slope(up_pre)).astype(jnp.bfloat16)
        grad_up = outer_sum(normed[:, 3], grad_up_pre)
        grad_norm_feed = back_product(grad_up_pre, up_back)
        feed_shards = (
            lax.psum_scatter(
                grad_up.astype(jnp.bfloat16), "fsdp", scatter_dimension=0, tiled=True
            ).astype(jnp.float32),
            lax.psum_scatter(
                grad_down.astype(jnp.bfloat16), "fsdp", scatter_dimension=0, tiled=True
            ).astype(jnp.float32),
        )
        grad_out_weight = outer_sum(attended, grad_rows)
        grad_attended = back_product(grad_rows, out_back).astype(jnp.bfloat16).reshape(head_shape)
        scores_again = masked_scores(queries, key_rot, allowed)
        probs_again = jnp.exp(scores_again - log_total)
        grad_probs = jnp.einsum(
            "nqhe,nkhe->nhqk", grad_attended, values, preferred_element_type=jnp.float32
        )
        grad_value = (
            jnp.einsum(
                "nhqk,nqhe->nkhe",
                probs_again.astype(jnp.bfloat16),
                grad_attended,
                preferred_element_type=jnp.float32,
            )
            .astype(jnp.bfloat16)
            .reshape(row_count, model_width)
        )
        delta_rows = jnp.sum(probs_again * grad_probs, axis=-1, keepdims=True)
        grad_scores = (probs_again * (grad_probs - delta_rows)).astype(jnp.bfloat16)
        score_scale = HEAD_DIM ** (-0.5)
        grad_query_rot = (
            jnp.einsum("nhqk,nkhe->nqhe", grad_scores, key_rot, preferred_element_type=jnp.float32)
            * score_scale
        )
        grad_key_rot = (
            jnp.einsum("nhqk,nqhe->nkhe", grad_scores, queries, preferred_element_type=jnp.float32)
            * score_scale
        )
        grad_query = (
            rotate(grad_query_rot, cos_table, -sin_table)
            .astype(jnp.bfloat16)
            .reshape(row_count, model_width)
        )
        grad_key = (
            rotate(grad_key_rot, cos_table, -sin_table)
            .astype(jnp.bfloat16)
            .reshape(row_count, model_width)
        )
        grad_linear = (grad_query, grad_key, grad_value)
        grad_projection = jnp.stack(
            [outer_sum(normed[:, stream], grad_linear[stream]) for stream in range(3)]
        )
        grad_normed = jnp.stack(
            [back_product(grad_linear[stream], projection_back[stream]) for stream in range(3)]
            + [grad_norm_feed],
            axis=1,
        )
        gain_grad = jnp.sum(grad_normed * scaled, axis=0)
        bias_grad = jnp.sum(grad_normed, axis=0)
        grad_scaled = grad_normed * norm_gain
        grad_streams = inv_std * (
            grad_scaled
            - jnp.mean(grad_scaled, axis=-1, keepdims=True)
            - scaled * jnp.mean(grad_scaled * scaled, axis=-1, keepdims=True)
        )
        grad_streams = grad_streams + jnp.concatenate(
            [
                jnp.zeros((row_count, 3, model_width), jnp.float32),
                grad_rows[:, None, :].astype(jnp.float32),
            ],
            axis=1,
        )
        grad_coef = jnp.stack(
            [
                jnp.sum(
                    grad_streams * flat_stack[:, None, layer_index, :].astype(jnp.float32), axis=-1
                )
                for layer_index in range(STREAMS_IN)
            ],
            axis=-1,
        )
        grad_coef_flat = grad_coef.reshape(row_count, 4 * STREAMS_IN)
        static_grad = jnp.sum(grad_coef_flat, axis=0).reshape(4, STREAMS_IN)
        down_mix_grad = jnp.dot(hidden_wide.T, grad_coef_flat, precision=HIGHEST)
        grad_hidden = (
            jnp.dot(grad_coef_flat, mix_down.T, precision=HIGHEST) * gelu_slope(hidden_pre)
        ).astype(jnp.bfloat16)
        grad_mix_up = outer_sum(mixed_in, grad_hidden)
        grad_mixed = back_product(grad_hidden, mix_up_back)
        gain_mix_grad = jnp.sum(grad_mixed * last_layer * rms_scale, axis=0)
        weighted = grad_mixed * mix_gain
        grad_last = rms_scale * (
            weighted
            - last_layer
            * rms_scale
            * rms_scale
            * jnp.mean(weighted * last_layer, axis=-1, keepdims=True)
        )
        per_layer = [
            jnp.sum(coef_rows[:, :, layer_index, None] * grad_streams, axis=1)
            for layer_index in range(STREAMS_IN)
        ]
        per_layer[STREAMS_IN - 1] = per_layer[STREAMS_IN - 1] + grad_last
        grad_list.append(jnp.stack(per_layer, axis=1).astype(jnp.bfloat16))
        attention_shards = (
            lax.psum_scatter(
                grad_mix_up.astype(jnp.bfloat16), "fsdp", scatter_dimension=0, tiled=True
            ).astype(jnp.float32),
            lax.psum_scatter(
                grad_projection.astype(jnp.bfloat16), "fsdp", scatter_dimension=1, tiled=True
            ).astype(jnp.float32),
            lax.psum_scatter(
                grad_out_weight.astype(jnp.bfloat16), "fsdp", scatter_dimension=0, tiled=True
            ).astype(jnp.float32),
        )
        shards = attention_shards + feed_shards
        shards = jax.tree.map(
            lambda part: part.astype(jnp.float32), lax.psum(as_sent(shards), "replica")
        )
        smalls = (gain_mix_grad, down_mix_grad, static_grad, gain_grad, bias_grad)
        if shard_total is None:
            shard_total = shards
            small_total = smalls
        else:
            shard_total = tuple(
                (total_item + new_item for total_item, new_item in zip(shard_total, shards))
            )
            small_total = tuple(
                (total_item + new_item for total_item, new_item in zip(small_total, smalls))
            )
    small_total = lax.psum(small_total, ("fsdp", "replica"))
    layer_output = jnp.concatenate(output_list, axis=0).reshape(
        micro_total, local_seqs, SEQ, model_width
    )
    coefficients = jnp.concatenate(coef_list, axis=0).reshape(
        micro_total, local_seqs, SEQ, 4, STREAMS_IN
    )
    stack_grad = jnp.concatenate(grad_list, axis=0).reshape(
        micro_total, local_seqs, SEQ, STREAMS_IN, model_width
    )
    return (
        layer_output,
        coefficients,
        stack_grad,
        small_total[0],
        shard_total[0],
        small_total[1],
        small_total[2],
        small_total[3],
        small_total[4],
        shard_total[1],
        shard_total[2],
        shard_total[3],
        shard_total[4],
    )


ROWS = 128
WIDTH = 1024
VMEM_FULL = pl.BlockSpec(memory_space=pltpu.VMEM)
SMEM_FULL = pl.BlockSpec(memory_space=pltpu.SMEM)
IN_PLACE = pl.BlockSpec(memory_space=pl.ANY)


def bits_swap(size, bit):
    return [(index, index ^ bit) for index in range(size)]


CORE_SWAP = bits_swap(4, 1)
X_SWAP = bits_swap(4, 2)
Y_SWAP = bits_swap(8, 1)
Z_SWAP_NEAR = bits_swap(8, 2)
Z_SWAP_FAR = bits_swap(8, 4)


def z_pairs(moves):
    return [(2 * src + col, 2 * dst + col) for src, dst in moves for col in range(2)]


def pick(cond, first, second):
    return jnp.where(cond, first, second)


def order_two(flag, own, other, axis):
    first = pick(flag == 0, own, other)
    second = pick(flag == 0, other, own)
    return jnp.concatenate([first, second], axis=axis)


def after(value, *others):
    return lax.optimization_barrier((value,) + others)[0]


Z_NEAR = z_pairs([(0, 1), (1, 0), (2, 3), (3, 2)])
Z_MIDDLE = [
    (index, (index ^ 1) if index // 8 in (0, 3) else (24 - index // 8 * 8 + index % 8))
    for index in range(32)
]


MIDDLE_OR_SIDE = [
    (index, (index ^ 4) if index // 8 in (0, 3) else (24 - index // 8 * 8 + index % 8))
    for index in range(32)
]
SIDE_OR_CORE = [
    (index, (index ^ 1) if index // 8 in (0, 3) else (index ^ 4)) for index in range(32)
]


def fsdp_move(value, pairs):
    return lax.ppermute(value, "fsdp" if len(pairs) == 8 else ("fsdp", "replica"), pairs)


PART = 7


def gather_fsdp(piece, z, front):
    inner = (z == 1) | (z == 2)
    near = fsdp_move(piece, Z_NEAR)
    middle = fsdp_move(piece, MIDDLE_OR_SIDE)
    side = fsdp_move(piece, SIDE_OR_CORE)
    early, late = front()
    middle_near = fsdp_move(after(near, *early, side), Z_MIDDLE)
    turned = fsdp_move(after(middle, *early), Z_NEAR)
    side_two = fsdp_move(pick(inner, middle, near), Y_SWAP)
    third = pick(inner, middle_near, turned)
    near_twice = fsdp_move(after(middle_near, side_two, third), Z_NEAR)
    side_three = fsdp_move(third, Y_SWAP)
    over_z = fsdp_move(side_three[:6], Z_NEAR)
    over_y = fsdp_move(after(near_twice[6:], side_three, *late), Y_SWAP)
    return [
        piece,
        side,
        near,
        middle,
        middle_near,
        turned,
        near_twice,
        side_two,
        side_three,
        over_z,
        over_y,
    ]


def position():
    member, partner = lax.axis_index("fsdp"), lax.axis_index("replica")
    return member // 2, member % 2, partner // 2, partner % 2


def table(values, z):
    found = jnp.int32(values[0])
    for index in range(1, 4):
        found = jnp.where(z == index, jnp.int32(values[index]), found)
    return found


def gather_order(z, y):
    places = []
    for z_from in (z, table([1, 0, 3, 2], z), table([2, 2, 1, 1], z), table([3, 3, 0, 0], z)):
        places += [2 * z_from + y, 2 * z_from + 1 - y]
    return places


def scatter_order(z, y):
    others = (table([3, 0, 3, 0], z), table([2, 3, 0, 1], z), table([1, 2, 1, 2], z), z)
    own = (table([3, 3, 0, 0], z), table([2, 2, 1, 1], z), table([1, 0, 3, 2], z), z)
    return [2 * z_to + 1 - y for z_to in others] + [2 * z_to + y for z_to in own]


def wide(value):
    return value.astype(jnp.float32)


def scatter_fsdp(chunks, z, first_wait, beside):
    inner = (z == 1) | (z == 2)
    side_low, side_high, side_one, side_two, side_own, last, third, near, own = chunks

    def low(value):
        return value.astype(jnp.bfloat16)

    def only(cond, value):
        return jnp.where(cond, wide(value), 0.0)

    over_z = fsdp_move(side_high, Z_NEAR)
    over_y = fsdp_move(side_low, Y_SWAP)
    over_z = jnp.pad(only(inner, over_z), ((PART, 0), (0, 0), (0, 0)))
    back_one = fsdp_move(low(wide(side_one) + over_z), Y_SWAP)
    over_y = jnp.pad(wide(over_y), ((0, 12 - PART), (0, 0), (0, 0)))
    back_far = fsdp_move(low(wide(after(last, first_wait)) + over_y), Z_NEAR)
    back_two = fsdp_move(after(side_two, first_wait), Y_SWAP)
    to_middle = low(wide(last) + wide(back_one) + wide(back_far))
    to_near = low(
        jnp.where(
            inner,
            wide(jnp.concatenate([side_low, side_high])),
            wide(third) + wide(back_one),
        )
    )
    middle_one = fsdp_move(to_middle, Z_MIDDLE)
    near_one = fsdp_move(to_near, Z_NEAR)
    back_own = fsdp_move(low(wide(side_own) + only(z % 3 == 0, near_one)), Y_SWAP)
    to_near = low(wide(near) + jnp.where(inner, wide(middle_one), wide(back_two)))
    to_middle = low(wide(third) + wide(back_two) + wide(near_one))
    to_near, to_middle, _ = lax.optimization_barrier((to_near, to_middle, beside()))
    near_two = fsdp_move(to_near, Z_NEAR)
    middle_two = fsdp_move(to_middle, Z_MIDDLE)
    return low(wide(own) + wide(back_own) + wide(near_two) + only(inner, middle_two))


def lanes_of(shape):
    return lax.broadcasted_iota(jnp.int32, shape, 1)


def rows_of(shape):
    return lax.broadcasted_iota(jnp.int32, shape, 0)


def prepare_kernel(
    projection,
    out_weight,
    up_weight,
    down_weight,
    piece,
    up_own,
    up_lent,
    heads,
    down_own,
    down_lent,
    out_rows,
    sems,
):
    _, member_parity, x, core = position()
    quarter, other = 2 * x + core, 2 * x + 1 - core
    copies = []

    def fetch(source, goal):
        copies.append(pltpu.make_async_copy(source, goal, sems.at[len(copies)]))
        copies[-1].start()

    def tile(place):
        return pl.ds(pl.multiple_of(place * 128, 128), 128)

    for index in range(8):
        fetch(up_weight.at[:, tile(index * 4 + quarter)], up_own.at[index])
    for pair in range(4):
        fetch(up_weight.at[:, tile((2 * pair + 1 - core) * 4 + other)], up_lent.at[pair])
    for low in range(4):
        fetch(projection.at[:, :, tile(low * 2 + core)], heads.at[:, low])
    fetch(down_weight.at[tile(quarter)], down_own)
    fetch(down_weight.at[pl.ds(pl.multiple_of(other * 128 + 96, 32), 32)], down_lent)
    fetch(out_weight.at[pl.ds(pl.multiple_of(x * 64, 64), 64)], out_rows)
    for copy in copies:
        copy.wait()
    lane = lanes_of((128, 128))
    for index in range(8):
        half = index % 2
        taken = (lane >= 96) & (core == half)
        piece[index // 2, :, half * 128 : half * 128 + 128] = jnp.where(
            taken, wide(up_lent[index // 2]), wide(up_own[index])
        ).astype(jnp.bfloat16)
    for stream in range(3):
        for twin in range(2):
            tiles = [wide(heads[stream, 2 * twin + low]) for low in range(2)]
            first = jnp.where(x == 0, tiles[0], pltpu.roll(tiles[0], 64, 1))
            second = jnp.where(x == 0, pltpu.roll(tiles[1], 64, 1), tiles[1])
            piece[4 + stream, :, twin * 128 : twin * 128 + 128] = jnp.where(
                lane < 64, first, second
            ).astype(jnp.bfloat16)
    for block in range(4):
        cols = slice(block * 256, block * 256 + 256)
        band = slice(block * 32, block * 32 + 32)
        piece[7 + block, 0:96] = down_own[0:96, cols]

        @pl.when(member_parity == core)
        def _():
            piece[7 + block, 96:128] = out_rows[0:32, cols]
            piece[11, band] = out_rows[32:64, cols]

        @pl.when(member_parity != core)
        def _():
            piece[7 + block, 96:128] = down_own[96:128, cols]
            piece[11, band] = down_lent[:, cols]


def front_kernel(
    bounds,
    stack,
    mix_gain,
    up_own,
    up_one,
    up_two,
    up_three,
    mix_down,
    mix_static,
    norm_gain,
    norm_bias,
    packet,
    scaled_out,
    stats,
    stream_out,
    mix_up,
    streams,
):
    seqs = stack.shape[0]
    z, y, _, core = position()
    for step, part in ((0, up_own), (1 + 2 * core, up_one), (2, up_two), (3 - 2 * core, up_three)):
        z_from = (z + step) % 4
        for half, col in enumerate((y, 1 - y)):
            lanes = pl.ds(pl.multiple_of((2 * z_from + col) * 128, 128), 128)
            mix_up[:, lanes] = part[:, half * 128 : half * 128 + 128]
    for seq in range(seqs):
        last = wide(stack[seq, STREAMS_IN - 1])
        rms = lax.rsqrt(jnp.mean(last * last, axis=-1, keepdims=True) + EPSILON)
        mixed_in = (last * rms * mix_gain[...]).astype(jnp.bfloat16)
        hidden_pre = back_product(mixed_in, mix_up[...])
        hidden = wide(gelu_value(hidden_pre).astype(jnp.bfloat16))
        coef = jnp.dot(
            hidden, mix_down[...], precision=HIGHEST, preferred_element_type=jnp.float32
        )
        coef = coef + mix_static[...]
        at = slice(seq * SEQ, seq * SEQ + SEQ)
        stats[0, at, 0:36] = coef
        stats[1, at, 0:36] = hidden_pre
        stats[2, at, 4:5] = rms

        def mix(step, carry):
            row = pl.multiple_of(step // 2 * 16, 16)
            col = pl.multiple_of(step % 2 * 512, 512)
            rows_coef = stats[0, pl.ds(seq * SEQ + row, 16), :]
            totals = [None] * 4
            for layer in range(STREAMS_IN):
                value = wide(stack[seq, layer, pl.ds(row, 16), pl.ds(col, 512)])
                for stream in range(4):
                    at_coef = stream * STREAMS_IN + layer
                    term = rows_coef[:, at_coef : at_coef + 1] * value
                    totals[stream] = term if layer == 0 else totals[stream] + term
            for stream in range(4):
                streams[stream, pl.ds(seq * SEQ + row, 16), pl.ds(col, 512)] = totals[stream]
            return carry

        lax.fori_loop(0, 8, mix, 0)

    def norm(step, carry):
        row = pl.multiple_of(step * 16, 16)
        for stream in range(4):
            value = streams[stream, pl.ds(row, 16), :]
            center = value - jnp.mean(value, axis=-1, keepdims=True)
            inverse = lax.rsqrt(jnp.mean(center * center, axis=-1, keepdims=True) + EPSILON)
            scaled = center * inverse
            stats[2, pl.ds(row, 16), stream : stream + 1] = inverse
            scaled_out[stream, pl.ds(row, 16), :] = scaled
            packet[pl.ds(stream * ROWS + row, 16), :] = (
                scaled * norm_gain[stream : stream + 1, :] + norm_bias[stream : stream + 1, :]
            ).astype(jnp.bfloat16)
            if stream == 3:
                stream_out[pl.ds(row, 16), :] = value
        return carry

    lax.fori_loop(0, seqs * SEQ // 16, norm, 0)
    packet[4 * ROWS :] = jnp.zeros((16, WIDTH), jnp.bfloat16)
    row = rows_of((16, 128))
    marks = jnp.zeros((16, 128), jnp.float32)
    for place in range(2 * seqs):
        marks = jnp.where(row == place, wide(bounds[place]), marks)
    packet[4 * ROWS :, 0:128] = marks.astype(jnp.bfloat16)


def main_kernel(
    rope,
    packet0,
    packet1,
    packet2,
    packet3,
    cotangent0,
    cotangent1,
    cotangent2,
    cotangent3,
    piece0,
    piece1,
    piece2,
    piece3,
    piece4,
    piece5,
    piece6,
    piece7,
    piece8,
    piece9,
    piece10,
    chunk_low,
    chunk_high,
    chunk1,
    chunk2,
    chunk3,
    chunk4,
    chunk5,
    chunk6,
    chunk7,
    keep_own,
    keep_far,
    send_norm,
    keep_out,
    send_out,
    acts,
    marks,
    up_all,
    lin_all,
    down_all,
    out_rows,
    lhs_all,
    grad_pre,
    linear,
    grad_att,
    grad_lin,
    parts,
    tokens,
    packet_sems,
    piece_sems,
    chunk_sems,
    token_sems,
):
    z, y, _, core = position()
    origin = gather_order(z, y)
    target = scatter_order(z, y)
    packets = (packet0, packet1, packet2, packet3)
    cotangents = (cotangent0, cotangent1, cotangent2, cotangent3)
    piece, side, near, middle, middle_near, turned = piece0, piece1, piece2, piece3, piece4, piece5
    near_twice, side_two, side_three, over_z, over_y = piece6, piece7, piece8, piece9, piece10
    inner = (z == 1) | (z == 2)
    sources = (
        (piece, piece),
        (side, middle),
        (near, near),
        (turned, side_two),
        (middle, turned),
        (side_two, side_three),
        (middle_near, near_twice),
        (side_three, None),
    )
    chunks = (chunk1, chunk2, chunk3, chunk4, chunk5, chunk6, chunk7)
    member_rows = [pl.ds(pl.multiple_of(place * 128, 128), 128) for place in origin]

    def unit_copies(unit):
        return [
            pltpu.make_async_copy(
                packets[block].at[pl.ds(unit * ROWS, ROWS)],
                acts.at[unit, pl.ds(block * ROWS, ROWS)],
                packet_sems.at[block, unit],
            )
            for block in range(4)
        ]

    def piece_copies(index, ref, tail_ref):
        rows = member_rows[index]
        down = 7 if tail_ref is ref else 1
        lin_copies = [
            pltpu.make_async_copy(
                source.at[pl.ds(at, count)],
                lin_all.at[pl.ds(stream, count), rows],
                piece_sems.at[index, place],
            )
            for place, source, at, stream, count in (
                (0, ref, 4, 0, 2),
                (3, tail_ref, down - 1, 2, 1),
            )
        ]
        return lin_copies + [
            pltpu.make_async_copy(
                tail_ref.at[pl.ds(down, 5)], down_all.at[origin[index]], piece_sems.at[index, 1]
            ),
            pltpu.make_async_copy(
                ref.at[pl.ds(0, 4)], up_all.at[:, rows], piece_sems.at[index, 2]
            ),
        ]

    first = unit_copies(0) + unit_copies(1) + unit_copies(2)
    second = [
        pltpu.make_async_copy(
            cotangents[block],
            acts.at[4, pl.ds(block * ROWS, ROWS)],
            packet_sems.at[block, 4],
        )
        for block in range(4)
    ]
    for block in range(4):
        second.append(
            pltpu.make_async_copy(
                packets[block].at[pl.ds(4 * ROWS, 16)], marks.at[block], packet_sems.at[block, 5]
            )
        )
    third = unit_copies(3)
    for copy in first + second + third:
        copy.start()
    for index, (for_inner, for_ends) in enumerate(sources):
        copies = piece_copies(index, for_inner, for_inner)
        first += copies[:2]
        second.append(copies[2])
        third.append(copies[3])
        if for_inner is for_ends:
            for copy in copies:
                copy.start()
            continue
        ends = (
            piece_copies(index, over_z, over_y)
            if for_ends is None
            else piece_copies(index, for_ends, for_ends)
        )

        @pl.when(inner)
        def _():
            for copy in copies:
                copy.start()

        @pl.when(jnp.logical_not(inner))
        def _():
            for copy in ends:
                copy.start()

    for copy in first:
        copy.wait()
    for stream in range(3):
        linear[stream] = matmul(acts[stream], lin_all[stream])
    for copy in second:
        copy.wait()
    for pair in range(4):
        even = 2 * pair + core
        odd = 2 * pair + 1 - core
        for block in range(4):
            band = slice(block * 32, block * 32 + 32)
            cols = slice(block * 256, block * 256 + 256)
            out_rows[pair * 64 : pair * 64 + 32, cols] = down_all[even, block, 96:128]
            out_rows[pair * 64 + 32 : pair * 64 + 64, cols] = down_all[even, 4, band]
            down_all[even, block, 96:128] = down_all[odd, 4, band]

    grad_att[...] = back_product(acts[4], out_rows[...]).astype(jnp.bfloat16)
    cos_table = rope[0]
    sin_left = rope[1]
    sin_right = rope[2]
    scale = HEAD_DIM ** (-0.5)

    def turn(value, sign):
        return (
            value * cos_table
            + pltpu.roll(value, 120, 1) * (sign * sin_left)
            + pltpu.roll(value, 8, 1) * (sign * sin_right)
        )

    def units(block, carry):
        row = rows_of((ROWS, ROWS))
        lane = lanes_of((ROWS, ROWS))
        bound = wide(marks[block])

        def both(low, high):
            return jnp.where(row < SEQ, low, high), jnp.where(lane < SEQ, low, high)

        start_q, start_k = both(bound[0:1, 0:128], bound[1:2, 0:128])
        split_q, split_k = both(bound[2:3, 0:128], bound[3:4, 0:128])
        at_q = wide(row % SEQ)
        at_k = wide(lane % SEQ)
        same = (row // SEQ == lane // SEQ) & ((at_q >= split_q) == (at_k >= split_k))
        pic_q = (at_q >= start_q) & (at_q < start_q + PIC)
        pic_k = (at_k >= start_k) & (at_k < start_k + PIC)
        penalty = jnp.where(same & ((at_q >= at_k) | (pic_q & pic_k)), 0.0, -1e30)
        span = pl.ds(pl.multiple_of(block * ROWS, ROWS), ROWS)
        twins = [slice(twin * 128, twin * 128 + 128) for twin in range(2)]
        heads = [(twin, head) for twin in range(2) for head in range(2)]
        query = [turn(linear[0, span, cols], 1.0) for cols in twins]
        query_low = [item.astype(jnp.bfloat16) for item in query]
        key_low = [turn(linear[1, span, cols], 1.0).astype(jnp.bfloat16) for cols in twins]
        value_low = [linear[2, span, cols].astype(jnp.bfloat16) for cols in twins]
        grad_low = [grad_att[span, cols] for cols in twins]

        def only(item, head):
            return jnp.where(lane // 64 == head, wide(item), 0.0).astype(jnp.bfloat16)

        scores = [
            back_product(only(query[twin], head), key_low[twin]) * scale + penalty
            for twin, head in heads
        ]
        grad_probs = [
            back_product(only(grad_low[twin], head), value_low[twin]) for twin, head in heads
        ]
        exponent = [jnp.exp(item - jnp.max(item, axis=-1, keepdims=True)) for item in scores]
        probs = [item / jnp.sum(item, axis=-1, keepdims=True) for item in exponent]
        probs_low = [item.astype(jnp.bfloat16) for item in probs]
        grad_scores = [
            (prob * (grad - jnp.sum(prob * grad, axis=-1, keepdims=True))).astype(jnp.bfloat16)
            for prob, grad in zip(probs, grad_probs)
        ]
        attended = [matmul(probs_low[i], value_low[heads[i][0]]) for i in range(4)]
        grad_value = [outer_sum(probs_low[i], grad_low[heads[i][0]]) for i in range(4)]
        grad_query = [matmul(grad_scores[i], key_low[heads[i][0]]) for i in range(4)]
        grad_key = [outer_sum(grad_scores[i], query_low[heads[i][0]]) for i in range(4)]

        def merge(items, twin):
            return jnp.where(lane < 64, items[2 * twin], items[2 * twin + 1])

        for twin, cols in enumerate(twins):
            side = slice(WIDTH + twin * 128, WIDTH + twin * 128 + 128)
            lhs_all[span, side] = merge(attended, twin).astype(jnp.bfloat16)
            grad_lin[0, span, cols] = turn(merge(grad_query, twin) * scale, -1.0).astype(
                jnp.bfloat16
            )
            grad_lin[1, span, cols] = turn(merge(grad_key, twin) * scale, -1.0).astype(
                jnp.bfloat16
            )
            grad_lin[2, span, cols] = merge(grad_value, twin).astype(jnp.bfloat16)
        return carry

    lax.fori_loop(0, 4, units, 0, unroll=2)

    for copy in third:
        copy.wait()

    def hidden(pair, carry):
        cols = pl.ds(pl.multiple_of(pair * 256, 256), 256)
        up_pre = matmul(acts[3], up_all[pair])
        bell = 0.5 * (1.0 + lax.erf(up_pre * ROOT_HALF))
        slope = bell + up_pre * NORMAL_PEAK * jnp.exp(-0.5 * up_pre * up_pre)
        lhs_all[:, cols] = (up_pre * bell).astype(jnp.bfloat16)
        rows_down = jnp.concatenate(
            [
                jnp.concatenate([down_all[2 * pair + half, block] for block in range(4)], axis=1)
                for half in range(2)
            ]
        )
        grad_gated = back_product(acts[4], rows_down)
        grad_pre[:, cols] = (grad_gated * slope).astype(jnp.bfloat16)
        return carry

    lax.fori_loop(0, 4, hidden, 0, unroll=4)

    def weights(pair, carry):
        cols = pl.ds(pl.multiple_of(pair * 256, 256), 256)
        halves = (slice(0, 128), slice(128, 256))
        grad = outer_sum(acts[3, :, cols], grad_pre[...]).astype(jnp.bfloat16)
        for block in range(4):
            for half, rows in enumerate(halves):
                parts[2 * pair + half, block] = grad[rows, block * 256 : block * 256 + 256]
        for stream in range(3):
            grad = outer_sum(acts[stream, :, cols], grad_lin[stream]).astype(jnp.bfloat16)
            for half, rows in enumerate(halves):
                parts[2 * pair + half, 4 + stream] = grad[rows]
        grad = outer_sum(lhs_all[:, cols], acts[4]).astype(jnp.bfloat16)
        for half in range(2):
            index, other = 2 * pair + half, 2 * pair + 1 - half
            for block in range(4):
                part = grad[half * 128 : half * 128 + 128, block * 256 : block * 256 + 256]
                parts[index, 7 + block, 0:96] = part[0:96]

                @pl.when(core == half)
                def _():
                    parts[other, 11, block * 32 : block * 32 + 32] = part[96:128]

                @pl.when(core != half)
                def _():
                    parts[index, 7 + block, 96:128] = part[96:128]

        return carry

    lax.fori_loop(0, 4, weights, 0, unroll=2)
    grad = outer_sum(lhs_all[:, WIDTH:], acts[4]).astype(jnp.bfloat16)
    for block in range(4):
        part = grad[:, block * 256 : block * 256 + 256]
        for pair in range(4):
            even = 2 * pair + core
            parts[even, 7 + block, 96:128] = part[pair * 64 : pair * 64 + 32]
            parts[even, 11, block * 32 : block * 32 + 32] = part[pair * 64 + 32 : pair * 64 + 64]
    sent = [
        pltpu.make_async_copy(
            parts.at[target[0], pl.ds(0, PART)], chunk_low, chunk_sems.at[0]
        ),
        pltpu.make_async_copy(
            parts.at[target[0], pl.ds(PART, 12 - PART)], chunk_high, chunk_sems.at[8]
        ),
    ] + [
        pltpu.make_async_copy(parts.at[target[index]], chunks[index - 1], chunk_sems.at[index])
        for index in range(1, 8)
    ]
    for copy in sent:
        copy.start()

    def put(unit, cols, value):
        low = value.astype(jnp.bfloat16)
        for half in range(2):
            for block in range(2):
                at = (2 * half + block) * ROWS
                tokens[half, block, unit, :, cols] = low[at : at + ROWS]

    def ship(unit):
        if unit < 4:
            routes = (
                (tokens.at[0, 0, unit], keep_own.at[unit]),
                (tokens.at[0, 1, unit], keep_far.at[unit]),
                (tokens.at[1, :, unit], send_norm.at[:, unit]),
            )
        else:
            routes = ((tokens.at[0, :, unit], keep_out), (tokens.at[1, :, unit], send_out))
        for place, (source, goal) in enumerate(routes):
            copy = pltpu.make_async_copy(source, goal, token_sems.at[place, unit])
            copy.start()
            sent.append(copy)

    for stream in range(3):
        put(stream, slice(0, WIDTH), back_product(grad_lin[stream], lin_all[stream]))
        ship(stream)

    def feed(block, carry):
        cols = pl.ds(pl.multiple_of(block * 256, 256), 256)
        rows_up = jnp.concatenate([up_all[part, cols] for part in range(4)], axis=1)
        put(3, cols, back_product(grad_pre[...], rows_up))
        right = [down_all[index, block] for index in range(8)] + [out_rows[:, cols]]
        put(4, cols, matmul(lhs_all[...], jnp.concatenate(right)))
        return carry

    lax.fori_loop(0, 4, feed, 0, unroll=2)
    ship(3)
    ship(4)
    for copy in sent:
        copy.wait()


def back_kernel(
    stack,
    cotangent,
    scaled,
    stats,
    keep,
    came,
    across,
    mix_gain,
    mix_up,
    mix_down,
    norm_gain,
    stack_grad,
    small_own,
    small_other,
    coefficients,
    grads,
    sums,
    coef_grad,
    small,
):
    seqs = stack.shape[0]
    sums[...] = jnp.zeros_like(sums)
    lane = lanes_of((16, 128))

    def unit(step, carry):
        row = pl.multiple_of(step * 16, 16)
        span = pl.ds(row, 16)

        def result(index):
            return wide(keep[index, span]) + wide(came[0, index, span]) + wide(across[index, span])

        for stream in range(4):
            item = result(stream)
            scale = scaled[stream, span]
            moved = item * scale
            sums[stream] += moved[:8] + moved[8:]
            sums[4 + stream] += item[:8] + item[8:]
            weighted = item * norm_gain[stream : stream + 1]
            mean = jnp.mean(weighted, axis=-1, keepdims=True)
            slant = jnp.mean(weighted * scale, axis=-1, keepdims=True)
            grad = stats[2, span, stream : stream + 1] * (weighted - mean - scale * slant)
            if stream == 3:
                grad = grad + wide(cotangent[span])
            grads[stream, span] = grad
        return carry

    lax.fori_loop(0, seqs * SEQ // 16, unit, 0)
    for seq in range(seqs):

        def coefs(step, carry):
            row = pl.multiple_of(step * 16, 16)
            span = pl.ds(seq * SEQ + row, 16)
            found = jnp.zeros((16, 128), jnp.float32)
            for layer in range(STREAMS_IN):
                value = wide(stack[seq, layer, pl.ds(row, 16), :])
                for stream in range(4):
                    got = jnp.sum(grads[stream, span] * value, axis=-1, keepdims=True)
                    found = jnp.where(lane == stream * STREAMS_IN + layer, got, found)
            coef_grad[span] = found
            return carry

        lax.fori_loop(0, SEQ // 16, coefs, 0)
    grad_coef = coef_grad[:, 0:36]
    hidden_pre = stats[1, :, 0:36]
    hidden_low = gelu_value(hidden_pre).astype(jnp.bfloat16)
    for seq in range(seqs):
        turned = stats[0, seq * SEQ : seq * SEQ + SEQ, :].T
        for stream in range(4):
            for layer in range(STREAMS_IN):
                at = stream * STREAMS_IN + layer
                coefficients[seq, layer, stream : stream + 1] = turned[at : at + 1]
    small[...] = jnp.zeros_like(small)
    small[0:36, WIDTH : WIDTH + 36] = lax.dot_general(
        wide(hidden_low),
        grad_coef,
        (((0,), (0,)), ((), ())),
        precision=HIGHEST,
        preferred_element_type=jnp.float32,
    )
    small[36:37, WIDTH : WIDTH + 36] = jnp.sum(grad_coef, axis=0, keepdims=True)
    grad_hidden = (
        lax.dot_general(
            grad_coef,
            mix_down[...],
            (((1,), (1,)), ((), ())),
            precision=HIGHEST,
            preferred_element_type=jnp.float32,
        )
        * gelu_slope(hidden_pre)
    ).astype(jnp.bfloat16)
    gain_row = jnp.zeros((8, WIDTH), jnp.float32)
    up_part = jnp.zeros((36, WIDTH), jnp.float32)
    for seq in range(seqs):
        at = slice(seq * SEQ, seq * SEQ + SEQ)
        last = wide(stack[seq, STREAMS_IN - 1])
        rms = stats[2, at, 4:5]
        mixed_in = (last * rms * mix_gain[...]).astype(jnp.bfloat16)
        up_part = up_part + outer_sum(grad_hidden[at], mixed_in)
        grad_mixed = matmul(grad_hidden[at], mix_up[...])
        along = grad_mixed * last * rms
        for place in range(SEQ // 8):
            gain_row = gain_row + along[place * 8 : place * 8 + 8]
        weighted = grad_mixed * mix_gain[...]
        mean = jnp.mean(weighted * last, axis=-1, keepdims=True)
        grads[4, at] = rms * (weighted - last * (rms * rms * mean))

        def layers(step, carry):
            row = pl.multiple_of(step // 2 * 16, 16)
            cols = pl.ds(pl.multiple_of(step % 2 * 512, 512), 512)
            span = pl.ds(seq * SEQ + row, 16)
            rows_coef = stats[0, span, :]
            parts = [grads[stream, span, cols] for stream in range(4)]
            for layer in range(STREAMS_IN):
                total = None
                for stream in range(4):
                    at_coef = stream * STREAMS_IN + layer
                    term = rows_coef[:, at_coef : at_coef + 1] * parts[stream]
                    total = term if total is None else total + term
                if layer == STREAMS_IN - 1:
                    total = total + grads[4, span, cols]
                stack_grad[seq, layer, pl.ds(row, 16), cols] = total.astype(jnp.bfloat16)
            return carry

        lax.fori_loop(0, 8, layers, 0)
    small[0:36, 0:WIDTH] = up_part
    for place in range(8):
        small[36 + place : 37 + place, 0:WIDTH] = jnp.sum(sums[place], axis=0, keepdims=True)
    small[44:45, 0:WIDTH] = jnp.sum(gain_row, axis=0, keepdims=True)
    _, _, _, core = position()
    small_own[...] = small[pl.ds(pl.multiple_of(core * 24, 8), 24), :]
    small_other[...] = small[pl.ds(pl.multiple_of(24 - core * 24, 8), 24), :]


def place_kernel(
    shard0,
    shard1,
    shard2,
    shard3,
    small_own,
    small_other,
    projection,
    out_grad,
    up_grad,
    down_grad,
    mix_gain_grad,
    mix_up_grad,
    mix_down_grad,
    mix_static_grad,
    gain_grad,
    bias_grad,
    small,
):
    z, member_parity, x, core = position()
    small[pl.ds(pl.multiple_of(core * 24, 8), 24), :] = small_own[...]
    small[pl.ds(pl.multiple_of(24 - core * 24, 8), 24), :] = small_other[...]
    lanes = pl.ds(pl.multiple_of((2 * z + member_parity) * 128, 128), 128)
    mix_up_grad[...] = small[0:36, lanes]
    gain_grad[...] = small[36:40, 0:WIDTH]
    bias_grad[...] = small[40:44, 0:WIDTH]
    mix_gain_grad[...] = small[44:45, 0:WIDTH]
    mix_down_grad[...] = small[0:36, WIDTH : WIDTH + 36]
    for stream in range(4):
        at = WIDTH + stream * STREAMS_IN
        mix_static_grad[stream : stream + 1] = small[36:37, at : at + STREAMS_IN]
    shards = (shard0, shard1, shard2, shard3)
    lane = lanes_of((128, 128))
    for back in range(4):
        from_x = x if back % 2 == 0 else 1 - x
        from_core = core if back < 2 else 1 - core
        quarter = 2 * from_x + from_core
        own, twin = shards[back], shards[back ^ 2]
        for index in range(8):
            half = index % 2
            mine = wide(own[index // 2, :, half * 128 : half * 128 + 128])
            half_b = 1 - half
            lent = wide(twin[index // 2, :, half_b * 128 : half_b * 128 + 128])
            col = pl.multiple_of((index * 4 + quarter) * 128, 128)
            up_grad[:, pl.ds(col, 128)] = jnp.where(
                (lane >= 96) & (from_core == half), lent, mine
            )
        row = pl.multiple_of(quarter * 128, 128)
        for block in range(4):
            cols = slice(block * 256, block * 256 + 256)
            down_grad[pl.ds(row, 96), cols] = wide(own[7 + block, 0:96])

            @pl.when(member_parity == from_core)
            def _():
                head_row = pl.multiple_of(from_x * 64, 64)
                out_grad[pl.ds(head_row, 32), cols] = wide(own[7 + block, 96:128])
                out_grad[pl.ds(head_row + 32, 32), cols] = wide(
                    own[11, block * 32 : block * 32 + 32]
                )
                down_grad[pl.ds(row + 96, 32), cols] = wide(
                    twin[11, block * 32 : block * 32 + 32]
                )

            @pl.when(member_parity != from_core)
            def _():
                down_grad[pl.ds(row + 96, 32), cols] = wide(own[7 + block, 96:128])

    for back in (0, 2):
        from_core = core if back < 2 else 1 - core
        for stream in range(3):
            for twin in range(2):
                tile = slice(twin * 128, twin * 128 + 128)
                mine = wide(shards[back][4 + stream, :, tile])
                across = wide(shards[back + 1][4 + stream, :, tile])
                even = jnp.where(x == 0, mine, across)
                odd = jnp.where(x == 0, across, mine)
                first = jnp.where(lane < 64, even, pltpu.roll(odd, 64, 1))
                second = jnp.where(lane < 64, pltpu.roll(even, 64, 1), odd)
                for low, value in ((0, first), (1, second)):
                    col = pl.multiple_of((2 * twin + low) * 256 + from_core * 128, 128)
                    projection[stream, :, pl.ds(col, 128)] = value


def call(kernel, outs, specs, out_specs, args, scratch=(), cost=None, vmem=60 << 20):
    return pl.pallas_call(
        kernel,
        out_shape=outs,
        in_specs=specs,
        out_specs=out_specs,
        scratch_shapes=list(scratch),
        compiler_params=pltpu.CompilerParams(vmem_limit_bytes=vmem),
        cost_estimate=cost,
    )(*args)


def shape_of(shape, dtype=jnp.bfloat16):
    return jax.ShapeDtypeStruct(shape, dtype)


def rope_tables():
    half_rot = ROTARY // 2
    step = 10000.0 ** (-2.0 * np.arange(half_rot) / ROTARY)
    angles = np.arange(SEQ)[:, None] * step[None, :]
    cos_table = np.ones((SEQ, HEAD_DIM))
    left = np.zeros((SEQ, HEAD_DIM))
    right = np.zeros((SEQ, HEAD_DIM))
    cos_table[:, :half_rot] = np.cos(angles)
    cos_table[:, half_rot:ROTARY] = np.cos(angles)
    left[:, :half_rot] = -np.sin(angles)
    right[:, half_rot:ROTARY] = np.sin(angles)
    return np.stack([np.tile(item, (2, 2)) for item in (cos_table, left, right)]).astype(np.float32)


def on_device_tensor(
    layer_stack,
    out_cotangent,
    pic_start,
    doc_split,
    mix_gain,
    mix_up,
    mix_down,
    mix_static,
    norm_gain,
    norm_bias,
    query_key_value,
    out_weight,
    up_weight,
    down_weight,
):
    z, y, _, _ = position()
    micro_total, local_seqs, _, _, width = layer_stack.shape
    seqs = micro_total * local_seqs
    stack = jnp.transpose(layer_stack, (0, 1, 3, 2, 4)).reshape(seqs, STREAMS_IN, SEQ, width)
    cotangent = out_cotangent.reshape(ROWS, width)
    gain_row = mix_gain.reshape(1, width)

    piece = call(
        prepare_kernel,
        shape_of((12, 128, 256)),
        [IN_PLACE] * 4,
        VMEM_FULL,
        (query_key_value, out_weight, up_weight, down_weight),
        scratch=[
            pltpu.VMEM((8, 128, 128), jnp.bfloat16),
            pltpu.VMEM((4, 128, 128), jnp.bfloat16),
            pltpu.VMEM((3, 4, 128, 128), jnp.bfloat16),
            pltpu.VMEM((128, width), jnp.bfloat16),
            pltpu.VMEM((32, width), jnp.bfloat16),
            pltpu.VMEM((64, width), jnp.bfloat16),
            pltpu.SemaphoreType.DMA((19,)),
        ],
        vmem=60 << 20,
    )
    up_own = mix_up.T
    up_pair = jnp.concatenate([up_own, after(lax.ppermute(up_own, "fsdp", Y_SWAP), piece)], axis=1)
    up_one = fsdp_move(
        up_pair,
        [((index + 8 + index % 2 * 16) % 32, index) for index in range(32)],
    )
    up_two = fsdp_move(up_pair, Z_SWAP_FAR)
    ups = (up_pair, up_one, up_two)
    piece = after(piece, *ups)
    up_three = lax.ppermute(up_one, "replica", CORE_SWAP)
    ups += (up_three,)
    bounds = jnp.concatenate([pic_start.reshape(seqs), doc_split.reshape(seqs)])
    kept = {}
    grad_across = lax.ppermute(cotangent, "replica", X_SWAP)
    grad_packets = (
        cotangent,
        grad_across,
        lax.ppermute(cotangent, "replica", CORE_SWAP),
        lax.ppermute(grad_across, "replica", CORE_SWAP),
    )

    def front():
        packet, *kept["rest"] = call(
            front_kernel,
            (
                shape_of((4 * ROWS + 16, width)),
                shape_of((4, ROWS, width), jnp.float32),
                shape_of((3, ROWS, 128), jnp.float32),
                shape_of((ROWS, width), jnp.float32),
                shape_of((36, width)),
            ),
            [SMEM_FULL] + [VMEM_FULL] * 10,
            (VMEM_FULL,) * 5,
            (
                bounds,
                stack,
                gain_row,
                *ups,
                mix_down,
                mix_static.reshape(1, 36),
                norm_gain,
                norm_bias,
            ),
            scratch=[pltpu.VMEM((4, ROWS, width), jnp.float32)],
            vmem=30 << 20,
        )
        across = lax.ppermute(packet, "replica", X_SWAP)
        beside = lax.ppermute(packet, "replica", CORE_SWAP)
        beside_across = lax.ppermute(across, "replica", CORE_SWAP)
        kept["packets"] = (packet, across, beside, beside_across)
        return (packet, grad_across), (across,)

    pieces = gather_fsdp(piece, z, front)
    packets = kept["packets"]
    scaled, stats, stream_last, mix_up_full = kept["rest"]

    results = call(
        main_kernel,
        (shape_of((PART, 128, 256)), shape_of((12 - PART, 128, 256)))
        + (shape_of((12, 128, 256)),) * 7
        + (shape_of((4, ROWS, width)),) * 2
        + (shape_of((2, 4, ROWS, width)),)
        + (shape_of((2, ROWS, width)),) * 2,
        [VMEM_FULL] + [IN_PLACE] * 19,
        (IN_PLACE,) * 14,
        (jnp.asarray(rope_tables()),) + packets + grad_packets + tuple(pieces),
        scratch=[
            pltpu.VMEM((5, 4 * ROWS, width), jnp.bfloat16),
            pltpu.VMEM((4, 16, width), jnp.bfloat16),
            pltpu.VMEM((4, width, 256), jnp.bfloat16),
            pltpu.VMEM((3, width, 256), jnp.bfloat16),
            pltpu.VMEM((8, 5, 128, 256), jnp.bfloat16),
            pltpu.VMEM((256, width), jnp.bfloat16),
            pltpu.VMEM((4 * ROWS, width + 256), jnp.bfloat16),
            pltpu.VMEM((4 * ROWS, width), jnp.bfloat16),
            pltpu.VMEM((3, 4 * ROWS, 256), jnp.float32),
            pltpu.VMEM((4 * ROWS, 256), jnp.bfloat16),
            pltpu.VMEM((3, 4 * ROWS, 256), jnp.bfloat16),
            pltpu.VMEM((8, 12, 128, 256), jnp.bfloat16),
            pltpu.VMEM((2, 2, 5, ROWS, width), jnp.bfloat16),
            pltpu.SemaphoreType.DMA((4, 6)),
            pltpu.SemaphoreType.DMA((8, 4)),
            pltpu.SemaphoreType.DMA((9,)),
            pltpu.SemaphoreType.DMA((3, 5)),
        ],
        vmem=42 << 20,
    )
    chunks = results[:9]
    keep_own, keep_far, send_norm, keep_out, send_out = results[9:]

    came = lax.ppermute(send_norm, "replica", CORE_SWAP)
    sum_across = (wide(keep_far) + wide(came[1])).astype(jnp.bfloat16)
    came_across = lax.ppermute(sum_across, "replica", X_SWAP)
    out_came = lax.ppermute(after(send_out, sum_across), "replica", CORE_SWAP)
    out_across = (wide(keep_out[1]) + wide(out_came[1])).astype(jnp.bfloat16)
    out_across = lax.ppermute(after(out_across, came_across), "replica", X_SWAP)
    layer_output = (
        stream_last + wide(keep_out[0]) + wide(out_came[0]) + wide(out_across)
    ).astype(jnp.bfloat16)

    first_half = pl.BlockSpec((1, 4, ROWS, width), lambda step: (0, 0, 0, 0))

    def whole(shape):
        return pl.BlockSpec(shape, lambda step: (0,) * len(shape))

    def back():
        kept["back"] = pl.pallas_call(
            back_kernel,
            grid=(1,),
            out_shape=(
                shape_of((seqs, STREAMS_IN, SEQ, width)),
                shape_of((24, width + 128), jnp.float32),
                shape_of((24, width + 128), jnp.float32),
                shape_of((seqs, STREAMS_IN, 4, SEQ), jnp.float32),
            ),
            in_specs=[
                whole((seqs, STREAMS_IN, SEQ, width)),
                whole((ROWS, width)),
                whole((4, ROWS, width)),
                whole((3, ROWS, 128)),
                whole((4, ROWS, width)),
                first_half,
                whole((4, ROWS, width)),
                whole((1, width)),
                whole((36, width)),
                whole((36, 36)),
                whole((4, width)),
            ],
            out_specs=(
                whole((seqs, STREAMS_IN, SEQ, width)),
                whole((24, width + 128)),
                whole((24, width + 128)),
                whole((seqs, STREAMS_IN, 4, SEQ)),
            ),
            scratch_shapes=[
                pltpu.VMEM((5, ROWS, width), jnp.float32),
                pltpu.VMEM((8, 8, width), jnp.float32),
                pltpu.VMEM((ROWS, 128), jnp.float32),
                pltpu.VMEM((48, width + 128), jnp.float32),
            ],
            compiler_params=pltpu.CompilerParams(vmem_limit_bytes=56 << 20),
        )(
            stack,
            cotangent,
            scaled,
            stats,
            keep_own,
            came,
            came_across,
            gain_row,
            mix_up_full,
            mix_down,
            norm_gain,
        )
        return kept["back"][1]

    shard = scatter_fsdp(chunks, z, sum_across, back)
    stack_grad, small, small_other, coefficients = kept["back"]

    small = small + lax.ppermute(small_other, "replica", CORE_SWAP)
    small = small + lax.ppermute(small, "replica", X_SWAP)
    small = small + lax.ppermute(small, "fsdp", Y_SWAP)
    shard = after(shard, small, out_across)
    shard_across = lax.ppermute(shard, "replica", X_SWAP)
    shard_beside = lax.ppermute(shard, "replica", CORE_SWAP)
    for perm in (Z_SWAP_NEAR, Z_SWAP_FAR):
        small = small + lax.ppermute(small, "fsdp", perm)
    small_beside = lax.ppermute(small, "replica", CORE_SWAP)
    shard_both = lax.ppermute(after(shard_across, small), "replica", CORE_SWAP)
    owned = call(
        place_kernel,
        (
            shape_of((3, 128, width), jnp.float32),
            shape_of((128, width), jnp.float32),
            shape_of((128, 4 * width), jnp.float32),
            shape_of((512, width), jnp.float32),
            shape_of((1, width), jnp.float32),
            shape_of((36, 128), jnp.float32),
            shape_of((36, 36), jnp.float32),
            shape_of((4, STREAMS_IN), jnp.float32),
            shape_of((4, width), jnp.float32),
            shape_of((4, width), jnp.float32),
        ),
        [VMEM_FULL] * 6,
        (VMEM_FULL,) * 10,
        (shard, shard_across, shard_beside, shard_both, small, small_beside),
        scratch=[pltpu.VMEM((48, width + 128), jnp.float32)],
        vmem=14 << 20,
    )
    projection_grad, out_grad, up_grad, down_grad, *small_grads = owned
    shape = (micro_total, local_seqs, SEQ)
    stack_grad = stack_grad.reshape(micro_total, local_seqs, STREAMS_IN, SEQ, width)
    coefficients = coefficients.reshape(micro_total, local_seqs, STREAMS_IN, 4, SEQ)
    return (
        layer_output.reshape(shape + (width,)),
        jnp.transpose(coefficients, (0, 1, 4, 3, 2)),
        jnp.transpose(stack_grad, (0, 1, 3, 2, 4)),
        small_grads[0].reshape(width),
        small_grads[1].T,
        small_grads[2],
        small_grads[3],
        small_grads[4],
        small_grads[5],
        projection_grad,
        out_grad,
        up_grad,
        down_grad,
    )


def solution(mesh):
    fits = mesh.shape["fsdp"] == 8 and mesh.shape["replica"] == 4
    body = on_device_tensor if fits else on_device
    return jax.shard_map(
        body,
        mesh=mesh,
        in_specs=(
            P(None, ("fsdp", "replica"), None, None, None),
            P(None, ("fsdp", "replica"), None, None),
            P(None, ("fsdp", "replica")),
            P(None, ("fsdp", "replica")),
            P(),
            P("fsdp", None),
            P(),
            P(),
            P(),
            P(),
            P(None, "fsdp", None),
            P("fsdp", None),
            P("fsdp", None),
            P("fsdp", None),
        ),
        out_specs=(
            P(None, ("fsdp", "replica"), None, None),
            P(None, ("fsdp", "replica"), None, None, None),
            P(None, ("fsdp", "replica"), None, None, None),
            P(),
            P("fsdp", None),
            P(),
            P(),
            P(),
            P(),
            P(None, "fsdp", None),
            P("fsdp", None),
            P("fsdp", None),
            P("fsdp", None),
        ),
        check_vma=False,
    )
```

```python
import math

import jax
import jax.numpy as jnp
import numpy as np
from jax import lax
from jax.experimental import pallas as pl
from jax.experimental.pallas import tpu as pltpu
from jax.sharding import PartitionSpec as P

HEADS = 16
HEAD_DIM = 64
ROTARY = 16
STREAMS_IN = 9
SEQ = 64
PIC = 32


EPSILON = 1e-05
ROOT_HALF = 0.7071067811865476
NORMAL_PEAK = 0.3989422804014327
HIGHEST = lax.Precision.HIGHEST


def as_sent(value):

    def short(part):
        return part.astype(jnp.bfloat16) if part.dtype == jnp.float32 else part

    return jax.tree.map(short, value)


def gelu_value(values):
    return 0.5 * values * (1.0 + lax.erf(values * ROOT_HALF))


def gelu_slope(values):
    return 0.5 * (1.0 + lax.erf(values * ROOT_HALF)) + values * NORMAL_PEAK * jnp.exp(
        -0.5 * values * values
    )


def matmul(left_side, right_side):
    return jnp.dot(left_side, right_side, preferred_element_type=jnp.float32)


def outer_sum(left_side, right_side):
    return lax.dot_general(
        left_side, right_side, (((0,), (0,)), ((), ())), preferred_element_type=jnp.float32
    )


def back_product(left_side, right_side):
    return lax.dot_general(
        left_side, right_side, (((1,), (1,)), ((), ())), preferred_element_type=jnp.float32
    )


def rotary_tables():
    half_rot = ROTARY // 2
    inverse = jnp.exp(-math.log(10000.0) * (2.0 * jnp.arange(half_rot, dtype=jnp.float32) / ROTARY))
    angles = jnp.arange(SEQ, dtype=jnp.float32)[:, None] * inverse[None, :]
    return (jnp.cos(angles)[:, None, :], jnp.sin(angles)[:, None, :])


def rotate(values, cos_table, sin_table):
    half_rot = ROTARY // 2
    first_half = values[..., :half_rot]
    second = values[..., half_rot:ROTARY]
    return jnp.concatenate(
        [
            first_half * cos_table - second * sin_table,
            second * cos_table + first_half * sin_table,
            values[..., ROTARY:],
        ],
        axis=-1,
    )


def allowed_mask(starts, splits):
    positions = jnp.arange(SEQ, dtype=jnp.int32)
    second_doc = positions[None, :] >= splits[:, None]
    picture = (positions[None, :] >= starts[:, None]) & (positions[None, :] < starts[:, None] + PIC)
    same_doc = second_doc[:, :, None] == second_doc[:, None, :]
    causal = positions[:, None] >= positions[None, :]
    both_pic = picture[:, :, None] & picture[:, None, :]
    return same_doc & (causal[None] | both_pic)


def masked_scores(queries, key_rot, allowed):
    scores = jnp.einsum(
        "nqhe,nkhe->nhqk", queries, key_rot, preferred_element_type=jnp.float32
    ) * HEAD_DIM ** (-0.5)
    return jnp.where(allowed[:, None], scores, -1e30)


def on_device(
    layer_stack,
    out_cotangent,
    pic_start,
    doc_split,
    mix_gain,
    mix_up,
    mix_down,
    mix_static,
    norm_gain,
    norm_bias,
    query_key_value,
    out_weight,
    up_weight,
    down_weight,
):
    micro_total = layer_stack.shape[0]
    local_seqs = layer_stack.shape[1]
    model_width = layer_stack.shape[-1]
    groups = [(0, micro_total)]
    cos_table, sin_table = rotary_tables()
    output_list = []
    coef_list = []
    grad_list = []
    shard_total = None
    small_total = None
    for first_micro, micro_count in groups:
        seq_count = micro_count * local_seqs
        row_count = seq_count * SEQ
        head_shape = (seq_count, SEQ, HEADS, HEAD_DIM)
        flat_stack = layer_stack[first_micro : first_micro + micro_count].reshape(
            row_count, STREAMS_IN, model_width
        )
        grad_rows = out_cotangent[first_micro : first_micro + micro_count].reshape(
            row_count, model_width
        )
        starts = pic_start[first_micro : first_micro + micro_count].reshape(seq_count)
        splits = doc_split[first_micro : first_micro + micro_count].reshape(seq_count)
        allowed = allowed_mask(starts, splits)
        mix_up_full, projection_full, out_full = (
            lax.all_gather(mix_up, "fsdp", axis=0, tiled=True),
            lax.all_gather(query_key_value, "fsdp", axis=1, tiled=True),
            lax.all_gather(out_weight, "fsdp", axis=0, tiled=True),
        )
        up_full, down_full = (
            lax.all_gather(up_weight, "fsdp", axis=0, tiled=True),
            lax.all_gather(down_weight, "fsdp", axis=0, tiled=True),
        )
        last_layer = flat_stack[:, STREAMS_IN - 1, :].astype(jnp.float32)
        rms_scale = lax.rsqrt(jnp.mean(last_layer * last_layer, axis=-1, keepdims=True) + EPSILON)
        mixed_in = (last_layer * rms_scale * mix_gain).astype(jnp.bfloat16)
        hidden_pre = matmul(mixed_in, mix_up_full)
        hidden_mix = gelu_value(hidden_pre).astype(jnp.bfloat16)
        hidden_wide = hidden_mix.astype(jnp.float32)
        coef_flat = jnp.dot(hidden_wide, mix_down, precision=HIGHEST) + mix_static.reshape(-1)
        coef_rows = coef_flat.reshape(row_count, 4, STREAMS_IN)
        streams = coef_rows[:, :, 0, None] * flat_stack[:, None, 0, :].astype(jnp.float32)
        for layer_index in range(1, STREAMS_IN):
            streams = streams + coef_rows[:, :, layer_index, None] * flat_stack[
                :, None, layer_index, :
            ].astype(jnp.float32)
        center = streams - jnp.mean(streams, axis=-1, keepdims=True)
        inv_std = lax.rsqrt(jnp.mean(center * center, axis=-1, keepdims=True) + EPSILON)
        scaled = center * inv_std
        normed = (scaled * norm_gain + norm_bias).astype(jnp.bfloat16)
        query_lin = matmul(normed[:, 0], projection_full[0])
        key_lin = matmul(normed[:, 1], projection_full[1])
        value_lin = matmul(normed[:, 2], projection_full[2])
        queries = rotate(query_lin.reshape(head_shape), cos_table, sin_table).astype(jnp.bfloat16)
        key_rot = rotate(key_lin.reshape(head_shape), cos_table, sin_table).astype(jnp.bfloat16)
        values = value_lin.astype(jnp.bfloat16).reshape(head_shape)
        scores = masked_scores(queries, key_rot, allowed)
        row_top = jnp.max(scores, axis=-1, keepdims=True)
        exponent = jnp.exp(scores - row_top)
        row_total = jnp.sum(exponent, axis=-1, keepdims=True)
        soft_probs = exponent / row_total
        log_total = row_top + jnp.log(row_total)
        attended = (
            jnp.einsum(
                "nhqk,nkhe->nqhe",
                soft_probs.astype(jnp.bfloat16),
                values,
                preferred_element_type=jnp.float32,
            )
            .astype(jnp.bfloat16)
            .reshape(row_count, model_width)
        )
        attn_out = matmul(attended, out_full)
        up_pre = matmul(normed[:, 3], up_full)
        gated_act = gelu_value(up_pre).astype(jnp.bfloat16)
        feed_out = matmul(gated_act, down_full)
        output_list.append((streams[:, 3] + attn_out + feed_out).astype(jnp.bfloat16))
        coef_list.append(coef_rows)
        mix_up_back, projection_back, out_back = (
            lax.all_gather(mix_up, "fsdp", axis=0, tiled=True),
            lax.all_gather(query_key_value, "fsdp", axis=1, tiled=True),
            lax.all_gather(out_weight, "fsdp", axis=0, tiled=True),
        )
        up_back, down_back = (
            lax.all_gather(up_weight, "fsdp", axis=0, tiled=True),
            lax.all_gather(down_weight, "fsdp", axis=0, tiled=True),
        )
        grad_down = outer_sum(gated_act, grad_rows)
        grad_gated = back_product(grad_rows, down_back)
        grad_up_pre = (grad_gated * gelu_slope(up_pre)).astype(jnp.bfloat16)
        grad_up = outer_sum(normed[:, 3], grad_up_pre)
        grad_norm_feed = back_product(grad_up_pre, up_back)
        feed_shards = (
            lax.psum_scatter(
                grad_up.astype(jnp.bfloat16), "fsdp", scatter_dimension=0, tiled=True
            ).astype(jnp.float32),
            lax.psum_scatter(
                grad_down.astype(jnp.bfloat16), "fsdp", scatter_dimension=0, tiled=True
            ).astype(jnp.float32),
        )
        grad_out_weight = outer_sum(attended, grad_rows)
        grad_attended = back_product(grad_rows, out_back).astype(jnp.bfloat16).reshape(head_shape)
        scores_again = masked_scores(queries, key_rot, allowed)
        probs_again = jnp.exp(scores_again - log_total)
        grad_probs = jnp.einsum(
            "nqhe,nkhe->nhqk", grad_attended, values, preferred_element_type=jnp.float32
        )
        grad_value = (
            jnp.einsum(
                "nhqk,nqhe->nkhe",
                probs_again.astype(jnp.bfloat16),
                grad_attended,
                preferred_element_type=jnp.float32,
            )
            .astype(jnp.bfloat16)
            .reshape(row_count, model_width)
        )
        delta_rows = jnp.sum(probs_again * grad_probs, axis=-1, keepdims=True)
        grad_scores = (probs_again * (grad_probs - delta_rows)).astype(jnp.bfloat16)
        score_scale = HEAD_DIM ** (-0.5)
        grad_query_rot = (
            jnp.einsum("nhqk,nkhe->nqhe", grad_scores, key_rot, preferred_element_type=jnp.float32)
            * score_scale
        )
        grad_key_rot = (
            jnp.einsum("nhqk,nqhe->nkhe", grad_scores, queries, preferred_element_type=jnp.float32)
            * score_scale
        )
        grad_query = (
            rotate(grad_query_rot, cos_table, -sin_table)
            .astype(jnp.bfloat16)
            .reshape(row_count, model_width)
        )
        grad_key = (
            rotate(grad_key_rot, cos_table, -sin_table)
            .astype(jnp.bfloat16)
            .reshape(row_count, model_width)
        )
        grad_linear = (grad_query, grad_key, grad_value)
        grad_projection = jnp.stack(
            [outer_sum(normed[:, stream], grad_linear[stream]) for stream in range(3)]
        )
        grad_normed = jnp.stack(
            [back_product(grad_linear[stream], projection_back[stream]) for stream in range(3)]
            + [grad_norm_feed],
            axis=1,
        )
        gain_grad = jnp.sum(grad_normed * scaled, axis=0)
        bias_grad = jnp.sum(grad_normed, axis=0)
        grad_scaled = grad_normed * norm_gain
        grad_streams = inv_std * (
            grad_scaled
            - jnp.mean(grad_scaled, axis=-1, keepdims=True)
            - scaled * jnp.mean(grad_scaled * scaled, axis=-1, keepdims=True)
        )
        grad_streams = grad_streams + jnp.concatenate(
            [
                jnp.zeros((row_count, 3, model_width), jnp.float32),
                grad_rows[:, None, :].astype(jnp.float32),
            ],
            axis=1,
        )
        grad_coef = jnp.stack(
            [
                jnp.sum(
                    grad_streams * flat_stack[:, None, layer_index, :].astype(jnp.float32), axis=-1
                )
                for layer_index in range(STREAMS_IN)
            ],
            axis=-1,
        )
        grad_coef_flat = grad_coef.reshape(row_count, 4 * STREAMS_IN)
        static_grad = jnp.sum(grad_coef_flat, axis=0).reshape(4, STREAMS_IN)
        down_mix_grad = jnp.dot(hidden_wide.T, grad_coef_flat, precision=HIGHEST)
        grad_hidden = (
            jnp.dot(grad_coef_flat, mix_down.T, precision=HIGHEST) * gelu_slope(hidden_pre)
        ).astype(jnp.bfloat16)
        grad_mix_up = outer_sum(mixed_in, grad_hidden)
        grad_mixed = back_product(grad_hidden, mix_up_back)
        gain_mix_grad = jnp.sum(grad_mixed * last_layer * rms_scale, axis=0)
        weighted = grad_mixed * mix_gain
        grad_last = rms_scale * (
            weighted
            - last_layer
            * rms_scale
            * rms_scale
            * jnp.mean(weighted * last_layer, axis=-1, keepdims=True)
        )
        per_layer = [
            jnp.sum(coef_rows[:, :, layer_index, None] * grad_streams, axis=1)
            for layer_index in range(STREAMS_IN)
        ]
        per_layer[STREAMS_IN - 1] = per_layer[STREAMS_IN - 1] + grad_last
        grad_list.append(jnp.stack(per_layer, axis=1).astype(jnp.bfloat16))
        attention_shards = (
            lax.psum_scatter(
                grad_mix_up.astype(jnp.bfloat16), "fsdp", scatter_dimension=0, tiled=True
            ).astype(jnp.float32),
            lax.psum_scatter(
                grad_projection.astype(jnp.bfloat16), "fsdp", scatter_dimension=1, tiled=True
            ).astype(jnp.float32),
            lax.psum_scatter(
                grad_out_weight.astype(jnp.bfloat16), "fsdp", scatter_dimension=0, tiled=True
            ).astype(jnp.float32),
        )
        shards = attention_shards + feed_shards
        shards = jax.tree.map(
            lambda part: part.astype(jnp.float32), lax.psum(as_sent(shards), "replica")
        )
        smalls = (gain_mix_grad, down_mix_grad, static_grad, gain_grad, bias_grad)
        if shard_total is None:
            shard_total = shards
            small_total = smalls
        else:
            shard_total = tuple(
                (total_item + new_item for total_item, new_item in zip(shard_total, shards))
            )
            small_total = tuple(
                (total_item + new_item for total_item, new_item in zip(small_total, smalls))
            )
    small_total = lax.psum(small_total, ("fsdp", "replica"))
    layer_output = jnp.concatenate(output_list, axis=0).reshape(
        micro_total, local_seqs, SEQ, model_width
    )
    coefficients = jnp.concatenate(coef_list, axis=0).reshape(
        micro_total, local_seqs, SEQ, 4, STREAMS_IN
    )
    stack_grad = jnp.concatenate(grad_list, axis=0).reshape(
        micro_total, local_seqs, SEQ, STREAMS_IN, model_width
    )
    return (
        layer_output,
        coefficients,
        stack_grad,
        small_total[0],
        shard_total[0],
        small_total[1],
        small_total[2],
        small_total[3],
        small_total[4],
        shard_total[1],
        shard_total[2],
        shard_total[3],
        shard_total[4],
    )


ROWS = 128
WIDTH = 1024
VMEM_FULL = pl.BlockSpec(memory_space=pltpu.VMEM)
SMEM_FULL = pl.BlockSpec(memory_space=pltpu.SMEM)
IN_PLACE = pl.BlockSpec(memory_space=pl.ANY)


def bits_swap(size, bit):
    return [(index, index ^ bit) for index in range(size)]


CORE_SWAP = bits_swap(4, 1)
X_SWAP = bits_swap(4, 2)
Y_SWAP = bits_swap(8, 1)
Z_SWAP_NEAR = bits_swap(8, 2)
Z_SWAP_FAR = bits_swap(8, 4)


def z_pairs(moves):
    return [(2 * src + col, 2 * dst + col) for src, dst in moves for col in range(2)]


def pick(cond, first, second):
    return jnp.where(cond, first, second)


def order_two(flag, own, other, axis):
    first = pick(flag == 0, own, other)
    second = pick(flag == 0, other, own)
    return jnp.concatenate([first, second], axis=axis)


def after(value, *others):
    return lax.optimization_barrier((value,) + others)[0]


Z_NEAR = z_pairs([(0, 1), (1, 0), (2, 3), (3, 2)])
Z_MIDDLE = [
    (index, (index ^ 1) if index // 8 in (0, 3) else (24 - index // 8 * 8 + index % 8))
    for index in range(32)
]


MIDDLE_OR_SIDE = [
    (index, (index ^ 4) if index // 8 in (0, 3) else (24 - index // 8 * 8 + index % 8))
    for index in range(32)
]
SIDE_OR_CORE = [
    (index, (index ^ 1) if index // 8 in (0, 3) else (index ^ 4)) for index in range(32)
]


def fsdp_move(value, pairs):
    return lax.ppermute(value, "fsdp" if len(pairs) == 8 else ("fsdp", "replica"), pairs)


PART = 7


def gather_fsdp(piece, z, front):
    inner = (z == 1) | (z == 2)
    near = fsdp_move(piece, Z_NEAR)
    middle = fsdp_move(piece, MIDDLE_OR_SIDE)
    side = fsdp_move(piece, SIDE_OR_CORE)
    early, late = front()
    middle_near = fsdp_move(after(near, *early, side), Z_MIDDLE)
    turned = fsdp_move(after(middle, *early), Z_NEAR)
    side_two = fsdp_move(pick(inner, middle, near), Y_SWAP)
    third = pick(inner, middle_near, turned)
    near_twice = fsdp_move(after(middle_near, side_two, third), Z_NEAR)
    side_three = fsdp_move(third, Y_SWAP)
    over_z = fsdp_move(side_three[:6], Z_NEAR)
    over_y = fsdp_move(after(near_twice[6:], side_three, *late), Y_SWAP)
    return [
        piece,
        side,
        near,
        middle,
        middle_near,
        turned,
        near_twice,
        side_two,
        side_three,
        over_z,
        over_y,
    ]


def position():
    member, partner = lax.axis_index("fsdp"), lax.axis_index("replica")
    return member // 2, member % 2, partner // 2, partner % 2


def table(values, z):
    found = jnp.int32(values[0])
    for index in range(1, 4):
        found = jnp.where(z == index, jnp.int32(values[index]), found)
    return found


def gather_order(z, y):
    places = []
    for z_from in (z, table([1, 0, 3, 2], z), table([2, 2, 1, 1], z), table([3, 3, 0, 0], z)):
        places += [2 * z_from + y, 2 * z_from + 1 - y]
    return places


def scatter_order(z, y):
    others = (table([3, 0, 3, 0], z), table([2, 3, 0, 1], z), table([1, 2, 1, 2], z), z)
    own = (table([3, 3, 0, 0], z), table([2, 2, 1, 1], z), table([1, 0, 3, 2], z), z)
    return [2 * z_to + 1 - y for z_to in others] + [2 * z_to + y for z_to in own]


def wide(value):
    return value.astype(jnp.float32)


def scatter_fsdp(chunks, z, first_wait, beside):
    inner = (z == 1) | (z == 2)
    side_low, side_high, side_one, side_two, side_own, last, third, near, own = chunks

    def low(value):
        return value.astype(jnp.bfloat16)

    def only(cond, value):
        return jnp.where(cond, wide(value), 0.0)

    over_z = fsdp_move(side_high, Z_NEAR)
    over_y = fsdp_move(side_low, Y_SWAP)
    over_z = jnp.pad(only(inner, over_z), ((PART, 0), (0, 0), (0, 0)))
    back_one = fsdp_move(low(wide(side_one) + over_z), Y_SWAP)
    over_y = jnp.pad(wide(over_y), ((0, 12 - PART), (0, 0), (0, 0)))
    back_far = fsdp_move(low(wide(after(last, first_wait)) + over_y), Z_NEAR)
    back_two = fsdp_move(after(side_two, first_wait), Y_SWAP)
    to_middle = low(wide(last) + wide(back_one) + wide(back_far))
    to_near = low(
        jnp.where(
            inner,
            wide(jnp.concatenate([side_low, side_high])),
            wide(third) + wide(back_one),
        )
    )
    middle_one = fsdp_move(to_middle, Z_MIDDLE)
    near_one = fsdp_move(to_near, Z_NEAR)
    back_own = fsdp_move(low(wide(side_own) + only(z % 3 == 0, near_one)), Y_SWAP)
    to_near = low(wide(near) + jnp.where(inner, wide(middle_one), wide(back_two)))
    to_middle = low(wide(third) + wide(back_two) + wide(near_one))
    to_near, to_middle, _ = lax.optimization_barrier((to_near, to_middle, beside()))
    near_two = fsdp_move(to_near, Z_NEAR)
    middle_two = fsdp_move(to_middle, Z_MIDDLE)
    return low(wide(own) + wide(back_own) + wide(near_two) + only(inner, middle_two))


def lanes_of(shape):
    return lax.broadcasted_iota(jnp.int32, shape, 1)


def rows_of(shape):
    return lax.broadcasted_iota(jnp.int32, shape, 0)


def prepare_kernel(
    projection,
    out_weight,
    up_weight,
    down_weight,
    piece,
    up_own,
    up_lent,
    heads,
    down_own,
    down_lent,
    out_rows,
    sems,
):
    _, member_parity, x, core = position()
    quarter, other = 2 * x + core, 2 * x + 1 - core
    copies = []

    def fetch(source, goal):
        copies.append(pltpu.make_async_copy(source, goal, sems.at[len(copies)]))
        copies[-1].start()

    def tile(place):
        return pl.ds(pl.multiple_of(place * 128, 128), 128)

    for index in range(8):
        fetch(up_weight.at[:, tile(index * 4 + quarter)], up_own.at[index])
    for pair in range(4):
        fetch(up_weight.at[:, tile((2 * pair + 1 - core) * 4 + other)], up_lent.at[pair])
    for low in range(4):
        fetch(projection.at[:, :, tile(low * 2 + core)], heads.at[:, low])
    fetch(down_weight.at[tile(quarter)], down_own)
    fetch(down_weight.at[pl.ds(pl.multiple_of(other * 128 + 96, 32), 32)], down_lent)
    fetch(out_weight.at[pl.ds(pl.multiple_of(x * 64, 64), 64)], out_rows)
    for copy in copies:
        copy.wait()
    lane = lanes_of((128, 128))
    for index in range(8):
        half = index % 2
        taken = (lane >= 96) & (core == half)
        piece[index // 2, :, half * 128 : half * 128 + 128] = jnp.where(
            taken, wide(up_lent[index // 2]), wide(up_own[index])
        ).astype(jnp.bfloat16)
    for stream in range(3):
        for twin in range(2):
            tiles = [wide(heads[stream, 2 * twin + low]) for low in range(2)]
            first = jnp.where(x == 0, tiles[0], pltpu.roll(tiles[0], 64, 1))
            second = jnp.where(x == 0, pltpu.roll(tiles[1], 64, 1), tiles[1])
            piece[4 + stream, :, twin * 128 : twin * 128 + 128] = jnp.where(
                lane < 64, first, second
            ).astype(jnp.bfloat16)
    for block in range(4):
        cols = slice(block * 256, block * 256 + 256)
        band = slice(block * 32, block * 32 + 32)
        piece[7 + block, 0:96] = down_own[0:96, cols]

        @pl.when(member_parity == core)
        def _():
            piece[7 + block, 96:128] = out_rows[0:32, cols]
            piece[11, band] = out_rows[32:64, cols]

        @pl.when(member_parity != core)
        def _():
            piece[7 + block, 96:128] = down_own[96:128, cols]
            piece[11, band] = down_lent[:, cols]


def front_kernel(
    bounds,
    stack,
    mix_gain,
    up_own,
    up_one,
    up_two,
    up_three,
    mix_down,
    mix_static,
    norm_gain,
    norm_bias,
    packet,
    scaled_out,
    stats,
    stream_out,
    mix_up,
    streams,
):
    seqs = stack.shape[0]
    z, y, _, core = position()
    for step, part in ((0, up_own), (1 + 2 * core, up_one), (2, up_two), (3 - 2 * core, up_three)):
        z_from = (z + step) % 4
        for half, col in enumerate((y, 1 - y)):
            lanes = pl.ds(pl.multiple_of((2 * z_from + col) * 128, 128), 128)
            mix_up[:, lanes] = part[:, half * 128 : half * 128 + 128]
    for seq in range(seqs):
        last = wide(stack[seq, STREAMS_IN - 1])
        rms = lax.rsqrt(jnp.mean(last * last, axis=-1, keepdims=True) + EPSILON)
        mixed_in = (last * rms * mix_gain[...]).astype(jnp.bfloat16)
        hidden_pre = back_product(mixed_in, mix_up[...])
        hidden = wide(gelu_value(hidden_pre).astype(jnp.bfloat16))
        coef = jnp.dot(
            hidden, mix_down[...], precision=HIGHEST, preferred_element_type=jnp.float32
        )
        coef = coef + mix_static[...]
        at = slice(seq * SEQ, seq * SEQ + SEQ)
        stats[0, at, 0:36] = coef
        stats[1, at, 0:36] = hidden_pre
        stats[2, at, 4:5] = rms

        def mix(step, carry):
            row = pl.multiple_of(step // 2 * 16, 16)
            col = pl.multiple_of(step % 2 * 512, 512)
            rows_coef = stats[0, pl.ds(seq * SEQ + row, 16), :]
            totals = [None] * 4
            for layer in range(STREAMS_IN):
                value = wide(stack[seq, layer, pl.ds(row, 16), pl.ds(col, 512)])
                for stream in range(4):
                    at_coef = stream * STREAMS_IN + layer
                    term = rows_coef[:, at_coef : at_coef + 1] * value
                    totals[stream] = term if layer == 0 else totals[stream] + term
            for stream in range(4):
                streams[stream, pl.ds(seq * SEQ + row, 16), pl.ds(col, 512)] = totals[stream]
            return carry

        lax.fori_loop(0, 8, mix, 0)

    def norm(step, carry):
        row = pl.multiple_of(step * 16, 16)
        for stream in range(4):
            value = streams[stream, pl.ds(row, 16), :]
            center = value - jnp.mean(value, axis=-1, keepdims=True)
            inverse = lax.rsqrt(jnp.mean(center * center, axis=-1, keepdims=True) + EPSILON)
            scaled = center * inverse
            stats[2, pl.ds(row, 16), stream : stream + 1] = inverse
            scaled_out[stream, pl.ds(row, 16), :] = scaled
            packet[pl.ds(stream * ROWS + row, 16), :] = (
                scaled * norm_gain[stream : stream + 1, :] + norm_bias[stream : stream + 1, :]
            ).astype(jnp.bfloat16)
            if stream == 3:
                stream_out[pl.ds(row, 16), :] = value
        return carry

    lax.fori_loop(0, seqs * SEQ // 16, norm, 0)
    packet[4 * ROWS :] = jnp.zeros((16, WIDTH), jnp.bfloat16)
    row = rows_of((16, 128))
    marks = jnp.zeros((16, 128), jnp.float32)
    for place in range(2 * seqs):
        marks = jnp.where(row == place, wide(bounds[place]), marks)
    packet[4 * ROWS :, 0:128] = marks.astype(jnp.bfloat16)


def main_kernel(
    rope,
    packet0,
    packet1,
    packet2,
    packet3,
    cotangent0,
    cotangent1,
    cotangent2,
    cotangent3,
    piece0,
    piece1,
    piece2,
    piece3,
    piece4,
    piece5,
    piece6,
    piece7,
    piece8,
    piece9,
    piece10,
    chunk_low,
    chunk_high,
    chunk1,
    chunk2,
    chunk3,
    chunk4,
    chunk5,
    chunk6,
    chunk7,
    keep_own,
    keep_far,
    send_norm,
    keep_out,
    send_out,
    acts,
    marks,
    up_all,
    lin_all,
    down_all,
    out_rows,
    lhs_all,
    grad_pre,
    linear,
    grad_att,
    grad_lin,
    parts,
    tokens,
    packet_sems,
    piece_sems,
    chunk_sems,
    token_sems,
):
    z, y, _, core = position()
    origin = gather_order(z, y)
    target = scatter_order(z, y)
    packets = (packet0, packet1, packet2, packet3)
    cotangents = (cotangent0, cotangent1, cotangent2, cotangent3)
    piece, side, near, middle, middle_near, turned = piece0, piece1, piece2, piece3, piece4, piece5
    near_twice, side_two, side_three, over_z, over_y = piece6, piece7, piece8, piece9, piece10
    inner = (z == 1) | (z == 2)
    sources = (
        (piece, piece),
        (side, middle),
        (near, near),
        (turned, side_two),
        (middle, turned),
        (side_two, side_three),
        (middle_near, near_twice),
        (side_three, None),
    )
    chunks = (chunk1, chunk2, chunk3, chunk4, chunk5, chunk6, chunk7)
    member_rows = [pl.ds(pl.multiple_of(place * 128, 128), 128) for place in origin]

    def unit_copies(unit):
        return [
            pltpu.make_async_copy(
                packets[block].at[pl.ds(unit * ROWS, ROWS)],
                acts.at[unit, pl.ds(block * ROWS, ROWS)],
                packet_sems.at[block, unit],
            )
            for block in range(4)
        ]

    def piece_copies(index, ref, tail_ref):
        rows = member_rows[index]
        down = 7 if tail_ref is ref else 1
        lin_copies = [
            pltpu.make_async_copy(
                source.at[pl.ds(at, count)],
                lin_all.at[pl.ds(stream, count), rows],
                piece_sems.at[index, place],
            )
            for place, source, at, stream, count in (
                (0, ref, 4, 0, 2),
                (3, tail_ref, down - 1, 2, 1),
            )
        ]
        return lin_copies + [
            pltpu.make_async_copy(
                tail_ref.at[pl.ds(down, 5)], down_all.at[origin[index]], piece_sems.at[index, 1]
            ),
            pltpu.make_async_copy(
                ref.at[pl.ds(0, 4)], up_all.at[:, rows], piece_sems.at[index, 2]
            ),
        ]

    first = unit_copies(0) + unit_copies(1) + unit_copies(2)
    second = [
        pltpu.make_async_copy(
            cotangents[block],
            acts.at[4, pl.ds(block * ROWS, ROWS)],
            packet_sems.at[block, 4],
        )
        for block in range(4)
    ]
    for block in range(4):
        second.append(
            pltpu.make_async_copy(
                packets[block].at[pl.ds(4 * ROWS, 16)], marks.at[block], packet_sems.at[block, 5]
            )
        )
    third = unit_copies(3)
    for copy in first + second + third:
        copy.start()
    for index, (for_inner, for_ends) in enumerate(sources):
        copies = piece_copies(index, for_inner, for_inner)
        first += copies[:2]
        second.append(copies[2])
        third.append(copies[3])
        if for_inner is for_ends:
            for copy in copies:
                copy.start()
            continue
        ends = (
            piece_copies(index, over_z, over_y)
            if for_ends is None
            else piece_copies(index, for_ends, for_ends)
        )

        @pl.when(inner)
        def _():
            for copy in copies:
                copy.start()

        @pl.when(jnp.logical_not(inner))
        def _():
            for copy in ends:
                copy.start()

    for copy in first:
        copy.wait()
    for stream in range(3):
        linear[stream] = matmul(acts[stream], lin_all[stream])
    for copy in second:
        copy.wait()
    for pair in range(4):
        even = 2 * pair + core
        odd = 2 * pair + 1 - core
        for block in range(4):
            band = slice(block * 32, block * 32 + 32)
            cols = slice(block * 256, block * 256 + 256)
            out_rows[pair * 64 : pair * 64 + 32, cols] = down_all[even, block, 96:128]
            out_rows[pair * 64 + 32 : pair * 64 + 64, cols] = down_all[even, 4, band]
            down_all[even, block, 96:128] = down_all[odd, 4, band]

    grad_att[...] = back_product(acts[4], out_rows[...]).astype(jnp.bfloat16)
    cos_table = rope[0]
    sin_left = rope[1]
    sin_right = rope[2]
    scale = HEAD_DIM ** (-0.5)

    def turn(value, sign):
        return (
            value * cos_table
            + pltpu.roll(value, 120, 1) * (sign * sin_left)
            + pltpu.roll(value, 8, 1) * (sign * sin_right)
        )

    def units(block, carry):
        row = rows_of((ROWS, ROWS))
        lane = lanes_of((ROWS, ROWS))
        bound = wide(marks[block])

        def both(low, high):
            return jnp.where(row < SEQ, low, high), jnp.where(lane < SEQ, low, high)

        start_q, start_k = both(bound[0:1, 0:128], bound[1:2, 0:128])
        split_q, split_k = both(bound[2:3, 0:128], bound[3:4, 0:128])
        at_q = wide(row % SEQ)
        at_k = wide(lane % SEQ)
        same = (row // SEQ == lane // SEQ) & ((at_q >= split_q) == (at_k >= split_k))
        pic_q = (at_q >= start_q) & (at_q < start_q + PIC)
        pic_k = (at_k >= start_k) & (at_k < start_k + PIC)
        penalty = jnp.where(same & ((at_q >= at_k) | (pic_q & pic_k)), 0.0, -1e30)
        span = pl.ds(pl.multiple_of(block * ROWS, ROWS), ROWS)
        twins = [slice(twin * 128, twin * 128 + 128) for twin in range(2)]
        heads = [(twin, head) for twin in range(2) for head in range(2)]
        query = [turn(linear[0, span, cols], 1.0) for cols in twins]
        query_low = [item.astype(jnp.bfloat16) for item in query]
        key_low = [turn(linear[1, span, cols], 1.0).astype(jnp.bfloat16) for cols in twins]
        value_low = [linear[2, span, cols].astype(jnp.bfloat16) for cols in twins]
        grad_low = [grad_att[span, cols] for cols in twins]

        def only(item, head):
            return jnp.where(lane // 64 == head, wide(item), 0.0).astype(jnp.bfloat16)

        scores = [
            back_product(only(query[twin], head), key_low[twin]) * scale + penalty
            for twin, head in heads
        ]
        grad_probs = [
            back_product(only(grad_low[twin], head), value_low[twin]) for twin, head in heads
        ]
        exponent = [jnp.exp(item - jnp.max(item, axis=-1, keepdims=True)) for item in scores]
        probs = [item / jnp.sum(item, axis=-1, keepdims=True) for item in exponent]
        probs_low = [item.astype(jnp.bfloat16) for item in probs]
        grad_scores = [
            (prob * (grad - jnp.sum(prob * grad, axis=-1, keepdims=True))).astype(jnp.bfloat16)
            for prob, grad in zip(probs, grad_probs)
        ]
        attended = [matmul(probs_low[i], value_low[heads[i][0]]) for i in range(4)]
        grad_value = [outer_sum(probs_low[i], grad_low[heads[i][0]]) for i in range(4)]
        grad_query = [matmul(grad_scores[i], key_low[heads[i][0]]) for i in range(4)]
        grad_key = [outer_sum(grad_scores[i], query_low[heads[i][0]]) for i in range(4)]

        def merge(items, twin):
            return jnp.where(lane < 64, items[2 * twin], items[2 * twin + 1])

        for twin, cols in enumerate(twins):
            side = slice(WIDTH + twin * 128, WIDTH + twin * 128 + 128)
            lhs_all[span, side] = merge(attended, twin).astype(jnp.bfloat16)
            grad_lin[0, span, cols] = turn(merge(grad_query, twin) * scale, -1.0).astype(
                jnp.bfloat16
            )
            grad_lin[1, span, cols] = turn(merge(grad_key, twin) * scale, -1.0).astype(
                jnp.bfloat16
            )
            grad_lin[2, span, cols] = merge(grad_value, twin).astype(jnp.bfloat16)
        return carry

    lax.fori_loop(0, 4, units, 0, unroll=4)

    for copy in third:
        copy.wait()

    def hidden(pair, carry):
        cols = pl.ds(pl.multiple_of(pair * 256, 256), 256)
        up_pre = matmul(acts[3], up_all[pair])
        bell = 0.5 * (1.0 + lax.erf(up_pre * ROOT_HALF))
        slope = bell + up_pre * NORMAL_PEAK * jnp.exp(-0.5 * up_pre * up_pre)
        lhs_all[:, cols] = (up_pre * bell).astype(jnp.bfloat16)
        rows_down = jnp.concatenate(
            [
                jnp.concatenate([down_all[2 * pair + half, block] for block in range(4)], axis=1)
                for half in range(2)
            ]
        )
        grad_gated = back_product(acts[4], rows_down)
        grad_pre[:, cols] = (grad_gated * slope).astype(jnp.bfloat16)
        return carry

    lax.fori_loop(0, 4, hidden, 0, unroll=4)

    def weights(pair, carry):
        cols = pl.ds(pl.multiple_of(pair * 256, 256), 256)
        halves = (slice(0, 128), slice(128, 256))
        grad = outer_sum(acts[3, :, cols], grad_pre[...]).astype(jnp.bfloat16)
        for block in range(4):
            for half, rows in enumerate(halves):
                parts[2 * pair + half, block] = grad[rows, block * 256 : block * 256 + 256]
        for stream in range(3):
            grad = outer_sum(acts[stream, :, cols], grad_lin[stream]).astype(jnp.bfloat16)
            for half, rows in enumerate(halves):
                parts[2 * pair + half, 4 + stream] = grad[rows]
        grad = outer_sum(lhs_all[:, cols], acts[4]).astype(jnp.bfloat16)
        for half in range(2):
            index, other = 2 * pair + half, 2 * pair + 1 - half
            for block in range(4):
                part = grad[half * 128 : half * 128 + 128, block * 256 : block * 256 + 256]
                parts[index, 7 + block, 0:96] = part[0:96]

                @pl.when(core == half)
                def _():
                    parts[other, 11, block * 32 : block * 32 + 32] = part[96:128]

                @pl.when(core != half)
                def _():
                    parts[index, 7 + block, 96:128] = part[96:128]

        return carry

    lax.fori_loop(0, 4, weights, 0, unroll=4)
    grad = outer_sum(lhs_all[:, WIDTH:], acts[4]).astype(jnp.bfloat16)
    for block in range(4):
        part = grad[:, block * 256 : block * 256 + 256]
        for pair in range(4):
            even = 2 * pair + core
            parts[even, 7 + block, 96:128] = part[pair * 64 : pair * 64 + 32]
            parts[even, 11, block * 32 : block * 32 + 32] = part[pair * 64 + 32 : pair * 64 + 64]
    sent = [
        pltpu.make_async_copy(
            parts.at[target[0], pl.ds(0, PART)], chunk_low, chunk_sems.at[0]
        ),
        pltpu.make_async_copy(
            parts.at[target[0], pl.ds(PART, 12 - PART)], chunk_high, chunk_sems.at[8]
        ),
    ] + [
        pltpu.make_async_copy(parts.at[target[index]], chunks[index - 1], chunk_sems.at[index])
        for index in range(1, 8)
    ]
    for copy in sent:
        copy.start()

    def put(unit, cols, value):
        low = value.astype(jnp.bfloat16)
        for half in range(2):
            for block in range(2):
                at = (2 * half + block) * ROWS
                tokens[half, block, unit, :, cols] = low[at : at + ROWS]

    def ship(unit):
        if unit < 4:
            routes = (
                (tokens.at[0, 0, unit], keep_own.at[unit]),
                (tokens.at[0, 1, unit], keep_far.at[unit]),
                (tokens.at[1, :, unit], send_norm.at[:, unit]),
            )
        else:
            routes = ((tokens.at[0, :, unit], keep_out), (tokens.at[1, :, unit], send_out))
        for place, (source, goal) in enumerate(routes):
            copy = pltpu.make_async_copy(source, goal, token_sems.at[place, unit])
            copy.start()
            sent.append(copy)

    for stream in range(3):
        put(stream, slice(0, WIDTH), back_product(grad_lin[stream], lin_all[stream]))
        ship(stream)

    def feed(block, carry):
        cols = pl.ds(pl.multiple_of(block * 256, 256), 256)
        rows_up = jnp.concatenate([up_all[part, cols] for part in range(4)], axis=1)
        put(3, cols, back_product(grad_pre[...], rows_up))
        right = [down_all[index, block] for index in range(8)] + [out_rows[:, cols]]
        put(4, cols, matmul(lhs_all[...], jnp.concatenate(right)))
        return carry

    lax.fori_loop(0, 4, feed, 0, unroll=4)
    ship(3)
    ship(4)
    for copy in sent:
        copy.wait()


def back_kernel(
    stack,
    cotangent,
    scaled,
    stats,
    keep,
    came,
    across,
    mix_gain,
    mix_up,
    mix_down,
    norm_gain,
    stack_grad,
    small_own,
    small_other,
    coefficients,
    grads,
    sums,
    coef_grad,
    small,
):
    seqs = stack.shape[0]
    sums[...] = jnp.zeros_like(sums)
    lane = lanes_of((16, 128))

    def unit(step, carry):
        row = pl.multiple_of(step * 16, 16)
        span = pl.ds(row, 16)

        def result(index):
            return wide(keep[index, span]) + wide(came[0, index, span]) + wide(across[index, span])

        for stream in range(4):
            item = result(stream)
            scale = scaled[stream, span]
            moved = item * scale
            sums[stream] += moved[:8] + moved[8:]
            sums[4 + stream] += item[:8] + item[8:]
            weighted = item * norm_gain[stream : stream + 1]
            mean = jnp.mean(weighted, axis=-1, keepdims=True)
            slant = jnp.mean(weighted * scale, axis=-1, keepdims=True)
            grad = stats[2, span, stream : stream + 1] * (weighted - mean - scale * slant)
            if stream == 3:
                grad = grad + wide(cotangent[span])
            grads[stream, span] = grad
        return carry

    lax.fori_loop(0, seqs * SEQ // 16, unit, 0)
    for seq in range(seqs):

        def coefs(step, carry):
            row = pl.multiple_of(step * 16, 16)
            span = pl.ds(seq * SEQ + row, 16)
            found = jnp.zeros((16, 128), jnp.float32)
            for layer in range(STREAMS_IN):
                value = wide(stack[seq, layer, pl.ds(row, 16), :])
                for stream in range(4):
                    got = jnp.sum(grads[stream, span] * value, axis=-1, keepdims=True)
                    found = jnp.where(lane == stream * STREAMS_IN + layer, got, found)
            coef_grad[span] = found
            return carry

        lax.fori_loop(0, SEQ // 16, coefs, 0)
    grad_coef = coef_grad[:, 0:36]
    hidden_pre = stats[1, :, 0:36]
    hidden_low = gelu_value(hidden_pre).astype(jnp.bfloat16)
    for seq in range(seqs):
        turned = stats[0, seq * SEQ : seq * SEQ + SEQ, :].T
        for stream in range(4):
            for layer in range(STREAMS_IN):
                at = stream * STREAMS_IN + layer
                coefficients[seq, layer, stream : stream + 1] = turned[at : at + 1]
    small[...] = jnp.zeros_like(small)
    small[0:36, WIDTH : WIDTH + 36] = lax.dot_general(
        wide(hidden_low),
        grad_coef,
        (((0,), (0,)), ((), ())),
        precision=HIGHEST,
        preferred_element_type=jnp.float32,
    )
    small[36:37, WIDTH : WIDTH + 36] = jnp.sum(grad_coef, axis=0, keepdims=True)
    grad_hidden = (
        lax.dot_general(
            grad_coef,
            mix_down[...],
            (((1,), (1,)), ((), ())),
            precision=HIGHEST,
            preferred_element_type=jnp.float32,
        )
        * gelu_slope(hidden_pre)
    ).astype(jnp.bfloat16)
    gain_row = jnp.zeros((8, WIDTH), jnp.float32)
    up_part = jnp.zeros((36, WIDTH), jnp.float32)
    for seq in range(seqs):
        at = slice(seq * SEQ, seq * SEQ + SEQ)
        last = wide(stack[seq, STREAMS_IN - 1])
        rms = stats[2, at, 4:5]
        mixed_in = (last * rms * mix_gain[...]).astype(jnp.bfloat16)
        up_part = up_part + outer_sum(grad_hidden[at], mixed_in)
        grad_mixed = matmul(grad_hidden[at], mix_up[...])
        along = grad_mixed * last * rms
        for place in range(SEQ // 8):
            gain_row = gain_row + along[place * 8 : place * 8 + 8]
        weighted = grad_mixed * mix_gain[...]
        mean = jnp.mean(weighted * last, axis=-1, keepdims=True)
        grads[4, at] = rms * (weighted - last * (rms * rms * mean))

        def layers(step, carry):
            row = pl.multiple_of(step // 2 * 16, 16)
            cols = pl.ds(pl.multiple_of(step % 2 * 512, 512), 512)
            span = pl.ds(seq * SEQ + row, 16)
            rows_coef = stats[0, span, :]
            parts = [grads[stream, span, cols] for stream in range(4)]
            for layer in range(STREAMS_IN):
                total = None
                for stream in range(4):
                    at_coef = stream * STREAMS_IN + layer
                    term = rows_coef[:, at_coef : at_coef + 1] * parts[stream]
                    total = term if total is None else total + term
                if layer == STREAMS_IN - 1:
                    total = total + grads[4, span, cols]
                stack_grad[seq, layer, pl.ds(row, 16), cols] = total.astype(jnp.bfloat16)
            return carry

        lax.fori_loop(0, 8, layers, 0)
    small[0:36, 0:WIDTH] = up_part
    for place in range(8):
        small[36 + place : 37 + place, 0:WIDTH] = jnp.sum(sums[place], axis=0, keepdims=True)
    small[44:45, 0:WIDTH] = jnp.sum(gain_row, axis=0, keepdims=True)
    _, _, _, core = position()
    small_own[...] = small[pl.ds(pl.multiple_of(core * 24, 8), 24), :]
    small_other[...] = small[pl.ds(pl.multiple_of(24 - core * 24, 8), 24), :]


def place_kernel(
    shard0,
    shard1,
    shard2,
    shard3,
    small_own,
    small_other,
    projection,
    out_grad,
    up_grad,
    down_grad,
    mix_gain_grad,
    mix_up_grad,
    mix_down_grad,
    mix_static_grad,
    gain_grad,
    bias_grad,
    small,
):
    z, member_parity, x, core = position()
    small[pl.ds(pl.multiple_of(core * 24, 8), 24), :] = small_own[...]
    small[pl.ds(pl.multiple_of(24 - core * 24, 8), 24), :] = small_other[...]
    lanes = pl.ds(pl.multiple_of((2 * z + member_parity) * 128, 128), 128)
    mix_up_grad[...] = small[0:36, lanes]
    gain_grad[...] = small[36:40, 0:WIDTH]
    bias_grad[...] = small[40:44, 0:WIDTH]
    mix_gain_grad[...] = small[44:45, 0:WIDTH]
    mix_down_grad[...] = small[0:36, WIDTH : WIDTH + 36]
    for stream in range(4):
        at = WIDTH + stream * STREAMS_IN
        mix_static_grad[stream : stream + 1] = small[36:37, at : at + STREAMS_IN]
    shards = (shard0, shard1, shard2, shard3)
    lane = lanes_of((128, 128))
    for back in range(4):
        from_x = x if back % 2 == 0 else 1 - x
        from_core = core if back < 2 else 1 - core
        quarter = 2 * from_x + from_core
        own, twin = shards[back], shards[back ^ 2]
        for index in range(8):
            half = index % 2
            mine = wide(own[index // 2, :, half * 128 : half * 128 + 128])
            half_b = 1 - half
            lent = wide(twin[index // 2, :, half_b * 128 : half_b * 128 + 128])
            col = pl.multiple_of((index * 4 + quarter) * 128, 128)
            up_grad[:, pl.ds(col, 128)] = jnp.where(
                (lane >= 96) & (from_core == half), lent, mine
            )
        row = pl.multiple_of(quarter * 128, 128)
        for block in range(4):
            cols = slice(block * 256, block * 256 + 256)
            down_grad[pl.ds(row, 96), cols] = wide(own[7 + block, 0:96])

            @pl.when(member_parity == from_core)
            def _():
                head_row = pl.multiple_of(from_x * 64, 64)
                out_grad[pl.ds(head_row, 32), cols] = wide(own[7 + block, 96:128])
                out_grad[pl.ds(head_row + 32, 32), cols] = wide(
                    own[11, block * 32 : block * 32 + 32]
                )
                down_grad[pl.ds(row + 96, 32), cols] = wide(
                    twin[11, block * 32 : block * 32 + 32]
                )

            @pl.when(member_parity != from_core)
            def _():
                down_grad[pl.ds(row + 96, 32), cols] = wide(own[7 + block, 96:128])

    for back in (0, 2):
        from_core = core if back < 2 else 1 - core
        for stream in range(3):
            for twin in range(2):
                tile = slice(twin * 128, twin * 128 + 128)
                mine = wide(shards[back][4 + stream, :, tile])
                across = wide(shards[back + 1][4 + stream, :, tile])
                even = jnp.where(x == 0, mine, across)
                odd = jnp.where(x == 0, across, mine)
                first = jnp.where(lane < 64, even, pltpu.roll(odd, 64, 1))
                second = jnp.where(lane < 64, pltpu.roll(even, 64, 1), odd)
                for low, value in ((0, first), (1, second)):
                    col = pl.multiple_of((2 * twin + low) * 256 + from_core * 128, 128)
                    projection[stream, :, pl.ds(col, 128)] = value


def call(kernel, outs, specs, out_specs, args, scratch=(), cost=None, vmem=60 << 20):
    return pl.pallas_call(
        kernel,
        out_shape=outs,
        in_specs=specs,
        out_specs=out_specs,
        scratch_shapes=list(scratch),
        compiler_params=pltpu.CompilerParams(vmem_limit_bytes=vmem),
        cost_estimate=cost,
    )(*args)


def shape_of(shape, dtype=jnp.bfloat16):
    return jax.ShapeDtypeStruct(shape, dtype)


def rope_tables():
    half_rot = ROTARY // 2
    step = 10000.0 ** (-2.0 * np.arange(half_rot) / ROTARY)
    angles = np.arange(SEQ)[:, None] * step[None, :]
    cos_table = np.ones((SEQ, HEAD_DIM))
    left = np.zeros((SEQ, HEAD_DIM))
    right = np.zeros((SEQ, HEAD_DIM))
    cos_table[:, :half_rot] = np.cos(angles)
    cos_table[:, half_rot:ROTARY] = np.cos(angles)
    left[:, :half_rot] = -np.sin(angles)
    right[:, half_rot:ROTARY] = np.sin(angles)
    return np.stack([np.tile(item, (2, 2)) for item in (cos_table, left, right)]).astype(np.float32)


def on_device_tensor(
    layer_stack,
    out_cotangent,
    pic_start,
    doc_split,
    mix_gain,
    mix_up,
    mix_down,
    mix_static,
    norm_gain,
    norm_bias,
    query_key_value,
    out_weight,
    up_weight,
    down_weight,
):
    z, y, _, _ = position()
    micro_total, local_seqs, _, _, width = layer_stack.shape
    seqs = micro_total * local_seqs
    stack = jnp.transpose(layer_stack, (0, 1, 3, 2, 4)).reshape(seqs, STREAMS_IN, SEQ, width)
    cotangent = out_cotangent.reshape(ROWS, width)
    gain_row = mix_gain.reshape(1, width)

    piece = call(
        prepare_kernel,
        shape_of((12, 128, 256)),
        [IN_PLACE] * 4,
        VMEM_FULL,
        (query_key_value, out_weight, up_weight, down_weight),
        scratch=[
            pltpu.VMEM((8, 128, 128), jnp.bfloat16),
            pltpu.VMEM((4, 128, 128), jnp.bfloat16),
            pltpu.VMEM((3, 4, 128, 128), jnp.bfloat16),
            pltpu.VMEM((128, width), jnp.bfloat16),
            pltpu.VMEM((32, width), jnp.bfloat16),
            pltpu.VMEM((64, width), jnp.bfloat16),
            pltpu.SemaphoreType.DMA((19,)),
        ],
        vmem=60 << 20,
    )
    up_own = mix_up.T
    up_pair = jnp.concatenate([up_own, after(lax.ppermute(up_own, "fsdp", Y_SWAP), piece)], axis=1)
    up_one = fsdp_move(
        up_pair,
        [((index + 8 + index % 2 * 16) % 32, index) for index in range(32)],
    )
    up_two = fsdp_move(up_pair, Z_SWAP_FAR)
    ups = (up_pair, up_one, up_two)
    piece = after(piece, *ups)
    up_three = lax.ppermute(up_one, "replica", CORE_SWAP)
    ups += (up_three,)
    bounds = jnp.concatenate([pic_start.reshape(seqs), doc_split.reshape(seqs)])
    kept = {}
    grad_across = lax.ppermute(cotangent, "replica", X_SWAP)
    grad_packets = (
        cotangent,
        grad_across,
        lax.ppermute(cotangent, "replica", CORE_SWAP),
        lax.ppermute(grad_across, "replica", CORE_SWAP),
    )

    def front():
        packet, *kept["rest"] = call(
            front_kernel,
            (
                shape_of((4 * ROWS + 16, width)),
                shape_of((4, ROWS, width), jnp.float32),
                shape_of((3, ROWS, 128), jnp.float32),
                shape_of((ROWS, width), jnp.float32),
                shape_of((36, width)),
            ),
            [SMEM_FULL] + [VMEM_FULL] * 10,
            (VMEM_FULL,) * 5,
            (
                bounds,
                stack,
                gain_row,
                *ups,
                mix_down,
                mix_static.reshape(1, 36),
                norm_gain,
                norm_bias,
            ),
            scratch=[pltpu.VMEM((4, ROWS, width), jnp.float32)],
            vmem=30 << 20,
        )
        across = lax.ppermute(packet, "replica", X_SWAP)
        beside = lax.ppermute(packet, "replica", CORE_SWAP)
        beside_across = lax.ppermute(across, "replica", CORE_SWAP)
        kept["packets"] = (packet, across, beside, beside_across)
        return (packet, grad_across), (across,)

    pieces = gather_fsdp(piece, z, front)
    packets = kept["packets"]
    scaled, stats, stream_last, mix_up_full = kept["rest"]

    results = call(
        main_kernel,
        (shape_of((PART, 128, 256)), shape_of((12 - PART, 128, 256)))
        + (shape_of((12, 128, 256)),) * 7
        + (shape_of((4, ROWS, width)),) * 2
        + (shape_of((2, 4, ROWS, width)),)
        + (shape_of((2, ROWS, width)),) * 2,
        [VMEM_FULL] + [IN_PLACE] * 19,
        (IN_PLACE,) * 14,
        (jnp.asarray(rope_tables()),) + packets + grad_packets + tuple(pieces),
        scratch=[
            pltpu.VMEM((5, 4 * ROWS, width), jnp.bfloat16),
            pltpu.VMEM((4, 16, width), jnp.bfloat16),
            pltpu.VMEM((4, width, 256), jnp.bfloat16),
            pltpu.VMEM((3, width, 256), jnp.bfloat16),
            pltpu.VMEM((8, 5, 128, 256), jnp.bfloat16),
            pltpu.VMEM((256, width), jnp.bfloat16),
            pltpu.VMEM((4 * ROWS, width + 256), jnp.bfloat16),
            pltpu.VMEM((4 * ROWS, width), jnp.bfloat16),
            pltpu.VMEM((3, 4 * ROWS, 256), jnp.float32),
            pltpu.VMEM((4 * ROWS, 256), jnp.bfloat16),
            pltpu.VMEM((3, 4 * ROWS, 256), jnp.bfloat16),
            pltpu.VMEM((8, 12, 128, 256), jnp.bfloat16),
            pltpu.VMEM((2, 2, 5, ROWS, width), jnp.bfloat16),
            pltpu.SemaphoreType.DMA((4, 6)),
            pltpu.SemaphoreType.DMA((8, 4)),
            pltpu.SemaphoreType.DMA((9,)),
            pltpu.SemaphoreType.DMA((3, 5)),
        ],
        vmem=42 << 20,
    )
    chunks = results[:9]
    keep_own, keep_far, send_norm, keep_out, send_out = results[9:]

    came = lax.ppermute(send_norm, "replica", CORE_SWAP)
    sum_across = (wide(keep_far) + wide(came[1])).astype(jnp.bfloat16)
    came_across = lax.ppermute(sum_across, "replica", X_SWAP)
    out_came = lax.ppermute(after(send_out, sum_across), "replica", CORE_SWAP)
    out_across = (wide(keep_out[1]) + wide(out_came[1])).astype(jnp.bfloat16)
    out_across = lax.ppermute(after(out_across, came_across), "replica", X_SWAP)
    layer_output = (
        stream_last + wide(keep_out[0]) + wide(out_came[0]) + wide(out_across)
    ).astype(jnp.bfloat16)

    first_half = pl.BlockSpec((1, 4, ROWS, width), lambda step: (0, 0, 0, 0))

    def whole(shape):
        return pl.BlockSpec(shape, lambda step: (0,) * len(shape))

    def back():
        kept["back"] = pl.pallas_call(
            back_kernel,
            grid=(1,),
            out_shape=(
                shape_of((seqs, STREAMS_IN, SEQ, width)),
                shape_of((24, width + 128), jnp.float32),
                shape_of((24, width + 128), jnp.float32),
                shape_of((seqs, STREAMS_IN, 4, SEQ), jnp.float32),
            ),
            in_specs=[
                whole((seqs, STREAMS_IN, SEQ, width)),
                whole((ROWS, width)),
                whole((4, ROWS, width)),
                whole((3, ROWS, 128)),
                whole((4, ROWS, width)),
                first_half,
                whole((4, ROWS, width)),
                whole((1, width)),
                whole((36, width)),
                whole((36, 36)),
                whole((4, width)),
            ],
            out_specs=(
                whole((seqs, STREAMS_IN, SEQ, width)),
                whole((24, width + 128)),
                whole((24, width + 128)),
                whole((seqs, STREAMS_IN, 4, SEQ)),
            ),
            scratch_shapes=[
                pltpu.VMEM((5, ROWS, width), jnp.float32),
                pltpu.VMEM((8, 8, width), jnp.float32),
                pltpu.VMEM((ROWS, 128), jnp.float32),
                pltpu.VMEM((48, width + 128), jnp.float32),
            ],
            compiler_params=pltpu.CompilerParams(vmem_limit_bytes=56 << 20),
        )(
            stack,
            cotangent,
            scaled,
            stats,
            keep_own,
            came,
            came_across,
            gain_row,
            mix_up_full,
            mix_down,
            norm_gain,
        )
        return kept["back"][1]

    shard = scatter_fsdp(chunks, z, sum_across, back)
    stack_grad, small, small_other, coefficients = kept["back"]

    small = small + lax.ppermute(small_other, "replica", CORE_SWAP)
    small = small + lax.ppermute(small, "replica", X_SWAP)
    small = small + lax.ppermute(small, "fsdp", Y_SWAP)
    shard = after(shard, small, out_across)
    shard_across = lax.ppermute(shard, "replica", X_SWAP)
    shard_beside = lax.ppermute(shard, "replica", CORE_SWAP)
    for perm in (Z_SWAP_NEAR, Z_SWAP_FAR):
        small = small + lax.ppermute(small, "fsdp", perm)
    small_beside = lax.ppermute(small, "replica", CORE_SWAP)
    shard_both = lax.ppermute(after(shard_across, small), "replica", CORE_SWAP)
    owned = call(
        place_kernel,
        (
            shape_of((3, 128, width), jnp.float32),
            shape_of((128, width), jnp.float32),
            shape_of((128, 4 * width), jnp.float32),
            shape_of((512, width), jnp.float32),
            shape_of((1, width), jnp.float32),
            shape_of((36, 128), jnp.float32),
            shape_of((36, 36), jnp.float32),
            shape_of((4, STREAMS_IN), jnp.float32),
            shape_of((4, width), jnp.float32),
            shape_of((4, width), jnp.float32),
        ),
        [VMEM_FULL] * 6,
        (VMEM_FULL,) * 10,
        (shard, shard_across, shard_beside, shard_both, small, small_beside),
        scratch=[pltpu.VMEM((48, width + 128), jnp.float32)],
        vmem=14 << 20,
    )
    projection_grad, out_grad, up_grad, down_grad, *small_grads = owned
    shape = (micro_total, local_seqs, SEQ)
    stack_grad = stack_grad.reshape(micro_total, local_seqs, STREAMS_IN, SEQ, width)
    coefficients = coefficients.reshape(micro_total, local_seqs, STREAMS_IN, 4, SEQ)
    return (
        layer_output.reshape(shape + (width,)),
        jnp.transpose(coefficients, (0, 1, 4, 3, 2)),
        jnp.transpose(stack_grad, (0, 1, 3, 2, 4)),
        small_grads[0].reshape(width),
        small_grads[1].T,
        small_grads[2],
        small_grads[3],
        small_grads[4],
        small_grads[5],
        projection_grad,
        out_grad,
        up_grad,
        down_grad,
    )


def solution(mesh):
    fits = mesh.shape["fsdp"] == 8 and mesh.shape["replica"] == 4
    body = on_device_tensor if fits else on_device
    return jax.shard_map(
        body,
        mesh=mesh,
        in_specs=(
            P(None, ("fsdp", "replica"), None, None, None),
            P(None, ("fsdp", "replica"), None, None),
            P(None, ("fsdp", "replica")),
            P(None, ("fsdp", "replica")),
            P(),
            P("fsdp", None),
            P(),
            P(),
            P(),
            P(),
            P(None, "fsdp", None),
            P("fsdp", None),
            P("fsdp", None),
            P("fsdp", None),
        ),
        out_specs=(
            P(None, ("fsdp", "replica"), None, None),
            P(None, ("fsdp", "replica"), None, None, None),
            P(None, ("fsdp", "replica"), None, None, None),
            P(),
            P("fsdp", None),
            P(),
            P(),
            P(),
            P(),
            P(None, "fsdp", None),
            P("fsdp", None),
            P("fsdp", None),
            P("fsdp", None),
        ),
        check_vma=False,
    )
```
